32 devices in a mesh: narrow: 2 (over y), wide: 16 (over z, x, core).
Axes of the slice: x: 2, y: 2, z: 4, core: 2. Of those that a mesh axis runs over, the one named last changes fastest.
Arguments:
- tokens: bfloat16 [2, 16384, 768], P(None, ('narrow', 'wide')), may hold values from -6 to 6
- image_ids: int32 [2, 16384], P(None, ('narrow', 'wide')), may hold values from -1 to 1, as said below
- cotangent: bfloat16 [2, 16384, 768], P(None, ('narrow', 'wide')), may hold values from -6 to 6
- w_joined: bfloat16 [768, 5376], P('wide'), may hold values from -0.21875 to 0.21875
- w_out: bfloat16 [768, 768], P('wide'), may hold values from -1 to 1
- w_mlp: bfloat16 [3072, 768], P('wide'), may hold values from -0.109375 to 0.109375
- norm_gain: bfloat16 [768], P('wide'), may hold values from 0.5 to 1.5
- bias_attn: bfloat16 [1536], P('wide'), may hold values from -1.1953125 to 1.1953125
- bias_mlp: bfloat16 [3072], P('wide'), may hold values from -1.1953125 to 1.1953125
- bias_out: bfloat16 [768], P('wide'), may hold values from -1.1953125 to 1.1953125
Outputs:
- block_out: bfloat16 [2, 16384, 768], P(None, ('narrow', 'wide'))
- d_tokens: bfloat16 [2, 16384, 768], P(None, ('narrow', 'wide'))
- grad_joined: float32 [768, 5376], P('wide')
- grad_out: float32 [768, 768], P('wide')
- grad_mlp: float32 [3072, 768], P('wide')
- grad_gain: float32 [768], P('wide')
- grad_bias_attn: float32 [1536], P('wide')
- grad_bias_mlp: float32 [3072], P('wide')
- grad_bias_out: float32 [768], P('wide')
The draws below stay inside these ranges and needn't reach their ends.
Inputs may be any that keep to these rules, and one draw needn't show every extreme that they name: `image_ids`: each block of 512 consecutive tokens (one device's share of a micro-batch) holds either one image of 512 tokens, all with id 0, or 2 images of 196 tokens in order with ids 0, 1, ..., followed by padding tokens with id -1. Every micro-batch has blocks of both kinds.
All inputs are finite; a program needn't handle non-finite values.
Results may differ from the reference program's by a relative error of at most 0.0083.
Values may be sent and summed in bfloat16 or wider, within the bound.
No kernel may reach another device: no remote copies, remote signals or barrier semaphores. Data moves between devices by JAX's collectives and lax.ppermute only.
A program may use at most 192 MiB of HBM per device.

```python
import jax
import jax.numpy as jnp
from jax import lax

D = 768
HEADS = 12
FF = 3072
BLK = 512
SMALL_IMG = 196
MICRO = 2
TOKENS = 16384
JOINED = 5376


def draw_image_ids(key, part):
    blocks = TOKENS // BLK
    key_rare, key_pick = jax.random.split(jax.random.fold_in(key, 11))
    rare = jax.random.randint(key_rare, (MICRO, blocks), 0, 16) == 0
    chosen = jax.random.randint(key_pick, (MICRO, 1), 0, blocks)
    block_index = jnp.arange(blocks)[None, :]
    whole_image = (rare | (block_index == chosen)) & (block_index != (chosen + 1) % blocks)
    position = jnp.arange(BLK)
    images = BLK // SMALL_IMG
    small_ids = jnp.where(position < images * SMALL_IMG, position // SMALL_IMG, -1)
    result = jnp.where(whole_image[:, :, None], 0, small_ids[None, None, :])
    return result.reshape(MICRO, TOKENS).astype(jnp.int32)


def steps_of(rng, dims, shards, smallest, high):
    factor_of = 1.0
    for axis_at, shards_of in shards:
        heights = jax.random.uniform(jax.random.fold_in(jax.random.fold_in(rng, 6), axis_at), (shards_of,), jnp.float32, smallest / len(shards), high / len(shards))
        factor_of = factor_of * jnp.repeat(jnp.exp(heights), dims[axis_at] // shards_of).reshape((-1,) + (1,) * (len(dims) - 1 - axis_at))
    return factor_of


def bell_draw(stream_key, extent, spread, most, pieces=(), dtype=jnp.bfloat16):
    values = jax.random.normal(stream_key, extent, jnp.float32) * spread
    if len(pieces) > 0:
        values = steps_of(stream_key, extent, pieces, -0.22, 0.18) * values
    return jnp.clip(values, min=-most, max=most).astype(dtype)


def setup_inputs(seed: int = 0) -> dict:
    streams_of = jax.random.split(jax.random.key(seed), 11)
    tokens = bell_draw(streams_of[0], (MICRO, TOKENS, D), 1.0, 6.0, ((1, 32),))
    image_ids = draw_image_ids(jax.random.fold_in(streams_of[10], 71), 0)
    cotangent = bell_draw(streams_of[2], (MICRO, TOKENS, D), 1.0, 6.0, ((1, 32),))
    w_joined = bell_draw(streams_of[3], (D, JOINED), D ** -0.5, 0.21875, ((0, 16),))
    w_out = bell_draw(streams_of[4], (D, D), 32 ** -0.5, 1.0, ((0, 16),))
    w_mlp = bell_draw(streams_of[5], (FF, D), FF ** -0.5, 0.109375, ((0, 16),))
    norm_gain = jnp.clip(1.0 + 0.1 * jax.random.normal(streams_of[6], (D,), jnp.float32), 0.5, 1.5).astype(jnp.bfloat16)
    bias_attn = bell_draw(streams_of[7], (2 * D,), 0.2, 1.1953125, ((0, 16),))
    bias_mlp = bell_draw(streams_of[8], (FF,), 0.2, 1.1953125, ((0, 16),))
    bias_out = bell_draw(streams_of[9], (D,), 0.2, 1.1953125, ((0, 16),))
    return {"tokens": tokens, "image_ids": image_ids, "cotangent": cotangent, "w_joined": w_joined, "w_out": w_out, "w_mlp": w_mlp, "norm_gain": norm_gain, "bias_attn": bias_attn, "bias_mlp": bias_mlp, "bias_out": bias_out}


@jax.custom_vjp
def low(v):
    return lax.optimization_barrier(v.astype(jnp.bfloat16)).astype(jnp.float32)

@jax.custom_vjp
def low_back(v):
    return v

def low_keep(v):
    return (low(v), None)

def low_pass(kept, grad):
    return (grad,)

def back_keep(v):
    return (v, None)

def back_low(kept, grad):
    return (low(grad),)
low.defvjp(low_keep, low_pass)
low_back.defvjp(back_keep, back_low)
norm_eps = 1e-06
masked_score = -1e+30
highest = lax.Precision.HIGHEST

def gelu_tanh(inputs):
    inner = 0.7978845608028654 * (inputs + 0.044715 * inputs * inputs * inputs)
    return 0.5 * inputs * (1.0 + jnp.tanh(inner))

def block_group(params, block_item):
    w_joined, w_out, w_mlp, norm_gain, bias_attn, bias_mlp, bias_out = params
    block_rows, block_ids = block_item
    block_count, block_len, model_width = block_rows.shape
    head_count = HEADS
    head_size = model_width // head_count
    score_scale = head_size ** (-0.5)
    row_mean = lax.optimization_barrier(jnp.mean(block_rows, axis=2, keepdims=True))
    centered = block_rows - row_mean
    inverse_std = lax.rsqrt(lax.optimization_barrier(jnp.mean(centered * centered, axis=2, keepdims=True)) + norm_eps)
    normed = low(centered * inverse_std * norm_gain)
    bias_full = jnp.concatenate([bias_attn[:model_width], jnp.zeros((model_width,), jnp.float32), bias_attn[model_width:], bias_mlp])
    joined = low_back(jnp.einsum('gtc,cf->gtf', normed, w_joined, precision=highest) + bias_full)
    attn_part = low(joined[:, :, :3 * model_width])
    pre_act = joined[:, :, 3 * model_width:]
    query_rows = attn_part[:, :, :model_width].reshape(block_count, block_len, head_count, head_size)
    key_rows = attn_part[:, :, model_width:2 * model_width].reshape(block_count, block_len, head_count, head_size)
    value_rows = attn_part[:, :, 2 * model_width:].reshape(block_count, block_len, head_count, head_size)
    scores = low_back(jnp.einsum('gqhe,gkhe->ghqk', query_rows, key_rows, precision=highest) * score_scale)
    same_image = (block_ids[:, :, None] == block_ids[:, None, :])[:, None]
    probs = low(jax.nn.softmax(jnp.where(same_image, scores, masked_score), axis=-1))
    attended = low(low_back(jnp.einsum('ghqk,gkhe->gqhe', probs, value_rows, precision=highest)))
    attended = attended.reshape(block_count, block_len, model_width)
    activated = low(gelu_tanh(pre_act))
    attn_branch = jnp.einsum('gtc,cd->gtd', attended, w_out, precision=highest)
    mlp_branch = jnp.einsum('gtf,fd->gtd', activated, w_mlp, precision=highest)
    return block_rows + attn_branch + mlp_branch + bias_out

def forward(tokens, w_joined, w_out, w_mlp, norm_gain, bias_attn, bias_mlp, bias_out, image_ids):
    micro_count, slot_count, model_width = tokens.shape
    blocks = micro_count * slot_count // BLK
    group_size = 4 if blocks % 4 == 0 else 1
    block_rows = tokens.reshape(blocks // group_size, group_size, BLK, model_width)
    block_ids = image_ids.reshape(blocks // group_size, group_size, BLK)
    params = (w_joined, w_out, w_mlp, norm_gain, bias_attn, bias_mlp, bias_out)
    step_fn = jax.checkpoint(lambda block_item: block_group(params, block_item))
    result = lax.map(step_fn, (block_rows, block_ids))
    return result.reshape(micro_count, slot_count, model_width)

def reference(tokens, image_ids, cotangent, w_joined, w_out, w_mlp, norm_gain, bias_attn, bias_mlp, bias_out):

    def closed(tok_arr, joined_arr, out_arr, mlp_arr, gain_arr, battn_arr, bmlp_arr, bout_arr):
        return forward(tok_arr, joined_arr, out_arr, mlp_arr, gain_arr, battn_arr, bmlp_arr, bout_arr, image_ids)
    output, back_fn = jax.vjp(closed, tokens.astype(jnp.float32), w_joined.astype(jnp.float32), w_out.astype(jnp.float32), w_mlp.astype(jnp.float32), norm_gain.astype(jnp.float32), bias_attn.astype(jnp.float32), bias_mlp.astype(jnp.float32), bias_out.astype(jnp.float32))
    grads = back_fn(cotangent.astype(jnp.float32))
    return (output.astype(jnp.bfloat16), grads[0].astype(jnp.bfloat16), grads[1], grads[2], grads[3], grads[4], grads[5], grads[6], grads[7])
```

```python
import functools

import jax
import jax.numpy as jnp
import numpy as np
from jax import lax
from jax.experimental import pallas as pl
from jax.experimental.pallas import tpu as pltpu
from jax.sharding import PartitionSpec as P

HEADS = 12
HEAD = 64
IMG = 196
EPS = 1e-06
GELU_C = 0.7978845608028654
GELU_A = 0.044715

F32 = jnp.float32
BF16 = jnp.bfloat16
ANY = pl.BlockSpec(memory_space=pl.ANY)
VMEM = pl.BlockSpec(memory_space=pltpu.VMEM)
SMEM = pl.BlockSpec(memory_space=pltpu.SMEM)


def dot_nn(a, b):
    return lax.dot_general(a, b, (((1,), (0,)), ((), ())), preferred_element_type=F32)


def dot_nt(a, b):
    return lax.dot_general(a, b, (((1,), (1,)), ((), ())), preferred_element_type=F32)


def dot_tn(a, b):
    return lax.dot_general(a, b, (((0,), (0,)), ((), ())), preferred_element_type=F32)


def norm_rows(rows):
    rows = rows.astype(F32)
    mean = jnp.mean(rows, axis=1, keepdims=True)
    centered = rows - mean
    inv = lax.rsqrt(jnp.mean(centered * centered, axis=1, keepdims=True) + EPS)
    return centered * inv, inv


def params(limit=63 << 20):
    return pltpu.CompilerParams(vmem_limit_bytes=limit)


def attend(q_ref, k_ref, v_ref, da_ref, o_ref, dq_ref, dk_ref, dv_ref, base, cols, start, rows, lo, hi, merge):
    win = pl.ds(pl.multiple_of(base + start, 16), rows)
    q2, k2, v2, da2 = q_ref[win, cols], k_ref[win, cols], v_ref[win, cols], da_ref[win, cols]
    lane = lax.broadcasted_iota(jnp.int32, (rows, 128), 1)
    masked = lo > 0 or hi < rows
    step = 256 if rows == 512 else rows
    outs, dqs = [], []
    dk = jnp.zeros((rows, 128), F32)
    dv = jnp.zeros((rows, 128), F32)
    zero = jnp.zeros((), BF16)
    heads = []
    for h in range(2):
        keep = (lane < 64) if h == 0 else (lane >= 64)
        heads.append([jnp.where(keep, t, zero) for t in (q2, k2, v2, da2)])
    for at in range(0, rows, step):
        qs = slice(at, at + step)
        out = jnp.zeros((step, 128), F32)
        dq = jnp.zeros((step, 128), F32)
        for h in range(2):
            qh, kh, vh, dah = heads[h]
            s = dot_nt(k2, qh[qs])
            if masked:
                key = lax.broadcasted_iota(jnp.int32, (rows, step), 0)
                s = jnp.where((key >= lo) & (key < hi), s, -1e30)
            top = jnp.max(s, axis=0, keepdims=True)
            e = jnp.exp(s - top)
            total = jnp.sum(e, axis=0, keepdims=True)
            scale = 1.0 / total
            if masked:
                query = lax.broadcasted_iota(jnp.int32, (1, step), 1) + at
                scale = jnp.where((query >= lo) & (query < hi), scale, 0.0)
            p = e * scale
            pb = p.astype(BF16)
            dp = dot_nt(v2, dah[qs])
            inner = jnp.sum(p * dp, axis=0, keepdims=True)
            ds = (p * (dp - inner)).astype(BF16)
            out += dot_tn(pb, vh)
            dq += dot_tn(ds, kh)
            dv += dot_nn(pb, dah[qs])
            dk += dot_nn(ds, qh[qs])
        outs.append(out)
        dqs.append(dq * 0.125)
    for ref, val in ((o_ref, outs), (dq_ref, dqs), (dk_ref, [dk]), (dv_ref, [dv])):
        val = val[0] if len(val) == 1 else jnp.concatenate(val, axis=0)
        val = val.astype(BF16)
        if merge:
            head = pl.ds(pl.multiple_of(base + start, 16), merge)
            rest = pl.ds(pl.multiple_of(base + start + merge, 16), rows - merge)
            ref[head, cols] = ref[head, cols] + val[:merge]
            ref[rest, cols] = val[merge:]
        else:
            ref[win, cols] = val


def attn_kernel(load, store, n_w, n_g, *refs):
    scal, x_ref, cot_ref, vec_ref = refs[:4]
    w_refs = refs[4 : 4 + n_w]
    at = 4 + n_w
    g_refs = refs[at : at + n_g]
    xn_ref, acc_ref, dn_ref, sums_ref = refs[at + n_g : at + n_g + 4]
    w, q, k, v, da, o, dq, dk, dv, g, wsem, gsem = refs[at + n_g + 4 :]
    width = x_ref.shape[1]
    tokens = x_ref.shape[0]
    waits = load(scal, w_refs, w, wsem)
    rb = 256

    def rows_of(i):
        return pl.ds(pl.multiple_of(i * rb, rb), rb)

    gain = vec_ref[0:1, :]

    def norm(i, c):
        r = rows_of(i)
        standard, _ = norm_rows(x_ref[r, :])
        xn_ref[r, :] = (standard * gain).astype(BF16)
        return c

    lax.fori_loop(0, tokens // rb, norm, 0)
    waits()

    def project(i, c):
        r = rows_of(i)
        xr = xn_ref[r, :]
        q[r, :] = (dot_nn(xr, w[0]) + vec_ref[1:2, :]).astype(BF16) * jnp.asarray(0.125, BF16)
        k[r, :] = dot_nn(xr, w[1]).astype(BF16)
        v[r, :] = (dot_nn(xr, w[2]) + vec_ref[2:3, :]).astype(BF16)
        da[r, :] = dot_nt(cot_ref[r, :], w[3]).astype(BF16)
        return c

    lax.fori_loop(0, tokens // rb, project, 0)
    blocks = tokens // 512
    pairs = width // 128

    for b in range(blocks):
        whole = scal[8 + b] == 0

        def pair(i, c, b=b, whole=whole):
            cols = pl.ds(pl.multiple_of(i * 128, 128), 128)
            args = (q, k, v, da, o, dq, dk, dv, b * 512, cols)

            @pl.when(whole)
            def _():
                attend(*args, 0, 512, 0, 512, 0)

            @pl.when(jnp.logical_not(whole))
            def _():
                attend(*args, 0, 208, 0, IMG, 0)
                attend(*args, 192, 208, IMG - 192, 2 * IMG - 192, 16)
                attend(*args, 384, 128, 2 * IMG - 384, 128, 16)

            return c

        lax.fori_loop(0, pairs, pair, 0)

    def finish(i, c):
        r = rows_of(i)
        acc_ref[r, :] = dot_nn(o[r, :], w[3])
        dn_ref[r, :] = dot_nt(dq[r, :], w[0]) + dot_nt(dk[r, :], w[1]) + dot_nt(dv[r, :], w[2])
        return c

    lax.fori_loop(0, tokens // rb, finish, 0)

    def grads(i, c):
        mc = pl.ds(pl.multiple_of(i * rb, rb), rb)
        xt = xn_ref[:, mc]
        g[0, mc, :] = dot_tn(xt, dq[...]).astype(BF16)
        g[1, mc, :] = dot_tn(xt, dk[...]).astype(BF16)
        g[2, mc, :] = dot_tn(xt, dv[...]).astype(BF16)
        g[3, mc, :] = dot_tn(o[:, mc], cot_ref[...]).astype(BF16)
        return c

    lax.fori_loop(0, width // rb, grads, 0)
    done = store(scal, g, g_refs, gsem)
    ones = jnp.ones((8, tokens), BF16)
    sums_ref[0:1, :] = dot_nn(ones, dq[...])[0:1]
    sums_ref[1:2, :] = dot_nn(ones, dv[...])[0:1]
    sums_ref[2:3, :] = dot_nn(ones, cot_ref[...])[0:1]
    done()


def attn_call(scal, x, cot, vec, weights, load, store, g_shapes):
    tokens, width = x.shape
    n_w, n_g = len(weights), len(g_shapes)
    act = pltpu.VMEM((tokens, width), BF16)
    return pl.pallas_call(
        functools.partial(attn_kernel, load, store, n_w, n_g),
        name="attention",
        out_shape=list(g_shapes)
        + [
            jax.ShapeDtypeStruct((tokens, width), BF16),
            jax.ShapeDtypeStruct((tokens, width), F32),
            jax.ShapeDtypeStruct((tokens, width), F32),
            jax.ShapeDtypeStruct((8, width), F32),
        ],
        in_specs=[SMEM, VMEM, VMEM, VMEM] + [ANY] * n_w,
        out_specs=[ANY] * n_g + [VMEM] * 4,
        scratch_shapes=[pltpu.VMEM((4, width, width), BF16)]
        + [act] * 8
        + [pltpu.VMEM((4, width, width), BF16), pltpu.SemaphoreType.DMA, pltpu.SemaphoreType.DMA((max(n_g, 1),))],
        compiler_params=params(),
        cost_estimate=pl.CostEstimate(flops=48 << 30, bytes_accessed=30 << 20, transcendentals=6 << 20),
    )(scal, x, cot, vec, *weights)


def gelu_parts(u):
    t = jnp.tanh(GELU_C * (u + GELU_A * u * u * u))
    half = 0.5 * (1.0 + t)
    act = u * half
    grad = half + (0.5 * GELU_C) * u * (1.0 - t * t) * (1.0 + (3.0 * GELU_A) * u * u)
    return act, grad


def mlp_up_kernel(load, store, n_w, n_g, *refs):
    scal, x_ref, cot_ref, xn_ref, part_ref, bias_ref, bout_ref = refs[:7]
    w_refs = refs[7 : 7 + n_w]
    at = 7 + n_w
    g_refs = refs[at : at + n_g]
    out_ref, gp_ref = refs[at + n_g : at + n_g + 2]
    w, acc, act, gpb, g, wsem, osem, gsem = refs[at + n_g + 2 :]
    tokens, width = x_ref.shape
    tiles = bias_ref.shape[0]
    waits = load(scal, w_refs, w, wsem)
    rb = 256

    def rows_of(i):
        return pl.ds(pl.multiple_of(i * rb, rb), rb)

    waits()
    gp_copies = []
    for t in range(tiles):
        m_t = pl.ds(t * width, width)
        p_t = pl.ds((tiles + t) * width, width)

        def up(i, c, t=t, m_t=m_t, p_t=p_t):
            r = rows_of(i)
            u = dot_nn(xn_ref[r, :], w[m_t, :]) + bias_ref[t : t + 1, :]
            a, gr = gelu_parts(u)
            act[r, :] = a.astype(BF16)
            gpb[t % 2, r, :] = gr.astype(BF16)
            prev = part_ref[r, :] if t == 0 else acc[r, :]
            acc[r, :] = prev + dot_nn(act[r, :], w[p_t, :])
            return c

        if t >= 2:
            gp_copies[t - 2].wait()
        lax.fori_loop(0, tokens // rb, up, 0)
        cp = pltpu.make_async_copy(gpb.at[t % 2], gp_ref.at[t], osem.at[t % 2])
        cp.start()
        gp_copies.append(cp)

        def grad(i, c, t=t):
            mc = pl.ds(pl.multiple_of(i * rb, rb), rb)
            g[pl.ds(pl.multiple_of(t * width + i * rb, rb), rb), :] = dot_tn(act[:, mc], cot_ref[...]).astype(BF16)
            return c

        lax.fori_loop(0, width // rb, grad, 0)
    done = store(scal, g, g_refs, gsem)

    def finish(i, c):
        r = rows_of(i)
        out_ref[r, :] = (acc[r, :] + x_ref[r, :].astype(F32) + bout_ref[...]).astype(BF16)
        return c

    lax.fori_loop(0, tokens // rb, finish, 0)
    for cp in gp_copies[-2:]:
        cp.wait()
    done()


def mlp_up_call(scal, x, cot, xn, part, bias, bout, weights, load, store, g_shapes):
    tokens, width = x.shape
    n_w, n_g = len(weights), len(g_shapes)
    tiles = bias.shape[0]
    return pl.pallas_call(
        functools.partial(mlp_up_kernel, load, store, n_w, n_g),
        name="mlp_up",
        out_shape=list(g_shapes)
        + [jax.ShapeDtypeStruct((tokens, width), BF16), jax.ShapeDtypeStruct((tiles, tokens, width), BF16)],
        in_specs=[SMEM] + [VMEM] * 6 + [ANY] * n_w,
        out_specs=[ANY] * n_g + [VMEM, ANY],
        scratch_shapes=[
            pltpu.VMEM((2 * tiles * width, width), BF16),
            pltpu.VMEM((tokens, width), F32),
            pltpu.VMEM((tokens, width), BF16),
            pltpu.VMEM((2, tokens, width), BF16),
            pltpu.VMEM((tiles * width, width), BF16),
            pltpu.SemaphoreType.DMA,
            pltpu.SemaphoreType.DMA((2,)),
            pltpu.SemaphoreType.DMA((max(n_g, 1),)),
        ],
        compiler_params=params(),
        cost_estimate=pl.CostEstimate(flops=15 << 30, bytes_accessed=30 << 20, transcendentals=3 << 20),
    )(scal, x, cot, xn, part, bias, bout, *weights)


def mlp_down_kernel(load, n_w, *refs):
    scal, x_ref, cot_ref, dn0_ref, gain_ref, gp_ref = refs[:6]
    w_refs = refs[6 : 6 + n_w]
    dx_ref, dpre_ref, sums_ref = refs[6 + n_w : 9 + n_w]
    w, dn, gpb, dpb, wsem, isem, osem = refs[9 + n_w :]
    tokens, width = x_ref.shape
    tiles = gp_ref.shape[0]
    rb = 256

    def gp_copy(t):
        return pltpu.make_async_copy(gp_ref.at[t], gpb.at[t % 2], isem.at[t % 2])

    def dp_copy(t):
        return pltpu.make_async_copy(dpb.at[t % 2], dpre_ref.at[t], osem.at[t % 2])

    gp_copy(0).start()
    load(scal, w_refs, w, wsem)()
    ones = jnp.ones((8, tokens), BF16)
    for t in range(tiles):
        m_t = pl.ds(t * width, width)
        p_t = pl.ds((tiles + t) * width, width)
        if t + 1 < tiles:
            gp_copy(t + 1).start()
        gp_copy(t).wait()
        if t >= 2:
            dp_copy(t - 2).wait()

        def down(i, c, t=t, m_t=m_t, p_t=p_t):
            r = pl.ds(pl.multiple_of(i * rb, rb), rb)
            d = dot_nt(cot_ref[r, :], w[p_t, :]) * gpb[t % 2, r, :].astype(F32)
            dpb[t % 2, r, :] = d.astype(BF16)
            prev = dn0_ref[r, :] if t == 0 else dn[r, :]
            dn[r, :] = prev + dot_nt(dpb[t % 2, r, :], w[m_t, :])
            return c

        lax.fori_loop(0, tokens // rb, down, 0)
        sums_ref[t : t + 1, :] = dot_nn(ones, dpb[t % 2])[0:1]
        dp_copy(t).start()
    gain = gain_ref[0:1, :]

    def finish(i, acc):
        r = pl.ds(pl.multiple_of(i * rb, rb), rb)
        standard, inv = norm_rows(x_ref[r, :])
        dnr = dn[r, :]
        acc = acc + jnp.sum(dnr * standard, axis=0, keepdims=True)
        gs = dnr * gain
        mean_g = jnp.mean(gs, axis=1, keepdims=True)
        mean_p = jnp.mean(gs * standard, axis=1, keepdims=True)
        dx_ref[r, :] = (cot_ref[r, :].astype(F32) + inv * (gs - mean_g - standard * mean_p)).astype(BF16)
        return acc

    sums_ref[tiles : tiles + 1, :] = lax.fori_loop(0, tokens // rb, finish, jnp.zeros((1, width), F32))
    for t in range(max(tiles - 2, 0), tiles):
        dp_copy(t).wait()


def mlp_down_call(scal, x, cot, dn0, gain, gp, weights, load):
    tokens, width = x.shape
    n_w = len(weights)
    tiles = gp.shape[0]
    return pl.pallas_call(
        functools.partial(mlp_down_kernel, load, n_w),
        name="mlp_down",
        out_shape=[
            jax.ShapeDtypeStruct((tokens, width), BF16),
            jax.ShapeDtypeStruct((tiles, tokens, width), BF16),
            jax.ShapeDtypeStruct((8, width), F32),
        ],
        in_specs=[SMEM] + [VMEM] * 4 + [ANY] + [ANY] * n_w,
        out_specs=[VMEM, ANY, VMEM],
        scratch_shapes=[
            pltpu.VMEM((2 * tiles * width, width), BF16),
            pltpu.VMEM((tokens, width), F32),
            pltpu.VMEM((2, tokens, width), BF16),
            pltpu.VMEM((2, tokens, width), BF16),
            pltpu.SemaphoreType.DMA,
            pltpu.SemaphoreType.DMA((2,)),
            pltpu.SemaphoreType.DMA((2,)),
        ],
        compiler_params=params(),
        cost_estimate=pl.CostEstimate(flops=10 << 30, bytes_accessed=30 << 20, transcendentals=0),
    )(scal, x, cot, dn0, gain, gp, *weights)


def mlp_grad_kernel(store, n_g, first, count, *refs):
    scal, xn_ref, dpre_ref = refs[:3]
    g_refs = refs[3 : 3 + n_g]
    dpb, g, isem, gsem = refs[3 + n_g :]
    tokens, width = xn_ref.shape
    rb = 256

    def dp_copy(t):
        return pltpu.make_async_copy(dpre_ref.at[first + t], dpb.at[t], isem.at[t])

    for t in range(count):
        dp_copy(t).start()
    for t in range(count):
        dp_copy(t).wait()

        def grad(i, c, t=t):
            mc = pl.ds(pl.multiple_of(i * rb, rb), rb)
            g[t, mc, :] = dot_tn(xn_ref[:, mc], dpb[t]).astype(BF16)
            return c

        lax.fori_loop(0, width // rb, grad, 0)
    store(scal, g, g_refs, gsem)()


def mlp_grad_call(scal, xn, dpre, first, count, store, g_shapes):
    tokens, width = xn.shape
    n_g = len(g_shapes)
    return pl.pallas_call(
        functools.partial(mlp_grad_kernel, store, n_g, first, count),
        name="mlp_grad",
        out_shape=list(g_shapes),
        in_specs=[SMEM, VMEM, ANY],
        out_specs=[ANY] * n_g,
        scratch_shapes=[
            pltpu.VMEM((count, tokens, width), BF16),
            pltpu.VMEM((count, width, width), BF16),
            pltpu.SemaphoreType.DMA((count,)),
            pltpu.SemaphoreType.DMA((max(n_g, 1),)),
        ],
        compiler_params=params(),
        cost_estimate=pl.CostEstimate(flops=count * (1 << 30), bytes_accessed=10 << 20, transcendentals=0),
    )(scal, xn, dpre)


def swap(value, mask):
    return lax.ppermute(value, "wide", [(i, i ^ mask) for i in range(16)])


def swap_y(value):
    return lax.ppermute(value, "narrow", [(0, 1), (1, 0)])


def slots():
    for part in range(2):
        for i in range(2):
            for s in range(2):
                half, side = (i, s) if part == 0 else (s, i)
                for k in range(4):
                    yield part, i, s * 4 + k, half, side, k


def device_of(scal, k, side, core):
    return ((scal[1] ^ k) * 2 + (scal[2] ^ side)) * 2 + (scal[3] ^ core)


def gather_group(own, n):
    half = lax.dynamic_index_in_dim(own, n, 0, keepdims=False)
    got = [half] + [swap(half, k << 2) for k in (1, 2, 3)]
    za = jnp.stack([t[0] for t in got])
    zb = jnp.stack([t[1] for t in got])
    a0 = jnp.concatenate([za, swap(za, 2)])
    b0 = jnp.concatenate([zb, swap_y(zb)])
    mine = [a0, swap_y(a0), b0, swap(b0, 2)]
    return mine + [swap(t, 1) for t in mine]


def scatter_group(keep0, keep1, send0, send1, n):
    add = lambda *t: sum(v.astype(F32) for v in t)
    got1 = swap(send1, 1)
    y1 = swap_y(add(keep1[0], got1[0]).astype(BF16))
    x1 = swap(add(keep1[1], got1[1]).astype(BF16), 2)
    got0 = swap(send0, 1)
    x2 = swap(add(keep0[0, 4:], got0[0, 4:], y1[4:]).astype(BF16), 2)
    y2 = swap_y(add(keep0[1, 4:], got0[1, 4:], x1[4:]).astype(BF16))
    ta = add(keep0[0, :4], got0[0, :4], y1[:4], x2)
    tb = add(keep0[1, :4], got0[1, :4], x1[:4], y2)
    t = jnp.stack([ta, tb], axis=1)
    tl = t.astype(BF16)
    total = t[0] + add(*[swap(tl[k], k << 2) for k in (1, 2, 3)])
    total = total.astype(BF16)
    other = swap_y(total)
    lo = jnp.where(n == 0, total, other)
    hi = jnp.where(n == 0, other, total)
    return jnp.stack([lo, hi])


def flip(value, axis, bit):
    return jnp.where(bit == 1, jnp.flip(value, axis), value)


def gather_vectors(own, scal):
    got = jnp.stack([own] + [swap(own, k << 2) for k in (1, 2, 3)])
    got = jnp.stack([got, swap(got, 2)], axis=1)
    got = jnp.stack([got, swap(got, 1)], axis=2)
    got = got.reshape(2, 2, 2, 2, -1)
    z = scal[1]
    got = flip(flip(flip(flip(got, 0, z >> 1), 1, z & 1), 2, scal[2]), 3, scal[3])
    return got.reshape(16, -1)


def scatter_vectors(value, scal):
    pick = lambda v, i: lax.dynamic_index_in_dim(v, i, 0, keepdims=False)
    z, x, c = scal[1], scal[2], scal[3]
    value = value.reshape(4, 2, 2, -1).transpose(2, 1, 0, 3)
    value = pick(value, c) + swap(pick(value, 1 - c), 1)
    value = pick(value, x) + swap(pick(value, 1 - x), 2)
    value = pick(value, z) + sum(swap(pick(value, z ^ k), k << 2) for k in (1, 2, 3))
    return value + swap_y(value)


def whole_wait(ref, sem):
    return pltpu.make_async_copy(ref, ref, sem).wait


def load_attn(scal, refs, w, sem):
    for core in range(2):
        for part, i, slot, half, side, k in slots():
            src = refs[core * 4 + part * 2 + i]
            rows = src.shape[1]
            at = pl.multiple_of(device_of(scal, k, side, core) * rows, 16)
            q = (scal[0] ^ half) * 2 + part
            pltpu.make_async_copy(src.at[slot], w.at[q, pl.ds(at, rows), :], sem).start()
    return whole_wait(w, sem)


def load_mlp(scal, refs, w, sem):
    for core in range(2):
        for part, i, slot, half, side, k in slots():
            src = refs[core * 4 + part * 2 + i]
            per, rows, width = src.shape[1:]
            dev = device_of(scal, k, side, core)
            up = (scal[0] ^ half) == 0
            tiles = 2 * per
            for b in range(per):
                block = part * per + b
                at = jnp.where(up, block * width + dev * rows, tiles * width + (dev * tiles + block) * rows)
                at = pl.multiple_of(at, 16)
                pltpu.make_async_copy(src.at[slot, b], w.at[pl.ds(at, rows), :], sem).start()
    return whole_wait(w, sem)


def store_with(source):
    def store(scal, g, refs, sem):
        for core in range(2):
            for part, i, slot, half, side, k in slots():
                at = core * 2 + i
                dst = refs[at]
                src = source(g, scal[0] ^ half, part, device_of(scal, k, side, core), dst.shape[2], dst.shape[3])
                pltpu.make_async_copy(src, dst.at[part, slot], sem.at[at]).start()

        def done():
            for at in range(4):
                whole_wait(refs[at], sem.at[at])()

        return done

    return store


def rows_at(base, rows):
    return pl.ds(pl.multiple_of(base, 16), rows)


def attn_source(g, half, part, dev, rows, cols):
    return g.at[half * 2 + part, rows_at(dev * rows, rows), :]


def down_source(g, half, part, dev, rows, cols):
    return g.at[rows_at((dev * 4 + half * 2 + part) * rows, rows), :]


def up_source(g, half, part, dev, rows, cols):
    return g.at[half, rows_at(dev * rows, rows), pl.ds(part * cols, cols)]


def load_whole_attn(scal, refs, w, sem):
    for i, r in enumerate(refs):
        pltpu.make_async_copy(r, w.at[i], sem).start()
    return whole_wait(w, sem)


def load_whole_mlp(scal, refs, w, sem):
    rows = 0
    for r in refs:
        pltpu.make_async_copy(r, w.at[pl.ds(rows, r.shape[0]), :], sem).start()
        rows += r.shape[0]
    return whole_wait(w, sem)


def store_whole(scal, g, refs, sem):
    if len(refs) == 1:
        copies = [pltpu.make_async_copy(g, refs[0], sem.at[0])]
    else:
        copies = [pltpu.make_async_copy(g.at[i], r, sem.at[i]) for i, r in enumerate(refs)]
    for cp in copies:
        cp.start()

    def done():
        for cp in copies:
            cp.wait()

    return done


def split_rows(value, count):
    rows, cols = value.shape
    return value.reshape(rows, count, cols // count).transpose(1, 0, 2)


def body(sizes, tokens, image_ids, cotangent, w_joined, w_out, w_mlp, norm_gain, bias_attn, bias_mlp, bias_out):
    micro, length, width = tokens.shape
    narrow, wide = sizes
    paired = narrow == 2 and wide == 16
    rows = width // wide
    tiles = w_mlp.shape[0] // rows
    x = tokens.reshape(micro * length, width)
    cot = cotangent.reshape(micro * length, width)
    n = lax.axis_index("narrow")
    w = lax.axis_index("wide")
    last = image_ids.reshape(-1, 512)[:, -1]
    scal = [n, w >> 2, (w >> 1) & 1, w & 1] + [jnp.int32(0)] * 4 + [last[b] for b in range(last.shape[0])]
    scal = jnp.stack([jnp.asarray(s, jnp.int32) for s in scal])

    vec_own = jnp.concatenate([norm_gain, bias_attn, bias_mlp, bias_out])
    if paired:
        qkv = split_rows(w_joined[:, : 3 * width], 3)
        own_attn = jnp.stack([qkv[0], qkv[1], qkv[2], w_out]).reshape(2, 2, rows, width)
        attn_w = gather_group(own_attn, n)
        vec = gather_vectors(vec_own, scal)
        own_up = split_rows(w_joined[:, 3 * width :], tiles)
        own_mlp = jnp.concatenate([own_up, w_mlp.reshape(tiles, rows, width)])
        mlp_w = gather_group(own_mlp.reshape(2, 2, tiles // 2, rows, width), n)
        loads = (load_attn, load_mlp)
    else:
        full = lax.all_gather(w_joined, "wide", axis=0, tiled=True)
        parts = [full[:, i * width : (i + 1) * width] for i in range(3 + tiles)]
        attn_w = parts[:3] + [lax.all_gather(w_out, "wide", axis=0, tiled=True)]
        mlp_w = parts[3:] + [lax.all_gather(w_mlp, "wide", axis=0, tiled=True)]
        vec = lax.all_gather(vec_own, "wide", axis=0)
        loads = (load_whole_attn, load_whole_mlp)
    vec = vec.astype(F32)
    b_at = rows + 2 * rows
    gain = vec[:, :rows].reshape(1, width)
    b_attn = vec[:, rows:b_at].reshape(2, width)
    b_mlp = vec[:, b_at : b_at + tiles * rows].reshape(tiles, width)
    b_out = vec[:, b_at + tiles * rows :].reshape(1, width)
    head_vec = jnp.concatenate([gain, b_attn, jnp.zeros((5, width), F32)])

    shape = lambda *s: jax.ShapeDtypeStruct(s, BF16)
    if paired:
        attn_shapes = [shape(2, 8, rows, width)] * 4
        down_shapes = attn_shapes
        up_shapes = [shape(2, 8, rows, width // 2)] * 4
        stores = (store_with(attn_source), store_with(down_source), store_with(up_source))
    else:
        attn_shapes = [shape(width, width)] * 4
        down_shapes = [shape(tiles * width, width)]
        up_shapes = [shape(width, width)] * 2
        stores = (store_whole,) * 3

    *g_attn, xn, part, dn, sums_a = attn_call(scal, x, cot, head_vec, attn_w, loads[0], stores[0], attn_shapes)
    *g_down, out, gp = mlp_up_call(scal, x, cot, xn, part, b_mlp, b_out, mlp_w, loads[1], stores[1], down_shapes)
    d_x, d_pre, sums_b = mlp_down_call(scal, x, cot, dn, gain, gp, mlp_w, loads[1])
    g_up = [mlp_grad_call(scal, xn, d_pre, t, 2, stores[2], up_shapes) for t in range(0, tiles, 2)]

    vec_grad = jnp.concatenate(
        [
            sums_b[tiles].reshape(wide, rows),
            sums_a[:2].reshape(wide, 2 * rows),
            sums_b[:tiles].reshape(wide, tiles * rows),
            sums_a[2].reshape(wide, rows),
        ],
        axis=1,
    )
    if paired:
        ga = scatter_group(*g_attn, n).reshape(4, rows, width)
        gd = scatter_group(*g_down, n).reshape(tiles, rows, width)
        vg = scatter_vectors(vec_grad, scal)
        gu = [scatter_group(*g, n) for g in g_up]
        ups = [g[h, p] for g in gu for h in range(2) for p in range(2)]
        grad_joined = jnp.concatenate([ga[0], ga[1], ga[2]] + ups, axis=1).astype(F32)
        grad_out = ga[3].astype(F32)
        grad_mlp = gd.reshape(tiles * rows, width).astype(F32)
    else:
        reduce = lambda g: lax.psum(
            lax.psum_scatter(g.astype(F32), "wide", scatter_dimension=0, tiled=True), "narrow"
        )
        grad_joined = reduce(jnp.concatenate([*g_attn[:3], *g_up[0], *g_up[1]], axis=1))
        grad_out = reduce(g_attn[3])
        grad_mlp = reduce(g_down[0])
        vg = reduce(vec_grad)[0]
    return (
        out.reshape(tokens.shape),
        d_x.reshape(tokens.shape),
        grad_joined,
        grad_out,
        grad_mlp,
        vg[:rows],
        vg[rows:b_at],
        vg[b_at : b_at + tiles * rows],
        vg[b_at + tiles * rows :],
    )


def solution(mesh):
    sizes = (mesh.shape["narrow"], mesh.shape["wide"])
    rows = P(None, ("narrow", "wide"), None)
    placed = (rows, P(None, ("narrow", "wide")), rows) + (P("wide", None),) * 3 + (P("wide"),) * 4
    return jax.shard_map(
        functools.partial(body, sizes),
        mesh=mesh,
        in_specs=placed,
        out_specs=(rows, rows) + (P("wide", None),) * 3 + (P("wide"),) * 4,
        check_vma=False,
    )
```

```python
import functools

import jax
import jax.numpy as jnp
from jax import lax
from jax.experimental import pallas as pl
from jax.experimental.pallas import tpu as pltpu
from jax.sharding import PartitionSpec as P

HEADS = 12
HEAD = 64
IMG = 196
EPS = 1e-06
GELU_C = 0.7978845608028654
GELU_A = 0.044715

F32 = jnp.float32
BF16 = jnp.bfloat16
HBM = pl.BlockSpec(memory_space=pltpu.HBM)
SMEM = pl.BlockSpec(memory_space=pltpu.SMEM)


def dot_nn(a, b):
    return lax.dot_general(a, b, (((1,), (0,)), ((), ())), preferred_element_type=F32)


def dot_nt(a, b):
    return lax.dot_general(a, b, (((1,), (1,)), ((), ())), preferred_element_type=F32)


def dot_tn(a, b):
    return lax.dot_general(a, b, (((0,), (0,)), ((), ())), preferred_element_type=F32)


def norm_rows(rows):
    rows = rows.astype(F32)
    mean = jnp.mean(rows, axis=1, keepdims=True)
    centered = rows - mean
    inv = lax.rsqrt(jnp.mean(centered * centered, axis=1, keepdims=True) + EPS)
    return centered * inv, inv


def attend(q_ref, k_ref, v_ref, da_ref, o_ref, dq_ref, dk_ref, dv_ref, start, rows, lo, hi, merge):
    win = pl.ds(start, rows)
    q2, k2, v2, da2 = q_ref[win, :], k_ref[win, :], v_ref[win, :], da_ref[win, :]
    lane = lax.broadcasted_iota(jnp.int32, (rows, 128), 1)
    masked = lo > 0 or hi < rows
    step = 256 if rows == 512 else rows
    outs, dqs = [], []
    dk = jnp.zeros((rows, 128), F32)
    dv = jnp.zeros((rows, 128), F32)
    zero = jnp.zeros((), BF16)
    heads = []
    for h in range(2):
        keep = (lane < 64) if h == 0 else (lane >= 64)
        heads.append([jnp.where(keep, t, zero) for t in (q2, k2, v2, da2)])
    for at in range(0, rows, step):
        qs = slice(at, at + step)
        out = jnp.zeros((step, 128), F32)
        dq = jnp.zeros((step, 128), F32)
        for h in range(2):
            qh, kh, vh, dah = heads[h]
            s = dot_nt(k2, qh[qs])
            if masked:
                key = lax.broadcasted_iota(jnp.int32, (rows, step), 0)
                s = jnp.where((key >= lo) & (key < hi), s, -1e30)
            top = jnp.max(s, axis=0, keepdims=True)
            e = jnp.exp(s - top)
            total = jnp.sum(e, axis=0, keepdims=True)
            scale = 1.0 / total
            if masked:
                query = lax.broadcasted_iota(jnp.int32, (1, step), 1) + at
                scale = jnp.where((query >= lo) & (query < hi), scale, 0.0)
            p = e * scale
            pb = p.astype(BF16)
            dp = dot_nt(v2, dah[qs])
            inner = jnp.sum(p * dp, axis=0, keepdims=True)
            ds = (p * (dp - inner)).astype(BF16)
            out += dot_tn(pb, vh)
            dq += dot_tn(ds, kh)
            dv += dot_nn(pb, dah[qs])
            dk += dot_nn(ds, qh[qs])
        outs.append(out)
        dqs.append(dq * 0.125)
    for ref, val in ((o_ref, outs), (dq_ref, dqs), (dk_ref, [dk]), (dv_ref, [dv])):
        val = val[0] if len(val) == 1 else jnp.concatenate(val, axis=0)
        val = val.astype(BF16)
        if merge:
            head, rest = pl.ds(start, merge), pl.ds(start + merge, rows - merge)
            ref[head, :] = ref[head, :] + val[:merge]
            ref[rest, :] = val[merge:]
        else:
            ref[win, :] = val


def call(kernel, name, grid, ins, outs, scratch, operands, flops, moved):
    return pl.pallas_call(
        kernel,
        name=name,
        grid=grid,
        out_shape=[s for s, _ in outs],
        in_specs=ins,
        out_specs=[m for _, m in outs],
        scratch_shapes=scratch,
        compiler_params=pltpu.CompilerParams(
            vmem_limit_bytes=60 << 20, dimension_semantics=("arbitrary",) * len(grid)
        ),
        cost_estimate=pl.CostEstimate(flops=flops, bytes_accessed=moved, transcendentals=0),
    )(*operands)


def sds(shape, dtype=BF16):
    return jax.ShapeDtypeStruct(shape, dtype)


def fixed(shape):
    return pl.BlockSpec(shape, lambda *i: (0,) * len(shape), pipeline_mode=pl.Buffered(1))


def by_rows(rows, width):
    return pl.BlockSpec((rows, width), lambda i: (i, 0))


def by_tile(tokens, width):
    return pl.BlockSpec((None, tokens, width), lambda i: (i, 0, 0))


def square_loop(width, fn, rb=256):
    def step(i, c):
        fn(pl.multiple_of(i * rb, rb), rb)
        return c

    lax.fori_loop(0, width // rb, step, 0)


ROWS = 256


def project_kernel(load, n_w, *refs):
    scal, x_ref, cot_ref, vec_ref = refs[:4]
    xn, q, k, v, da = refs[4 + n_w : 9 + n_w]
    w, sem = refs[9 + n_w :]
    first = pl.program_id(0) == 0

    @pl.when(first)
    def _():
        load(scal, refs[4 : 4 + n_w], w, sem, (0, 1, 2, 3))

    standard, _ = norm_rows(x_ref[...])
    xr = (standard * vec_ref[0:1, :]).astype(BF16)
    xn[...] = xr

    @pl.when(first)
    def _():
        for i in range(4):
            whole_wait(w.at[i], sem.at[i])()

    q[...] = (dot_nn(xr, w[0]) + vec_ref[1:2, :]).astype(BF16) * jnp.asarray(0.125, BF16)
    k[...] = dot_nn(xr, w[1]).astype(BF16)
    v[...] = (dot_nn(xr, w[2]) + vec_ref[2:3, :]).astype(BF16)
    da[...] = dot_nt(cot_ref[...], w[3]).astype(BF16)


def project_call(scal, x, cot, vec, weights, load):
    tokens, width = x.shape
    return call(
        functools.partial(project_kernel, load, len(weights)),
        "project",
        (tokens // ROWS,),
        [SMEM, by_rows(ROWS, width), by_rows(ROWS, width), fixed(vec.shape)] + [HBM] * len(weights),
        [(sds(x.shape), by_rows(ROWS, width))] * 5,
        [pltpu.VMEM((4, width, width), BF16), pltpu.SemaphoreType.DMA((4,))],
        (scal, x, cot, vec, *weights),
        8 * tokens * width * width,
        16 << 20,
    )


def core_kernel(scal, q, k, v, da, o, dq, dk, dv):
    whole = scal[8 + pl.program_id(0)] == 0
    args = (q, k, v, da, o, dq, dk, dv)

    @pl.when(whole)
    def _():
        attend(*args, 0, 512, 0, 512, 0)

    @pl.when(jnp.logical_not(whole))
    def _():
        attend(*args, 0, 208, 0, IMG, 0)
        attend(*args, 192, 208, IMG - 192, 2 * IMG - 192, 16)
        attend(*args, 384, 128, 2 * IMG - 384, 128, 16)


def core_call(scal, q, k, v, da):
    tokens, width = q.shape
    spec = pl.BlockSpec((512, 128), lambda b, i: (b, i))
    return call(
        core_kernel,
        "core",
        (tokens // 512, width // 128),
        [SMEM] + [spec] * 4,
        [(sds(q.shape), spec)] * 4,
        [],
        (scal, q, k, v, da),
        20 << 30,
        12 << 20,
    )


def attn_grad_kernel(store, n_g, *refs):
    scal = refs[0]
    g_refs = refs[7 : 7 + n_g]
    sums = refs[7 + n_g]
    xn, o, dq, dk, dv, cot, g, isem, sem = refs[8 + n_g :]
    tokens, width = xn.shape
    order = ((1, xn), (3, dq), (4, dk), (5, dv), (2, o), (6, cot))
    copies = [pltpu.make_async_copy(refs[i], ref, isem.at[j]) for j, (i, ref) in enumerate(order)]
    for cp in copies:
        cp.start()
    ones = jnp.ones((8, tokens), BF16)
    copies[0].wait()
    for b, rhs in enumerate((dq, dk, dv)):
        copies[1 + b].wait()

        def grads(at, n, b=b, rhs=rhs):
            g[b, pl.ds(at, n), :] = dot_tn(xn[:, pl.ds(at, n)], rhs[...]).astype(BF16)

        square_loop(width, grads)
    copies[4].wait()
    copies[5].wait()

    def grads(at, n):
        g[3, pl.ds(at, n), :] = dot_tn(o[:, pl.ds(at, n)], cot[...]).astype(BF16)

    square_loop(width, grads)
    done = store(scal, g, g_refs, sem)
    sums[0:1, :] = dot_nn(ones, dq[...])[0:1]
    sums[1:2, :] = dot_nn(ones, dv[...])[0:1]
    sums[2:3, :] = dot_nn(ones, cot[...])[0:1]
    done()


def attn_grad_call(scal, xn, o, dq, dk, dv, cot, store, g_shapes):
    tokens, width = xn.shape
    n_g = len(g_shapes)
    return call(
        functools.partial(attn_grad_kernel, store, n_g),
        "attn_grad",
        (1,),
        [SMEM] + [HBM] * 6,
        [(s, HBM) for s in g_shapes] + [(sds((8, width), F32), fixed((8, width)))],
        [pltpu.VMEM((tokens, width), BF16)] * 6
        + [pltpu.VMEM((4, width, width), BF16), pltpu.SemaphoreType.DMA((6,)), pltpu.SemaphoreType.DMA((n_g,))],
        (scal, xn, o, dq, dk, dv, cot),
        8 * tokens * width * width,
        14 << 20,
    )


def gelu_parts(u):
    t = jnp.tanh(GELU_C * (u + GELU_A * u * u * u))
    half = 0.5 * (1.0 + t)
    act = u * half
    grad = half + (0.5 * GELU_C) * u * (1.0 - t * t) * (1.0 + (3.0 * GELU_A) * u * u)
    return act, grad

def tile_of(t, width):
    return pl.ds(pl.multiple_of(t * width, 128), width)


def wait_tile(w, sem, t, width):
    whole_wait(w.at[tile_of(t, width), :], sem.at[t])()


def up_kernel(load, n_w, *refs):
    scal, xn, bias = refs[:3]
    act, gp = refs[3 + n_w : 5 + n_w]
    w, sem = refs[5 + n_w :]
    tokens, width = xn.shape
    t = pl.program_id(0)

    @pl.when(t == 0)
    def _():
        load(scal, refs[3 : 3 + n_w], w, sem)

    wait_tile(w, sem, t, width)

    def up(at, n):
        r = pl.ds(at, n)
        u = dot_nn(xn[r, :], w[tile_of(t, width), :]) + bias[...]
        a, gr = gelu_parts(u)
        act[r, :] = a.astype(BF16)
        gp[r, :] = gr.astype(BF16)

    square_loop(tokens, up)


def up_call(scal, xn, bias, weights, load):
    tokens, width = xn.shape
    tiles = bias.shape[0]
    return call(
        functools.partial(up_kernel, load, len(weights)),
        "up",
        (tiles,),
        [SMEM, fixed(xn.shape), pl.BlockSpec((None, 1, width), lambda i: (i, 0, 0))] + [HBM] * len(weights),
        [(sds((tiles, tokens, width)), by_tile(tokens, width))] * 2,
        [pltpu.VMEM((tiles * width, width), BF16), pltpu.SemaphoreType.DMA((tiles,))],
        (scal, xn, bias.reshape(tiles, 1, width), *weights),
        2 * tiles * tokens * width * width,
        19 << 20,
    )


def down_grad_kernel(store, n_g, *refs):
    scal, act, cot = refs[:3]
    g_refs = refs[3 : 3 + n_g]
    g, sem = refs[3 + n_g :]
    tokens, width = cot.shape
    t = pl.program_id(0)

    def grad(at, n):
        g[pl.ds(pl.multiple_of(t * width + at, 128), n), :] = dot_tn(act[:, pl.ds(at, n)], cot[...]).astype(BF16)

    square_loop(width, grad)

    @pl.when(t == pl.num_programs(0) - 1)
    def _():
        store(scal, g, g_refs, sem)()


def down_grad_call(scal, act, cot, store, g_shapes):
    tiles, tokens, width = act.shape
    n_g = len(g_shapes)
    return call(
        functools.partial(down_grad_kernel, store, n_g),
        "down_grad",
        (tiles,),
        [SMEM, by_tile(tokens, width), fixed(cot.shape)],
        [(s, HBM) for s in g_shapes],
        [pltpu.VMEM((tiles * width, width), BF16), pltpu.SemaphoreType.DMA((n_g,))],
        (scal, act, cot),
        2 * tiles * tokens * width * width,
        13 << 20,
    )


def dpre_kernel(load, n_w, *refs):
    scal, cot, gp = refs[:3]
    dpre, sums = refs[3 + n_w : 5 + n_w]
    w, sem = refs[5 + n_w :]
    tokens, width = cot.shape
    t = pl.program_id(0)

    @pl.when(t == 0)
    def _():
        load(scal, refs[3 : 3 + n_w], w, sem)

    wait_tile(w, sem, t, width)

    def down(at, n):
        r = pl.ds(at, n)
        d = dot_nt(cot[r, :], w[tile_of(t, width), :]) * gp[r, :].astype(F32)
        dpre[r, :] = d.astype(BF16)

    square_loop(tokens, down)
    sums[...] = dot_nn(jnp.ones((8, tokens), BF16), dpre[...])


def dpre_call(scal, cot, gp, weights, load):
    tiles, tokens, width = gp.shape
    return call(
        functools.partial(dpre_kernel, load, len(weights)),
        "dpre",
        (tiles,),
        [SMEM, fixed(cot.shape), by_tile(tokens, width)] + [HBM] * len(weights),
        [(sds(gp.shape), by_tile(tokens, width)), (sds((tiles, 8, width), F32), by_tile(8, width))],
        [pltpu.VMEM((tiles * width, width), BF16), pltpu.SemaphoreType.DMA((tiles,))],
        (scal, cot, gp, *weights),
        2 * tiles * tokens * width * width,
        19 << 20,
    )


def up_grad_kernel(store, n_g, *refs):
    scal, xn, dpre = refs[:3]
    g_refs = refs[3 : 3 + n_g]
    g, sem = refs[3 + n_g :]
    tokens, width = xn.shape
    t = pl.program_id(0)

    def grad(at, n):
        g[t, pl.ds(at, n), :] = dot_tn(xn[:, pl.ds(at, n)], dpre[...]).astype(BF16)

    square_loop(width, grad)

    @pl.when(t == pl.num_programs(0) - 1)
    def _():
        store(scal, g, g_refs, sem)()


def up_grad_call(scal, xn, dpre, store, g_shapes):
    tiles, tokens, width = dpre.shape
    n_g = len(g_shapes)
    return call(
        functools.partial(up_grad_kernel, store, n_g),
        "up_grad",
        (tiles,),
        [SMEM, fixed(xn.shape), by_tile(tokens, width)],
        [(s, HBM) for s in g_shapes],
        [pltpu.VMEM((tiles, width, width), BF16), pltpu.SemaphoreType.DMA((n_g,))],
        (scal, xn, dpre),
        2 * tiles * tokens * width * width,
        13 << 20,
    )


def input_grad_kernel(load_a, load_u, n_a, n_u, *refs):
    scal, x, cot, dq, dk, dv, dpre, vec = refs[:8]
    dx, sums = refs[8 + n_a + n_u : 10 + n_a + n_u]
    wa, wu, sem_a, sem_u = refs[10 + n_a + n_u :]
    tiles, _, width = dpre.shape
    first = pl.program_id(0) == 0

    @pl.when(first)
    def _():
        load_a(scal, refs[8 : 8 + n_a], wa, sem_a, (0, 1, 2))
        load_u(scal, refs[8 + n_a : 8 + n_a + n_u], wu, sem_u)
        sums[...] = jnp.zeros_like(sums)
        for i in range(3):
            whole_wait(wa.at[i], sem_a.at[i])()

    dnr = dot_nt(dq[...], wa[0]) + dot_nt(dk[...], wa[1]) + dot_nt(dv[...], wa[2])

    @pl.when(first)
    def _():
        for t in range(tiles):
            wait_tile(wu, sem_u, t, width)

    for t in range(tiles):
        dnr += dot_nt(dpre[t], wu[pl.ds(t * width, width), :])
    standard, inv = norm_rows(x[...])
    sums[0:1, :] += jnp.sum(dnr * standard, axis=0, keepdims=True)
    gs = dnr * vec[0:1, :]
    mean_g = jnp.mean(gs, axis=1, keepdims=True)
    mean_p = jnp.mean(gs * standard, axis=1, keepdims=True)
    dx[...] = (cot[...].astype(F32) + inv * (gs - mean_g - standard * mean_p)).astype(BF16)


def input_grad_call(scal, x, cot, dq, dk, dv, dpre, vec, attn_w, up_w, load_a, load_u):
    tiles, tokens, width = dpre.shape
    return call(
        functools.partial(input_grad_kernel, load_a, load_u, len(attn_w), len(up_w)),
        "input_grad",
        (tokens // ROWS,),
        [SMEM]
        + [by_rows(ROWS, width)] * 5
        + [pl.BlockSpec((tiles, ROWS, width), lambda i: (0, i, 0)), fixed(vec.shape)]
        + [HBM] * (len(attn_w) + len(up_w)),
        [(sds(x.shape), by_rows(ROWS, width)), (sds((8, width), F32), fixed((8, width)))],
        [
            pltpu.VMEM((4, width, width), BF16),
            pltpu.VMEM((tiles * width, width), BF16),
            pltpu.SemaphoreType.DMA((4,)),
            pltpu.SemaphoreType.DMA((tiles,)),
        ],
        (scal, x, cot, dq, dk, dv, dpre, vec, *attn_w, *up_w),
        2 * (tiles + 3) * tokens * width * width,
        28 << 20,
    )


def out_kernel(load_a, load_d, n_a, n_d, *refs):
    scal, x, o, act, vec = refs[:5]
    out = refs[5 + n_a + n_d]
    wa, wd, sem_a, sem_d = refs[6 + n_a + n_d :]
    tiles, _, width = act.shape
    first = pl.program_id(0) == 0

    @pl.when(first)
    def _():
        load_a(scal, refs[5 : 5 + n_a], wa, sem_a, (3,))
        load_d(scal, refs[5 + n_a : 5 + n_a + n_d], wd, sem_d)
        whole_wait(wa.at[3], sem_a.at[3])()

    total = x[...].astype(F32) + vec[3:4, :] + dot_nn(o[...], wa[3])

    @pl.when(first)
    def _():
        for t in range(tiles):
            wait_tile(wd, sem_d, t, width)

    for t in range(tiles):
        total += dot_nn(act[t], wd[pl.ds(t * width, width), :])
    out[...] = total.astype(BF16)


def out_call(scal, x, o, act, vec, attn_w, down_w, load_a, load_d):
    tiles, tokens, width = act.shape
    (out,) = call(
        functools.partial(out_kernel, load_a, load_d, len(attn_w), len(down_w)),
        "out",
        (tokens // ROWS,),
        [SMEM]
        + [by_rows(ROWS, width)] * 2
        + [pl.BlockSpec((tiles, ROWS, width), lambda i: (0, i, 0)), fixed(vec.shape)]
        + [HBM] * (len(attn_w) + len(down_w)),
        [(sds(x.shape), by_rows(ROWS, width))],
        [
            pltpu.VMEM((4, width, width), BF16),
            pltpu.VMEM((tiles * width, width), BF16),
            pltpu.SemaphoreType.DMA((4,)),
            pltpu.SemaphoreType.DMA((tiles,)),
        ],
        (scal, x, o, act, vec, *attn_w, *down_w),
        2 * (tiles + 1) * tokens * width * width,
        20 << 20,
    )
    return out


def swap(value, mask):
    return lax.ppermute(value, "wide", [(i, i ^ mask) for i in range(16)])


def swap_y(value):
    return lax.ppermute(value, "narrow", [(0, 1), (1, 0)])


def slots():
    for part in range(2):
        for i in range(2):
            for s in range(2):
                half, side = (i, s) if part == 0 else (s, i)
                for k in range(4):
                    yield part, i, s * 4 + k, half, side, k


def device_of(scal, k, side, core):
    return ((scal[1] ^ k) * 2 + (scal[2] ^ side)) * 2 + (scal[3] ^ core)


def behind(value, *marks):
    return lax.optimization_barrier((value, marks))[0]


def gather_z(own, n):
    half = lax.dynamic_index_in_dim(own, n, 0, keepdims=False)
    return half, [swap(half, k << 2) for k in (1, 2, 3)]


def gather_stack(half, got):
    got = [half] + got
    return [jnp.stack([t[i] for t in got]) for i in range(2)]


def gather_xy(za, zb):
    return swap(za, 2), swap_y(zb)


def total(*parts):
    return sum(v.astype(F32) for v in parts)


def scatter_sum1(keep1, got1):
    return [total(keep1[i], got1[i]).astype(BF16) for i in range(2)]


def scatter_sum2(keep0, got0, got):
    return [total(keep0[i, 4:], got0[i, 4:], got[i][4:]).astype(BF16) for i in range(2)]


def scatter_sum3(keep0, got0, got, got2):
    parts = [total(keep0[i, :4], got0[i, :4], got[i][:4], got2[i]).astype(BF16) for i in range(2)]
    return [jnp.stack([p[k] for p in parts]) for k in range(4)]


def scatter_sum4(own, got):
    return total(own, *got).astype(BF16)


def scatter_join(mine, other, n):
    return jnp.stack([jnp.where(n == 0, mine, other), jnp.where(n == 0, other, mine)])


def flip(value, axis, bit):
    return jnp.where(bit == 1, jnp.flip(value, axis), value)


def gather_vectors(own, scal):
    got = jnp.stack([own] + [swap(own, k << 2) for k in (1, 2, 3)])
    got = jnp.stack([got, swap(got, 2)], axis=1)
    got = jnp.stack([got, swap(got, 1)], axis=2)
    got = got.reshape(2, 2, 2, 2, -1)
    z = scal[1]
    got = flip(flip(flip(flip(got, 0, z >> 1), 1, z & 1), 2, scal[2]), 3, scal[3])
    return got.reshape(16, -1)


def scatter_vectors(value, scal):
    pick = lambda v, i: lax.dynamic_index_in_dim(v, i, 0, keepdims=False)
    z, x, c = scal[1], scal[2], scal[3]
    value = value.reshape(4, 2, 2, -1).transpose(2, 1, 0, 3)
    value = pick(value, c) + swap(pick(value, 1 - c), 1)
    value = pick(value, x) + swap(pick(value, 1 - x), 2)
    value = pick(value, z) + sum(swap(pick(value, z ^ k), k << 2) for k in (1, 2, 3))
    return value + swap_y(value)


def whole_wait(ref, sem):
    return pltpu.make_async_copy(ref, ref, sem).wait


def load_attn(scal, refs, w, sem, blocks):
    def start(own):
        for block in blocks:
            for core in range(2):
                for part, i, slot, half, side, k in slots():
                    if (own ^ half) * 2 + part != block:
                        continue
                    src = refs[core * 4 + part * 2 + i]
                    rows = src.shape[1]
                    at = pl.multiple_of(device_of(scal, k, side, core) * rows, 16)
                    pltpu.make_async_copy(src.at[slot], w.at[block, pl.ds(at, rows), :], sem.at[block]).start()

    @pl.when(scal[0] == 0)
    def _():
        start(0)

    @pl.when(scal[0] != 0)
    def _():
        start(1)


def load_half(which):
    def load(scal, refs, w, sem):
        def start(rel):
            for core in range(2):
                for part, i, slot, half, side, k in slots():
                    if half != rel:
                        continue
                    src = refs[core * 4 + part * 2 + i]
                    per, rows, width = src.shape[1:]
                    dev = device_of(scal, k, side, core)
                    for b in range(per):
                        block = part * per + b
                        if which == 0:
                            at, tile = block * width + dev * rows, block
                        else:
                            at, tile = (dev * 2 * per + block) * rows, scal[1] ^ k
                        dst = w.at[pl.ds(pl.multiple_of(at, 16), rows), :]
                        pltpu.make_async_copy(src.at[slot, b], dst, sem.at[tile]).start()

        @pl.when(scal[0] == which)
        def _():
            start(0)

        @pl.when(scal[0] != which)
        def _():
            start(1)

    return load


def store_with(source):
    def store(scal, g, refs, sem):
        for core in range(2):
            for part, i, slot, half, side, k in slots():
                at = core * 2 + i
                dst = refs[at]
                src = source(g, scal[0] ^ half, part, device_of(scal, k, side, core), dst.shape[2], dst.shape[3])
                pltpu.make_async_copy(src, dst.at[part, slot], sem.at[at]).start()

        def done():
            for at in range(4):
                whole_wait(refs[at], sem.at[at])()

        return done

    return store


def rows_at(base, rows):
    return pl.ds(pl.multiple_of(base, 16), rows)


def attn_source(g, half, part, dev, rows, cols):
    return g.at[half * 2 + part, rows_at(dev * rows, rows), :]


def down_source(g, half, part, dev, rows, cols):
    return g.at[rows_at((dev * 4 + half * 2 + part) * rows, rows), :]


def load_whole_attn(scal, refs, w, sem, blocks):
    for i in blocks:
        pltpu.make_async_copy(refs[i], w.at[i], sem.at[i]).start()


def load_whole_mlp(scal, refs, w, sem):
    width = w.shape[1]
    for i, r in enumerate(refs):
        for t in range(r.shape[0] // width):
            at = i + t
            src = r.at[pl.ds(t * width, width), :]
            pltpu.make_async_copy(src, w.at[pl.ds(at * width, width), :], sem.at[at]).start()


def store_whole(scal, g, refs, sem):
    if len(refs) == 1:
        copies = [pltpu.make_async_copy(g, refs[0], sem.at[0])]
    else:
        copies = [pltpu.make_async_copy(g.at[i], r, sem.at[i]) for i, r in enumerate(refs)]
    for cp in copies:
        cp.start()

    def done():
        for cp in copies:
            cp.wait()

    return done


def split_rows(value, count):
    rows, cols = value.shape
    return value.reshape(rows, count, cols // count).transpose(1, 0, 2)


def body(sizes, tokens, image_ids, cotangent, w_joined, w_out, w_mlp, norm_gain, bias_attn, bias_mlp, bias_out):
    micro, length, width = tokens.shape
    narrow, wide = sizes
    paired = narrow == 2 and wide == 16
    rows = width // wide
    tiles = w_mlp.shape[0] // rows
    x = tokens.reshape(micro * length, width)
    cot = cotangent.reshape(micro * length, width)
    n = lax.axis_index("narrow")
    w = lax.axis_index("wide")
    last = image_ids.reshape(-1, 512)[:, -1]
    scal = [n, w >> 2, (w >> 1) & 1, w & 1] + [jnp.int32(0)] * 4 + [last[b] for b in range(last.shape[0])]
    scal = jnp.stack([jnp.asarray(s, jnp.int32) for s in scal])
    vec_own = jnp.concatenate([norm_gain, bias_attn, bias_mlp, bias_out])

    def vectors(vec):
        vec = vec.astype(F32)
        b_at = 3 * rows
        b_mlp = vec[:, b_at : b_at + tiles * rows].reshape(tiles, width)
        head = [
            vec[:, :rows].reshape(1, width),
            vec[:, rows:b_at].reshape(2, width),
            vec[:, b_at + tiles * rows :].reshape(1, width),
            jnp.zeros((4, width), F32),
        ]
        return jnp.concatenate(head), b_mlp

    def vector_grads(sums_a, sums_d, sums_x):
        return jnp.concatenate(
            [
                sums_x[0].reshape(wide, rows),
                sums_a[:2].reshape(wide, 2 * rows),
                sums_d[:, 0].reshape(wide, tiles * rows),
                sums_a[2].reshape(wide, rows),
            ],
            axis=1,
        )

    if not paired:
        full = lax.all_gather(w_joined, "wide", axis=0, tiled=True)
        parts = [full[:, i * width : (i + 1) * width] for i in range(3 + tiles)]
        attn_w = parts[:3] + [lax.all_gather(w_out, "wide", axis=0, tiled=True)]
        up_w = parts[3:]
        down_w = [lax.all_gather(w_mlp, "wide", axis=0, tiled=True)]
        vec, b_mlp = vectors(lax.all_gather(vec_own, "wide", axis=0))
        square = [sds((width, width))]
        xn, q, k, v, da = project_call(scal, x, cot, vec, attn_w, load_whole_attn)
        o, dq, dk, dv = core_call(scal, q, k, v, da)
        *g_attn, sums_a = attn_grad_call(scal, xn, o, dq, dk, dv, cot, store_whole, square * 4)
        act, gp = up_call(scal, xn, b_mlp, up_w, load_whole_mlp)
        g_down = down_grad_call(scal, act, cot, store_whole, [sds((tiles * width, width))])
        dpre, sums_d = dpre_call(scal, cot, gp, down_w, load_whole_mlp)
        g_up = up_grad_call(scal, xn, dpre, store_whole, square * tiles)
        d_x, sums_x = input_grad_call(
            scal, x, cot, dq, dk, dv, dpre, vec, attn_w, up_w, load_whole_attn, load_whole_mlp
        )
        out = out_call(scal, x, o, act, vec, attn_w, down_w, load_whole_attn, load_whole_mlp)

        def reduce(g):
            g = lax.psum_scatter(g.astype(F32), "wide", scatter_dimension=0, tiled=True)
            return lax.psum(g, "narrow")

        grad_joined = reduce(jnp.concatenate([*g_attn[:3], *g_up], axis=1))
        grad_out = reduce(g_attn[3])
        grad_mlp = reduce(g_down[0])
        vg = reduce(vector_grads(sums_a, sums_d, sums_x))[0]
    else:
        own_attn = jnp.concatenate([split_rows(w_joined[:, : 3 * width], 3), w_out[None]])
        own_mlp = jnp.concatenate([split_rows(w_joined[:, 3 * width :], tiles), w_mlp.reshape(tiles, rows, width)])
        half, got = gather_z(own_attn.reshape(2, 2, rows, width), n)
        za, zb = gather_stack(half, got)
        xa, yb = gather_xy(za, zb)
        vec, b_mlp = vectors(gather_vectors(behind(vec_own, za), scal))
        c_half, c_got = gather_z(behind(own_mlp.reshape(2, 2, tiles // 2, rows, width), za, zb), n)
        a0, b0 = jnp.concatenate([za, xa]), jnp.concatenate([zb, yb])
        a1, b1 = swap_y(a0), swap(b0, 2)
        a0s, b0s = swap(a0, 1), swap(b0, 1)
        attn_w = [a0, a1, b0, b1, a0s, swap(a1, 1), b0s, swap(b1, 1)]

        cza, czb = gather_stack(c_half, c_got)
        xp, attn_w, vec, cza, czb = lax.optimization_barrier((x, attn_w, vec, cza, czb))
        cxa, cyb = gather_xy(cza, czb)
        xn, q, k, v, da = project_call(scal, xp, cot, vec, attn_w, load_attn)

        cxa, cyb = behind((cxa, cyb), q)
        ca0, cb0 = jnp.concatenate([cza, cxa]), jnp.concatenate([czb, cyb])
        q, ca0, cb0 = lax.optimization_barrier((q, ca0, cb0))
        ca1, cb1 = swap_y(ca0), swap(cb0, 2)
        ca0s, cb0s = swap(ca0, 1), swap(cb0, 1)
        o, dq, dk, dv = core_call(scal, q, k, v, da)

        ca1, cb1 = behind((ca1, cb1), dq)
        dq, ca1, cb1 = lax.optimization_barrier((dq, ca1, cb1))
        ca1s, cb1s = swap(ca1, 1), swap(cb1, 1)
        attn_shapes = [sds((2, 8, rows, width))] * 4
        *ga, sums_a = attn_grad_call(scal, xn, o, dq, dk, dv, cot, store_with(attn_source), attn_shapes)
        mlp_w = [ca0, ca1, cb0, cb1, ca0s, *behind([ca1s, cb0s, cb1s], sums_a)]

        a_got1, a_got0 = swap(ga[3], 1), swap(ga[2], 1)
        xn_u = behind(xn, ga)
        act, gp = up_call(scal, xn_u, b_mlp, mlp_w, load_half(0))

        a_got1, a_got0 = behind((a_got1, a_got0), gp)
        sa, sb = scatter_sum1(ga[1], a_got1)
        act_g, sa, sb = lax.optimization_barrier((act, sa, sb))
        a_xy = swap_y(sa), swap(sb, 2)
        gd = down_grad_call(scal, act_g, cot, store_with(down_source), attn_shapes)

        a_xy = behind(a_xy, gd)
        sa, sb = scatter_sum2(ga[0], a_got0, a_xy)
        gp, sa, sb, gd = lax.optimization_barrier((gp, sa, sb, gd))
        a_yx = swap(sa, 2), swap_y(sb)
        d_got1, d_got0 = swap(gd[3], 1), swap(gd[2], 1)
        dpre, sums_d = dpre_call(scal, cot, gp, mlp_w, load_half(1))

        a_yx, d_got1, d_got0 = behind((a_yx, d_got1, d_got0), dpre)
        a_t = scatter_sum3(ga[0], a_got0, a_xy, a_yx)
        sa, sb = scatter_sum1(gd[1], d_got1)
        dpre_g, a_t, sa, sb = lax.optimization_barrier((dpre, a_t, sa, sb))
        d_xy = swap_y(sa), swap(sb, 2)
        a_z = [swap(a_t[k], k << 2) for k in (1, 2, 3)]
        gu = up_grad_call(scal, xn, dpre_g, store_with(attn_source), attn_shapes)

        a_z, d_xy = behind((a_z, d_xy), gu)
        a_sum = scatter_sum4(a_t[0], a_z)
        sa, sb = scatter_sum2(gd[0], d_got0, d_xy)
        x_i, sa, sb, gu, a_sum = lax.optimization_barrier((x, sa, sb, gu, a_sum))
        u_got1, u_got0 = swap(gu[3], 1), swap(gu[2], 1)
        d_yx = swap(sa, 2), swap_y(sb)
        a_other = swap_y(a_sum)
        d_x, sums_x = input_grad_call(
            scal, x_i, cot, dq, dk, dv, dpre, vec, attn_w, mlp_w, load_attn, load_half(0)
        )

        d_yx, u_got1, u_got0, a_other = behind((d_yx, u_got1, u_got0, a_other), d_x)
        sa, sb = scatter_sum1(gu[1], u_got1)
        d_t = scatter_sum3(gd[0], d_got0, d_xy, d_yx)
        x_o, sa, sb, d_t, sums_x = lax.optimization_barrier((x, sa, sb, d_t, sums_x))
        u_xy = swap_y(sa), swap(sb, 2)
        d_z = [swap(d_t[k], k << 2) for k in (1, 2, 3)]
        out = out_call(scal, x_o, o, act, vec, attn_w, mlp_w, load_attn, load_half(1))

        u_xy, d_z = behind((u_xy, d_z), out)
        sa, sb = scatter_sum2(gu[0], u_got0, u_xy)
        u_yx = swap(sa, 2), swap_y(sb)
        d_sum = scatter_sum4(d_t[0], d_z)
        u_t = scatter_sum3(gu[0], u_got0, u_xy, u_yx)
        u_z = [swap(u_t[k], k << 2) for k in (1, 2, 3)]
        d_other = swap_y(behind(d_sum, u_t))
        vg = scatter_vectors(vector_grads(sums_a, sums_d, behind(sums_x, u_t)), scal)
        u_sum = scatter_sum4(u_t[0], u_z)
        u_other = swap_y(u_sum)
        g_attn = scatter_join(a_sum, a_other, n).reshape(4, rows, width).astype(F32)
        g_up = scatter_join(u_sum, u_other, n).reshape(tiles, rows, width).astype(F32)
        grad_joined = jnp.concatenate([g_attn[0], g_attn[1], g_attn[2], *[g_up[t] for t in range(tiles)]], axis=1)
        grad_out = g_attn[3]
        grad_mlp = scatter_join(d_sum, d_other, n).reshape(tiles * rows, width).astype(F32)
    b_at = 3 * rows
    return (
        out.reshape(tokens.shape),
        d_x.reshape(tokens.shape),
        grad_joined,
        grad_out,
        grad_mlp,
        vg[:rows],
        vg[rows:b_at],
        vg[b_at : b_at + tiles * rows],
        vg[b_at + tiles * rows :],
    )


def solution(mesh):
    sizes = (mesh.shape["narrow"], mesh.shape["wide"])
    rows = P(None, ("narrow", "wide"), None)
    placed = (rows, P(None, ("narrow", "wide")), rows) + (P("wide", None),) * 3 + (P("wide"),) * 4
    return jax.shard_map(
        functools.partial(body, sizes),
        mesh=mesh,
        in_specs=placed,
        out_specs=(rows, rows) + (P("wide", None),) * 3 + (P("wide"),) * 4,
        check_vma=False,
    )
```

```python
import functools

import jax
import jax.numpy as jnp
from jax import lax
from jax.experimental import pallas as pl
from jax.experimental.pallas import tpu as pltpu
from jax.sharding import PartitionSpec as P

HEADS = 12
HEAD = 64
IMG = 196
EPS = 1e-06
GELU_C = 0.7978845608028654
GELU_A = 0.044715

F32 = jnp.float32
BF16 = jnp.bfloat16
HBM = pl.BlockSpec(memory_space=pltpu.HBM)
VMEM = pl.BlockSpec(memory_space=pltpu.VMEM)
SMEM = pl.BlockSpec(memory_space=pltpu.SMEM)


def dot_nn(a, b):
    return lax.dot_general(a, b, (((1,), (0,)), ((), ())), preferred_element_type=F32)


def dot_nt(a, b):
    return lax.dot_general(a, b, (((1,), (1,)), ((), ())), preferred_element_type=F32)


def dot_tn(a, b):
    return lax.dot_general(a, b, (((0,), (0,)), ((), ())), preferred_element_type=F32)


def norm_rows(rows):
    rows = rows.astype(F32)
    mean = jnp.mean(rows, axis=1, keepdims=True)
    centered = rows - mean
    inv = lax.rsqrt(jnp.mean(centered * centered, axis=1, keepdims=True) + EPS)
    return centered * inv, inv


def attend(refs, base, cols, windows):
    q_ref, k_ref, v_ref, da_ref, o_ref, dq_ref, dk_ref, dv_ref = refs
    zero = jnp.zeros((), BF16)
    jobs, ends = [], {}
    for start, rows, lo, hi, merge in windows:
        win = pl.ds(pl.multiple_of(base + start, 16), rows)
        tiles = [r[win, cols] for r in (q_ref, k_ref, v_ref, da_ref)]
        lane = lax.broadcasted_iota(jnp.int32, (rows, 128), 1)
        sums = {}
        step = 256 if rows == 512 else rows
        for at in range(0, rows, step):
            for h in range(2):
                keep = (lane < 64) if h == 0 else (lane >= 64)
                heads = [jnp.where(keep, t, zero) for t in tiles]
                jobs.append([tiles, heads, rows, lo, hi, at, step, sums])
        ends[len(jobs) - 1] = (start, rows, merge, sums)

    def products(job):
        tiles, heads, _, _, _, at, step, _ = job
        qs = slice(at, at + step)
        job += [dot_nt(tiles[1], heads[0][qs]), dot_nt(tiles[2], heads[3][qs])]

    def soften(job):
        _, _, rows, lo, hi, at, step, _, s, dp = job
        masked = lo > 0 or hi < rows
        if masked:
            key = lax.broadcasted_iota(jnp.int32, (rows, step), 0)
            s = jnp.where((key >= lo) & (key < hi), s, -1e30)
        e = jnp.exp(s - jnp.max(s, axis=0, keepdims=True))
        scale = 1.0 / jnp.sum(e, axis=0, keepdims=True)
        if masked:
            query = lax.broadcasted_iota(jnp.int32, (1, step), 1) + at
            scale = jnp.where((query >= lo) & (query < hi), scale, 0.0)
        p = e * scale
        inner = jnp.sum(p * dp, axis=0, keepdims=True)
        job[8:] = [p.astype(BF16), (p * (dp - inner)).astype(BF16)]

    def gather(job):
        _, heads, _, _, _, at, step, sums, p, ds = job
        qs = slice(at, at + step)
        parts = (
            (("o", at), dot_tn(p, heads[2])),
            (("q", at), dot_tn(ds, heads[1])),
            (("v", 0), dot_nn(p, heads[3][qs])),
            (("k", 0), dot_nn(ds, heads[0][qs])),
        )
        for key, val in parts:
            sums[key] = sums[key] + val if key in sums else val

    def write(start, rows, merge, sums):
        for name, ref in (("o", o_ref), ("q", dq_ref), ("k", dk_ref), ("v", dv_ref)):
            for (n, at), val in sums.items():
                if n != name:
                    continue
                val = (val * 0.125 if n == "q" else val).astype(BF16)
                size = val.shape[0]
                if merge and at == 0:
                    head = pl.ds(pl.multiple_of(base + start, 16), merge)
                    ref[head, cols] = ref[head, cols] + val[:merge]
                    val, at, size = val[merge:], merge, size - merge
                ref[pl.ds(pl.multiple_of(base + start + at, 16), size), cols] = val

    for i in range(len(jobs) + 2):
        if i < len(jobs):
            products(jobs[i])
        if 0 <= i - 1 < len(jobs):
            soften(jobs[i - 1])
        if 0 <= i - 2:
            gather(jobs[i - 2])
            if i - 2 in ends:
                write(*ends[i - 2])


WHOLE = ((0, 512, 0, 512, 0),)
SMALL = (
    (0, 208, 0, IMG, 0),
    (192, 208, IMG - 192, 2 * IMG - 192, 16),
    (384, 128, 2 * IMG - 384, 128, 16),
)


def sds(shape, dtype=BF16):
    return jax.ShapeDtypeStruct(shape, dtype)


def kept(shape, dtype=BF16):
    return pltpu.VMEM(shape, dtype)


def call(kernel, name, operands, pieces, outs, g_shapes, scratch, flops, limit=14, alias=None):
    n_p, n_g = len(pieces), len(g_shapes)
    scal, *rest = operands
    rest = [pltpu.with_memory_space_constraint(v, pltpu.VMEM) for v in rest]
    pieces = [pltpu.with_memory_space_constraint(v, pltpu.HBM) for v in pieces]
    g_shapes = [pltpu.HBM(g.shape, g.dtype) for g in g_shapes]
    return pl.pallas_call(
        kernel,
        name=name,
        out_shape=list(outs) + list(g_shapes),
        in_specs=[SMEM] + [VMEM] * len(rest) + [HBM] * n_p,
        out_specs=[VMEM] * len(outs) + [HBM] * n_g,
        scratch_shapes=scratch,
        compiler_params=pltpu.CompilerParams(vmem_limit_bytes=limit << 20),
        input_output_aliases=alias or {},
        cost_estimate=pl.CostEstimate(flops=flops, bytes_accessed=1 << 20, transcendentals=0),
    )(scal, *rest, *pieces)


def loop(count, fn, after=None):
    def step(i, c):
        fn(i)
        if after is not None:
            after(i)
        return c

    lax.fori_loop(0, count, step, 0)


def send_rows(src, dst, i, size, sem):
    per = dst.shape[1] // size
    pltpu.make_async_copy(src.at[rows_of(i, size), :], dst.at[i // per, rows_of(i % per, size), :], sem).start()


def rows_of(i, size):
    return pl.ds(pl.multiple_of(i * size, size), size)


def project_kernel(load, n_w, *refs):
    scal, x_ref, cot_ref, vec_ref = refs[:4]
    xn, q, k, v, da, w = refs[4 + n_w : 10 + n_w]
    (sem,) = refs[10 + n_w :]
    load(scal, refs[4 : 4 + n_w], w, sem, (0, 1, 2, 3))
    tokens = x_ref.shape[0]

    def norm(i):
        r = rows_of(i, 256)
        standard, _ = norm_rows(x_ref[r, :])
        xn[r, :] = (standard * vec_ref[0:1, :]).astype(BF16)

    loop(tokens // 256, norm)

    def ready(i):
        whole_wait(w.at[i], sem.at[i])()

    ready(0)
    q[...] = (dot_nn(xn[...], w[0]) + vec_ref[1:2, :]).astype(BF16) * jnp.asarray(0.125, BF16)
    ready(1)
    k[...] = dot_nn(xn[...], w[1]).astype(BF16)
    ready(2)
    v[...] = (dot_nn(xn[...], w[2]) + vec_ref[2:3, :]).astype(BF16)
    ready(3)
    da[...] = dot_nt(cot_ref[...], w[3]).astype(BF16)


def project_call(scal, x, cot, vec, weights, load):
    tokens, width = x.shape
    return call(
        functools.partial(project_kernel, load, len(weights)),
        "project",
        (scal, x, cot, vec),
        weights,
        [kept(x.shape)] * 5 + [kept((4, width, width))],
        [],
        [pltpu.SemaphoreType.DMA((4,))],
        8 * tokens * width * width,
    )


def core_kernel(scal, q, k, v, da, o, dq, dk, dv):
    tokens, width = q.shape
    pairs = width // 128

    def pair(i):
        b = i // pairs
        cols = pl.ds(pl.multiple_of(i % pairs * 128, 128), 128)
        refs = (q, k, v, da, o, dq, dk, dv)
        whole = scal[8 + b] == 0

        @pl.when(whole)
        def _():
            attend(refs, b * 512, cols, WHOLE)

        @pl.when(jnp.logical_not(whole))
        def _():
            attend(refs, b * 512, cols, SMALL)

    loop(tokens // 512 * pairs, pair)


def core_call(scal, q, k, v, da):
    return call(core_kernel, "core", (scal, q, k, v, da), [], [kept(q.shape)] * 4, [], [], 20 << 30)


def attn_grad_kernel(store, scal, xn, o, dq, dk, dv, cot, sums, *refs):
    *g_refs, g, sem = refs
    tokens, width = xn.shape
    for b, (lhs, rhs) in enumerate(((xn, dq), (xn, dk), (xn, dv), (o, cot))):
        g[b] = dot_tn(lhs[...], rhs[...]).astype(BF16)
    done = store(scal, g, g_refs, sem)
    ones = jnp.ones((8, tokens), BF16)
    sums[0:1, :] = dot_nn(ones, dq[...])[0:1]
    sums[1:2, :] = dot_nn(ones, dv[...])[0:1]
    sums[2:3, :] = dot_nn(ones, cot[...])[0:1]
    done()


def attn_grad_call(scal, xn, o, dq, dk, dv, cot, store, g_shapes):
    tokens, width = xn.shape
    return call(
        functools.partial(attn_grad_kernel, store),
        "attn_grad",
        (scal, xn, o, dq, dk, dv, cot),
        [],
        [kept((8, width), F32)],
        g_shapes,
        [pltpu.VMEM((4, width, width), BF16), pltpu.SemaphoreType.DMA((len(g_shapes),))],
        8 * tokens * width * width,
    )


def gelu_parts(u):
    u2 = u * u
    half = 0.5 * jnp.tanh(u * (GELU_C + (GELU_C * GELU_A) * u2)) + 0.5
    act = u * half
    grad = half + act * (1.0 - half) * (2.0 * GELU_C + (6.0 * GELU_C * GELU_A) * u2)
    return act, grad

def tile_of(t, width):
    return pl.ds(t * width if isinstance(t, int) else pl.multiple_of(t * width, 128), width)


def wait_tile(w, sem, t, width):
    whole_wait(w.at[tile_of(t, width), :], sem.at[t])()


def up_kernel(load_u, load_d, n_u, n_d, *refs):
    scal, xn, bias = refs[:3]
    act, gp, wu, wd = refs[3 + n_u + n_d : 7 + n_u + n_d]
    even, odd, sem_u, sem_d = refs[7 + n_u + n_d :]
    tokens, width = xn.shape
    load_u(scal, refs[3 : 3 + n_u], wu, sem_u)
    load_d(scal, refs[3 + n_u : 3 + n_u + n_d] or refs[3 : 3 + n_u], wd, sem_d)
    tiles = bias.shape[0]
    rows = even.shape[0]
    per = tokens // rows

    def product(i):
        t = i // per
        return dot_nn(xn[rows_of(i % per, rows), :], wu[tile_of(t, width), :])

    def finish(i, u):
        t, r = i // per, rows_of(i % per, rows)
        a, gr = gelu_parts(u + bias[pl.ds(t, 1), :])
        act[t, r, :] = a.astype(BF16)
        gp[t, r, :] = gr.astype(BF16)

    for t in range(tiles):
        wait_tile(wu, sem_u, t, width)
    even[...] = product(0)

    def step(i):
        odd[...] = product(2 * i + 1)
        finish(2 * i, even[...])
        even[...] = product(2 * i + 2)
        finish(2 * i + 1, odd[...])

    last = tiles * per - 1
    loop(last // 2, step)
    odd[...] = product(last)
    finish(last - 1, even[...])
    finish(last, odd[...])
    for t in range(tiles):
        wait_tile(wd, sem_d, t, width)


def up_call(scal, xn, bias, up_w, down_w, load_u, load_d):
    tokens, width = xn.shape
    tiles = bias.shape[0]
    return call(
        functools.partial(up_kernel, load_u, load_d, len(up_w), len(down_w)),
        "up",
        (scal, xn, bias),
        [*up_w, *down_w],
        [kept((tiles, tokens, width))] * 2 + [kept((tiles * width, width))] * 2,
        [],
        [pltpu.VMEM((256, width), F32)] * 2 + [pltpu.SemaphoreType.DMA((tiles,)), pltpu.SemaphoreType.DMA((tiles,))],
        2 * tiles * tokens * width * width,
    )


def down_grad_kernel(store, scal, act, cot, *refs):
    *g_refs, g, sem = refs
    tiles, tokens, width = act.shape

    def grad(t):
        g[tile_of(t, width), :] = dot_tn(act[t], cot[...]).astype(BF16)

    loop(tiles, grad)
    store(scal, g, g_refs, sem)()


def down_grad_call(scal, act, cot, store, g_shapes):
    tiles, tokens, width = act.shape
    return call(
        functools.partial(down_grad_kernel, store),
        "down_grad",
        (scal, act, cot),
        [],
        [],
        g_shapes,
        [pltpu.VMEM((tiles * width, width), BF16), pltpu.SemaphoreType.DMA((len(g_shapes),))],
        2 * tiles * tokens * width * width,
    )


def dpre_kernel(scal, cot, gp, w, dpre, sums):
    tiles, tokens, width = gp.shape
    ones = jnp.ones((8, tokens), BF16)

    def down(t):
        dpre[t] = (dot_nt(cot[...], w[tile_of(t, width), :]) * gp[t].astype(F32)).astype(BF16)

    loop(tiles, down)
    for t in range(tiles):
        sums[t : t + 1, :] = dot_nn(ones, dpre[t])[0:1]


def dpre_call(scal, cot, gp, w):
    tiles, tokens, width = gp.shape
    return call(
        dpre_kernel,
        "dpre",
        (scal, cot, gp, w),
        [],
        [kept(gp.shape), kept((8, width), F32)],
        [],
        [],
        2 * tiles * tokens * width * width,
        alias={2: 0},
    )


def up_grad_kernel(store, scal, xn, dpre, *refs):
    *g_refs, g, sem = refs
    tiles, tokens, width = dpre.shape

    def grad(t):
        g[t] = dot_tn(xn[...], dpre[t]).astype(BF16)

    loop(tiles, grad)
    store(scal, g, g_refs, sem)()


def up_grad_call(scal, xn, dpre, store, g_shapes):
    tiles, tokens, width = dpre.shape
    return call(
        functools.partial(up_grad_kernel, store),
        "up_grad",
        (scal, xn, dpre),
        [],
        [],
        g_shapes,
        [pltpu.VMEM((tiles, width, width), BF16), pltpu.SemaphoreType.DMA((len(g_shapes),))],
        2 * tiles * tokens * width * width,
    )


def input_grad_kernel(scal, x, cot, dq, dk, dv, dpre, vec, wa, wu, sums, dx_ref, dx, sem):
    tiles, tokens, width = dpre.shape
    sums[...] = jnp.zeros_like(sums)

    def step(i):
        r = rows_of(i, 256)
        dnr = dot_nt(dq[r, :], wa[0]) + dot_nt(dk[r, :], wa[1]) + dot_nt(dv[r, :], wa[2])
        for t in range(tiles):
            dnr += dot_nt(dpre[t, r, :], wu[tile_of(t, width), :])
        standard, inv = norm_rows(x[r, :])
        sums[0:1, :] += jnp.sum(dnr * standard, axis=0, keepdims=True)
        gs = dnr * vec[0:1, :]
        mean_g = jnp.mean(gs, axis=1, keepdims=True)
        mean_p = jnp.mean(gs * standard, axis=1, keepdims=True)
        dx[r, :] = (cot[r, :].astype(F32) + inv * (gs - mean_g - standard * mean_p)).astype(BF16)

    loop(tokens // 256, step, lambda i: send_rows(dx, dx_ref, i, 256, sem))
    whole_wait(dx_ref, sem)()


def input_grad_call(scal, x, cot, dq, dk, dv, dpre, vec, wa, wu):
    tiles, tokens, width = dpre.shape
    return call(
        input_grad_kernel,
        "input_grad",
        (scal, x, cot, dq, dk, dv, dpre, vec, wa, wu),
        [],
        [kept((8, width), F32)],
        [sds((tokens // 512, 512, width))],
        [pltpu.VMEM((tokens, width), BF16), pltpu.SemaphoreType.DMA],
        2 * (tiles + 3) * tokens * width * width,
    )


def out_kernel(scal, x, o, act, vec, wa, wd, out_ref, out, sem):
    tiles, tokens, width = act.shape

    def step(i):
        r = rows_of(i, 256)
        total = x[r, :].astype(F32) + vec[3:4, :] + dot_nn(o[r, :], wa[3])
        for t in range(tiles):
            total += dot_nn(act[t, r, :], wd[tile_of(t, width), :])
        out[r, :] = total.astype(BF16)

    loop(tokens // 256, step, lambda i: send_rows(out, out_ref, i, 256, sem))
    whole_wait(out_ref, sem)()


def out_call(scal, x, o, act, vec, wa, wd):
    tiles, tokens, width = act.shape
    (out,) = call(
        out_kernel,
        "out",
        (scal, x, o, act, vec, wa, wd),
        [],
        [],
        [sds((tokens // 512, 512, width))],
        [pltpu.VMEM((tokens, width), BF16), pltpu.SemaphoreType.DMA],
        2 * (tiles + 1) * tokens * width * width,
    )
    return out


def swap(value, mask):
    return lax.ppermute(value, "wide", [(i, i ^ mask) for i in range(16)])


def swap_y(value):
    return lax.ppermute(value, "narrow", [(0, 1), (1, 0)])


def slots():
    for part in range(2):
        for i in range(2):
            for s in range(2):
                half, side = (i, s) if part == 0 else (s, i)
                for k in range(4):
                    yield part, i, s * 4 + k, half, side, k


def device_of(scal, k, side, core):
    return ((scal[1] ^ k) * 2 + (scal[2] ^ side)) * 2 + (scal[3] ^ core)


def behind(value, *marks):
    return lax.optimization_barrier((value, marks))[0]


def gather_z(value):
    return [swap(value, k << 2) for k in (1, 2, 3)]


def gather_stack(half, got):
    got = [half] + got
    return [jnp.stack([t[i] for t in got]) for i in range(2)]


def gather_xy(za, zb):
    return swap(za, 2), swap_y(zb)


def total(*parts):
    return sum(v.astype(F32) for v in parts)


def mix(name, jobs):
    held = [v for job in jobs for v in job[1]]
    near = [v for job in jobs for v in job[2]]
    outs = [o for job in jobs for o in job[3]]

    def kernel(*refs):
        at = len(near) + len(held)
        scratch = refs[at + len(outs) :]
        copies = [
            pltpu.make_async_copy(refs[len(near) + i], scratch[i], scratch[-1].at[i]) for i in range(len(held))
        ]
        for cp in copies:
            cp.start()
        h = n = o = 0
        for fn, job_h, job_n, job_o in jobs:
            for i in range(len(job_h)):
                copies[h + i].wait()
            fn(
                scratch[h : h + len(job_h)],
                refs[n : n + len(job_n)],
                refs[at + o : at + o + len(job_o)],
            )
            h, n, o = h + len(job_h), n + len(job_n), o + len(job_o)

    got = pl.pallas_call(
        kernel,
        name=name,
        out_shape=outs,
        in_specs=[VMEM] * len(near) + [HBM] * len(held),
        out_specs=[VMEM] * len(outs),
        scratch_shapes=[pltpu.VMEM(v.shape, v.dtype) for v in held]
        + [pltpu.SemaphoreType.DMA((max(len(held), 1),))],
        compiler_params=pltpu.CompilerParams(vmem_limit_bytes=8 << 20),
        cost_estimate=pl.CostEstimate(flops=1 << 20, bytes_accessed=1 << 20, transcendentals=0),
    )(
        *[pltpu.with_memory_space_constraint(v, pltpu.VMEM) for v in near],
        *[pltpu.with_memory_space_constraint(v, pltpu.HBM) for v in held],
    )
    split, at = [], 0
    for job in jobs:
        split.append(got[at : at + len(job[3])])
        at += len(job[3])
    return split


def total(*parts):
    return sum(v.astype(F32) for v in parts)


def join_job(pairs):
    def fn(held, near, outs):
        for i, out in enumerate(outs):
            size = near[2 * i].shape[0]
            out[:size] = near[2 * i][...]
            out[size:] = near[2 * i + 1][...]

    near = [v for pair in pairs for v in pair]
    return fn, [], near, [kept((2 * a.shape[0], *a.shape[1:])) for a, _ in pairs]


def sum1_job(keep1, got1):
    def fn(held, near, outs):
        for i in range(2):
            outs[i][...] = total(held[0][i], near[0][i]).astype(BF16)

    return fn, [keep1], [got1], [kept(keep1.shape[1:])] * 2


def sum2_job(keep0, got0, got):
    half = keep0.shape[1] // 2

    def fn(held, near, outs):
        for i in range(2):
            outs[i][...] = total(held[0][i, half:], near[0][i, half:], near[1 + i][half:]).astype(BF16)

    return fn, [keep0], [got0, *got], [kept((half, *keep0.shape[2:]))] * 2


def sum3_job(keep0, got0, got, got2):
    half = keep0.shape[1] // 2

    def fn(held, near, outs):
        for k in range(half):
            for i in range(2):
                outs[k][i] = total(held[0][i, k], near[0][i, k], near[1 + i][k], near[3 + i][k]).astype(BF16)

    return fn, [keep0], [got0, *got, *got2], [kept((2, *keep0.shape[2:]))] * half


def sum4_job(own, got):
    def fn(held, near, outs):
        outs[0][...] = total(*[v[...] for v in near]).astype(BF16)

    return fn, [], [own, *got], [kept(own.shape)]


def place_kernel(scal, a_mine, a_other, d_mine, d_other, u_mine, u_other, joined, out, down):
    _, rows, width = a_mine.shape

    def place(half, a, d, u):
        for p in range(2):
            block = half * 2 + p
            down[pl.ds(block * rows, rows), :] = d[p].astype(F32)
            joined[:, (3 + block) * width : (4 + block) * width] = u[p].astype(F32)
            if block < 3:
                joined[:, block * width : (block + 1) * width] = a[p].astype(F32)
            else:
                out[...] = a[p].astype(F32)

    @pl.when(scal[0] == 0)
    def _():
        place(0, a_mine, d_mine, u_mine)
        place(1, a_other, d_other, u_other)

    @pl.when(scal[0] != 0)
    def _():
        place(1, a_mine, d_mine, u_mine)
        place(0, a_other, d_other, u_other)


def place_call(scal, parts):
    _, rows, width = parts[0].shape
    return pl.pallas_call(
        place_kernel,
        name="place",
        out_shape=[sds((rows, 7 * width), F32), sds((rows, width), F32), sds((4 * rows, width), F32)],
        in_specs=[SMEM] + [VMEM] * 6,
        out_specs=[VMEM] * 3,
    )(scal, *[pltpu.with_memory_space_constraint(v, pltpu.VMEM) for v in parts])


def whole_wait(ref, sem):
    return pltpu.make_async_copy(ref, ref, sem).wait


def load_attn(scal, refs, w, sem, blocks):
    def start(own):
        for block in blocks:
            for core in range(2):
                for part, i, slot, half, side, k in slots():
                    if (own ^ half) * 2 + part != block:
                        continue
                    src = refs[core * 4 + part * 2 + i]
                    rows = src.shape[1]
                    at = pl.multiple_of(device_of(scal, k, side, core) * rows, 16)
                    pltpu.make_async_copy(src.at[slot], w.at[block, pl.ds(at, rows), :], sem.at[block]).start()

    @pl.when(scal[0] == 0)
    def _():
        start(0)

    @pl.when(scal[0] != 0)
    def _():
        start(1)


def load_half(which):
    def load(scal, refs, w, sem):
        def start(rel):
            for core in range(2):
                for part, i, slot, half, side, k in slots():
                    if half != rel:
                        continue
                    src = refs[core * 4 + part * 2 + i]
                    per, rows, width = src.shape[1:]
                    dev = device_of(scal, k, side, core)
                    for b in range(per):
                        block = part * per + b
                        if which == 0:
                            at, tile = block * width + dev * rows, block
                        else:
                            at, tile = (dev * 2 * per + block) * rows, scal[1] ^ k
                        dst = w.at[pl.ds(pl.multiple_of(at, 16), rows), :]
                        pltpu.make_async_copy(src.at[slot, b], dst, sem.at[tile]).start()

        @pl.when(scal[0] == which)
        def _():
            start(0)

        @pl.when(scal[0] != which)
        def _():
            start(1)

    return load


def store_with(source):
    def store(scal, g, refs, sem):
        for core in range(2):
            for part, i, slot, half, side, k in slots():
                at = core * 2 + i
                dst = refs[at]
                src = source(g, scal[0] ^ half, part, device_of(scal, k, side, core), dst.shape[2], dst.shape[3])
                pltpu.make_async_copy(src, dst.at[part, slot], sem.at[at]).start()

        def done():
            for at in range(4):
                whole_wait(refs[at], sem.at[at])()

        return done

    return store


def rows_at(base, rows):
    return pl.ds(pl.multiple_of(base, 16), rows)


def attn_source(g, half, part, dev, rows, cols):
    return g.at[half * 2 + part, rows_at(dev * rows, rows), :]


def down_source(g, half, part, dev, rows, cols):
    return g.at[rows_at((dev * 4 + half * 2 + part) * rows, rows), :]


def load_whole_attn(scal, refs, w, sem, blocks):
    for i in blocks:
        pltpu.make_async_copy(refs[i], w.at[i], sem.at[i]).start()


def load_whole_mlp(scal, refs, w, sem):
    width = w.shape[1]
    for i, r in enumerate(refs):
        for t in range(r.shape[0] // width):
            at = i + t
            src = r.at[pl.ds(t * width, width), :]
            pltpu.make_async_copy(src, w.at[pl.ds(at * width, width), :], sem.at[at]).start()


def store_whole(scal, g, refs, sem):
    if len(refs) == 1:
        copies = [pltpu.make_async_copy(g, refs[0], sem.at[0])]
    else:
        copies = [pltpu.make_async_copy(g.at[i], r, sem.at[i]) for i, r in enumerate(refs)]
    for cp in copies:
        cp.start()

    def done():
        for cp in copies:
            cp.wait()

    return done


def body(sizes, tokens, image_ids, cotangent, w_joined, w_out, w_mlp, norm_gain, bias_attn, bias_mlp, bias_out):
    micro, length, width = tokens.shape
    narrow, wide = sizes
    paired = narrow == 2 and wide == 16
    rows = width // wide
    tiles = w_mlp.shape[0] // rows
    x = tokens.reshape(micro * length, width)
    cot = cotangent.reshape(micro * length, width)
    n = lax.axis_index("narrow")
    w = lax.axis_index("wide")
    last = image_ids.reshape(-1, 512)[:, -1]
    scal = [n, w >> 2, (w >> 1) & 1, w & 1] + [jnp.int32(0)] * 4 + [last[b] for b in range(last.shape[0])]
    scal = jnp.stack([jnp.asarray(s, jnp.int32) for s in scal])
    vec_own = jnp.concatenate([norm_gain, bias_attn, bias_mlp, bias_out])

    def vectors(vec):
        vec = vec.astype(F32)
        b_at = 3 * rows
        b_mlp = vec[:, b_at : b_at + tiles * rows].reshape(tiles, width)
        head = [
            vec[:, :rows].reshape(1, width),
            vec[:, rows:b_at].reshape(2, width),
            vec[:, b_at + tiles * rows :].reshape(1, width),
            jnp.zeros((4, width), F32),
        ]
        return jnp.concatenate(head), b_mlp

    def vector_grads(sums_a, sums_d, sums_x):
        return jnp.concatenate(
            [
                sums_x[0].reshape(wide, rows),
                sums_a[:2].reshape(wide, 2 * rows),
                sums_d[:tiles].reshape(wide, tiles * rows),
                sums_a[2].reshape(wide, rows),
            ],
            axis=1,
        )

    if not paired:
        full = lax.all_gather(w_joined, "wide", axis=0, tiled=True)
        parts = [full[:, i * width : (i + 1) * width] for i in range(3 + tiles)]
        attn_w = parts[:3] + [lax.all_gather(w_out, "wide", axis=0, tiled=True)]
        up_w = parts[3:]
        down_w = [lax.all_gather(w_mlp, "wide", axis=0, tiled=True)]
        vec, b_mlp = vectors(lax.all_gather(vec_own, "wide", axis=0))
        square = [sds((width, width))]
        xn, q, k, v, da, wa = project_call(scal, x, cot, vec, attn_w, load_whole_attn)
        o, dq, dk, dv = core_call(scal, q, k, v, da)
        sums_a, *g_attn = attn_grad_call(scal, xn, o, dq, dk, dv, cot, store_whole, square * 4)
        act, gp, wu, wd = up_call(scal, xn, b_mlp, up_w, down_w, load_whole_mlp, load_whole_mlp)
        g_down = down_grad_call(scal, act, cot, store_whole, [sds((tiles * width, width))])
        dpre, sums_d = dpre_call(scal, cot, gp, wd)
        g_up = up_grad_call(scal, xn, dpre, store_whole, square * tiles)
        sums_x, d_x = input_grad_call(scal, x, cot, dq, dk, dv, dpre, vec, wa, wu)
        out = out_call(scal, x, o, act, vec, wa, wd)

        def reduce(g):
            g = lax.psum_scatter(g.astype(F32), "wide", scatter_dimension=0, tiled=True)
            return lax.psum(g, "narrow")

        grad_joined = reduce(jnp.concatenate([*g_attn[:3], *g_up], axis=1))
        grad_out = reduce(g_attn[3])
        grad_mlp = reduce(g_down[0])
        vg = reduce(vector_grads(sums_a, sums_d, sums_x))[0]
    else:
        col = lambda i: w_joined[:, i * width : (i + 1) * width]
        half = jnp.stack([jnp.where(n == 0, col(0), col(2)), jnp.where(n == 0, col(1), w_out)])
        got = gather_z(half)
        v_own = behind(vec_own, half)
        v_all = lax.all_to_all(jnp.broadcast_to(v_own, (wide, *v_own.shape)), "wide", 0, 0, tiled=True)
        w_up, v_all = lax.optimization_barrier((behind(w_joined, half), v_all))
        cols = jnp.stack([w_up[:, (3 + t) * width : (4 + t) * width] for t in range(tiles)])
        c_half = jnp.where(n == 0, cols, w_mlp.reshape(tiles, rows, width))
        c_half = c_half.reshape(2, tiles // 2, rows, width)
        c_got = gather_z(c_half)
        za, zb = gather_stack(half, got)
        xa, yb = gather_xy(za, zb)
        vec, b_mlp = vectors(v_all)
        a0, b0 = jnp.concatenate([za, xa]), jnp.concatenate([zb, yb])
        a1, b1 = swap_y(a0), swap(b0, 2)
        a0s, b0s = swap(a0, 1), swap(b0, 1)
        attn_w = [a0, a1, b0, b1, a0s, swap(a1, 1), b0s, swap(b1, 1)]

        cza, czb = gather_stack(c_half, c_got)
        xp, attn_w, vec, b_mlp, cza, czb = lax.optimization_barrier((x, attn_w, vec, b_mlp, cza, czb))
        cxa, cyb = gather_xy(cza, czb)
        xn, q, k, v, da, wa = project_call(scal, xp, cot, vec, attn_w, load_attn)

        cxa, cyb = behind((cxa, cyb), q)
        ((ca0, cb0),) = mix("join", [join_job([(cza, cxa), (czb, cyb)])])
        q, ca0, cb0 = lax.optimization_barrier((q, ca0, cb0))
        ca1, cb1 = swap_y(ca0), swap(cb0, 2)
        ca0s, cb0s = swap(ca0, 1), swap(cb0, 1)
        o, dq, dk, dv = core_call(scal, q, k, v, da)

        ca1, cb1 = behind((ca1, cb1), dq)
        dq, ca1, cb1 = lax.optimization_barrier((dq, ca1, cb1))
        ca1s, cb1s = swap(ca1, 1), swap(cb1, 1)
        attn_shapes = [sds((2, 8, rows, width))] * 4
        sums_a, *ga = attn_grad_call(scal, xn, o, dq, dk, dv, cot, store_with(attn_source), attn_shapes)
        mlp_w = [ca0, ca1, cb0, cb1, ca0s, *behind([ca1s, cb0s, cb1s], sums_a)]

        a_got1, a_got0 = swap(ga[3], 1), swap(ga[2], 1)
        xn_u = behind(xn, ga)
        act, gp, wu, wd = up_call(scal, xn_u, b_mlp, mlp_w, [], load_half(0), load_half(1))

        a_got1, a_got0 = behind((a_got1, a_got0), gp)
        ((sa, sb),) = mix("sums_1", [sum1_job(ga[1], a_got1)])
        act_g, sa, sb = lax.optimization_barrier((act, sa, sb))
        a_xy = swap_y(sa), swap(sb, 2)
        gd = down_grad_call(scal, act_g, cot, store_with(down_source), attn_shapes)

        a_xy = behind(a_xy, gd)
        ((sa, sb),) = mix("sums_2", [sum2_job(ga[0], a_got0, a_xy)])
        gp, sa, sb, gd = lax.optimization_barrier((gp, sa, sb, gd))
        a_yx = swap(sa, 2), swap_y(sb)
        d_got1, d_got0 = swap(gd[3], 1), swap(gd[2], 1)
        dpre, sums_d = dpre_call(scal, cot, gp, wd)

        a_yx, d_got1, d_got0 = behind((a_yx, d_got1, d_got0), dpre)
        a_t, (sa, sb) = mix("sums_3", [sum3_job(ga[0], a_got0, a_xy, a_yx), sum1_job(gd[1], d_got1)])
        dpre_g, a_t, sa, sb = lax.optimization_barrier((dpre, a_t, sa, sb))
        d_xy = swap_y(sa), swap(sb, 2)
        a_z = [swap(a_t[k], k << 2) for k in (1, 2, 3)]
        gu = up_grad_call(scal, xn, dpre_g, store_with(attn_source), attn_shapes)

        a_z, d_xy = behind((a_z, d_xy), gu)
        (a_sum,), (sa, sb) = mix("sums_4", [sum4_job(a_t[0], a_z), sum2_job(gd[0], d_got0, d_xy)])
        x_i, sa, sb, gu, a_sum = lax.optimization_barrier((x, sa, sb, gu, a_sum))
        u_got1, u_got0 = swap(gu[3], 1), swap(gu[2], 1)
        d_yx = swap(sa, 2), swap_y(sb)
        a_other = swap_y(a_sum)
        sums_x, d_x = input_grad_call(scal, x_i, cot, dq, dk, dv, dpre, vec, wa, wu)

        d_yx, u_got1, u_got0, a_other = behind((d_yx, u_got1, u_got0, a_other), d_x)
        (sa, sb), d_t = mix("sums_5", [sum1_job(gu[1], u_got1), sum3_job(gd[0], d_got0, d_xy, d_yx)])
        x_o, sa, sb, d_t, sums_x = lax.optimization_barrier((x, sa, sb, d_t, sums_x))
        u_xy = swap_y(sa), swap(sb, 2)
        d_z = [swap(d_t[k], k << 2) for k in (1, 2, 3)]
        out = out_call(scal, x_o, o, act, vec, wa, wd)

        late = (u_xy, d_z, a_sum, a_other, sums_a, sums_d, sums_x)
        u_xy, d_z, a_sum, a_other, sums_a, sums_d, sums_x = behind(late, out)
        ((sa, sb),) = mix("sums_6", [sum2_job(gu[0], u_got0, u_xy)])
        u_yx = swap(sa, 2), swap_y(sb)
        sums_a, sums_d, sums_x, d_z = behind((sums_a, sums_d, sums_x, d_z), sa, sb)
        v_sum = lax.all_to_all(vector_grads(sums_a, sums_d, sums_x), "wide", 0, 0, tiled=True)
        v_sum = jnp.sum(v_sum, axis=0)
        (d_sum,), u_t = mix(
            "sums_7", [sum4_job(d_t[0], behind(d_z, v_sum)), sum3_job(gu[0], u_got0, u_xy, u_yx)]
        )
        u_z = [swap(u_t[k], k << 2) for k in (1, 2, 3)]
        d_other = swap_y(d_sum)
        vg = v_sum + swap_y(v_sum)
        ((u_sum,),) = mix("sums_8", [sum4_job(u_t[0], u_z)])
        u_other = swap_y(u_sum)
        grad_joined, grad_out, grad_mlp = place_call(
            scal, [a_sum, a_other, d_sum, d_other, u_sum, u_other]
        )
    b_at = 3 * rows
    return (
        out.reshape(tokens.shape),
        d_x.reshape(tokens.shape),
        grad_joined,
        grad_out,
        grad_mlp,
        vg[:rows],
        vg[rows:b_at],
        vg[b_at : b_at + tiles * rows],
        vg[b_at + tiles * rows :],
    )


def solution(mesh):
    sizes = (mesh.shape["narrow"], mesh.shape["wide"])
    rows = P(None, ("narrow", "wide"), None)
    placed = (rows, P(None, ("narrow", "wide")), rows) + (P("wide", None),) * 3 + (P("wide"),) * 4
    return jax.shard_map(
        functools.partial(body, sizes),
        mesh=mesh,
        in_specs=placed,
        out_specs=(rows, rows) + (P("wide", None),) * 3 + (P("wide"),) * 4,
        check_vma=False,
    )
```

```python
import functools

import jax
import jax.numpy as jnp
from jax import lax
from jax.experimental import pallas as pl
from jax.experimental.pallas import tpu as pltpu
from jax.sharding import PartitionSpec as P

HEADS = 12
HEAD = 64
IMG = 196
EPS = 1e-06
GELU_C = 0.7978845608028654
GELU_A = 0.044715

F32 = jnp.float32
BF16 = jnp.bfloat16
HBM = pl.BlockSpec(memory_space=pltpu.HBM)
VMEM = pl.BlockSpec(memory_space=pltpu.VMEM)
SMEM = pl.BlockSpec(memory_space=pltpu.SMEM)


def dot_nn(a, b):
    return lax.dot_general(a, b, (((1,), (0,)), ((), ())), preferred_element_type=F32)


def dot_nt(a, b):
    return lax.dot_general(a, b, (((1,), (1,)), ((), ())), preferred_element_type=F32)


def dot_tn(a, b):
    return lax.dot_general(a, b, (((0,), (0,)), ((), ())), preferred_element_type=F32)


def norm_rows(rows):
    rows = rows.astype(F32)
    mean = jnp.mean(rows, axis=1, keepdims=True)
    centered = rows - mean
    inv = lax.rsqrt(jnp.mean(centered * centered, axis=1, keepdims=True) + EPS)
    return centered * inv, inv


def attend(refs, base, cols, windows):
    q_ref, k_ref, v_ref, da_ref, o_ref, dq_ref, dk_ref, dv_ref = refs
    zero = jnp.zeros((), BF16)
    jobs, ends = [], {}
    for start, rows, lo, hi, merge in windows:
        win = pl.ds(pl.multiple_of(base + start, 16), rows)
        tiles = [r[win, cols] for r in (q_ref, k_ref, v_ref, da_ref)]
        lane = lax.broadcasted_iota(jnp.int32, (rows, 128), 1)
        sums = {}
        step = 256 if rows == 512 else rows
        for at in range(0, rows, step):
            for h in range(2):
                keep = (lane < 64) if h == 0 else (lane >= 64)
                heads = [jnp.where(keep, t, zero) for t in tiles]
                jobs.append([tiles, heads, rows, lo, hi, at, step, sums])
        ends[len(jobs) - 1] = (start, rows, merge, sums)

    def products(job):
        tiles, heads, _, _, _, at, step, _ = job
        qs = slice(at, at + step)
        job += [dot_nt(tiles[1], heads[0][qs]), dot_nt(tiles[2], heads[3][qs])]

    def soften(job):
        _, _, rows, lo, hi, at, step, _, s, dp = job
        masked = lo > 0 or hi < rows
        if masked:
            key = lax.broadcasted_iota(jnp.int32, (rows, step), 0)
            s = jnp.where((key >= lo) & (key < hi), s, -1e30)
        e = jnp.exp(s - jnp.max(s, axis=0, keepdims=True))
        scale = 1.0 / jnp.sum(e, axis=0, keepdims=True)
        if masked:
            query = lax.broadcasted_iota(jnp.int32, (1, step), 1) + at
            scale = jnp.where((query >= lo) & (query < hi), scale, 0.0)
        p = e * scale
        inner = jnp.sum(p * dp, axis=0, keepdims=True)
        job[8:] = [p.astype(BF16), (p * (dp - inner)).astype(BF16)]

    def gather(job):
        _, heads, _, _, _, at, step, sums, p, ds = job
        qs = slice(at, at + step)
        parts = (
            (("o", at), dot_tn(p, heads[2])),
            (("q", at), dot_tn(ds, heads[1])),
            (("v", 0), dot_nn(p, heads[3][qs])),
            (("k", 0), dot_nn(ds, heads[0][qs])),
        )
        for key, val in parts:
            sums[key] = sums[key] + val if key in sums else val

    def write(start, rows, merge, sums):
        for name, ref in (("o", o_ref), ("q", dq_ref), ("k", dk_ref), ("v", dv_ref)):
            for (n, at), val in sums.items():
                if n != name:
                    continue
                val = (val * 0.125 if n == "q" else val).astype(BF16)
                size = val.shape[0]
                if merge and at == 0:
                    head = pl.ds(pl.multiple_of(base + start, 16), merge)
                    ref[head, cols] = ref[head, cols] + val[:merge]
                    val, at, size = val[merge:], merge, size - merge
                ref[pl.ds(pl.multiple_of(base + start + at, 16), size), cols] = val

    for i in range(len(jobs) + 2):
        if i < len(jobs):
            products(jobs[i])
        if 0 <= i - 1 < len(jobs):
            soften(jobs[i - 1])
        if 0 <= i - 2:
            gather(jobs[i - 2])
            if i - 2 in ends:
                write(*ends[i - 2])


WHOLE = ((0, 512, 0, 512, 0),)
SMALL = (
    (0, 208, 0, IMG, 0),
    (192, 208, IMG - 192, 2 * IMG - 192, 16),
    (384, 128, 2 * IMG - 384, 128, 16),
)


def sds(shape, dtype=BF16):
    return jax.ShapeDtypeStruct(shape, dtype)


def kept(shape, dtype=BF16):
    return pltpu.VMEM(shape, dtype)


def call(kernel, name, operands, pieces, outs, g_shapes, scratch, flops, limit=14, alias=None):
    n_p, n_g = len(pieces), len(g_shapes)
    scal, *rest = operands
    rest = [pltpu.with_memory_space_constraint(v, pltpu.VMEM) for v in rest]
    pieces = [pltpu.with_memory_space_constraint(v, pltpu.HBM) for v in pieces]
    g_shapes = [pltpu.HBM(g.shape, g.dtype) for g in g_shapes]
    return pl.pallas_call(
        kernel,
        name=name,
        out_shape=list(outs) + list(g_shapes),
        in_specs=[SMEM] + [VMEM] * len(rest) + [HBM] * n_p,
        out_specs=[VMEM] * len(outs) + [HBM] * n_g,
        scratch_shapes=scratch,
        compiler_params=pltpu.CompilerParams(vmem_limit_bytes=limit << 20),
        input_output_aliases=alias or {},
        cost_estimate=pl.CostEstimate(flops=flops, bytes_accessed=1 << 20, transcendentals=0),
    )(scal, *rest, *pieces)


def loop(count, fn, after=None):
    def step(i, c):
        fn(i)
        if after is not None:
            after(i)
        return c

    lax.fori_loop(0, count, step, 0)


def send_rows(src, dst, i, size, sem):
    per = dst.shape[1] // size
    pltpu.make_async_copy(src.at[rows_of(i, size), :], dst.at[i // per, rows_of(i % per, size), :], sem).start()


def rows_of(i, size):
    return pl.ds(pl.multiple_of(i * size, size), size)


def project_kernel(load, n_w, *refs):
    scal, x_ref, cot_ref, vec_ref = refs[:4]
    xn, q, k, v, da, w = refs[4 + n_w : 10 + n_w]
    (sem,) = refs[10 + n_w :]
    load(scal, refs[4 : 4 + n_w], w, sem)
    tokens = x_ref.shape[0]

    def norm(i):
        r = rows_of(i, 256)
        standard, _ = norm_rows(x_ref[r, :])
        xn[r, :] = (standard * vec_ref[0:1, :]).astype(BF16)

    loop(tokens // 256, norm)

    def ready(i):
        whole_wait(w.at[i], sem.at[i])()

    def each(fn):
        loop(tokens // 512, lambda i: fn(rows_of(i, 512)))

    def queries(r):
        q[r, :] = (dot_nn(xn[r, :], w[0]) + vec_ref[1:2, :]).astype(BF16) * jnp.asarray(0.125, BF16)

    def keys(r):
        k[r, :] = dot_nn(xn[r, :], w[1]).astype(BF16)

    def values(r):
        v[r, :] = (dot_nn(xn[r, :], w[2]) + vec_ref[2:3, :]).astype(BF16)

    def attended(r):
        da[r, :] = dot_nt(cot_ref[r, :], w[3]).astype(BF16)

    for i, fn in enumerate((queries, keys, values, attended)):
        ready(i)
        each(fn)


def project_call(scal, x, cot, vec, weights, load):
    tokens, width = x.shape
    return call(
        functools.partial(project_kernel, load, len(weights)),
        "project",
        (scal, x, cot, vec),
        weights,
        [kept(x.shape)] * 5 + [kept((4, width, width))],
        [],
        [pltpu.SemaphoreType.DMA((4,))],
        8 * tokens * width * width,
    )


def core_kernel(b, scal, q, k, v, da, *refs):
    o, d = refs[-2:]
    refs = (q, k, v, da, o, d.at[0], d.at[1], d.at[2])
    whole = scal[8 + b] == 0

    def pair(i):
        cols = pl.ds(pl.multiple_of(i * 128, 128), 128)

        @pl.when(whole)
        def _():
            attend(refs, b * 512, cols, WHOLE)

        @pl.when(jnp.logical_not(whole))
        def _():
            attend(refs, b * 512, cols, SMALL)

    loop(q.shape[1] // 128, pair)


def core_call(b, scal, q, k, v, da, *before):
    return call(
        functools.partial(core_kernel, b),
        "core",
        (scal, q, k, v, da, *before),
        [],
        [kept(q.shape), kept((3, *q.shape))],
        [],
        [],
        10 << 30,
        alias={5 + i: i for i in range(len(before))},
    )


def attn_grad_kernel(store, scal, xn, o, d, cot, sums, *refs):
    *g_refs, g, sem = refs
    tokens, width = xn.shape

    def grad(b):
        g[b] = dot_tn(xn[...], d[b]).astype(BF16)

    loop(3, grad)
    g[3] = dot_tn(o[...], cot[...]).astype(BF16)
    done = store(scal, g, g_refs, sem)
    ones = jnp.ones((8, tokens), BF16)
    sums[0:1, :] = dot_nn(ones, d[0])[0:1]
    sums[1:2, :] = dot_nn(ones, d[2])[0:1]
    sums[2:3, :] = dot_nn(ones, cot[...])[0:1]
    done()


def attn_grad_call(scal, xn, o, d, cot, store, g_shapes):
    tokens, width = xn.shape
    return call(
        functools.partial(attn_grad_kernel, store),
        "attn_grad",
        (scal, xn, o, d, cot),
        [],
        [kept((8, width), F32)],
        g_shapes,
        [pltpu.VMEM((4, width, width), BF16), pltpu.SemaphoreType.DMA((len(g_shapes),))],
        8 * tokens * width * width,
    )


def gelu_parts(u):
    u2 = u * u
    half = 0.5 * jnp.tanh(u * (GELU_C + (GELU_C * GELU_A) * u2)) + 0.5
    act = u * half
    grad = half + act * (1.0 - half) * (2.0 * GELU_C + (6.0 * GELU_C * GELU_A) * u2)
    return act, grad

def tile_of(t, width):
    return pl.ds(t * width if isinstance(t, int) else pl.multiple_of(t * width, 128), width)


def wait_tile(w, sem, t, width):
    whole_wait(w.at[tile_of(t, width), :], sem.at[t])()


def up_kernel(load, first, count, n_p, *refs):
    scal, xn, bias = refs[:3]
    even, odd, sem = refs[-3:]
    tokens, width = xn.shape
    if n_p:
        act, gp, w = refs[-6:-3]
        load(scal, refs[3 : 3 + n_p], w, sem)
        for t in range(bias.shape[0]):
            whole_wait(w.at[t], sem.at[t])()
    else:
        act, gp = refs[-5:-3]
        w = refs[5]
    rows = even.shape[0]
    per = tokens // rows

    def product(i):
        return dot_nn(xn[rows_of(i % per, rows), :], w[first + i // per])

    def finish(i, u):
        t, r = first + i // per, rows_of(i % per, rows)
        a, gr = gelu_parts(u + bias[pl.ds(t, 1), :])
        act[t, r, :] = a.astype(BF16)
        gp[t, r, :] = gr.astype(BF16)

    even[...] = product(0)

    def step(i):
        odd[...] = product(2 * i + 1)
        finish(2 * i, even[...])
        even[...] = product(jnp.minimum(2 * i + 2, count * per - 1))
        finish(2 * i + 1, odd[...])

    loop(count * per // 2, step)


def up_call(first, count, scal, xn, bias, before, pieces, load):
    tokens, width = xn.shape
    tiles = bias.shape[0]
    return call(
        functools.partial(up_kernel, load, first, count, len(pieces)),
        "up",
        (scal, xn, bias, *before),
        pieces,
        [kept((tiles, tokens, width))] * 2 + [kept((tiles, width, width))] * (1 if pieces else 0),
        [],
        [pltpu.VMEM((256, width), F32)] * 2 + [pltpu.SemaphoreType.DMA((tiles,))],
        2 * count * tokens * width * width,
        alias={3: 0, 4: 1} if before else None,
    )


def down_grad_kernel(store, scal, act, cot, *refs):
    *g_refs, g, sem = refs
    tiles, tokens, width = act.shape

    def grad(t):
        g[tile_of(t, width), :] = dot_tn(act[t], cot[...]).astype(BF16)

    loop(tiles, grad)
    store(scal, g, g_refs, sem)()


def down_grad_call(scal, act, cot, store, g_shapes):
    tiles, tokens, width = act.shape
    return call(
        functools.partial(down_grad_kernel, store),
        "down_grad",
        (scal, act, cot),
        [],
        [],
        g_shapes,
        [pltpu.VMEM((tiles * width, width), BF16), pltpu.SemaphoreType.DMA((len(g_shapes),))],
        2 * tiles * tokens * width * width,
    )


def dpre_kernel(load, n_p, *refs):
    scal, cot, gp = refs[:3]
    dpre, sums, w, sem = refs[3 + n_p :]
    tiles, tokens, width = gp.shape
    load(scal, refs[3 : 3 + n_p], w, sem)
    ones = jnp.ones((8, tokens), BF16)

    def down(t):
        wait_tile(w, sem, t, width)
        dpre[t] = (dot_nt(cot[...], w[tile_of(t, width), :]) * gp[t].astype(F32)).astype(BF16)

    loop(tiles, down)
    for t in range(tiles):
        sums[t : t + 1, :] = dot_nn(ones, dpre[t])[0:1]


def dpre_call(scal, cot, gp, pieces, load):
    tiles, tokens, width = gp.shape
    return call(
        functools.partial(dpre_kernel, load, len(pieces)),
        "dpre",
        (scal, cot, gp),
        pieces,
        [kept(gp.shape), kept((8, width), F32), kept((tiles * width, width))],
        [],
        [pltpu.SemaphoreType.DMA((tiles,))],
        2 * tiles * tokens * width * width,
        alias={2: 0},
    )


def up_grad_kernel(store, scal, xn, dpre, *refs):
    *g_refs, g, sem = refs
    tiles, tokens, width = dpre.shape

    def grad(t):
        g[t] = dot_tn(xn[...], dpre[t]).astype(BF16)

    loop(tiles, grad)
    store(scal, g, g_refs, sem)()


def up_grad_call(scal, xn, dpre, store, g_shapes):
    tiles, tokens, width = dpre.shape
    return call(
        functools.partial(up_grad_kernel, store),
        "up_grad",
        (scal, xn, dpre),
        [],
        [],
        g_shapes,
        [pltpu.VMEM((tiles, width, width), BF16), pltpu.SemaphoreType.DMA((len(g_shapes),))],
        2 * tiles * tokens * width * width,
    )


def input_grad_kernel(scal, x, cot, d, dpre, vec, wa, wu, sums, dx_ref, dx, sem):
    tiles, tokens, width = dpre.shape
    sums[...] = jnp.zeros_like(sums)

    def step(i):
        r = rows_of(i, 256)
        dnr = dot_nt(d[0, r, :], wa[0]) + dot_nt(d[1, r, :], wa[1]) + dot_nt(d[2, r, :], wa[2])
        for t in range(tiles):
            dnr += dot_nt(dpre[t, r, :], wu[t])
        standard, inv = norm_rows(x[r, :])
        sums[0:1, :] += jnp.sum(dnr * standard, axis=0, keepdims=True)
        gs = dnr * vec[0:1, :]
        mean_g = jnp.mean(gs, axis=1, keepdims=True)
        mean_p = jnp.mean(gs * standard, axis=1, keepdims=True)
        dx[r, :] = (cot[r, :].astype(F32) + inv * (gs - mean_g - standard * mean_p)).astype(BF16)

    loop(tokens // 256, step, lambda i: send_rows(dx, dx_ref, i, 256, sem))
    whole_wait(dx_ref, sem)()


def input_grad_call(scal, x, cot, d, dpre, vec, wa, wu):
    tiles, tokens, width = dpre.shape
    return call(
        input_grad_kernel,
        "input_grad",
        (scal, x, cot, d, dpre, vec, wa, wu),
        [],
        [kept((8, width), F32)],
        [sds((tokens // 512, 512, width))],
        [pltpu.VMEM((tokens, width), BF16), pltpu.SemaphoreType.DMA],
        2 * (tiles + 3) * tokens * width * width,
    )


def out_kernel(scal, x, o, act, vec, wa, wd, out_ref, out, sem):
    tiles, tokens, width = act.shape

    def step(i):
        r = rows_of(i, 256)
        total = x[r, :].astype(F32) + vec[3:4, :] + dot_nn(o[r, :], wa[3])
        for t in range(tiles):
            total += dot_nn(act[t, r, :], wd[tile_of(t, width), :])
        out[r, :] = total.astype(BF16)

    loop(tokens // 256, step, lambda i: send_rows(out, out_ref, i, 256, sem))
    whole_wait(out_ref, sem)()


def out_call(scal, x, o, act, vec, wa, wd):
    tiles, tokens, width = act.shape
    (out,) = call(
        out_kernel,
        "out",
        (scal, x, o, act, vec, wa, wd),
        [],
        [],
        [sds((tokens // 512, 512, width))],
        [pltpu.VMEM((tokens, width), BF16), pltpu.SemaphoreType.DMA],
        2 * (tiles + 1) * tokens * width * width,
    )
    return out


def swap(value, mask):
    return lax.ppermute(value, "wide", [(i, i ^ mask) for i in range(16)])


def swap_y(value):
    return lax.ppermute(value, "narrow", [(0, 1), (1, 0)])


def slots():
    for part in range(2):
        for i in range(2):
            for s in range(2):
                half, side = (i, s) if part == 0 else (s, i)
                for k in range(4):
                    yield part, i, s * 4 + k, half, side, k


def device_of(scal, k, side, core):
    return ((scal[1] ^ k) * 2 + (scal[2] ^ side)) * 2 + (scal[3] ^ core)


def behind(value, *marks):
    return lax.optimization_barrier((value, marks))[0]


def gather_z(value):
    return [swap(value, k << 2) for k in (1, 2, 3)]


def gather_first(za, zb):
    return swap(za, 2), swap_y(zb), swap_y(za), swap(zb, 2)


def gather_second(xa, yb):
    return swap_y(xa), swap(yb, 2)


def pieces_of(za, zb, first, second):
    xa, yb, ya, xb = first
    return [za, xa, ya, second[0], zb, xb, yb, second[1]]


def join_job(values):
    def fn(held, near, outs):
        size = near[0].shape[0]
        for i, v in enumerate(near):
            outs[0][i * size : (i + 1) * size] = v[...]

    return fn, [], values, [kept((len(values) * values[0].shape[0], *values[0].shape[1:]))]


def mix(name, jobs):
    held = [v for job in jobs for v in job[1]]
    near = [v for job in jobs for v in job[2]]
    outs = [o for job in jobs for o in job[3]]

    def kernel(*refs):
        at = len(near) + len(held)
        scratch = refs[at + len(outs) :]
        copies = [
            pltpu.make_async_copy(refs[len(near) + i], scratch[i], scratch[-1].at[i]) for i in range(len(held))
        ]
        for cp in copies:
            cp.start()
        h = n = o = 0
        for fn, job_h, job_n, job_o in jobs:
            for i in range(len(job_h)):
                copies[h + i].wait()
            fn(
                scratch[h : h + len(job_h)],
                refs[n : n + len(job_n)],
                refs[at + o : at + o + len(job_o)],
            )
            h, n, o = h + len(job_h), n + len(job_n), o + len(job_o)

    got = pl.pallas_call(
        kernel,
        name=name,
        out_shape=outs,
        in_specs=[VMEM] * len(near) + [HBM] * len(held),
        out_specs=[VMEM] * len(outs),
        scratch_shapes=[pltpu.VMEM(v.shape, v.dtype) for v in held]
        + [pltpu.SemaphoreType.DMA((max(len(held), 1),))],
        compiler_params=pltpu.CompilerParams(vmem_limit_bytes=8 << 20),
        cost_estimate=pl.CostEstimate(flops=1 << 20, bytes_accessed=1 << 20, transcendentals=0),
    )(
        *[pltpu.with_memory_space_constraint(v, pltpu.VMEM) for v in near],
        *[pltpu.with_memory_space_constraint(v, pltpu.HBM) for v in held],
    )
    split, at = [], 0
    for job in jobs:
        split.append(got[at : at + len(job[3])])
        at += len(job[3])
    return split


def total(*parts):
    return sum(v.astype(F32) for v in parts)


def stack_job(values):
    def fn(held, near, outs):
        for k, v in enumerate(near):
            for i in range(2):
                outs[i][k] = v[i]

    return fn, [], list(values), [kept((len(values), *values[0].shape[1:]))] * 2


def vector_job(sums_a, sums_d, sums_x, wide, rows):
    width = sums_a.shape[1]

    def spread(rows_in, per):
        flat = jnp.concatenate([rows_in[w * per // width][None] for w in range(wide)])
        col = lax.broadcasted_iota(jnp.int32, (wide, width), 1)
        own = lax.broadcasted_iota(jnp.int32, (wide, width), 0) * per % width
        flat = jnp.where((col >= own) & (col < own + per), flat, 0.0)
        pick = lax.broadcasted_iota(jnp.int32, (width, per), 0) % per
        pick = (pick == lax.broadcasted_iota(jnp.int32, (width, per), 1)).astype(F32)
        return lax.dot_general(
            flat, pick, (((1,), (0,)), ((), ())), precision=lax.Precision.HIGHEST, preferred_element_type=F32
        )

    def fn(held, near, outs):
        a, d, x = near
        tiles = 4
        at = 0
        outs[0][...] = jnp.zeros_like(outs[0])
        for got in (
            spread([x[0]], rows),
            spread([a[0], a[1]], 2 * rows),
            spread([d[t] for t in range(tiles)], tiles * rows),
            spread([a[2]], rows),
        ):
            outs[0][:, 0, at : at + got.shape[1]] = got
            at += got.shape[1]

    return fn, [], [sums_a, sums_d, sums_x], [kept((wide, 8, 8 * rows), F32)]


def vector_sum_job(value):
    def fn(held, near, outs):
        outs[0][...] = jnp.sum(near[0][...], axis=0)

    return fn, [], [value], [kept(value.shape[1:], F32)]


def sum1_job(keep1, got1):
    def fn(held, near, outs):
        for i in range(2):
            outs[i][...] = total(held[0][i], near[0][i]).astype(BF16)

    return fn, [keep1], [got1], [kept(keep1.shape[1:])] * 2


def sum2_job(keep0, got0, got):
    half = keep0.shape[1] // 2

    def fn(held, near, outs):
        for i in range(2):
            outs[i][...] = total(held[0][i, half:], near[0][i, half:], near[1 + i][half:]).astype(BF16)

    return fn, [keep0], [got0, *got], [kept((half, *keep0.shape[2:]))] * 2


def sum3_job(keep0, got0, got, got2):
    half = keep0.shape[1] // 2

    def fn(held, near, outs):
        for k in range(half):
            for i in range(2):
                outs[k][i] = total(held[0][i, k], near[0][i, k], near[1 + i][k], near[3 + i][k]).astype(BF16)

    return fn, [keep0], [got0, *got, *got2], [kept((2, *keep0.shape[2:]))] * half


def sum4_job(own, got):
    def fn(held, near, outs):
        outs[0][...] = total(*[v[...] for v in near]).astype(BF16)

    return fn, [], [own, *got], [kept(own.shape)]


def place_kernel(scal, a_mine, a_other, d_mine, d_other, u_mine, u_other, joined, out, down):
    _, rows, width = a_mine.shape

    def place(half, a, d, u):
        for p in range(2):
            block = half * 2 + p
            down[pl.ds(block * rows, rows), :] = d[p].astype(F32)
            joined[:, (3 + block) * width : (4 + block) * width] = u[p].astype(F32)
            if block < 3:
                joined[:, block * width : (block + 1) * width] = a[p].astype(F32)
            else:
                out[...] = a[p].astype(F32)

    @pl.when(scal[0] == 0)
    def _():
        place(0, a_mine, d_mine, u_mine)
        place(1, a_other, d_other, u_other)

    @pl.when(scal[0] != 0)
    def _():
        place(1, a_mine, d_mine, u_mine)
        place(0, a_other, d_other, u_other)


def place_call(scal, parts):
    _, rows, width = parts[0].shape
    return pl.pallas_call(
        place_kernel,
        name="place",
        out_shape=[sds((rows, 7 * width), F32), sds((rows, width), F32), sds((4 * rows, width), F32)],
        in_specs=[SMEM] + [VMEM] * 6,
        out_specs=[VMEM] * 3,
    )(scal, *[pltpu.with_memory_space_constraint(v, pltpu.VMEM) for v in parts])


def whole_wait(ref, sem):
    return pltpu.make_async_copy(ref, ref, sem).wait


def piece(refs, at, core, k, alone):
    if core == 0:
        return refs[at].at[k]
    if at in alone:
        return refs[9 + alone.index(at)].at[k]
    return refs[8].at[(at - sum(i < at for i in alone)) * 4 + k]


def load_columns(scal, refs, w, sem):
    rows = w.shape[1] // 16

    def start(own):
        for block in range(4):
            for core in range(2):
                for part, _, _, half, side, k in slots():
                    if (own ^ half) * 2 + part != block:
                        continue
                    src = piece(refs, part * 4 + half * 2 + side, core, k, (3, 7)).at[pl.ds(0, rows), :]
                    dst = w.at[block, rows_at(device_of(scal, k, side, core) * rows, rows), :]
                    pltpu.make_async_copy(src, dst, sem.at[block]).start()

    @pl.when(scal[0] == 0)
    def _():
        start(0)

    @pl.when(scal[0] != 0)
    def _():
        start(1)


def load_half(which):
    def load(scal, refs, w, sem):
        def start(rel):
            for core in range(2):
                for part, _, _, half, side, k in slots():
                    if half != rel:
                        continue
                    src = piece(refs, part * 4 + half * 2 + side, core, k, (0, 4))
                    per, rows, width = src.shape
                    dev = device_of(scal, k, side, core)
                    for b in range(per):
                        block = part * per + b
                        if which == 0:
                            dst, tile = w.at[block, rows_at(dev * rows, rows), :], block
                        else:
                            dst, tile = w.at[rows_at((dev * 2 * per + block) * rows, rows), :], scal[1] ^ k
                        pltpu.make_async_copy(src.at[b], dst, sem.at[tile]).start()

        @pl.when(scal[0] == which)
        def _():
            start(0)

        @pl.when(scal[0] != which)
        def _():
            start(1)

    return load


def vectors_kernel(rows, scal, *refs):
    pieces, (vec, b_mlp, buf, sem) = refs[:3], refs[3:]
    width = vec.shape[1]
    for core in range(2):
        for side in range(2):
            for k in range(4):
                src = pieces[side].at[k] if core == 0 else pieces[2].at[side * 4 + k]
                src = src.at[pl.ds(rows, 8), :]
                pltpu.make_async_copy(src, buf.at[device_of(scal, k, side, core)], sem).start()
    whole_wait(buf, sem)()
    values = buf[:, 0, :].astype(F32)
    devices = values.shape[0]

    def line(at, per):
        pick = lax.broadcasted_iota(jnp.int32, (per, width), 1) % per
        pick = (pick == lax.broadcasted_iota(jnp.int32, (per, width), 0)).astype(BF16)
        flat = dot_nn(values[:, at : at + per].astype(BF16), pick)
        dev = lax.broadcasted_iota(jnp.int32, flat.shape, 0)
        col = lax.broadcasted_iota(jnp.int32, flat.shape, 1)
        count = devices * per // width
        share = devices // count
        keep = col // per == dev % share
        return [
            jnp.sum(jnp.where(keep & (dev // share == i), flat, 0.0), axis=0, keepdims=True) for i in range(count)
        ]

    lines = line(0, rows) + line(rows, 2 * rows) + line(7 * rows, rows)
    vec[...] = jnp.zeros_like(vec)
    for i, v in enumerate(lines):
        vec[i : i + 1, :] = v
    for i, v in enumerate(line(3 * rows, 4 * rows)):
        b_mlp[i : i + 1, :] = v


def vectors_call(scal, pieces, rows):
    width = pieces[0].shape[2]
    return pl.pallas_call(
        functools.partial(vectors_kernel, rows),
        name="vectors",
        out_shape=[kept((8, width), F32), kept((4, width), F32)],
        in_specs=[SMEM] + [HBM] * 3,
        out_specs=[VMEM] * 2,
        scratch_shapes=[pltpu.VMEM((16, 8, width), BF16), pltpu.SemaphoreType.DMA],
        compiler_params=pltpu.CompilerParams(vmem_limit_bytes=8 << 20),
    )(scal, *[pltpu.with_memory_space_constraint(v, pltpu.HBM) for v in pieces])


def store_with(source):
    def store(scal, g, refs, sem):
        for core in range(2):
            for part, i, slot, half, side, k in slots():
                at = core * 2 + i
                dst = refs[at]
                src = source(g, scal[0] ^ half, part, device_of(scal, k, side, core), dst.shape[2], dst.shape[3])
                pltpu.make_async_copy(src, dst.at[part, slot], sem.at[at]).start()

        def done():
            for at in range(4):
                whole_wait(refs[at], sem.at[at])()

        return done

    return store


def rows_at(base, rows):
    return pl.ds(pl.multiple_of(base, 16), rows)


def attn_source(g, half, part, dev, rows, cols):
    return g.at[half * 2 + part, rows_at(dev * rows, rows), :]


def down_source(g, half, part, dev, rows, cols):
    return g.at[rows_at((dev * 4 + half * 2 + part) * rows, rows), :]


def load_whole_blocks(scal, refs, w, sem):
    for i, r in enumerate(refs):
        pltpu.make_async_copy(r, w.at[i], sem.at[i]).start()


def load_whole_rows(scal, refs, w, sem):
    width = w.shape[1]
    for t in range(w.shape[0] // width):
        r = tile_of(t, width)
        pltpu.make_async_copy(refs[0].at[r, :], w.at[r, :], sem.at[t]).start()


def store_whole(scal, g, refs, sem):
    if len(refs) == 1:
        copies = [pltpu.make_async_copy(g, refs[0], sem.at[0])]
    else:
        copies = [pltpu.make_async_copy(g.at[i], r, sem.at[i]) for i, r in enumerate(refs)]
    for cp in copies:
        cp.start()

    def done():
        for cp in copies:
            cp.wait()

    return done


def body(sizes, tokens, image_ids, cotangent, w_joined, w_out, w_mlp, norm_gain, bias_attn, bias_mlp, bias_out):
    micro, length, width = tokens.shape
    narrow, wide = sizes
    paired = narrow == 2 and wide == 16
    rows = width // wide
    tiles = w_mlp.shape[0] // rows
    x = tokens.reshape(micro * length, width)
    cot = cotangent.reshape(micro * length, width)
    n = lax.axis_index("narrow")
    w = lax.axis_index("wide")
    last = image_ids.reshape(-1, 512)[:, -1]
    scal = [n, w >> 2, (w >> 1) & 1, w & 1] + [jnp.int32(0)] * 4 + [last[b] for b in range(last.shape[0])]
    scal = jnp.stack([jnp.asarray(s, jnp.int32) for s in scal])
    vec_own = jnp.concatenate([norm_gain, bias_attn, bias_mlp, bias_out])

    def vectors(vec):
        vec = vec.astype(F32)
        b_at = 3 * rows
        b_mlp = vec[:, b_at : b_at + tiles * rows].reshape(tiles, width)
        head = [
            vec[:, :rows].reshape(1, width),
            vec[:, rows:b_at].reshape(2, width),
            vec[:, b_at + tiles * rows :].reshape(1, width),
            jnp.zeros((4, width), F32),
        ]
        return jnp.concatenate(head), b_mlp

    def vector_grads(sums_a, sums_d, sums_x):
        return jnp.concatenate(
            [
                sums_x[0].reshape(wide, rows),
                sums_a[:2].reshape(wide, 2 * rows),
                sums_d[:tiles].reshape(wide, tiles * rows),
                sums_a[2].reshape(wide, rows),
            ],
            axis=1,
        )

    if not paired:
        full = lax.all_gather(w_joined, "wide", axis=0, tiled=True)
        parts = [full[:, i * width : (i + 1) * width] for i in range(3 + tiles)]
        attn_w = parts[:3] + [lax.all_gather(w_out, "wide", axis=0, tiled=True)]
        up_w = parts[3:]
        down_w = [lax.all_gather(w_mlp, "wide", axis=0, tiled=True)]
        vec, b_mlp = vectors(lax.all_gather(vec_own, "wide", axis=0))
        square = [sds((width, width))]
        xn, q, k, v, da, wa = project_call(scal, x, cot, vec, attn_w, load_whole_blocks)
        o, d = core_call(0, scal, q, k, v, da)
        for b in range(1, last.shape[0]):
            o, d = core_call(b, scal, q, k, v, da, o, d)
        sums_a, *g_attn = attn_grad_call(scal, xn, o, d, cot, store_whole, square * 4)
        act, gp, wu = up_call(0, tiles // 2, scal, xn, b_mlp, (), up_w, load_whole_blocks)
        act, gp = up_call(tiles // 2, tiles - tiles // 2, scal, xn, b_mlp, (act, gp, wu), [], None)
        g_down = down_grad_call(scal, act, cot, store_whole, [sds((tiles * width, width))])
        dpre, sums_d, wd = dpre_call(scal, cot, gp, down_w, load_whole_rows)
        g_up = up_grad_call(scal, xn, dpre, store_whole, square * tiles)
        sums_x, d_x = input_grad_call(scal, x, cot, d, dpre, vec, wa, wu)
        out = out_call(scal, x, o, act, vec, wa, wd)

        def reduce(g):
            g = lax.psum_scatter(g.astype(F32), "wide", scatter_dimension=0, tiled=True)
            return lax.psum(g, "narrow")

        grad_joined = reduce(jnp.concatenate([*g_attn[:3], *g_up], axis=1))
        grad_out = reduce(g_attn[3])
        grad_mlp = reduce(g_down[0])
        vg = reduce(vector_grads(sums_a, sums_d, sums_x))[0]
    else:
        col = lambda i: w_joined[:, i * width : (i + 1) * width]
        pair = lambda f: jnp.stack([jnp.where(n == 0, f(0), f(2)), jnp.where(n == 0, f(1), f(3))])
        half = pair(lambda i: col(i) if i < 3 else w_out)
        v_rows = jnp.pad(vec_own, (0, width - vec_own.shape[0]))
        half = jnp.concatenate([half, jnp.broadcast_to(v_rows, (2, 8, width))], axis=1)
        got = gather_z(half)
        za, zb = [jnp.stack([t[i] for t in (half, *got)]) for i in range(2)]
        c_half = jnp.stack([jnp.where(n == 0, col(3 + t), w_mlp[t * rows : (t + 1) * rows]) for t in range(tiles)])
        c_half = behind(c_half.reshape(2, tiles // 2, rows, width), za, zb)
        first = gather_first(za, zb)
        c2 = swap(c_half, 8)
        first, c2, c_half = lax.optimization_barrier((first, c2, c_half))
        second = gather_second(*first[:2])
        own = pieces_of(za, zb, first, second)
        ((joined,),) = mix("join_a", [join_job([own[i] for i in (0, 1, 2, 4, 5, 6)])])
        joined, c1, c3 = swap(joined, 1), swap(c_half, 4), swap(c_half, 12)
        second, joined, c1, c3 = lax.optimization_barrier((second, joined, c1, c3))
        own = pieces_of(za, zb, first, second)
        attn_w = [*own, joined, swap(second[0], 1), swap(second[1], 1)]
        cza, czb = [jnp.stack([t[i] for t in (c_half, c1, c2, c3)]) for i in range(2)]
        x_p, attn_w, cza, czb = lax.optimization_barrier((x, attn_w, cza, czb))
        vec, b_mlp = vectors_call(scal, [attn_w[0], attn_w[1], attn_w[8]], rows)
        c_first = gather_first(cza, czb)
        xn, q, k, v, da, wa = project_call(scal, x_p, cot, vec, attn_w, load_columns)
        part = core_call(0, scal, q, k, v, da)

        part, c_first = lax.optimization_barrier((part, c_first))
        c_second = gather_second(*c_first[:2])
        czs = [swap(cza, 1), swap(czb, 1)]
        o, d = core_call(1, scal, q, k, v, da, *part)

        d, c_second, czs = lax.optimization_barrier((d, c_second, czs))
        c_own = pieces_of(cza, czb, c_first, c_second)
        ((c_joined,),) = mix("join_c", [join_job([t for t in c_own if t is not cza and t is not czb])])
        d, c_joined = lax.optimization_barrier((d, c_joined))
        c_other = swap(c_joined, 1)
        attn_shapes = [sds((2, 8, rows, width))] * 4
        sums_a, *ga = attn_grad_call(scal, xn, o, d, cot, store_with(attn_source), attn_shapes)

        c_other, ga = behind((c_other, ga), sums_a)
        xn_u, ga, c_own, c_other = lax.optimization_barrier((xn, ga, c_own, c_other))
        a_got1, a_got0 = swap(ga[3], 1), swap(ga[2], 1)
        half_tiles = tiles // 2
        c_all = [*c_own, c_other, *czs]
        act, gp, wu = up_call(0, half_tiles, scal, xn_u, b_mlp, (), c_all, load_half(0))

        a_got1, a_got0 = behind((a_got1, a_got0), gp)
        ((sa, sb),) = mix("sums_1", [sum1_job(ga[1], a_got1)])
        act, sa, sb = lax.optimization_barrier((act, sa, sb))
        a_xy = swap_y(sa), swap(sb, 2)
        act, gp = up_call(half_tiles, half_tiles, scal, xn_u, b_mlp, (act, gp, wu), [], None)
        gd = down_grad_call(scal, act, cot, store_with(down_source), attn_shapes)

        a_xy = behind(a_xy, gd)
        ((sa, sb),) = mix("sums_2", [sum2_job(ga[0], a_got0, a_xy)])
        gp, sa, sb, gd = lax.optimization_barrier((gp, sa, sb, gd))
        a_yx = swap(sa, 2), swap_y(sb)
        d_got1, d_got0 = swap(gd[3], 1), swap(gd[2], 1)
        dpre, sums_d, wd = dpre_call(scal, cot, gp, c_all, load_half(1))

        a_yx, d_got1, d_got0 = behind((a_yx, d_got1, d_got0), dpre)
        a_t, (sa, sb) = mix("sums_3", [sum3_job(ga[0], a_got0, a_xy, a_yx), sum1_job(gd[1], d_got1)])
        dpre_g, a_t, sa, sb = lax.optimization_barrier((dpre, a_t, sa, sb))
        d_xy = swap_y(sa), swap(sb, 2)
        a_z = [swap(a_t[k], k << 2) for k in (1, 2, 3)]
        gu = up_grad_call(scal, xn, dpre_g, store_with(attn_source), attn_shapes)

        a_z, d_xy = behind((a_z, d_xy), gu)
        (a_sum,), (sa, sb) = mix("sums_4", [sum4_job(a_t[0], a_z), sum2_job(gd[0], d_got0, d_xy)])
        x_i, sa, sb, gu, a_sum = lax.optimization_barrier((x, sa, sb, gu, a_sum))
        u_got1, u_got0 = swap(gu[3], 1), swap(gu[2], 1)
        d_yx = swap(sa, 2), swap_y(sb)
        a_other = swap_y(a_sum)
        sums_x, d_x = input_grad_call(scal, x_i, cot, d, dpre, vec, wa, wu)

        d_yx, u_got1, u_got0, a_other = behind((d_yx, u_got1, u_got0, a_other), d_x)
        (sa, sb), d_t, (v_grad,) = mix(
            "sums_5",
            [
                sum1_job(gu[1], u_got1),
                sum3_job(gd[0], d_got0, d_xy, d_yx),
                vector_job(sums_a, sums_d, sums_x, wide, rows),
            ],
        )
        x_o, sa, sb, d_t = lax.optimization_barrier((x, sa, sb, d_t))
        u_xy = swap_y(sa), swap(sb, 2)
        d_z = [swap(d_t[k], k << 2) for k in (1, 2, 3)]
        out = out_call(scal, x_o, o, act, vec, wa, wd)

        u_xy, d_z, v_grad = behind((u_xy, d_z, v_grad), out)
        (sa, sb), (d_sum,) = mix("sums_6", [sum2_job(gu[0], u_got0, u_xy), sum4_job(d_t[0], d_z)])
        sa, sb, d_sum, v_grad = lax.optimization_barrier((sa, sb, d_sum, v_grad))
        u_yx = swap(sa, 2), swap_y(sb)
        d_other = swap_y(d_sum)
        v_got = lax.all_to_all(v_grad.reshape(wide * 8, 8 * rows), "wide", 0, 0, tiled=True)
        u_t, (v_sum,) = mix(
            "sums_7",
            [sum3_job(gu[0], u_got0, u_xy, u_yx), vector_sum_job(v_got.reshape(wide, 8, 8 * rows))],
        )
        v_other = swap_y(v_sum)
        u_z = [swap(u_t[k], k << 2) for k in (1, 2, 3)]
        vg = (v_sum + v_other)[0]
        ((u_sum,),) = mix("sums_8", [sum4_job(u_t[0], u_z)])
        u_other = swap_y(u_sum)
        grad_joined, grad_out, grad_mlp = place_call(
            scal, [a_sum, a_other, d_sum, d_other, u_sum, u_other]
        )
    b_at = 3 * rows
    return (
        out.reshape(tokens.shape),
        d_x.reshape(tokens.shape),
        grad_joined,
        grad_out,
        grad_mlp,
        vg[:rows],
        vg[rows:b_at],
        vg[b_at : b_at + tiles * rows],
        vg[b_at + tiles * rows :],
    )


def solution(mesh):
    sizes = (mesh.shape["narrow"], mesh.shape["wide"])
    rows = P(None, ("narrow", "wide"), None)
    placed = (rows, P(None, ("narrow", "wide")), rows) + (P("wide", None),) * 3 + (P("wide"),) * 4
    return jax.shard_map(
        functools.partial(body, sizes),
        mesh=mesh,
        in_specs=placed,
        out_specs=(rows, rows) + (P("wide", None),) * 3 + (P("wide"),) * 4,
        check_vma=False,
    )
```

```python
import functools

import jax
import jax.numpy as jnp
from jax import lax
from jax.experimental import pallas as pl
from jax.experimental.pallas import tpu as pltpu
from jax.sharding import PartitionSpec as P

HEADS = 12
HEAD = 64
IMG = 196
EPS = 1e-06
GELU_C = 0.7978845608028654
GELU_A = 0.044715

F32 = jnp.float32
BF16 = jnp.bfloat16
HBM = pl.BlockSpec(memory_space=pltpu.HBM)
VMEM = pl.BlockSpec(memory_space=pltpu.VMEM)
SMEM = pl.BlockSpec(memory_space=pltpu.SMEM)


def dot_nn(a, b):
    return lax.dot_general(a, b, (((1,), (0,)), ((), ())), preferred_element_type=F32)


def dot_nt(a, b):
    return lax.dot_general(a, b, (((1,), (1,)), ((), ())), preferred_element_type=F32)


def dot_tn(a, b):
    return lax.dot_general(a, b, (((0,), (0,)), ((), ())), preferred_element_type=F32)


def norm_rows(rows):
    rows = rows.astype(F32)
    mean = jnp.mean(rows, axis=1, keepdims=True)
    centered = rows - mean
    inv = lax.rsqrt(jnp.mean(centered * centered, axis=1, keepdims=True) + EPS)
    return centered * inv, inv


def attend(refs, base, cols, windows):
    q_ref, k_ref, v_ref, da_ref, o_ref, dq_ref, dk_ref, dv_ref = refs
    zero = jnp.zeros((), BF16)
    jobs, ends = [], {}
    for start, rows, lo, hi, merge in windows:
        win = pl.ds(pl.multiple_of(base + start, 16), rows)
        tiles = [r[win, cols] for r in (q_ref, k_ref, v_ref, da_ref)]
        lane = lax.broadcasted_iota(jnp.int32, (rows, 128), 1)
        sums = {}
        step = 256 if rows == 512 else rows
        for at in range(0, rows, step):
            for h in range(2):
                keep = (lane < 64) if h == 0 else (lane >= 64)
                heads = [jnp.where(keep, t, zero) for t in tiles]
                jobs.append([tiles, heads, rows, lo, hi, at, step, sums])
        ends[len(jobs) - 1] = (start, rows, merge, sums)

    def products(job):
        tiles, heads, _, _, _, at, step, _ = job
        qs = slice(at, at + step)
        job += [dot_nt(tiles[1], heads[0][qs]), dot_nt(tiles[2], heads[3][qs])]

    def soften(job):
        _, _, rows, lo, hi, at, step, _, s, dp = job
        masked = lo > 0 or hi < rows
        if masked:
            key = lax.broadcasted_iota(jnp.int32, (rows, step), 0)
            s = jnp.where((key >= lo) & (key < hi), s, -1e30)
        e = jnp.exp(s - jnp.max(s, axis=0, keepdims=True))
        scale = 1.0 / jnp.sum(e, axis=0, keepdims=True)
        if masked:
            query = lax.broadcasted_iota(jnp.int32, (1, step), 1) + at
            scale = jnp.where((query >= lo) & (query < hi), scale, 0.0)
        p = e * scale
        inner = jnp.sum(p * dp, axis=0, keepdims=True)
        job[8:] = [p.astype(BF16), (p * (dp - inner)).astype(BF16)]

    def gather(job):
        _, heads, _, _, _, at, step, sums, p, ds = job
        qs = slice(at, at + step)
        parts = (
            (("o", at), dot_tn(p, heads[2])),
            (("q", at), dot_tn(ds, heads[1])),
            (("v", 0), dot_nn(p, heads[3][qs])),
            (("k", 0), dot_nn(ds, heads[0][qs])),
        )
        for key, val in parts:
            sums[key] = sums[key] + val if key in sums else val

    def write(start, rows, merge, sums):
        for name, ref in (("o", o_ref), ("q", dq_ref), ("k", dk_ref), ("v", dv_ref)):
            for (n, at), val in sums.items():
                if n != name:
                    continue
                val = (val * 0.125 if n == "q" else val).astype(BF16)
                size = val.shape[0]
                if merge and at == 0:
                    head = pl.ds(pl.multiple_of(base + start, 16), merge)
                    ref[head, cols] = ref[head, cols] + val[:merge]
                    val, at, size = val[merge:], merge, size - merge
                ref[pl.ds(pl.multiple_of(base + start + at, 16), size), cols] = val

    for i in range(len(jobs) + 2):
        if i < len(jobs):
            products(jobs[i])
        if 0 <= i - 1 < len(jobs):
            soften(jobs[i - 1])
        if 0 <= i - 2:
            gather(jobs[i - 2])
            if i - 2 in ends:
                write(*ends[i - 2])


WHOLE = ((0, 512, 0, 512, 0),)
SMALL = (
    (0, 208, 0, IMG, 0),
    (192, 208, IMG - 192, 2 * IMG - 192, 16),
    (384, 128, 2 * IMG - 384, 128, 16),
)


def sds(shape, dtype=BF16):
    return jax.ShapeDtypeStruct(shape, dtype)


def kept(shape, dtype=BF16):
    return pltpu.VMEM(shape, dtype)


def call(kernel, name, operands, pieces, outs, g_shapes, scratch, flops, limit=14, alias=None):
    n_p, n_g = len(pieces), len(g_shapes)
    scal, *rest = operands
    rest = [pltpu.with_memory_space_constraint(v, pltpu.VMEM) for v in rest]
    pieces = [pltpu.with_memory_space_constraint(v, pltpu.HBM) for v in pieces]
    g_shapes = [pltpu.HBM(g.shape, g.dtype) for g in g_shapes]
    return pl.pallas_call(
        kernel,
        name=name,
        out_shape=list(outs) + list(g_shapes),
        in_specs=[SMEM] + [VMEM] * len(rest) + [HBM] * n_p,
        out_specs=[VMEM] * len(outs) + [HBM] * n_g,
        scratch_shapes=scratch,
        compiler_params=pltpu.CompilerParams(vmem_limit_bytes=limit << 20),
        input_output_aliases=alias or {},
        cost_estimate=pl.CostEstimate(flops=flops, bytes_accessed=1 << 20, transcendentals=0),
    )(scal, *rest, *pieces)


def loop(count, fn, after=None):
    def step(i, c):
        fn(i)
        if after is not None:
            after(i)
        return c

    lax.fori_loop(0, count, step, 0)


def send_rows(src, dst, i, size, sem):
    per = dst.shape[1] // size
    pltpu.make_async_copy(src.at[rows_of(i, size), :], dst.at[i // per, rows_of(i % per, size), :], sem).start()


def rows_of(i, size):
    return pl.ds(pl.multiple_of(i * size, size), size)


def project_kernel(load, n_w, *refs):
    scal, x_ref, cot_ref, vec_ref = refs[:4]
    xn, q, k, v, da, w = refs[4 + n_w : 10 + n_w]
    (sem,) = refs[10 + n_w :]
    load(scal, refs[4 : 4 + n_w], w, sem)
    tokens = x_ref.shape[0]

    def norm(i):
        r = rows_of(i, 256)
        standard, _ = norm_rows(x_ref[r, :])
        xn[r, :] = (standard * vec_ref[0:1, :]).astype(BF16)

    loop(tokens // 256, norm)

    def ready(i):
        whole_wait(w.at[i], sem.at[i])()

    def each(fn):
        loop(tokens // 512, lambda i: fn(rows_of(i, 512)))

    def queries(r):
        q[r, :] = (dot_nn(xn[r, :], w[0]) + vec_ref[1:2, :]).astype(BF16) * jnp.asarray(0.125, BF16)

    def keys(r):
        k[r, :] = dot_nn(xn[r, :], w[1]).astype(BF16)

    def values(r):
        v[r, :] = (dot_nn(xn[r, :], w[2]) + vec_ref[2:3, :]).astype(BF16)

    def attended(r):
        da[r, :] = dot_nt(cot_ref[r, :], w[3]).astype(BF16)

    for i, fn in enumerate((queries, keys, values, attended)):
        ready(i)
        each(fn)


def project_call(scal, x, cot, vec, weights, load):
    tokens, width = x.shape
    return call(
        functools.partial(project_kernel, load, len(weights)),
        "project",
        (scal, x, cot, vec),
        weights,
        [kept(x.shape)] * 5 + [kept((4, width, width))],
        [],
        [pltpu.SemaphoreType.DMA((4,))],
        8 * tokens * width * width,
    )


def core_kernel(b, scal, q, k, v, da, *refs):
    o, d = refs[-2:]
    refs = (q, k, v, da, o, d.at[0], d.at[1], d.at[2])
    whole = scal[8 + b] == 0

    def pair(i):
        cols = pl.ds(pl.multiple_of(i * 128, 128), 128)

        @pl.when(whole)
        def _():
            attend(refs, b * 512, cols, WHOLE)

        @pl.when(jnp.logical_not(whole))
        def _():
            attend(refs, b * 512, cols, SMALL)

    loop(q.shape[1] // 128, pair)


def core_call(b, scal, q, k, v, da, *before):
    return call(
        functools.partial(core_kernel, b),
        "core",
        (scal, q, k, v, da, *before),
        [],
        [kept(q.shape), kept((3, *q.shape))],
        [],
        [],
        10 << 30,
        alias={5 + i: i for i in range(len(before))},
    )


def attn_grad_kernel(store, scal, xn, o, d, cot, sums, *refs):
    *g_refs, g, sem = refs
    tokens, width = xn.shape

    def grad(b):
        g[b] = dot_tn(xn[...], d[b]).astype(BF16)

    loop(3, grad)
    g[3] = dot_tn(o[...], cot[...]).astype(BF16)
    done = store(scal, g, g_refs, sem)
    ones = jnp.ones((8, tokens), BF16)
    sums[0:1, :] = dot_nn(ones, d[0])[0:1]
    sums[1:2, :] = dot_nn(ones, d[2])[0:1]
    sums[2:3, :] = dot_nn(ones, cot[...])[0:1]
    done()


def attn_grad_call(scal, xn, o, d, cot, store, g_shapes):
    tokens, width = xn.shape
    return call(
        functools.partial(attn_grad_kernel, store),
        "attn_grad",
        (scal, xn, o, d, cot),
        [],
        [kept((8, width), F32)],
        g_shapes,
        [pltpu.VMEM((4, width, width), BF16), pltpu.SemaphoreType.DMA((len(g_shapes),))],
        8 * tokens * width * width,
    )


def gelu_parts(u):
    u2 = u * u
    half = 0.5 * jnp.tanh(u * (GELU_C + (GELU_C * GELU_A) * u2)) + 0.5
    act = u * half
    grad = half + act * (1.0 - half) * (2.0 * GELU_C + (6.0 * GELU_C * GELU_A) * u2)
    return act, grad

def tile_of(t, width):
    return pl.ds(t * width if isinstance(t, int) else pl.multiple_of(t * width, 128), width)


def wait_tile(w, sem, t, width):
    whole_wait(w.at[tile_of(t, width), :], sem.at[t])()


def up_kernel(load, first, count, n_p, *refs):
    scal, xn, bias = refs[:3]
    even, odd, sem = refs[-3:]
    tokens, width = xn.shape
    if n_p:
        act, gp, w = refs[-6:-3]
        load(scal, refs[3 : 3 + n_p], w, sem)
        for t in range(count):
            whole_wait(w.at[t], sem.at[t])()
    else:
        act, gp = refs[-5:-3]
        w = refs[5]
    rows = even.shape[0]
    per = tokens // rows

    def product(i):
        return dot_nn(xn[rows_of(i % per, rows), :], w[first + i // per])

    def finish(i, u):
        t, r = first + i // per, rows_of(i % per, rows)
        a, gr = gelu_parts(u + bias[pl.ds(t, 1), :])
        act[t, r, :] = a.astype(BF16)
        gp[t, r, :] = gr.astype(BF16)

    even[...] = product(0)

    def step(i):
        odd[...] = product(2 * i + 1)
        finish(2 * i, even[...])
        even[...] = product(jnp.minimum(2 * i + 2, count * per - 1))
        finish(2 * i + 1, odd[...])

    loop(count * per // 2, step)
    if n_p:
        for t in range(count, bias.shape[0]):
            whole_wait(w.at[t], sem.at[t])()


def up_call(first, count, scal, xn, bias, before, pieces, load):
    tokens, width = xn.shape
    tiles = bias.shape[0]
    return call(
        functools.partial(up_kernel, load, first, count, len(pieces)),
        "up",
        (scal, xn, bias, *before),
        pieces,
        [kept((tiles, tokens, width))] * 2 + [kept((tiles, width, width))] * (1 if pieces else 0),
        [],
        [pltpu.VMEM((256, width), F32)] * 2 + [pltpu.SemaphoreType.DMA((tiles,))],
        2 * count * tokens * width * width,
        alias={3: 0, 4: 1} if before else None,
    )


def down_grad_kernel(load, store, n_p, scal, act, cot, *refs):
    w, *g_refs, g, wsem, sem = refs[n_p:]
    tiles, tokens, width = act.shape
    load(scal, refs[:n_p], w, wsem)

    def grad(t):
        g[tile_of(t, width), :] = dot_tn(act[t], cot[...]).astype(BF16)

    loop(tiles, grad)
    done = store(scal, g, g_refs, sem)
    for t in range(tiles):
        wait_tile(w, wsem, t, width)
    done()


def down_grad_call(scal, act, cot, pieces, load, store, g_shapes):
    tiles, tokens, width = act.shape
    return call(
        functools.partial(down_grad_kernel, load, store, len(pieces)),
        "down_grad",
        (scal, act, cot),
        pieces,
        [kept((tiles * width, width))],
        g_shapes,
        [
            pltpu.VMEM((tiles * width, width), BF16),
            pltpu.SemaphoreType.DMA((tiles,)),
            pltpu.SemaphoreType.DMA((len(g_shapes),)),
        ],
        2 * tiles * tokens * width * width,
    )


def dpre_kernel(scal, cot, gp, w, dpre, sums):
    tiles, tokens, width = gp.shape
    ones = jnp.ones((8, tokens), BF16)

    def down(t):
        dpre[t] = (dot_nt(cot[...], w[tile_of(t, width), :]) * gp[t].astype(F32)).astype(BF16)

    loop(tiles, down)
    for t in range(tiles):
        sums[t : t + 1, :] = dot_nn(ones, dpre[t])[0:1]


def dpre_call(scal, cot, gp, w):
    tiles, tokens, width = gp.shape
    return call(
        dpre_kernel,
        "dpre",
        (scal, cot, gp, w),
        [],
        [kept(gp.shape), kept((8, width), F32)],
        [],
        [],
        2 * tiles * tokens * width * width,
        alias={2: 0},
    )


def up_grad_kernel(store, scal, xn, dpre, *refs):
    *g_refs, g, sem = refs
    tiles, tokens, width = dpre.shape

    def grad(t):
        g[t] = dot_tn(xn[...], dpre[t]).astype(BF16)

    loop(tiles, grad)
    store(scal, g, g_refs, sem)()


def up_grad_call(scal, xn, dpre, store, g_shapes):
    tiles, tokens, width = dpre.shape
    return call(
        functools.partial(up_grad_kernel, store),
        "up_grad",
        (scal, xn, dpre),
        [],
        [],
        g_shapes,
        [pltpu.VMEM((tiles, width, width), BF16), pltpu.SemaphoreType.DMA((len(g_shapes),))],
        2 * tiles * tokens * width * width,
    )


def input_grad_kernel(scal, x, cot, d, dpre, vec, wa, wu, sums, dx_ref, dx, sem):
    tiles, tokens, width = dpre.shape
    sums[...] = jnp.zeros_like(sums)

    def step(i):
        r = rows_of(i, 256)
        dnr = dot_nt(d[0, r, :], wa[0]) + dot_nt(d[1, r, :], wa[1]) + dot_nt(d[2, r, :], wa[2])
        for t in range(tiles):
            dnr += dot_nt(dpre[t, r, :], wu[t])
        standard, inv = norm_rows(x[r, :])
        sums[0:1, :] += jnp.sum(dnr * standard, axis=0, keepdims=True)
        gs = dnr * vec[0:1, :]
        mean_g = jnp.mean(gs, axis=1, keepdims=True)
        mean_p = jnp.mean(gs * standard, axis=1, keepdims=True)
        dx[r, :] = (cot[r, :].astype(F32) + inv * (gs - mean_g - standard * mean_p)).astype(BF16)

    loop(tokens // 256, step, lambda i: send_rows(dx, dx_ref, i, 256, sem))
    whole_wait(dx_ref, sem)()


def input_grad_call(scal, x, cot, d, dpre, vec, wa, wu):
    tiles, tokens, width = dpre.shape
    return call(
        input_grad_kernel,
        "input_grad",
        (scal, x, cot, d, dpre, vec, wa, wu),
        [],
        [kept((8, width), F32)],
        [sds((tokens // 512, 512, width))],
        [pltpu.VMEM((tokens, width), BF16), pltpu.SemaphoreType.DMA],
        2 * (tiles + 3) * tokens * width * width,
    )


def out_kernel(scal, x, o, act, vec, wa, wd, out_ref, out, sem):
    tiles, tokens, width = act.shape

    def step(i):
        r = rows_of(i, 256)
        total = x[r, :].astype(F32) + vec[3:4, :] + dot_nn(o[r, :], wa[3])
        for t in range(tiles):
            total += dot_nn(act[t, r, :], wd[tile_of(t, width), :])
        out[r, :] = total.astype(BF16)

    loop(tokens // 256, step, lambda i: send_rows(out, out_ref, i, 256, sem))
    whole_wait(out_ref, sem)()


def out_call(scal, x, o, act, vec, wa, wd):
    tiles, tokens, width = act.shape
    (out,) = call(
        out_kernel,
        "out",
        (scal, x, o, act, vec, wa, wd),
        [],
        [],
        [sds((tokens // 512, 512, width))],
        [pltpu.VMEM((tokens, width), BF16), pltpu.SemaphoreType.DMA],
        2 * (tiles + 1) * tokens * width * width,
    )
    return out


def swap(value, mask):
    return lax.ppermute(value, "wide", [(i, i ^ mask) for i in range(16)])


def swap_y(value):
    return lax.ppermute(value, "narrow", [(0, 1), (1, 0)])


def slots():
    for part in range(2):
        for i in range(2):
            for s in range(2):
                half, side = (i, s) if part == 0 else (s, i)
                for k in range(4):
                    yield part, i, s * 4 + k, half, side, k


def device_of(scal, k, side, core):
    return ((scal[1] ^ k) * 2 + (scal[2] ^ side)) * 2 + (scal[3] ^ core)


def behind(value, *marks):
    return lax.optimization_barrier((value, marks))[0]


def gather_z(value):
    return [swap(value, k << 2) for k in (1, 2, 3)]


def gather_first(za, zb):
    return swap(za, 2), swap_y(zb), swap_y(za), swap(zb, 2)


def gather_second(xa, yb):
    return swap_y(xa), swap(yb, 2)


def pieces_of(za, zb, first, second):
    xa, yb, ya, xb = first
    return [za, xa, ya, second[0], zb, xb, yb, second[1]]


def join_job(values):
    def fn(held, near, outs):
        size = near[0].shape[0]
        for i, v in enumerate(near):
            outs[0][i * size : (i + 1) * size] = v[...]

    return fn, [], values, [kept((len(values) * values[0].shape[0], *values[0].shape[1:]))]


def mix(name, jobs, scal=None):
    extra = [] if scal is None else [scal]
    held = [v for job in jobs for v in job[1]]
    near = [v for job in jobs for v in job[2]]
    outs = [o for job in jobs for o in job[3]]

    def kernel(*refs):
        last, refs = refs[: len(extra)], refs[len(extra) :]
        at = len(near) + len(held)
        scratch = refs[at + len(outs) :]
        copies = [
            pltpu.make_async_copy(refs[len(near) + i], scratch[i], scratch[-1].at[i]) for i in range(len(held))
        ]
        for cp in copies:
            cp.start()
        h = n = o = 0
        for fn, job_h, job_n, job_o in jobs:
            for i in range(len(job_h)):
                copies[h + i].wait()
            fn(
                scratch[h : h + len(job_h)],
                (*refs[n : n + len(job_n)], *last),
                refs[at + o : at + o + len(job_o)],
            )
            h, n, o = h + len(job_h), n + len(job_n), o + len(job_o)

    got = pl.pallas_call(
        kernel,
        name=name,
        out_shape=outs,
        in_specs=[SMEM] * len(extra) + [VMEM] * len(near) + [HBM] * len(held),
        out_specs=[VMEM] * len(outs),
        scratch_shapes=[pltpu.VMEM(v.shape, v.dtype) for v in held]
        + [pltpu.SemaphoreType.DMA((max(len(held), 1),))],
        compiler_params=pltpu.CompilerParams(vmem_limit_bytes=8 << 20),
        cost_estimate=pl.CostEstimate(flops=1 << 20, bytes_accessed=1 << 20, transcendentals=0),
    )(
        *extra,
        *[pltpu.with_memory_space_constraint(v, pltpu.VMEM) for v in near],
        *[pltpu.with_memory_space_constraint(v, pltpu.HBM) for v in held],
    )
    split, at = [], 0
    for job in jobs:
        split.append(got[at : at + len(job[3])])
        at += len(job[3])
    return split


def total(*parts):
    return sum(v.astype(F32) for v in parts)


def stack_job(values):
    def fn(held, near, outs):
        for k, v in enumerate(near):
            for i in range(2):
                outs[i][k] = v[i]

    return fn, [], list(values), [kept((len(values), *values[0].shape[1:]))] * 2


def vector_job(sums_a, sums_d, sums_x, wide, rows):
    width = sums_a.shape[1]

    def spread(rows_in, per):
        flat = jnp.concatenate([rows_in[w * per // width][None] for w in range(wide)])
        col = lax.broadcasted_iota(jnp.int32, (wide, width), 1)
        own = lax.broadcasted_iota(jnp.int32, (wide, width), 0) * per % width
        flat = jnp.where((col >= own) & (col < own + per), flat, 0.0)
        pick = lax.broadcasted_iota(jnp.int32, (width, per), 0) % per
        pick = (pick == lax.broadcasted_iota(jnp.int32, (width, per), 1)).astype(BF16)
        got = jnp.zeros((wide, per), F32)
        for _ in range(3):
            high = flat.astype(BF16)
            flat = flat - high.astype(F32)
            got += dot_nn(high, pick)
        return got

    def fn(held, near, outs):
        a, d, x, scal = near
        tiles = 4
        at = 0
        for got in (
            spread([x[0]], rows),
            spread([a[0], a[1]], 2 * rows),
            spread([d[t] for t in range(tiles)], tiles * rows),
            spread([a[2]], rows),
        ):
            outs[4][:, at : at + got.shape[1]] = got
            at += got.shape[1]
        for side in range(2):
            for core in range(2):
                out = outs[side * 2 + core]
                out[...] = jnp.zeros_like(out)
                for z in range(wide // 4):
                    dev = (z * 2 + (scal[2] ^ side)) * 2 + (scal[3] ^ core)
                    out[z : z + 1, :] = outs[4][pl.ds(dev, 1), :]

    return fn, [], [sums_a, sums_d, sums_x], [kept((8, 8 * rows), F32)] * 4 + [kept((wide, 8 * rows), F32)]


def add_job(values):
    def fn(held, near, outs):
        outs[0][...] = sum(near[i][...] for i in range(len(values)))

    return fn, [], list(values), [kept(values[0].shape, F32)]


def vector_z_job(mine, other):
    def fn(held, near, outs):
        outs[4][...] = near[0][...] + near[1][...]
        for k in range(4):
            outs[k][...] = jnp.zeros_like(outs[k])
            outs[k][0:1, :] = outs[4][pl.ds(near[2][1] ^ k, 1), :]

    return fn, [], [mine, other], [kept(mine.shape, F32)] * 5


def sum1_job(keep1, got1):
    def fn(held, near, outs):
        for i in range(2):
            outs[i][...] = total(held[0][i], near[0][i]).astype(BF16)

    return fn, [keep1], [got1], [kept(keep1.shape[1:])] * 2


def sum2_job(keep0, got0, got):
    half = keep0.shape[1] // 2

    def fn(held, near, outs):
        for i in range(2):
            outs[i][...] = total(held[0][i, half:], near[0][i, half:], near[1 + i][half:]).astype(BF16)

    return fn, [keep0], [got0, *got], [kept((half, *keep0.shape[2:]))] * 2


def sum3_job(keep0, got0, got, got2):
    half = keep0.shape[1] // 2

    def fn(held, near, outs):
        for k in range(half):
            for i in range(2):
                outs[k][i] = total(held[0][i, k], near[0][i, k], near[1 + i][k], near[3 + i][k]).astype(BF16)

    return fn, [keep0], [got0, *got, *got2], [kept((2, *keep0.shape[2:]))] * half


def sum4_job(own, got):
    def fn(held, near, outs):
        outs[0][...] = total(*[near[i][...] for i in range(1 + len(got))]).astype(BF16)

    return fn, [], [own, *got], [kept(own.shape)]


def place_kernel(scal, a_mine, a_other, d_mine, d_other, u_mine, joined_ref, out, down, joined, sem):
    _, rows, width = a_mine.shape

    def place(half, a, d, u):
        for p in range(2):
            block = half * 2 + p
            down[pl.ds(block * rows, rows), :] = d[p].astype(F32)
            if u is not None:
                joined[3 + p] = u[p].astype(F32)
                send(joined.at[3 + p], 3 + block)
            if block < 3:
                joined[block] = a[p].astype(F32)
                send(joined.at[block], block)
            else:
                out[...] = a[p].astype(F32)

    def send(src, block):
        pltpu.make_async_copy(src, joined_ref.at[:, block * width : (block + 1) * width], sem).start()

    @pl.when(scal[0] == 0)
    def _():
        place(0, a_mine, d_mine, u_mine)
        place(1, a_other, d_other, None)

    @pl.when(scal[0] != 0)
    def _():
        place(1, a_mine, d_mine, u_mine)
        place(0, a_other, d_other, None)

    whole_wait(joined, sem)()


def place_call(scal, parts):
    _, rows, width = parts[0].shape
    return pl.pallas_call(
        place_kernel,
        name="place",
        out_shape=[sds((rows, 7 * width), F32), sds((rows, width), F32), sds((4 * rows, width), F32)],
        in_specs=[SMEM] + [VMEM] * 5,
        out_specs=[HBM, VMEM, VMEM],
        scratch_shapes=[pltpu.VMEM((5, rows, width), F32), pltpu.SemaphoreType.DMA],
    )(scal, *[pltpu.with_memory_space_constraint(v, pltpu.VMEM) for v in parts])


def place_last_kernel(scal, placed, other, joined_ref, wide, sem):
    _, rows, width = other.shape
    for p in range(2):
        wide[p] = other[p].astype(F32)
        at = pl.multiple_of((3 + (1 - scal[0]) * 2 + p) * width, 128)
        pltpu.make_async_copy(wide.at[p], joined_ref.at[:, pl.ds(at, width)], sem).start()
    whole_wait(wide, sem)()


def place_last_call(scal, placed, other):
    return pl.pallas_call(
        place_last_kernel,
        name="place_last",
        out_shape=sds(placed.shape, F32),
        in_specs=[SMEM, HBM, VMEM],
        out_specs=HBM,
        scratch_shapes=[pltpu.VMEM(other.shape, F32), pltpu.SemaphoreType.DMA],
        input_output_aliases={1: 0},
    )(scal, placed, pltpu.with_memory_space_constraint(other, pltpu.VMEM))


def whole_wait(ref, sem):
    return pltpu.make_async_copy(ref, ref, sem).wait


def piece(refs, at, core, k, alone):
    if core == 0:
        return refs[at].at[k]
    if at in alone:
        return refs[9 + alone.index(at)].at[k]
    return refs[8].at[(at - sum(i < at for i in alone)) * 4 + k]


def load_columns(scal, refs, w, sem):
    rows = w.shape[1] // 16

    def start(own):
        for block in range(4):
            for core in range(2):
                for part, _, _, half, side, k in slots():
                    if (own ^ half) * 2 + part != block:
                        continue
                    src = piece(refs, part * 4 + half * 2 + side, core, k, (3, 7)).at[pl.ds(0, rows), :]
                    dst = w.at[block, rows_at(device_of(scal, k, side, core) * rows, rows), :]
                    pltpu.make_async_copy(src, dst, sem.at[block]).start()

    @pl.when(scal[0] == 0)
    def _():
        start(0)

    @pl.when(scal[0] != 0)
    def _():
        start(1)


def load_half(which):
    def load(scal, refs, w, sem):
        def start(rel):
            for core in range(2):
                for part, _, _, half, side, k in slots():
                    if half != rel:
                        continue
                    src = piece(refs, part * 4 + half * 2 + side, core, k, (0, 4))
                    per, rows, width = src.shape
                    dev = device_of(scal, k, side, core)
                    for b in range(per):
                        block = part * per + b
                        if which == 0:
                            dst, tile = w.at[block, rows_at(dev * rows, rows), :], block
                        else:
                            dst, tile = w.at[rows_at((dev * 2 * per + block) * rows, rows), :], scal[1] ^ k
                        pltpu.make_async_copy(src.at[b], dst, sem.at[tile]).start()

        @pl.when(scal[0] == which)
        def _():
            start(0)

        @pl.when(scal[0] != which)
        def _():
            start(1)

    return load


def vectors_kernel(rows, scal, *refs):
    pieces, (vec, b_mlp, buf, sem) = refs[:3], refs[3:]
    width = vec.shape[1]
    for core in range(2):
        for side in range(2):
            for k in range(4):
                src = pieces[side].at[k] if core == 0 else pieces[2].at[side * 4 + k]
                src = src.at[pl.ds(rows, 8), :]
                pltpu.make_async_copy(src, buf.at[device_of(scal, k, side, core)], sem).start()
    whole_wait(buf, sem)()
    values = buf[:, 0, :].astype(F32)
    devices = values.shape[0]

    def line(at, per):
        pick = lax.broadcasted_iota(jnp.int32, (per, width), 1) % per
        pick = (pick == lax.broadcasted_iota(jnp.int32, (per, width), 0)).astype(BF16)
        flat = dot_nn(values[:, at : at + per].astype(BF16), pick)
        dev = lax.broadcasted_iota(jnp.int32, flat.shape, 0)
        col = lax.broadcasted_iota(jnp.int32, flat.shape, 1)
        count = devices * per // width
        share = devices // count
        keep = col // per == dev % share
        return [
            jnp.sum(jnp.where(keep & (dev // share == i), flat, 0.0), axis=0, keepdims=True) for i in range(count)
        ]

    lines = line(0, rows) + line(rows, 2 * rows) + line(7 * rows, rows)
    vec[...] = jnp.zeros_like(vec)
    for i, v in enumerate(lines):
        vec[i : i + 1, :] = v
    for i, v in enumerate(line(3 * rows, 4 * rows)):
        b_mlp[i : i + 1, :] = v


def vectors_call(scal, pieces, rows):
    width = pieces[0].shape[2]
    return pl.pallas_call(
        functools.partial(vectors_kernel, rows),
        name="vectors",
        out_shape=[kept((8, width), F32), kept((4, width), F32)],
        in_specs=[SMEM] + [HBM] * 3,
        out_specs=[VMEM] * 2,
        scratch_shapes=[pltpu.VMEM((16, 8, width), BF16), pltpu.SemaphoreType.DMA],
        compiler_params=pltpu.CompilerParams(vmem_limit_bytes=8 << 20),
    )(scal, *[pltpu.with_memory_space_constraint(v, pltpu.HBM) for v in pieces])


def store_with(source):
    def store(scal, g, refs, sem):
        for core in range(2):
            for part, i, slot, half, side, k in slots():
                at = core * 2 + i
                dst = refs[at]
                src = source(g, scal[0] ^ half, part, device_of(scal, k, side, core), dst.shape[2], dst.shape[3])
                pltpu.make_async_copy(src, dst.at[part, slot], sem.at[at]).start()

        def done():
            for at in range(4):
                whole_wait(refs[at], sem.at[at])()

        return done

    return store


def rows_at(base, rows):
    return pl.ds(pl.multiple_of(base, 16), rows)


def attn_source(g, half, part, dev, rows, cols):
    return g.at[half * 2 + part, rows_at(dev * rows, rows), :]


def down_source(g, half, part, dev, rows, cols):
    return g.at[rows_at((dev * 4 + half * 2 + part) * rows, rows), :]


def load_whole_blocks(scal, refs, w, sem):
    for i, r in enumerate(refs):
        pltpu.make_async_copy(r, w.at[i], sem.at[i]).start()


def load_whole_rows(scal, refs, w, sem):
    width = w.shape[1]
    for t in range(w.shape[0] // width):
        r = tile_of(t, width)
        pltpu.make_async_copy(refs[0].at[r, :], w.at[r, :], sem.at[t]).start()


def store_whole(scal, g, refs, sem):
    if len(refs) == 1:
        copies = [pltpu.make_async_copy(g, refs[0], sem.at[0])]
    else:
        copies = [pltpu.make_async_copy(g.at[i], r, sem.at[i]) for i, r in enumerate(refs)]
    for cp in copies:
        cp.start()

    def done():
        for cp in copies:
            cp.wait()

    return done


def body(sizes, tokens, image_ids, cotangent, w_joined, w_out, w_mlp, norm_gain, bias_attn, bias_mlp, bias_out):
    micro, length, width = tokens.shape
    narrow, wide = sizes
    paired = narrow == 2 and wide == 16
    rows = width // wide
    tiles = w_mlp.shape[0] // rows
    x = tokens.reshape(micro * length, width)
    cot = cotangent.reshape(micro * length, width)
    n = lax.axis_index("narrow")
    w = lax.axis_index("wide")
    last = image_ids.reshape(-1, 512)[:, -1]
    scal = [n, w >> 2, (w >> 1) & 1, w & 1] + [jnp.int32(0)] * 4 + [last[b] for b in range(last.shape[0])]
    scal = jnp.stack([jnp.asarray(s, jnp.int32) for s in scal])
    vec_own = jnp.concatenate([norm_gain, bias_attn, bias_mlp, bias_out])

    def vectors(vec):
        vec = vec.astype(F32)
        b_at = 3 * rows
        b_mlp = vec[:, b_at : b_at + tiles * rows].reshape(tiles, width)
        head = [
            vec[:, :rows].reshape(1, width),
            vec[:, rows:b_at].reshape(2, width),
            vec[:, b_at + tiles * rows :].reshape(1, width),
            jnp.zeros((4, width), F32),
        ]
        return jnp.concatenate(head), b_mlp

    def vector_grads(sums_a, sums_d, sums_x):
        return jnp.concatenate(
            [
                sums_x[0].reshape(wide, rows),
                sums_a[:2].reshape(wide, 2 * rows),
                sums_d[:tiles].reshape(wide, tiles * rows),
                sums_a[2].reshape(wide, rows),
            ],
            axis=1,
        )

    if not paired:
        full = lax.all_gather(w_joined, "wide", axis=0, tiled=True)
        parts = [full[:, i * width : (i + 1) * width] for i in range(3 + tiles)]
        attn_w = parts[:3] + [lax.all_gather(w_out, "wide", axis=0, tiled=True)]
        up_w = parts[3:]
        down_w = [lax.all_gather(w_mlp, "wide", axis=0, tiled=True)]
        vec, b_mlp = vectors(lax.all_gather(vec_own, "wide", axis=0))
        square = [sds((width, width))]
        xn, q, k, v, da, wa = project_call(scal, x, cot, vec, attn_w, load_whole_blocks)
        o, d = core_call(0, scal, q, k, v, da)
        for b in range(1, last.shape[0]):
            o, d = core_call(b, scal, q, k, v, da, o, d)
        sums_a, *g_attn = attn_grad_call(scal, xn, o, d, cot, store_whole, square * 4)
        act, gp, wu = up_call(0, tiles // 2, scal, xn, b_mlp, (), up_w, load_whole_blocks)
        act, gp = up_call(tiles // 2, tiles - tiles // 2, scal, xn, b_mlp, (act, gp, wu), [], None)
        wd, *g_down = down_grad_call(
            scal, act, cot, down_w, load_whole_rows, store_whole, [sds((tiles * width, width))]
        )
        dpre, sums_d = dpre_call(scal, cot, gp, wd)
        g_up = up_grad_call(scal, xn, dpre, store_whole, square * tiles)
        sums_x, d_x = input_grad_call(scal, x, cot, d, dpre, vec, wa, wu)
        out = out_call(scal, x, o, act, vec, wa, wd)

        def reduce(g):
            g = lax.psum_scatter(g.astype(F32), "wide", scatter_dimension=0, tiled=True)
            return lax.psum(g, "narrow")

        grad_joined = reduce(jnp.concatenate([*g_attn[:3], *g_up], axis=1))
        grad_out = reduce(g_attn[3])
        grad_mlp = reduce(g_down[0])
        vg = reduce(vector_grads(sums_a, sums_d, sums_x))[0]
    else:
        col = lambda i: w_joined[:, i * width : (i + 1) * width]
        pair = lambda f: jnp.stack([jnp.where(n == 0, f(0), f(2)), jnp.where(n == 0, f(1), f(3))])
        half = pair(lambda i: col(i) if i < 3 else w_out)
        v_rows = jnp.pad(vec_own, (0, width - vec_own.shape[0]))
        half = jnp.concatenate([half, jnp.broadcast_to(v_rows, (2, 8, width))], axis=1)
        got = gather_z(half)
        za, zb = [jnp.stack([t[i] for t in (half, *got)]) for i in range(2)]
        c_half = jnp.stack([jnp.where(n == 0, col(3 + t), w_mlp[t * rows : (t + 1) * rows]) for t in range(tiles)])
        c_half = behind(c_half.reshape(2, tiles // 2, rows, width), za, zb)
        first = gather_first(za, zb)
        c2 = swap(c_half, 8)
        first, c2, c_half = lax.optimization_barrier((first, c2, c_half))
        second = gather_second(*first[:2])
        own = pieces_of(za, zb, first, second)
        ((joined,),) = mix("join_a", [join_job([own[i] for i in (0, 1, 2, 4, 5, 6)])])
        joined, c1, c3 = swap(joined, 1), swap(c_half, 4), swap(c_half, 12)
        second, joined, c1, c3 = lax.optimization_barrier((second, joined, c1, c3))
        vec, b_mlp = vectors_call(scal, [za, first[0], joined], rows)
        own = pieces_of(za, zb, first, second)
        attn_w = [*own, joined, swap(second[0], 1), swap(second[1], 1)]
        cza, czb = [jnp.stack([t[i] for t in (c_half, c1, c2, c3)]) for i in range(2)]
        x_p, attn_w, cza, czb, vec, b_mlp = lax.optimization_barrier((x, attn_w, cza, czb, vec, b_mlp))
        c_first = gather_first(cza, czb)
        xn, q, k, v, da, wa = project_call(scal, x_p, cot, vec, attn_w, load_columns)
        part = core_call(0, scal, q, k, v, da)

        part, c_first = lax.optimization_barrier((part, c_first))
        c_second = gather_second(*c_first[:2])
        czs = [swap(cza, 1), swap(czb, 1)]
        o, d = core_call(1, scal, q, k, v, da, *part)

        d, c_second, czs = lax.optimization_barrier((d, c_second, czs))
        c_own = pieces_of(cza, czb, c_first, c_second)
        ((c_joined,),) = mix("join_c", [join_job([t for t in c_own if t is not cza and t is not czb])])
        d, c_joined = lax.optimization_barrier((d, c_joined))
        c_other = swap(c_joined, 1)
        attn_shapes = [sds((2, 8, rows, width))] * 4
        sums_a, *ga = attn_grad_call(scal, xn, o, d, cot, store_with(attn_source), attn_shapes)

        c_other, ga = behind((c_other, ga), sums_a)
        xn_u, ga, c_own, c_other = lax.optimization_barrier((xn, ga, c_own, c_other))
        a_got1, a_got0 = swap(ga[3], 1), swap(ga[2], 1)
        half_tiles = tiles // 2
        c_all = [*c_own, c_other, *czs]
        act, gp, wu = up_call(0, half_tiles, scal, xn_u, b_mlp, (), c_all, load_half(0))

        a_got1, a_got0 = behind((a_got1, a_got0), gp)
        ((sa, sb),) = mix("sums_1", [sum1_job(ga[1], a_got1)])
        act, sa, sb = lax.optimization_barrier((act, sa, sb))
        a_xy = swap_y(sa), swap(sb, 2)
        act, gp = up_call(half_tiles, half_tiles, scal, xn_u, b_mlp, (act, gp, wu), [], None)
        wd, *gd = down_grad_call(
            scal, act, cot, c_all, load_half(1), store_with(down_source), attn_shapes
        )

        a_xy = behind(a_xy, gd)
        ((sa, sb),) = mix("sums_2", [sum2_job(ga[0], a_got0, a_xy)])
        gp, sa, sb, gd = lax.optimization_barrier((gp, sa, sb, gd))
        a_yx = swap(sa, 2), swap_y(sb)
        d_got1, d_got0 = swap(gd[3], 1), swap(gd[2], 1)
        dpre, sums_d = dpre_call(scal, cot, gp, wd)

        a_yx, d_got1, d_got0 = behind((a_yx, d_got1, d_got0), dpre)
        a_t, (sa, sb) = mix("sums_3", [sum3_job(ga[0], a_got0, a_xy, a_yx), sum1_job(gd[1], d_got1)])
        dpre_g, a_t, sa, sb = lax.optimization_barrier((dpre, a_t, sa, sb))
        d_xy = swap_y(sa), swap(sb, 2)
        a_z = [swap(a_t[k], k << 2) for k in (1, 2, 3)]
        gu = up_grad_call(scal, xn, dpre_g, store_with(attn_source), attn_shapes)

        a_z, d_xy = behind((a_z, d_xy), gu)
        (a_sum,), (sa, sb) = mix("sums_4", [sum4_job(a_t[0], a_z), sum2_job(gd[0], d_got0, d_xy)])
        x_i, sa, sb, gu, a_sum = lax.optimization_barrier((x, sa, sb, gu, a_sum))
        u_got1, u_got0 = swap(gu[3], 1), swap(gu[2], 1)
        d_yx = swap(sa, 2), swap_y(sb)
        a_other = swap_y(a_sum)
        sums_x, d_x = input_grad_call(scal, x_i, cot, d, dpre, vec, wa, wu)

        d_yx, u_got1, u_got0, a_other = behind((d_yx, u_got1, u_got0, a_other), d_x)
        (sa, sb), d_t, (*v_part, _) = mix(
            "sums_5",
            [
                sum1_job(gu[1], u_got1),
                sum3_job(gd[0], d_got0, d_xy, d_yx),
                vector_job(sums_a, sums_d, sums_x, wide, rows),
            ],
            scal,
        )
        x_o, sa, sb, d_t = lax.optimization_barrier((x, sa, sb, d_t))
        u_xy = swap_y(sa), swap(sb, 2)
        d_z = [swap(d_t[k], k << 2) for k in (1, 2, 3)]
        out = out_call(scal, x_o, o, act, vec, wa, wd)

        u_xy, d_z, v_part = behind((u_xy, d_z, v_part), out)
        (sa, sb), (d_sum,) = mix("sums_6", [sum2_job(gu[0], u_got0, u_xy), sum4_job(d_t[0], d_z)])
        sa, sb, d_sum, v_part = lax.optimization_barrier((sa, sb, d_sum, v_part))
        u_yx = swap(sa, 2), swap_y(sb)
        v_got = [swap(v_part[i], i) for i in (1, 2, 3)]
        u_t, (v_sum,) = mix("sums_7", [sum3_job(gu[0], u_got0, u_xy, u_yx), add_job([v_part[0], *v_got])])
        u_t, v_sum, d_sum = lax.optimization_barrier((u_t, v_sum, d_sum))
        u_z = [swap(u_t[k], k << 2) for k in (1, 2, 3)]
        v_other, d_other = swap_y(v_sum), swap_y(d_sum)
        (u_sum,), (*v_z, _) = mix("sums_8", [sum4_job(u_t[0], u_z), vector_z_job(v_sum, v_other)], scal)
        u_other = swap_y(u_sum)
        vg = sum([v_z[0], *[swap(v_z[k], k << 2) for k in (1, 2, 3)]])[0]
        d_other = behind(d_other, u_sum)
        placed, grad_out, grad_mlp = place_call(scal, [a_sum, a_other, d_sum, d_other, u_sum])
        grad_joined = place_last_call(scal, placed, behind(u_other, grad_out))
    b_at = 3 * rows
    return (
        out.reshape(tokens.shape),
        d_x.reshape(tokens.shape),
        grad_joined,
        grad_out,
        grad_mlp,
        vg[:rows],
        vg[rows:b_at],
        vg[b_at : b_at + tiles * rows],
        vg[b_at + tiles * rows :],
    )


def solution(mesh):
    sizes = (mesh.shape["narrow"], mesh.shape["wide"])
    rows = P(None, ("narrow", "wide"), None)
    placed = (rows, P(None, ("narrow", "wide")), rows) + (P("wide", None),) * 3 + (P("wide"),) * 4
    return jax.shard_map(
        functools.partial(body, sizes),
        mesh=mesh,
        in_specs=placed,
        out_specs=(rows, rows) + (P("wide", None),) * 3 + (P("wide"),) * 4,
        check_vma=False,
    )
```

```python
import functools

import jax
import jax.numpy as jnp
from jax import lax
from jax.experimental import pallas as pl
from jax.experimental.pallas import tpu as pltpu
from jax.sharding import PartitionSpec as P

HEADS = 12
HEAD = 64
IMG = 196
EPS = 1e-06
GELU_C = 0.7978845608028654
GELU_A = 0.044715

F32 = jnp.float32
BF16 = jnp.bfloat16
HBM = pl.BlockSpec(memory_space=pltpu.HBM)
VMEM = pl.BlockSpec(memory_space=pltpu.VMEM)
SMEM = pl.BlockSpec(memory_space=pltpu.SMEM)


def dot_nn(a, b):
    return lax.dot_general(a, b, (((1,), (0,)), ((), ())), preferred_element_type=F32)


def dot_nt(a, b):
    return lax.dot_general(a, b, (((1,), (1,)), ((), ())), preferred_element_type=F32)


def dot_tn(a, b):
    return lax.dot_general(a, b, (((0,), (0,)), ((), ())), preferred_element_type=F32)


def norm_rows(rows):
    rows = rows.astype(F32)
    mean = jnp.mean(rows, axis=1, keepdims=True)
    centered = rows - mean
    inv = lax.rsqrt(jnp.mean(centered * centered, axis=1, keepdims=True) + EPS)
    return centered * inv, inv


def attend(refs, base, cols, windows):
    q_ref, k_ref, v_ref, da_ref, o_ref, dq_ref, dk_ref, dv_ref = refs
    zero = jnp.zeros((), BF16)
    jobs, ends = [], {}
    for start, rows, lo, hi, merge in windows:
        win = pl.ds(pl.multiple_of(base + start, 16), rows)
        tiles = [r[win, cols] for r in (q_ref, k_ref, v_ref, da_ref)]
        lane = lax.broadcasted_iota(jnp.int32, (rows, 128), 1)
        sums = {}
        step = 256 if rows == 512 else rows
        for at in range(0, rows, step):
            for h in range(2):
                keep = (lane < 64) if h == 0 else (lane >= 64)
                heads = [jnp.where(keep, t, zero) for t in tiles]
                jobs.append([tiles, heads, rows, lo, hi, at, step, sums])
        ends[len(jobs) - 1] = (start, rows, merge, sums)

    def products(job):
        tiles, heads, _, _, _, at, step, _ = job
        qs = slice(at, at + step)
        job += [dot_nt(tiles[1], heads[0][qs]), dot_nt(tiles[2], heads[3][qs])]

    def soften(job):
        _, _, rows, lo, hi, at, step, _, s, dp = job
        masked = lo > 0 or hi < rows
        if masked:
            key = lax.broadcasted_iota(jnp.int32, (rows, step), 0)
            s = jnp.where((key >= lo) & (key < hi), s, -1e30)
        e = jnp.exp(s - jnp.max(s, axis=0, keepdims=True))
        scale = 1.0 / jnp.sum(e, axis=0, keepdims=True)
        if masked:
            query = lax.broadcasted_iota(jnp.int32, (1, step), 1) + at
            scale = jnp.where((query >= lo) & (query < hi), scale, 0.0)
        p = e * scale
        inner = jnp.sum(p * dp, axis=0, keepdims=True)
        job[8:] = [p.astype(BF16), (p * (dp - inner)).astype(BF16)]

    def gather(job):
        _, heads, _, _, _, at, step, sums, p, ds = job
        qs = slice(at, at + step)
        parts = (
            (("o", at), dot_tn(p, heads[2])),
            (("q", at), dot_tn(ds, heads[1])),
            (("v", 0), dot_nn(p, heads[3][qs])),
            (("k", 0), dot_nn(ds, heads[0][qs])),
        )
        for key, val in parts:
            sums[key] = sums[key] + val if key in sums else val

    def write(start, rows, merge, sums):
        for name, ref in (("o", o_ref), ("q", dq_ref), ("k", dk_ref), ("v", dv_ref)):
            for (n, at), val in sums.items():
                if n != name:
                    continue
                val = (val * 0.125 if n == "q" else val).astype(BF16)
                size = val.shape[0]
                if merge and at == 0:
                    head = pl.ds(pl.multiple_of(base + start, 16), merge)
                    ref[head, cols] = ref[head, cols] + val[:merge]
                    val, at, size = val[merge:], merge, size - merge
                ref[pl.ds(pl.multiple_of(base + start + at, 16), size), cols] = val

    for i in range(len(jobs) + 2):
        if i < len(jobs):
            products(jobs[i])
        if 0 <= i - 1 < len(jobs):
            soften(jobs[i - 1])
        if 0 <= i - 2:
            gather(jobs[i - 2])
            if i - 2 in ends:
                write(*ends[i - 2])


WHOLE = ((0, 512, 0, 512, 0),)
SMALL = (
    (0, 208, 0, IMG, 0),
    (192, 208, IMG - 192, 2 * IMG - 192, 16),
    (384, 128, 2 * IMG - 384, 128, 16),
)


def sds(shape, dtype=BF16):
    return jax.ShapeDtypeStruct(shape, dtype)


def kept(shape, dtype=BF16):
    return pltpu.VMEM(shape, dtype)


def call(kernel, name, operands, pieces, outs, g_shapes, scratch, flops, limit=14, alias=None):
    n_p, n_g = len(pieces), len(g_shapes)
    scal, *rest = operands
    rest = [pltpu.with_memory_space_constraint(v, pltpu.VMEM) for v in rest]
    pieces = [pltpu.with_memory_space_constraint(v, pltpu.HBM) for v in pieces]
    g_shapes = [pltpu.HBM(g.shape, g.dtype) for g in g_shapes]
    return pl.pallas_call(
        kernel,
        name=name,
        out_shape=list(outs) + list(g_shapes),
        in_specs=[SMEM] + [VMEM] * len(rest) + [HBM] * n_p,
        out_specs=[VMEM] * len(outs) + [HBM] * n_g,
        scratch_shapes=scratch,
        compiler_params=pltpu.CompilerParams(vmem_limit_bytes=limit << 20),
        input_output_aliases=alias or {},
        cost_estimate=pl.CostEstimate(flops=flops, bytes_accessed=1 << 20, transcendentals=0),
    )(scal, *rest, *pieces)


def loop(count, fn, after=None):
    def step(i, c):
        fn(i)
        if after is not None:
            after(i)
        return c

    lax.fori_loop(0, count, step, 0)


def send_rows(src, dst, i, size, sem):
    per = dst.shape[1] // size
    pltpu.make_async_copy(src.at[rows_of(i, size), :], dst.at[i // per, rows_of(i % per, size), :], sem).start()


def rows_of(i, size):
    return pl.ds(pl.multiple_of(i * size, size), size)


def project_kernel(load, n_w, *refs):
    scal, x_ref, cot_ref, vec_ref = refs[:4]
    xn, q, k, v, da, w, sem = refs[4 + n_w :]
    load(scal, refs[4 : 4 + n_w], w, sem)
    tokens = x_ref.shape[0]

    def norm(i):
        r = rows_of(i, 256)
        standard, _ = norm_rows(x_ref[r, :])
        xn[r, :] = (standard * vec_ref[0:1, :]).astype(BF16)

    loop(tokens // 256, norm)

    def ready(i):
        whole_wait(w.at[i], sem.at[i])()

    def each(fn):
        loop(tokens // 512, lambda i: fn(rows_of(i, 512)))

    def queries(r):
        q[r, :] = (dot_nn(xn[r, :], w[0]) + vec_ref[1:2, :]).astype(BF16) * jnp.asarray(0.125, BF16)

    def keys(r):
        k[r, :] = dot_nn(xn[r, :], w[1]).astype(BF16)

    def values(r):
        v[r, :] = (dot_nn(xn[r, :], w[2]) + vec_ref[2:3, :]).astype(BF16)

    def attended(r):
        da[r, :] = dot_nt(cot_ref[r, :], w[3]).astype(BF16)

    for i, fn in enumerate((queries, keys, values, attended)):
        ready(i)
        each(fn)


def project_call(scal, x, cot, vec, weights, load):
    tokens, width = x.shape
    return call(
        functools.partial(project_kernel, load, len(weights)),
        "project",
        (scal, x, cot, vec),
        weights,
        [kept(x.shape)] * 5,
        [],
        [pltpu.VMEM((4, width, width), BF16), pltpu.SemaphoreType.DMA((4,))],
        8 * tokens * width * width,
        limit=10,
    )


def core_kernel(b, scal, q, k, v, da, *refs):
    o, d = refs[-2:]
    refs = (q, k, v, da, o, d.at[0], d.at[1], d.at[2])
    whole = scal[8 + b] == 0

    def pair(i):
        cols = pl.ds(pl.multiple_of(i * 128, 128), 128)

        @pl.when(whole)
        def _():
            attend(refs, b * 512, cols, WHOLE)

        @pl.when(jnp.logical_not(whole))
        def _():
            attend(refs, b * 512, cols, SMALL)

    loop(q.shape[1] // 128, pair)


def core_call(b, scal, q, k, v, da, *before):
    return call(
        functools.partial(core_kernel, b),
        "core",
        (scal, q, k, v, da, *before),
        [],
        [kept(q.shape), kept((3, *q.shape))],
        [],
        [],
        10 << 30,
        alias={5 + i: i for i in range(len(before))},
        limit=8,
    )


def attn_grad_kernel(store, scal, xn, o, d, cot, sums, *refs):
    *g_refs, g, sem = refs
    tokens, width = xn.shape

    def grad(b):
        g[b] = dot_tn(xn[...], d[b]).astype(BF16)
        store(scal, g, g_refs, sem, b)

    loop(3, grad)
    g[3] = dot_tn(o[...], cot[...]).astype(BF16)
    store(scal, g, g_refs, sem, 3)
    for i, v in enumerate((d[0], d[2], cot[...])):
        sums[i : i + 1, :] = jnp.sum(v.astype(F32), axis=0, keepdims=True)
    stored(g_refs, sem)


def attn_grad_call(scal, xn, o, d, cot, store, g_shapes):
    tokens, width = xn.shape
    return call(
        functools.partial(attn_grad_kernel, store),
        "attn_grad",
        (scal, xn, o, d, cot),
        [],
        [kept((8, width), F32)],
        g_shapes,
        [pltpu.VMEM((4, width, width), BF16), pltpu.SemaphoreType.DMA((len(g_shapes),))],
        8 * tokens * width * width,
        limit=10,
    )


def gelu_parts(u):
    u2 = u * u
    half = 0.5 * jnp.tanh(u * (GELU_C + (GELU_C * GELU_A) * u2)) + 0.5
    act = u * half
    grad = half + act * (1.0 - half) * (2.0 * GELU_C + (6.0 * GELU_C * GELU_A) * u2)
    return act, grad

def tile_of(t, width):
    return pl.ds(t * width if isinstance(t, int) else pl.multiple_of(t * width, 128), width)


def wait_tile(w, sem, t, width):
    whole_wait(w.at[tile_of(t, width), :], sem.at[t])()


def up_kernel(load, first, count, n_p, *refs):
    scal, xn, bias = refs[:3]
    even, odd, sem = refs[-3:]
    tokens, width = xn.shape
    if n_p:
        act, gp, w = refs[-6:-3]
        load(scal, refs[3 : 3 + n_p], w, sem)
        for t in range(count):
            whole_wait(w.at[t], sem.at[t])()
    else:
        act, gp = refs[-5:-3]
        w = refs[5]
    rows = even.shape[0]
    per = tokens // rows

    def product(i):
        return dot_nn(xn[rows_of(i % per, rows), :], w[first + i // per])

    def finish(i, u):
        t, r = first + i // per, rows_of(i % per, rows)
        a, gr = gelu_parts(u + bias[pl.ds(t, 1), :])
        act[t, r, :] = a.astype(BF16)
        gp[t, r, :] = gr.astype(BF16)

    even[...] = product(0)

    def step(i):
        odd[...] = product(2 * i + 1)
        finish(2 * i, even[...])
        even[...] = product(jnp.minimum(2 * i + 2, count * per - 1))
        finish(2 * i + 1, odd[...])

    loop(count * per // 2, step)
    if n_p:
        for t in range(count, bias.shape[0]):
            whole_wait(w.at[t], sem.at[t])()


def up_call(first, count, scal, xn, bias, before, pieces, load):
    tokens, width = xn.shape
    tiles = bias.shape[0]
    return call(
        functools.partial(up_kernel, load, first, count, len(pieces)),
        "up",
        (scal, xn, bias, *before),
        pieces,
        [kept((tiles, tokens, width))] * 2 + [kept((tiles, width, width))] * (1 if pieces else 0),
        [],
        [pltpu.VMEM((256, width), F32)] * 2 + [pltpu.SemaphoreType.DMA((tiles,))],
        2 * count * tokens * width * width,
        alias={3: 0, 4: 1} if before else None,
        limit=7,
    )


def down_grad_kernel(load, store, n_p, scal, act, cot, *refs):
    w, *g_refs, g, wsem, sem = refs[n_p:]
    tiles, tokens, width = act.shape
    load(scal, refs[:n_p], w, wsem)

    def grad(t):
        g[tile_of(t, width), :] = dot_tn(act[t], cot[...]).astype(BF16)
        store(scal, g, g_refs, sem, t)

    loop(tiles, grad)
    for t in range(tiles):
        wait_tile(w, wsem, t, width)
    stored(g_refs, sem)


def down_grad_call(scal, act, cot, pieces, load, store, g_shapes):
    tiles, tokens, width = act.shape
    return call(
        functools.partial(down_grad_kernel, load, store, len(pieces)),
        "down_grad",
        (scal, act, cot),
        pieces,
        [kept((tiles * width, width))],
        g_shapes,
        [
            pltpu.VMEM((tiles * width, width), BF16),
            pltpu.SemaphoreType.DMA((tiles,)),
            pltpu.SemaphoreType.DMA((len(g_shapes),)),
        ],
        2 * tiles * tokens * width * width,
        limit=12,
    )


def dpre_kernel(scal, cot, gp, w, dpre, sums):
    tiles, tokens, width = gp.shape

    def down(t):
        d = (dot_nt(cot[...], w[tile_of(t, width), :]) * gp[t].astype(F32)).astype(BF16)
        dpre[t] = d
        sums[pl.ds(t, 1), :] = jnp.sum(d.astype(F32), axis=0, keepdims=True)

    loop(tiles, down)


def dpre_call(scal, cot, gp, w):
    tiles, tokens, width = gp.shape
    return call(
        dpre_kernel,
        "dpre",
        (scal, cot, gp, w),
        [],
        [kept(gp.shape), kept((8, width), F32)],
        [],
        [],
        2 * tiles * tokens * width * width,
        alias={2: 0},
        limit=8,
    )


def up_grad_kernel(load, store, n_p, scal, xn, dpre, *refs):
    w, *g_refs, g, wsem, sem = refs[n_p:]
    load(scal, refs[:n_p], w, wsem)

    def grad(t):
        g[t] = dot_tn(xn[...], dpre[t]).astype(BF16)
        store(scal, g, g_refs, sem, t)

    loop(dpre.shape[0], grad)
    for i in range(4):
        whole_wait(w.at[i], wsem.at[i])()
    stored(g_refs, sem)


def up_grad_call(scal, xn, dpre, pieces, load, store, g_shapes):
    tiles, tokens, width = dpre.shape
    return call(
        functools.partial(up_grad_kernel, load, store, len(pieces)),
        "up_grad",
        (scal, xn, dpre),
        pieces,
        [kept((4, width, width))],
        g_shapes,
        [
            pltpu.VMEM((tiles, width, width), BF16),
            pltpu.SemaphoreType.DMA((4,)),
            pltpu.SemaphoreType.DMA((len(g_shapes),)),
        ],
        2 * tiles * tokens * width * width,
        limit=10,
    )


def input_grad_kernel(scal, x, cot, d, dpre, vec, wa, wu, sums, dx_ref, dx, sem):
    tiles, tokens, width = dpre.shape
    sums[...] = jnp.zeros_like(sums)

    def step(i):
        r = rows_of(i, 256)
        dnr = dot_nt(d[0, r, :], wa[0]) + dot_nt(d[1, r, :], wa[1]) + dot_nt(d[2, r, :], wa[2])
        for t in range(tiles):
            dnr += dot_nt(dpre[t, r, :], wu[t])
        standard, inv = norm_rows(x[r, :])
        sums[0:1, :] += jnp.sum(dnr * standard, axis=0, keepdims=True)
        gs = dnr * vec[0:1, :]
        mean_g = jnp.mean(gs, axis=1, keepdims=True)
        mean_p = jnp.mean(gs * standard, axis=1, keepdims=True)
        dx[r, :] = (cot[r, :].astype(F32) + inv * (gs - mean_g - standard * mean_p)).astype(BF16)

    loop(tokens // 256, step, lambda i: send_rows(dx, dx_ref, i, 256, sem))
    whole_wait(dx_ref, sem)()


def input_grad_call(scal, x, cot, d, dpre, vec, wa, wu):
    tiles, tokens, width = dpre.shape
    return call(
        input_grad_kernel,
        "input_grad",
        (scal, x, cot, d, dpre, vec, wa, wu),
        [],
        [kept((8, width), F32)],
        [sds((tokens // 512, 512, width))],
        [pltpu.VMEM((tokens, width), BF16), pltpu.SemaphoreType.DMA],
        2 * (tiles + 3) * tokens * width * width,
        limit=8,
    )


def out_kernel(scal, x, o, act, vec, wa, wd, out_ref, out, sem):
    tiles, tokens, width = act.shape

    def step(i):
        r = rows_of(i, 256)
        total = x[r, :].astype(F32) + vec[3:4, :] + dot_nn(o[r, :], wa[3])
        for t in range(tiles):
            total += dot_nn(act[t, r, :], wd[tile_of(t, width), :])
        out[r, :] = total.astype(BF16)

    loop(tokens // 256, step, lambda i: send_rows(out, out_ref, i, 256, sem))
    whole_wait(out_ref, sem)()


def out_call(scal, x, o, act, vec, wa, wd):
    tiles, tokens, width = act.shape
    (out,) = call(
        out_kernel,
        "out",
        (scal, x, o, act, vec, wa, wd),
        [],
        [],
        [sds((tokens // 512, 512, width))],
        [pltpu.VMEM((tokens, width), BF16), pltpu.SemaphoreType.DMA],
        2 * (tiles + 1) * tokens * width * width,
        limit=8,
    )
    return out


def swap(value, mask):
    return lax.ppermute(value, "wide", [(i, i ^ mask) for i in range(16)])


def swap_y(value):
    return lax.ppermute(value, "narrow", [(0, 1), (1, 0)])


def slots():
    for part in range(2):
        for i in range(2):
            for s in range(2):
                half, side = (i, s) if part == 0 else (s, i)
                for k in range(4):
                    yield part, i, s * 4 + k, half, side, k


def device_of(scal, k, side, core):
    return ((scal[1] ^ k) * 2 + (scal[2] ^ side)) * 2 + (scal[3] ^ core)


def behind(value, *marks):
    return lax.optimization_barrier((value, marks))[0]


def gather_z(value):
    return [swap(value, k << 2) for k in (1, 2, 3)]


def gather_first(za, zb):
    return swap(za, 2), swap_y(zb), swap_y(za), swap(zb, 2)


def gather_second(xa, yb):
    return swap_y(xa), swap(yb, 2)


def pieces_of(za, zb, first, second):
    xa, yb, ya, xb = first
    return [za, xa, ya, second[0], zb, xb, yb, second[1]]


def join_job(values):
    def fn(held, near, outs):
        size = near[0].shape[0]
        for i, v in enumerate(near):
            outs[0][i * size : (i + 1) * size] = v[...]

    return fn, [], values, [kept((len(values) * values[0].shape[0], *values[0].shape[1:]))]


def mix(name, jobs):
    held = [v for job in jobs for v in job[1]]
    near = [v for job in jobs for v in job[2]]
    outs = [o for job in jobs for o in job[3]]

    def kernel(*refs):
        at = len(near) + len(held)
        scratch = refs[at + len(outs) :]
        copies = [
            pltpu.make_async_copy(refs[len(near) + i], scratch[i], scratch[-1].at[i]) for i in range(len(held))
        ]
        for cp in copies:
            cp.start()
        h = n = o = 0
        for fn, job_h, job_n, job_o in jobs:
            for i in range(len(job_h)):
                copies[h + i].wait()
            fn(
                scratch[h : h + len(job_h)],
                refs[n : n + len(job_n)],
                refs[at + o : at + o + len(job_o)],
            )
            h, n, o = h + len(job_h), n + len(job_n), o + len(job_o)

    got = pl.pallas_call(
        kernel,
        name=name,
        out_shape=outs,
        in_specs=[VMEM] * len(near) + [HBM] * len(held),
        out_specs=[VMEM] * len(outs),
        scratch_shapes=[pltpu.VMEM(v.shape, v.dtype) for v in held]
        + [pltpu.SemaphoreType.DMA((max(len(held), 1),))],
        compiler_params=pltpu.CompilerParams(vmem_limit_bytes=8 << 20),
        cost_estimate=pl.CostEstimate(flops=1 << 20, bytes_accessed=1 << 20, transcendentals=0),
    )(
        *[pltpu.with_memory_space_constraint(v, pltpu.VMEM) for v in near],
        *[pltpu.with_memory_space_constraint(v, pltpu.HBM) for v in held],
    )
    split, at = [], 0
    for job in jobs:
        split.append(got[at : at + len(job[3])])
        at += len(job[3])
    return split


def total(*parts):
    return sum(v.astype(F32) for v in parts)


def stack_job(values):
    def fn(held, near, outs):
        for k, v in enumerate(near):
            for i in range(2):
                outs[i][k] = v[i]

    return fn, [], list(values), [kept((len(values), *values[0].shape[1:]))] * 2


def vector_job(sums_a, sums_d, sums_x, wide, rows):
    width = sums_a.shape[1]

    def spread(rows_in, per):
        flat = jnp.concatenate([rows_in[w * per // width][None] for w in range(wide)])
        col = lax.broadcasted_iota(jnp.int32, (wide, width), 1)
        own = lax.broadcasted_iota(jnp.int32, (wide, width), 0) * per % width
        flat = jnp.where((col >= own) & (col < own + per), flat, 0.0)
        pick = lax.broadcasted_iota(jnp.int32, (width, per), 0) % per
        pick = (pick == lax.broadcasted_iota(jnp.int32, (width, per), 1)).astype(BF16)
        got = jnp.zeros((wide, per), F32)
        for _ in range(3):
            high = flat.astype(BF16)
            flat = flat - high.astype(F32)
            got += dot_nn(high, pick)
        return got

    def fn(held, near, outs):
        a, d, x, scal = near
        tiles = 4
        at = 0
        for got in (
            spread([x[0]], rows),
            spread([a[0], a[1]], 2 * rows),
            spread([d[t] for t in range(tiles)], tiles * rows),
            spread([a[2]], rows),
        ):
            outs[4][:, at : at + got.shape[1]] = got
            at += got.shape[1]
        for k in range(4):
            outs[k][...] = jnp.zeros_like(outs[k])
            for r in range(4):
                outs[k][r : r + 1, :] = outs[4][pl.ds((scal[1] ^ k) * 4 + r, 1), :]

    return fn, [], [sums_a, sums_d, sums_x], [kept((8, 8 * rows), F32)] * 4 + [kept((wide, 8 * rows), F32)]


def add_job(values):
    def fn(held, near, outs):
        outs[0][...] = sum(near[i][...] for i in range(len(values)))

    return fn, [], list(values), [kept(values[0].shape, F32)]


def vector_job(sums_a, sums_d, sums_x):
    def fn(held, near, outs):
        a, d, x = near
        outs[0][0:1, :] = x[0:1, :]
        outs[0][1:3, :] = a[0:2, :]
        outs[0][3:7, :] = d[0:4, :]
        outs[0][7:8, :] = a[2:3, :]

    return fn, [], [sums_a, sums_d, sums_x], [kept(sums_a.shape, F32)]


def sum1_job(keep1, got1):
    def fn(held, near, outs):
        for i in range(2):
            outs[i][...] = total(held[0][i], near[0][i]).astype(BF16)

    return fn, [keep1], [got1], [kept(keep1.shape[1:])] * 2


def sum2_job(keep0, got0, got):
    half = keep0.shape[1] // 2

    def fn(held, near, outs):
        for i in range(2):
            outs[i][...] = total(held[0][i, half:], near[0][i, half:], near[1 + i][half:]).astype(BF16)

    return fn, [keep0], [got0, *got], [kept((half, *keep0.shape[2:]))] * 2


def sum3_job(keep0, got0, got, got2):
    half = keep0.shape[1] // 2

    def fn(held, near, outs):
        for k in range(half):
            for i in range(2):
                outs[k][i] = total(held[0][i, k], near[0][i, k], near[1 + i][k], near[3 + i][k]).astype(BF16)

    return fn, [keep0], [got0, *got, *got2], [kept((2, *keep0.shape[2:]))] * half


def sum4_job(own, got):
    def fn(held, near, outs):
        outs[0][...] = total(*[near[i][...] for i in range(1 + len(got))]).astype(BF16)

    return fn, [], [own, *got], [kept(own.shape)]


def place_kernel(scal, a_mine, a_other, d_mine, d_other, u_mine, joined_ref, out, down, joined, sem):
    _, rows, width = a_mine.shape

    def place(half, a, d, u):
        for p in range(2):
            block = half * 2 + p
            down[pl.ds(block * rows, rows), :] = d[p].astype(F32)
            if u is not None:
                joined[3 + p] = u[p].astype(F32)
                send(joined.at[3 + p], 3 + block)
            if block < 3:
                joined[block] = a[p].astype(F32)
                send(joined.at[block], block)
            else:
                out[...] = a[p].astype(F32)

    def send(src, block):
        pltpu.make_async_copy(src, joined_ref.at[:, block * width : (block + 1) * width], sem).start()

    @pl.when(scal[0] == 0)
    def _():
        place(0, a_mine, d_mine, u_mine)
        place(1, a_other, d_other, None)

    @pl.when(scal[0] != 0)
    def _():
        place(1, a_mine, d_mine, u_mine)
        place(0, a_other, d_other, None)

    whole_wait(joined, sem)()


def place_call(scal, parts):
    _, rows, width = parts[0].shape
    return pl.pallas_call(
        place_kernel,
        name="place",
        out_shape=[sds((rows, 7 * width), F32), sds((rows, width), F32), sds((4 * rows, width), F32)],
        in_specs=[SMEM] + [VMEM] * 5,
        out_specs=[HBM, VMEM, VMEM],
        scratch_shapes=[pltpu.VMEM((5, rows, width), F32), pltpu.SemaphoreType.DMA],
    )(scal, *[pltpu.with_memory_space_constraint(v, pltpu.VMEM) for v in parts])


def place_last_kernel(scal, placed, other, joined_ref, wide, sem):
    _, rows, width = other.shape
    for p in range(2):
        wide[p] = other[p].astype(F32)
        at = pl.multiple_of((3 + (1 - scal[0]) * 2 + p) * width, 128)
        pltpu.make_async_copy(wide.at[p], joined_ref.at[:, pl.ds(at, width)], sem).start()
    whole_wait(wide, sem)()


def place_last_call(scal, placed, other):
    return pl.pallas_call(
        place_last_kernel,
        name="place_last",
        out_shape=sds(placed.shape, F32),
        in_specs=[SMEM, HBM, VMEM],
        out_specs=HBM,
        scratch_shapes=[pltpu.VMEM(other.shape, F32), pltpu.SemaphoreType.DMA],
        input_output_aliases={1: 0},
    )(scal, placed, pltpu.with_memory_space_constraint(other, pltpu.VMEM))


def whole_wait(ref, sem):
    return pltpu.make_async_copy(ref, ref, sem).wait


def piece(refs, at, core, k, alone):
    if core == 0:
        return refs[at].at[k]
    if at in alone:
        return refs[9 + alone.index(at)].at[k]
    return refs[8].at[(at - sum(i < at for i in alone)) * 4 + k]


def load_columns(scal, refs, w, sem):
    rows = w.shape[1] // 16

    def start(own):
        for block in range(4):
            for core in range(2):
                for part, _, _, half, side, k in slots():
                    if (own ^ half) * 2 + part != block:
                        continue
                    src = piece(refs, part * 4 + half * 2 + side, core, k, (3, 7)).at[pl.ds(0, rows), :]
                    dst = w.at[block, rows_at(device_of(scal, k, side, core) * rows, rows), :]
                    pltpu.make_async_copy(src, dst, sem.at[block]).start()

    @pl.when(scal[0] == 0)
    def _():
        start(0)

    @pl.when(scal[0] != 0)
    def _():
        start(1)


def load_half(which):
    def load(scal, refs, w, sem):
        def start(rel):
            for core in range(2):
                for part, _, _, half, side, k in slots():
                    if half != rel:
                        continue
                    src = piece(refs, part * 4 + half * 2 + side, core, k, (0, 4))
                    per, rows, width = src.shape
                    dev = device_of(scal, k, side, core)
                    for b in range(per):
                        block = part * per + b
                        if which == 0:
                            dst, tile = w.at[block, rows_at(dev * rows, rows), :], block
                        else:
                            dst, tile = w.at[rows_at((dev * 2 * per + block) * rows, rows), :], scal[1] ^ k
                        pltpu.make_async_copy(src.at[b], dst, sem.at[tile]).start()

        @pl.when(scal[0] == which)
        def _():
            start(0)

        @pl.when(scal[0] != which)
        def _():
            start(1)

    return load


def vectors_kernel(rows, scal, *refs):
    pieces, (vec, b_mlp, buf, sem) = refs[:3], refs[3:]
    width = vec.shape[1]
    for core in range(2):
        for side in range(2):
            for k in range(4):
                src = pieces[side].at[k] if core == 0 else pieces[2].at[side * 4 + k]
                src = src.at[pl.ds(rows, 8), :]
                pltpu.make_async_copy(src, buf.at[device_of(scal, k, side, core)], sem).start()
    whole_wait(buf, sem)()
    values = buf[:, 0, :].astype(F32)
    devices = values.shape[0]

    def line(at, per):
        pick = lax.broadcasted_iota(jnp.int32, (per, width), 1) % per
        pick = (pick == lax.broadcasted_iota(jnp.int32, (per, width), 0)).astype(BF16)
        flat = dot_nn(values[:, at : at + per].astype(BF16), pick)
        dev = lax.broadcasted_iota(jnp.int32, flat.shape, 0)
        col = lax.broadcasted_iota(jnp.int32, flat.shape, 1)
        count = devices * per // width
        share = devices // count
        keep = col // per == dev % share
        return [
            jnp.sum(jnp.where(keep & (dev // share == i), flat, 0.0), axis=0, keepdims=True) for i in range(count)
        ]

    lines = line(0, rows) + line(rows, 2 * rows) + line(7 * rows, rows)
    vec[...] = jnp.zeros_like(vec)
    for i, v in enumerate(lines):
        vec[i : i + 1, :] = v
    for i, v in enumerate(line(3 * rows, 4 * rows)):
        b_mlp[i : i + 1, :] = v


def vectors_call(scal, pieces, rows):
    width = pieces[0].shape[2]
    return pl.pallas_call(
        functools.partial(vectors_kernel, rows),
        name="vectors",
        out_shape=[kept((8, width), F32), kept((4, width), F32)],
        in_specs=[SMEM] + [HBM] * 3,
        out_specs=[VMEM] * 2,
        scratch_shapes=[pltpu.VMEM((16, 8, width), BF16), pltpu.SemaphoreType.DMA],
        compiler_params=pltpu.CompilerParams(vmem_limit_bytes=8 << 20),
    )(scal, *[pltpu.with_memory_space_constraint(v, pltpu.HBM) for v in pieces])


def rows_at(base, rows):
    return pl.ds(pl.multiple_of(base, 16), rows)


def stored(refs, sem):
    for i, r in enumerate(refs):
        whole_wait(r, sem.at[i])()


def store_block(scal, g, refs, sem, t):
    half, part = scal[0] ^ (t // 2), t % 2
    rows = refs[0].shape[2]

    def send(at, core, side, k, slot, p):
        src = g.at[t, rows_at(device_of(scal, k, side, core) * rows, rows), :]
        pltpu.make_async_copy(src, refs[at].at[p, slot], sem.at[at]).start()

    for i in range(2):

        @pl.when((part == 0) & (half == i))
        def _(i=i):
            for core in range(2):
                for side in range(2):
                    for k in range(4):
                        send(core * 2 + i, core, side, k, side * 4 + k, 0)

    @pl.when(part == 1)
    def _():
        for core in range(2):
            for side in range(2):
                for k in range(4):
                    send(core * 2 + side, core, side, k, half * 4 + k, 1)


def store_rows(scal, g, refs, sem, t):
    k = scal[1] ^ t
    rows = refs[0].shape[2]
    for core in range(2):
        for side in range(2):
            dev = (t * 2 + (scal[2] ^ side)) * 2 + (scal[3] ^ core)
            for half in range(2):
                for part in range(2):
                    i, s = (half, side) if part == 0 else (side, half)
                    at = core * 2 + i
                    src = g.at[rows_at((dev * 4 + (scal[0] ^ half) * 2 + part) * rows, rows), :]
                    pltpu.make_async_copy(src, refs[at].at[part, s * 4 + k], sem.at[at]).start()


def load_whole_blocks(scal, refs, w, sem):
    for i, r in enumerate(refs):
        pltpu.make_async_copy(r, w.at[i], sem.at[i]).start()


def load_whole_rows(scal, refs, w, sem):
    width = w.shape[1]
    for t in range(w.shape[0] // width):
        r = tile_of(t, width)
        pltpu.make_async_copy(refs[0].at[r, :], w.at[r, :], sem.at[t]).start()


def store_whole_blocks(scal, g, refs, sem, t):
    for i, r in enumerate(refs):

        @pl.when(t == i)
        def _(i=i, r=r):
            pltpu.make_async_copy(g.at[i], r, sem.at[i]).start()


def store_whole_rows(scal, g, refs, sem, t):
    r = tile_of(t, g.shape[1])
    pltpu.make_async_copy(g.at[r, :], refs[0].at[r, :], sem.at[0]).start()


def body(sizes, tokens, image_ids, cotangent, w_joined, w_out, w_mlp, norm_gain, bias_attn, bias_mlp, bias_out):
    micro, length, width = tokens.shape
    narrow, wide = sizes
    paired = narrow == 2 and wide == 16
    rows = width // wide
    tiles = w_mlp.shape[0] // rows
    x = tokens.reshape(micro * length, width)
    cot = cotangent.reshape(micro * length, width)
    n = lax.axis_index("narrow")
    w = lax.axis_index("wide")
    last = image_ids.reshape(-1, 512)[:, -1]
    scal = [n, w >> 2, (w >> 1) & 1, w & 1] + [jnp.int32(0)] * 4 + [last[b] for b in range(last.shape[0])]
    scal = jnp.stack([jnp.asarray(s, jnp.int32) for s in scal])
    vec_own = jnp.concatenate([norm_gain, bias_attn, bias_mlp, bias_out])

    def vectors(vec):
        vec = vec.astype(F32)
        b_at = 3 * rows
        b_mlp = vec[:, b_at : b_at + tiles * rows].reshape(tiles, width)
        head = [
            vec[:, :rows].reshape(1, width),
            vec[:, rows:b_at].reshape(2, width),
            vec[:, b_at + tiles * rows :].reshape(1, width),
            jnp.zeros((4, width), F32),
        ]
        return jnp.concatenate(head), b_mlp

    def vector_grads(sums_a, sums_d, sums_x):
        return jnp.concatenate(
            [
                sums_x[0].reshape(wide, rows),
                sums_a[:2].reshape(wide, 2 * rows),
                sums_d[:tiles].reshape(wide, tiles * rows),
                sums_a[2].reshape(wide, rows),
            ],
            axis=1,
        )

    if not paired:
        full = lax.all_gather(w_joined, "wide", axis=0, tiled=True)
        parts = [full[:, i * width : (i + 1) * width] for i in range(3 + tiles)]
        attn_w = parts[:3] + [lax.all_gather(w_out, "wide", axis=0, tiled=True)]
        up_w = parts[3:]
        down_w = [lax.all_gather(w_mlp, "wide", axis=0, tiled=True)]
        vec, b_mlp = vectors(lax.all_gather(vec_own, "wide", axis=0))
        square = [sds((width, width))]
        xn, q, k, v, da = project_call(scal, x, cot, vec, attn_w, load_whole_blocks)
        o, d = core_call(0, scal, q, k, v, da)
        for b in range(1, last.shape[0]):
            o, d = core_call(b, scal, q, k, v, da, o, d)
        sums_a, *g_attn = attn_grad_call(scal, xn, o, d, cot, store_whole_blocks, square * 4)
        act, gp, wu = up_call(0, tiles // 2, scal, xn, b_mlp, (), up_w, load_whole_blocks)
        act, gp = up_call(tiles // 2, tiles - tiles // 2, scal, xn, b_mlp, (act, gp, wu), [], None)
        wd, *g_down = down_grad_call(
            scal, act, cot, down_w, load_whole_rows, store_whole_rows, [sds((tiles * width, width))]
        )
        dpre, sums_d = dpre_call(scal, cot, gp, wd)
        wa, *g_up = up_grad_call(scal, xn, dpre, attn_w, load_whole_blocks, store_whole_blocks, square * tiles)
        sums_x, d_x = input_grad_call(scal, x, cot, d, dpre, vec, wa, wu)
        out = out_call(scal, x, o, act, vec, wa, wd)

        def reduce(g):
            g = lax.psum_scatter(g.astype(F32), "wide", scatter_dimension=0, tiled=True)
            return lax.psum(g, "narrow")

        grad_joined = reduce(jnp.concatenate([*g_attn[:3], *g_up], axis=1))
        grad_out = reduce(g_attn[3])
        grad_mlp = reduce(g_down[0])
        vg = reduce(vector_grads(sums_a, sums_d, sums_x))[0]
        vg = jnp.split(vg, [rows, 3 * rows, (3 + tiles) * rows])
    else:
        col = lambda i: w_joined[:, i * width : (i + 1) * width]
        pair = lambda f: jnp.stack([jnp.where(n == 0, f(0), f(2)), jnp.where(n == 0, f(1), f(3))])
        half = pair(lambda i: col(i) if i < 3 else w_out)
        v_rows = jnp.pad(vec_own, (0, width - vec_own.shape[0]))
        half = jnp.concatenate([half, jnp.broadcast_to(v_rows, (2, 8, width))], axis=1)
        got = gather_z(half)
        za, zb = [jnp.stack([t[i] for t in (half, *got)]) for i in range(2)]
        c_half = jnp.stack([jnp.where(n == 0, col(3 + t), w_mlp[t * rows : (t + 1) * rows]) for t in range(tiles)])
        c_half = behind(c_half.reshape(2, tiles // 2, rows, width), za, zb)
        first = gather_first(za, zb)
        c2 = swap(c_half, 8)
        first, c2, c_half = lax.optimization_barrier((first, c2, c_half))
        second = gather_second(*first[:2])
        own = pieces_of(za, zb, first, second)
        ((joined,),) = mix("join_a", [join_job([own[i] for i in (0, 1, 2, 4, 5, 6)])])
        joined, c1, c3 = swap(joined, 1), swap(c_half, 4), swap(c_half, 12)
        second, joined, c1, c3 = lax.optimization_barrier((second, joined, c1, c3))
        vec, b_mlp = vectors_call(scal, [za, first[0], joined], rows)
        own = pieces_of(za, zb, first, second)
        attn_w = [*own, joined, swap(second[0], 1), swap(second[1], 1)]
        cza, czb = [jnp.stack([t[i] for t in (c_half, c1, c2, c3)]) for i in range(2)]
        x_p, attn_w, cza, czb, vec, b_mlp = lax.optimization_barrier((x, attn_w, cza, czb, vec, b_mlp))
        c_first = gather_first(cza, czb)
        xn, q, k, v, da = project_call(scal, x_p, cot, vec, attn_w, load_columns)
        part = core_call(0, scal, q, k, v, da)

        part, c_first = lax.optimization_barrier((part, c_first))
        c_second = gather_second(*c_first[:2])
        czs = [swap(cza, 1), swap(czb, 1)]
        o, d = core_call(1, scal, q, k, v, da, *part)

        d, c_second, czs = lax.optimization_barrier((d, c_second, czs))
        c_own = pieces_of(cza, czb, c_first, c_second)
        ((c_joined,),) = mix("join_c", [join_job([t for t in c_own if t is not cza and t is not czb])])
        d, c_joined = lax.optimization_barrier((d, c_joined))
        c_other = swap(c_joined, 1)
        attn_shapes = [sds((2, 8, rows, width))] * 4
        sums_a, *ga = attn_grad_call(scal, xn, o, d, cot, store_block, attn_shapes)

        c_other, ga = behind((c_other, ga), sums_a)
        xn_u, ga, c_own, c_other = lax.optimization_barrier((xn, ga, c_own, c_other))
        a_got1, a_got0 = swap(ga[3], 1), swap(ga[2], 1)
        half_tiles = tiles // 2
        c_all = [*c_own, c_other, *czs]
        act, gp, wu = up_call(0, half_tiles, scal, xn_u, b_mlp, (), c_all, load_half(0))

        a_got1, a_got0 = behind((a_got1, a_got0), gp)
        ((sa, sb),) = mix("sums_1", [sum1_job(ga[1], a_got1)])
        act, sa, sb = lax.optimization_barrier((act, sa, sb))
        a_xy = swap_y(sa), swap(sb, 2)
        act, gp = up_call(half_tiles, half_tiles, scal, xn_u, b_mlp, (act, gp, wu), [], None)
        wd, *gd = down_grad_call(
            scal, act, cot, c_all, load_half(1), store_rows, attn_shapes
        )

        a_xy = behind(a_xy, gd)
        ((sa, sb),) = mix("sums_2", [sum2_job(ga[0], a_got0, a_xy)])
        gp, sa, sb, gd = lax.optimization_barrier((gp, sa, sb, gd))
        a_yx = swap(sa, 2), swap_y(sb)
        d_got1, d_got0 = swap(gd[3], 1), swap(gd[2], 1)
        dpre, sums_d = dpre_call(scal, cot, gp, wd)

        a_yx, d_got1, d_got0 = behind((a_yx, d_got1, d_got0), dpre)
        a_t, (sa, sb) = mix("sums_3", [sum3_job(ga[0], a_got0, a_xy, a_yx), sum1_job(gd[1], d_got1)])
        dpre_g, a_t, sa, sb = lax.optimization_barrier((dpre, a_t, sa, sb))
        d_xy = swap_y(sa), swap(sb, 2)
        a_z = [swap(a_t[k], k << 2) for k in (1, 2, 3)]
        wa, *gu = up_grad_call(scal, xn, dpre_g, attn_w, load_columns, store_block, attn_shapes)

        a_z, d_xy = behind((a_z, d_xy), gu)
        (a_sum,), (sa, sb) = mix("sums_4", [sum4_job(a_t[0], a_z), sum2_job(gd[0], d_got0, d_xy)])
        x_i, sa, sb, gu, a_sum = lax.optimization_barrier((x, sa, sb, gu, a_sum))
        u_got1, u_got0 = swap(gu[3], 1), swap(gu[2], 1)
        d_yx = swap(sa, 2), swap_y(sb)
        a_other = swap_y(a_sum)
        sums_x, d_x = input_grad_call(scal, x_i, cot, d, dpre, vec, wa, wu)

        d_yx, u_got1, u_got0, a_other = behind((d_yx, u_got1, u_got0, a_other), d_x)
        (sa, sb), d_t, (v_own,) = mix(
            "sums_5",
            [
                sum1_job(gu[1], u_got1),
                sum3_job(gd[0], d_got0, d_xy, d_yx),
                vector_job(sums_a, sums_d, sums_x),
            ],
        )
        x_o, sa, sb, d_t = lax.optimization_barrier((x, sa, sb, d_t))
        u_xy = swap_y(sa), swap(sb, 2)
        d_z = [swap(d_t[k], k << 2) for k in (1, 2, 3)]
        out = out_call(scal, x_o, o, act, vec, wa, wd)

        u_xy, d_z, v_own = behind((u_xy, d_z, v_own), out)
        (sa, sb), (d_sum,) = mix("sums_6", [sum2_job(gu[0], u_got0, u_xy), sum4_job(d_t[0], d_z)])
        sa, sb, d_sum, v_own = lax.optimization_barrier((sa, sb, d_sum, v_own))
        u_yx = swap(sa, 2), swap_y(sb)
        v_got = [swap(v_own, k << 2) for k in (1, 2, 3)]
        u_t, (v_sum,) = mix("sums_7", [sum3_job(gu[0], u_got0, u_xy, u_yx), add_job([v_own, *v_got])])
        u_t, v_sum, d_sum = lax.optimization_barrier((u_t, v_sum, d_sum))
        u_z = [swap(u_t[k], k << 2) for k in (1, 2, 3)]
        v_other, d_other = swap_y(v_sum), swap_y(d_sum)
        (u_sum,), (v_sum,) = mix("sums_8", [sum4_job(u_t[0], u_z), add_job([v_sum, v_other])])
        u_other = swap_y(u_sum)
        vg = sum([v_sum, *[swap(v_sum, i) for i in (1, 2, 3)]])
        own = lambda v, per: lax.dynamic_slice(v.reshape(-1), (w * per,), (per,))
        vg = [own(vg[0], rows), own(vg[1:3], 2 * rows), own(vg[3:7], tiles * rows), own(vg[7], rows)]
        d_other = behind(d_other, u_sum)
        placed, grad_out, grad_mlp = place_call(scal, [a_sum, a_other, d_sum, d_other, u_sum])
        grad_joined = place_last_call(scal, placed, behind(u_other, grad_out))
    return (out.reshape(tokens.shape), d_x.reshape(tokens.shape), grad_joined, grad_out, grad_mlp, *vg)


def solution(mesh):
    sizes = (mesh.shape["narrow"], mesh.shape["wide"])
    rows = P(None, ("narrow", "wide"), None)
    placed = (rows, P(None, ("narrow", "wide")), rows) + (P("wide", None),) * 3 + (P("wide"),) * 4
    return jax.shard_map(
        functools.partial(body, sizes),
        mesh=mesh,
        in_specs=placed,
        out_specs=(rows, rows) + (P("wide", None),) * 3 + (P("wide"),) * 4,
        check_vma=False,
    )
```

```python
import functools

import jax
import jax.numpy as jnp
from jax import lax
from jax.experimental import pallas as pl
from jax.experimental.pallas import tpu as pltpu
from jax.sharding import PartitionSpec as P

HEADS = 12
HEAD = 64
IMG = 196
EPS = 1e-06
GELU_C = 0.7978845608028654
GELU_A = 0.044715

F32 = jnp.float32
BF16 = jnp.bfloat16
HBM = pl.BlockSpec(memory_space=pltpu.HBM)
VMEM = pl.BlockSpec(memory_space=pltpu.VMEM)
SMEM = pl.BlockSpec(memory_space=pltpu.SMEM)


def dot_nn(a, b):
    return lax.dot_general(a, b, (((1,), (0,)), ((), ())), preferred_element_type=F32)


def dot_nt(a, b):
    return lax.dot_general(a, b, (((1,), (1,)), ((), ())), preferred_element_type=F32)


def dot_tn(a, b):
    return lax.dot_general(a, b, (((0,), (0,)), ((), ())), preferred_element_type=F32)


def norm_rows(rows):
    rows = rows.astype(F32)
    mean = jnp.mean(rows, axis=1, keepdims=True)
    centered = rows - mean
    inv = lax.rsqrt(jnp.mean(centered * centered, axis=1, keepdims=True) + EPS)
    return centered * inv, inv


def attend(refs, base, cols, windows):
    q_ref, k_ref, v_ref, da_ref, o_ref, dq_ref, dk_ref, dv_ref = refs
    zero = jnp.zeros((), BF16)
    jobs, ends = [], {}
    for start, rows, lo, hi, merge in windows:
        win = pl.ds(pl.multiple_of(base + start, 16), rows)
        tiles = [r[win, cols] for r in (q_ref, k_ref, v_ref, da_ref)]
        lane = lax.broadcasted_iota(jnp.int32, (rows, 128), 1)
        sums = {}
        step = 256 if rows == 512 else rows
        for at in range(0, rows, step):
            for h in range(2):
                keep = (lane < 64) if h == 0 else (lane >= 64)
                heads = [jnp.where(keep, t, zero) for t in tiles]
                jobs.append([tiles, heads, rows, lo, hi, at, step, sums])
        ends[len(jobs) - 1] = (start, rows, merge, sums)

    def products(job):
        tiles, heads, _, _, _, at, step, _ = job
        qs = slice(at, at + step)
        job += [dot_nt(tiles[1], heads[0][qs]), dot_nt(tiles[2], heads[3][qs])]

    def soften(job):
        _, _, rows, lo, hi, at, step, _, s, dp = job
        masked = lo > 0 or hi < rows
        if masked:
            key = lax.broadcasted_iota(jnp.int32, (rows, step), 0)
            s = jnp.where((key >= lo) & (key < hi), s, -1e30)
        e = jnp.exp(s - jnp.max(s, axis=0, keepdims=True))
        scale = 1.0 / jnp.sum(e, axis=0, keepdims=True)
        if masked:
            query = lax.broadcasted_iota(jnp.int32, (1, step), 1) + at
            scale = jnp.where((query >= lo) & (query < hi), scale, 0.0)
        p = e * scale
        inner = jnp.sum(p * dp, axis=0, keepdims=True)
        job[8:] = [p.astype(BF16), (p * (dp - inner)).astype(BF16)]

    def gather(job):
        _, heads, _, _, _, at, step, sums, p, ds = job
        qs = slice(at, at + step)
        parts = (
            (("o", at), dot_tn(p, heads[2])),
            (("q", at), dot_tn(ds, heads[1])),
            (("v", 0), dot_nn(p, heads[3][qs])),
            (("k", 0), dot_nn(ds, heads[0][qs])),
        )
        for key, val in parts:
            sums[key] = sums[key] + val if key in sums else val

    def write(start, rows, merge, sums):
        for name, ref in (("o", o_ref), ("q", dq_ref), ("k", dk_ref), ("v", dv_ref)):
            for (n, at), val in sums.items():
                if n != name:
                    continue
                val = (val * 0.125 if n == "q" else val).astype(BF16)
                size = val.shape[0]
                if merge and at == 0:
                    head = pl.ds(pl.multiple_of(base + start, 16), merge)
                    ref[head, cols] = ref[head, cols] + val[:merge]
                    val, at, size = val[merge:], merge, size - merge
                ref[pl.ds(pl.multiple_of(base + start + at, 16), size), cols] = val

    for i in range(len(jobs) + 2):
        if i < len(jobs):
            products(jobs[i])
        if 0 <= i - 1 < len(jobs):
            soften(jobs[i - 1])
        if 0 <= i - 2:
            gather(jobs[i - 2])
            if i - 2 in ends:
                write(*ends[i - 2])


WHOLE = ((0, 512, 0, 512, 0),)
SMALL = (
    (0, 208, 0, IMG, 0),
    (192, 208, IMG - 192, 2 * IMG - 192, 16),
    (384, 128, 2 * IMG - 384, 128, 16),
)


def sds(shape, dtype=BF16):
    return jax.ShapeDtypeStruct(shape, dtype)


def kept(shape, dtype=BF16):
    return pltpu.VMEM(shape, dtype)


def call(kernel, name, operands, pieces, outs, g_shapes, scratch, flops, limit=14, alias=None):
    n_p, n_g = len(pieces), len(g_shapes)
    scal, *rest = operands
    rest = [pltpu.with_memory_space_constraint(v, pltpu.VMEM) for v in rest]
    pieces = [pltpu.with_memory_space_constraint(v, pltpu.HBM) for v in pieces]
    g_shapes = [pltpu.HBM(g.shape, g.dtype) for g in g_shapes]
    return pl.pallas_call(
        kernel,
        name=name,
        out_shape=list(outs) + list(g_shapes),
        in_specs=[SMEM] + [VMEM] * len(rest) + [HBM] * n_p,
        out_specs=[VMEM] * len(outs) + [HBM] * n_g,
        scratch_shapes=scratch,
        compiler_params=pltpu.CompilerParams(vmem_limit_bytes=limit << 20),
        input_output_aliases=alias or {},
        cost_estimate=pl.CostEstimate(flops=flops, bytes_accessed=1 << 20, transcendentals=0),
    )(scal, *rest, *pieces)


def loop(count, fn, after=None):
    def step(i, c):
        fn(i)
        if after is not None:
            after(i)
        return c

    lax.fori_loop(0, count, step, 0)


def send_rows(src, dst, i, size, sem):
    per = dst.shape[1] // size
    pltpu.make_async_copy(src.at[rows_of(i, size), :], dst.at[i // per, rows_of(i % per, size), :], sem).start()


def rows_of(i, size):
    return pl.ds(pl.multiple_of(i * size, size), size)


def project_kernel(load, read, n_w, *refs):
    n_v = 0 if read else 1
    scal, x_ref, cot_ref = refs[:3]
    w_refs = refs[3 + n_v : 3 + n_v + n_w]
    xn, q, k, v, da, w, *rest = refs[3 + n_v + n_w :]
    sem = rest[-1]
    if read:
        vec_ref, b_mlp, buf, vsem = rest[:4]
        steps = read(scal, w_refs, vec_ref, b_mlp, buf, vsem)
        next(steps)
        load(scal, w_refs, w, sem)
        next(steps)
    else:
        vec_ref = refs[3]
        load(scal, w_refs, w, sem)
    tokens = x_ref.shape[0]

    def norm(i):
        r = rows_of(i, 256)
        standard, _ = norm_rows(x_ref[r, :])
        xn[r, :] = (standard * vec_ref[0:1, :]).astype(BF16)

    loop(tokens // 256, norm)

    def ready(i):
        whole_wait(w.at[i], sem.at[i])()

    def each(fn):
        loop(tokens // 512, lambda i: fn(rows_of(i, 512)))

    def queries(r):
        q[r, :] = (dot_nn(xn[r, :], w[0]) + vec_ref[1:2, :]).astype(BF16) * jnp.asarray(0.125, BF16)

    def keys(r):
        k[r, :] = dot_nn(xn[r, :], w[1]).astype(BF16)

    def values(r):
        v[r, :] = (dot_nn(xn[r, :], w[2]) + vec_ref[2:3, :]).astype(BF16)

    def attended(r):
        da[r, :] = dot_nt(cot_ref[r, :], w[3]).astype(BF16)

    for i, fn in enumerate((queries, keys, values, attended)):
        ready(i)
        each(fn)


def project_call(scal, x, cot, vec, weights, load, read=None):
    tokens, width = x.shape
    return call(
        functools.partial(project_kernel, load, read, len(weights)),
        "project",
        (scal, x, cot) if read else (scal, x, cot, vec),
        weights,
        [kept(x.shape)] * 5
        + [kept((4, width, width))]
        + ([kept((8, width), F32), kept((4, width), F32)] if read else []),
        [],
        ([pltpu.VMEM((16, 8, width), BF16), pltpu.SemaphoreType.DMA] if read else [])
        + [pltpu.SemaphoreType.DMA((4,))],
        8 * tokens * width * width,
        limit=10,
    )


def core_kernel(b, scal, q, k, v, da, w, *refs):
    o, d, dn = refs[-3:]
    refs = (q, k, v, da, o, d.at[0], d.at[1], d.at[2])
    whole = scal[8 + b] == 0

    def pair(i):
        cols = pl.ds(pl.multiple_of(i * 128, 128), 128)

        @pl.when(whole)
        def _():
            attend(refs, b * 512, cols, WHOLE)

        @pl.when(jnp.logical_not(whole))
        def _():
            attend(refs, b * 512, cols, SMALL)

    loop(q.shape[1] // 128, pair)

    def back(i):
        r = rows_of(b * 2 + i, 256)
        dn[r, :] = dot_nt(d[0, r, :], w[0]) + dot_nt(d[1, r, :], w[1]) + dot_nt(d[2, r, :], w[2])

    loop(2, back)


def core_call(b, scal, q, k, v, da, w, *before):
    return call(
        functools.partial(core_kernel, b),
        "core",
        (scal, q, k, v, da, w, *before),
        [],
        [kept(q.shape), kept((3, *q.shape)), kept(q.shape, F32)],
        [],
        [],
        10 << 30,
        alias={6 + i: i for i in range(len(before))},
        limit=8,
    )


def attn_grad_kernel(store, scal, xn, o, d, cot, sums, *refs):
    *g_refs, g, sem = refs
    tokens, width = xn.shape

    def grad(b):
        g[b] = dot_tn(xn[...], d[b]).astype(BF16)
        store(scal, g, g_refs, sem, b)

    loop(3, grad)
    g[3] = dot_tn(o[...], cot[...]).astype(BF16)
    store(scal, g, g_refs, sem, 3)
    for i, v in enumerate((d[0], d[2], cot[...])):
        sums[i : i + 1, :] = jnp.sum(v.astype(F32), axis=0, keepdims=True)
    stored(g_refs, sem)


def attn_grad_call(scal, xn, o, d, cot, store, g_shapes):
    tokens, width = xn.shape
    return call(
        functools.partial(attn_grad_kernel, store),
        "attn_grad",
        (scal, xn, o, d, cot),
        [],
        [kept((8, width), F32)],
        g_shapes,
        [pltpu.VMEM((4, width, width), BF16), pltpu.SemaphoreType.DMA((len(g_shapes),))],
        8 * tokens * width * width,
        limit=10,
    )


def gelu_parts(u):
    u2 = u * u
    half = 0.5 * jnp.tanh(u * (GELU_C + (GELU_C * GELU_A) * u2)) + 0.5
    act = u * half
    grad = half + act * (1.0 - half) * (2.0 * GELU_C + (6.0 * GELU_C * GELU_A) * u2)
    return act, grad

def tile_of(t, width):
    return pl.ds(t * width if isinstance(t, int) else pl.multiple_of(t * width, 128), width)


def wait_tile(w, sem, t, width):
    whole_wait(w.at[tile_of(t, width), :], sem.at[t])()


def up_kernel(load, first, count, n_p, *refs):
    scal, xn, bias = refs[:3]
    even, odd, sem = refs[-3:]
    tokens, width = xn.shape
    if n_p:
        act, gp, w = refs[-6:-3]
        load(scal, refs[3 : 3 + n_p], w, sem)
        for t in range(count):
            whole_wait(w.at[t], sem.at[t])()
    else:
        act, gp = refs[-5:-3]
        w = refs[5]
    rows = even.shape[0]
    per = tokens // rows

    def product(i):
        return dot_nn(xn[rows_of(i % per, rows), :], w[first + i // per])

    def finish(i, u):
        t, r = first + i // per, rows_of(i % per, rows)
        a, gr = gelu_parts(u + bias[pl.ds(t, 1), :])
        act[t, r, :] = a.astype(BF16)
        gp[t, r, :] = gr.astype(BF16)

    even[...] = product(0)

    def step(i):
        odd[...] = product(2 * i + 1)
        finish(2 * i, even[...])
        even[...] = product(jnp.minimum(2 * i + 2, count * per - 1))
        finish(2 * i + 1, odd[...])

    loop(count * per // 2, step)
    if n_p:
        for t in range(count, bias.shape[0]):
            whole_wait(w.at[t], sem.at[t])()


def up_call(first, count, scal, xn, bias, before, pieces, load):
    tokens, width = xn.shape
    tiles = bias.shape[0]
    return call(
        functools.partial(up_kernel, load, first, count, len(pieces)),
        "up",
        (scal, xn, bias, *before),
        pieces,
        [kept((tiles, tokens, width))] * 2 + [kept((tiles, width, width))] * (1 if pieces else 0),
        [],
        [pltpu.VMEM((256, width), F32)] * 2 + [pltpu.SemaphoreType.DMA((tiles,))],
        2 * count * tokens * width * width,
        alias={3: 0, 4: 1} if before else None,
        limit=7,
    )


def down_grad_kernel(load, store, n_p, scal, act, cot, *refs):
    w, *g_refs, g, wsem, sem = refs[n_p:]
    tiles, tokens, width = act.shape
    load(scal, refs[:n_p], w, wsem)

    def grad(t):
        g[tile_of(t, width), :] = dot_tn(act[t], cot[...]).astype(BF16)
        store(scal, g, g_refs, sem, t)

    loop(tiles, grad)
    for t in range(tiles):
        wait_tile(w, wsem, t, width)
    stored(g_refs, sem)


def down_grad_call(scal, act, cot, pieces, load, store, g_shapes):
    tiles, tokens, width = act.shape
    return call(
        functools.partial(down_grad_kernel, load, store, len(pieces)),
        "down_grad",
        (scal, act, cot),
        pieces,
        [kept((tiles * width, width))],
        g_shapes,
        [
            pltpu.VMEM((tiles * width, width), BF16),
            pltpu.SemaphoreType.DMA((tiles,)),
            pltpu.SemaphoreType.DMA((len(g_shapes),)),
        ],
        2 * tiles * tokens * width * width,
        limit=12,
    )


def dpre_kernel(scal, cot, gp, w, dpre, sums):
    tiles, tokens, width = gp.shape

    def down(t):
        d = (dot_nt(cot[...], w[tile_of(t, width), :]) * gp[t].astype(F32)).astype(BF16)
        dpre[t] = d
        sums[pl.ds(t, 1), :] = jnp.sum(d.astype(F32), axis=0, keepdims=True)

    loop(tiles, down)


def dpre_call(scal, cot, gp, w):
    tiles, tokens, width = gp.shape
    return call(
        dpre_kernel,
        "dpre",
        (scal, cot, gp, w),
        [],
        [kept(gp.shape), kept((8, width), F32)],
        [],
        [],
        2 * tiles * tokens * width * width,
        alias={2: 0},
        limit=8,
    )


def up_grad_kernel(load, store, n_p, scal, xn, dpre, *refs):
    w, *g_refs, g, wsem, sem = refs[n_p:]
    load(scal, refs[:n_p], w, wsem, (3,))

    def grad(t):
        g[t] = dot_tn(xn[...], dpre[t]).astype(BF16)
        store(scal, g, g_refs, sem, t)

    loop(dpre.shape[0], grad)
    whole_wait(w, wsem.at[3])()
    stored(g_refs, sem)


def up_grad_call(scal, xn, dpre, pieces, load, store, g_shapes):
    tiles, tokens, width = dpre.shape
    return call(
        functools.partial(up_grad_kernel, load, store, len(pieces)),
        "up_grad",
        (scal, xn, dpre),
        pieces,
        [kept((1, width, width))],
        g_shapes,
        [
            pltpu.VMEM((tiles, width, width), BF16),
            pltpu.SemaphoreType.DMA((4,)),
            pltpu.SemaphoreType.DMA((len(g_shapes),)),
        ],
        2 * tiles * tokens * width * width,
        limit=10,
    )


def input_grad_kernel(scal, x, cot, dn, dpre, vec, wu, sums, dx_ref, dx, sem):
    tiles, tokens, width = dpre.shape
    sums[...] = jnp.zeros_like(sums)

    def step(i):
        r = rows_of(i, 256)
        dnr = dn[r, :]
        for t in range(tiles):
            dnr += dot_nt(dpre[t, r, :], wu[t])
        standard, inv = norm_rows(x[r, :])
        sums[0:1, :] += jnp.sum(dnr * standard, axis=0, keepdims=True)
        gs = dnr * vec[0:1, :]
        mean_g = jnp.mean(gs, axis=1, keepdims=True)
        mean_p = jnp.mean(gs * standard, axis=1, keepdims=True)
        dx[r, :] = (cot[r, :].astype(F32) + inv * (gs - mean_g - standard * mean_p)).astype(BF16)

    loop(tokens // 256, step, lambda i: send_rows(dx, dx_ref, i, 256, sem))
    whole_wait(dx_ref, sem)()


def input_grad_call(scal, x, cot, dn, dpre, vec, wu):
    tiles, tokens, width = dpre.shape
    return call(
        input_grad_kernel,
        "input_grad",
        (scal, x, cot, dn, dpre, vec, wu),
        [],
        [kept((8, width), F32)],
        [sds((tokens // 512, 512, width))],
        [pltpu.VMEM((tokens, width), BF16), pltpu.SemaphoreType.DMA],
        2 * (tiles + 3) * tokens * width * width,
        limit=8,
    )


def out_kernel(scal, x, o, act, vec, wo, wd, out_ref, out, sem):
    tiles, tokens, width = act.shape

    def step(i):
        r = rows_of(i, 256)
        total = x[r, :].astype(F32) + vec[3:4, :] + dot_nn(o[r, :], wo[0])
        for t in range(tiles):
            total += dot_nn(act[t, r, :], wd[tile_of(t, width), :])
        out[r, :] = total.astype(BF16)

    loop(tokens // 256, step, lambda i: send_rows(out, out_ref, i, 256, sem))
    whole_wait(out_ref, sem)()


def out_call(scal, x, o, act, vec, wo, wd):
    tiles, tokens, width = act.shape
    (out,) = call(
        out_kernel,
        "out",
        (scal, x, o, act, vec, wo, wd),
        [],
        [],
        [sds((tokens // 512, 512, width))],
        [pltpu.VMEM((tokens, width), BF16), pltpu.SemaphoreType.DMA],
        2 * (tiles + 1) * tokens * width * width,
        limit=8,
    )
    return out


def swap(value, mask):
    return lax.ppermute(value, "wide", [(i, i ^ mask) for i in range(16)])


def swap_y(value):
    return lax.ppermute(value, "narrow", [(0, 1), (1, 0)])


def slots():
    for part in range(2):
        for i in range(2):
            for s in range(2):
                half, side = (i, s) if part == 0 else (s, i)
                for k in range(4):
                    yield part, i, s * 4 + k, half, side, k


def device_of(scal, k, side, core):
    return ((scal[1] ^ k) * 2 + (scal[2] ^ side)) * 2 + (scal[3] ^ core)


def behind(value, *marks):
    return lax.optimization_barrier((value, marks))[0]


def gather_z(value):
    return [swap(value, k << 2) for k in (1, 2, 3)]


def gather_first(za, zb):
    return swap(za, 2), swap_y(zb), swap_y(za), swap(zb, 2)


def gather_second(xa, yb):
    return swap_y(xa), swap(yb, 2)


def pieces_of(za, zb, first, second):
    xa, yb, ya, xb = first
    return [za, xa, ya, second[0], zb, xb, yb, second[1]]


def join_job(values):
    def fn(held, near, outs):
        size = near[0].shape[0]
        for i, v in enumerate(near):
            at = slice(i * size, (i + 1) * size)
            if v.ndim == 3:
                outs[0][at, : v.shape[1], :] = v[...]
            else:
                outs[0][at] = v[...]

    return fn, [], values, [kept((len(values) * values[0].shape[0], *values[0].shape[1:]))]


def mix(name, jobs):
    held = [v for job in jobs for v in job[1]]
    near = [v for job in jobs for v in job[2]]
    outs = [o for job in jobs for o in job[3]]

    def kernel(*refs):
        at = len(near) + len(held)
        scratch = refs[at + len(outs) :]
        copies = [
            pltpu.make_async_copy(refs[len(near) + i].at[:, pl.ds(v[1], v[2])], scratch[i], scratch[-1].at[i])
            for i, v in enumerate(held)
        ]
        for cp in copies:
            cp.start()
        h = n = o = 0
        for fn, job_h, job_n, job_o in jobs:
            for i in range(len(job_h)):
                copies[h + i].wait()
            fn(
                scratch[h : h + len(job_h)],
                refs[n : n + len(job_n)],
                refs[at + o : at + o + len(job_o)],
            )
            h, n, o = h + len(job_h), n + len(job_n), o + len(job_o)

    got = pl.pallas_call(
        kernel,
        name=name,
        out_shape=outs,
        in_specs=[VMEM] * len(near) + [HBM] * len(held),
        out_specs=[VMEM] * len(outs),
        scratch_shapes=[pltpu.VMEM((v.shape[0], size, *v.shape[2:]), v.dtype) for v, _, size in held]
        + [pltpu.SemaphoreType.DMA((max(len(held), 1),))],
        compiler_params=pltpu.CompilerParams(vmem_limit_bytes=8 << 20),
        cost_estimate=pl.CostEstimate(flops=1 << 20, bytes_accessed=1 << 20, transcendentals=0),
    )(
        *[pltpu.with_memory_space_constraint(v, pltpu.VMEM) for v in near],
        *[pltpu.with_memory_space_constraint(v[0], pltpu.HBM) for v in held],
    )
    split, at = [], 0
    for job in jobs:
        split.append(got[at : at + len(job[3])])
        at += len(job[3])
    return split


def total(*parts):
    return sum(v.astype(F32) for v in parts)


def stack_job(values):
    def fn(held, near, outs):
        for k, v in enumerate(near):
            for i in range(2):
                outs[i][k] = v[i]

    return fn, [], list(values), [kept((len(values), *values[0].shape[1:]))] * 2


def vector_job(sums_a, sums_d, sums_x, wide, rows):
    width = sums_a.shape[1]

    def spread(rows_in, per):
        flat = jnp.concatenate([rows_in[w * per // width][None] for w in range(wide)])
        col = lax.broadcasted_iota(jnp.int32, (wide, width), 1)
        own = lax.broadcasted_iota(jnp.int32, (wide, width), 0) * per % width
        flat = jnp.where((col >= own) & (col < own + per), flat, 0.0)
        pick = lax.broadcasted_iota(jnp.int32, (width, per), 0) % per
        pick = (pick == lax.broadcasted_iota(jnp.int32, (width, per), 1)).astype(BF16)
        got = jnp.zeros((wide, per), F32)
        for _ in range(3):
            high = flat.astype(BF16)
            flat = flat - high.astype(F32)
            got += dot_nn(high, pick)
        return got

    def fn(held, near, outs):
        a, d, x, scal = near
        tiles = 4
        at = 0
        for got in (
            spread([x[0]], rows),
            spread([a[0], a[1]], 2 * rows),
            spread([d[t] for t in range(tiles)], tiles * rows),
            spread([a[2]], rows),
        ):
            outs[4][:, at : at + got.shape[1]] = got
            at += got.shape[1]
        for k in range(4):
            outs[k][...] = jnp.zeros_like(outs[k])
            for r in range(4):
                outs[k][r : r + 1, :] = outs[4][pl.ds((scal[1] ^ k) * 4 + r, 1), :]

    return fn, [], [sums_a, sums_d, sums_x], [kept((8, 8 * rows), F32)] * 4 + [kept((wide, 8 * rows), F32)]


def add_job(values):
    def fn(held, near, outs):
        outs[0][...] = sum(near[i][...] for i in range(len(values)))

    return fn, [], list(values), [kept(values[0].shape, F32)]


def vector_job(sums_a, sums_d, sums_x):
    def fn(held, near, outs):
        a, d, x = near
        outs[0][0:1, :] = x[0:1, :]
        outs[0][1:3, :] = a[0:2, :]
        outs[0][3:7, :] = d[0:4, :]
        outs[0][7:8, :] = a[2:3, :]

    return fn, [], [sums_a, sums_d, sums_x], [kept(sums_a.shape, F32)]


def sum1_job(keep1, got1):
    def fn(held, near, outs):
        for i in range(2):
            outs[i][...] = total(held[0][i], near[0][i]).astype(BF16)

    return fn, [(keep1, 0, keep1.shape[1])], [got1], [kept(keep1.shape[1:])] * 2


def sum2_job(keep0, got0, got):
    half = keep0.shape[1] // 2

    def fn(held, near, outs):
        for i in range(2):
            outs[i][...] = total(held[0][i], near[0][i, half:], near[1 + i][half:]).astype(BF16)

    return fn, [(keep0, half, half)], [got0, *got], [kept((half, *keep0.shape[2:]))] * 2


def sum3_job(keep0, got0, got, got2):
    half = keep0.shape[1] // 2

    def fn(held, near, outs):
        for k in range(half):
            for i in range(2):
                outs[k][i] = total(held[0][i, k], near[0][i, k], near[1 + i][k], near[3 + i][k]).astype(BF16)

    return fn, [(keep0, 0, half)], [got0, *got, *got2], [kept((2, *keep0.shape[2:]))] * half


def sum4_job(own, got):
    def fn(held, near, outs):
        outs[0][...] = total(*[near[i][...] for i in range(1 + len(got))]).astype(BF16)

    return fn, [], [own, *got], [kept(own.shape)]


def place_kernel(scal, a_mine, a_other, d_mine, d_other, joined_ref, out, down, joined, sem):
    _, rows, width = a_mine.shape

    def place(half, a, d):
        for p in range(2):
            block = half * 2 + p
            down[pl.ds(block * rows, rows), :] = d[p].astype(F32)
            if block < 3:
                joined[block] = a[p].astype(F32)
                dst = joined_ref.at[:, block * width : (block + 1) * width]
                pltpu.make_async_copy(joined.at[block], dst, sem).start()
            else:
                out[...] = a[p].astype(F32)

    @pl.when(scal[0] == 0)
    def _():
        place(0, a_mine, d_mine)
        place(1, a_other, d_other)

    @pl.when(scal[0] != 0)
    def _():
        place(1, a_mine, d_mine)
        place(0, a_other, d_other)

    whole_wait(joined, sem)()


def place_call(scal, parts):
    _, rows, width = parts[0].shape
    return pl.pallas_call(
        place_kernel,
        name="place",
        out_shape=[sds((rows, 7 * width), F32), sds((rows, width), F32), sds((4 * rows, width), F32)],
        in_specs=[SMEM] + [VMEM] * 4,
        out_specs=[HBM, VMEM, VMEM],
        scratch_shapes=[pltpu.VMEM((3, rows, width), F32), pltpu.SemaphoreType.DMA],
        compiler_params=pltpu.CompilerParams(vmem_limit_bytes=8 << 20),
    )(scal, *[pltpu.with_memory_space_constraint(v, pltpu.VMEM) for v in parts])


def place_last_kernel(scal, placed, mine, other, joined_ref, wide, sem):
    _, rows, width = other.shape
    for i, ref in enumerate((mine, other)):
        for p in range(2):
            wide[i * 2 + p] = ref[p].astype(F32)
            at = pl.multiple_of((3 + (scal[0] ^ i) * 2 + p) * width, 128)
            pltpu.make_async_copy(wide.at[i * 2 + p], joined_ref.at[:, pl.ds(at, width)], sem).start()
    whole_wait(wide, sem)()


def place_last_call(scal, placed, mine, other):
    return pl.pallas_call(
        place_last_kernel,
        name="place_last",
        out_shape=sds(placed.shape, F32),
        in_specs=[SMEM, HBM, VMEM, VMEM],
        out_specs=HBM,
        scratch_shapes=[pltpu.VMEM((4, *other.shape[1:]), F32), pltpu.SemaphoreType.DMA],
        compiler_params=pltpu.CompilerParams(vmem_limit_bytes=8 << 20),
        input_output_aliases={1: 0},
    )(scal, placed, *[pltpu.with_memory_space_constraint(v, pltpu.VMEM) for v in (mine, other)])


def whole_wait(ref, sem):
    return pltpu.make_async_copy(ref, ref, sem).wait


def piece(refs, at, core, k, alone):
    if core == 0:
        return refs[at].at[k]
    if at in alone:
        return refs[9 + alone.index(at)].at[k]
    return refs[8].at[(at - sum(i < at for i in alone)) * 4 + k]


def load_columns(scal, refs, w, sem, blocks=(0, 1, 2, 3)):
    rows = w.shape[1] // 16

    def start(own):
        for block in blocks:
            for core in range(2):
                for part, _, _, half, side, k in slots():
                    if (own ^ half) * 2 + part != block:
                        continue
                    src = piece(refs, part * 4 + half * 2 + side, core, k, (3, 7)).at[pl.ds(0, rows), :]
                    dst = w.at[blocks.index(block), rows_at(device_of(scal, k, side, core) * rows, rows), :]
                    pltpu.make_async_copy(src, dst, sem.at[block]).start()

    @pl.when(scal[0] == 0)
    def _():
        start(0)

    @pl.when(scal[0] != 0)
    def _():
        start(1)


def load_half(which):
    def load(scal, refs, w, sem):
        def start(rel):
            for core in range(2):
                for part, _, _, half, side, k in slots():
                    if half != rel:
                        continue
                    src = piece(refs, part * 4 + half * 2 + side, core, k, (0, 4))
                    per, rows, width = src.shape
                    dev = device_of(scal, k, side, core)
                    for b in range(per):
                        block = part * per + b
                        if which == 0:
                            dst, tile = w.at[block, rows_at(dev * rows, rows), :], block
                        else:
                            dst, tile = w.at[rows_at((dev * 2 * per + block) * rows, rows), :], scal[1] ^ k
                        pltpu.make_async_copy(src.at[b], dst, sem.at[tile]).start()

        @pl.when(scal[0] == which)
        def _():
            start(0)

        @pl.when(scal[0] != which)
        def _():
            start(1)

    return load


def read_vectors(scal, refs, vec, b_mlp, buf, sem):
    width = vec.shape[1]
    rows = width // 16
    for core in range(2):
        for side in range(2):
            for k in range(4):
                src = piece(refs, side, core, k, (3, 7)).at[pl.ds(rows, 8), :]
                pltpu.make_async_copy(src, buf.at[device_of(scal, k, side, core)], sem).start()
    yield
    whole_wait(buf, sem)()
    values = buf[:, 0, :].astype(F32)
    devices = values.shape[0]

    def line(at, per):
        pick = lax.broadcasted_iota(jnp.int32, (per, width), 1) % per
        pick = (pick == lax.broadcasted_iota(jnp.int32, (per, width), 0)).astype(BF16)
        flat = dot_nn(values[:, at : at + per].astype(BF16), pick)
        dev = lax.broadcasted_iota(jnp.int32, flat.shape, 0)
        col = lax.broadcasted_iota(jnp.int32, flat.shape, 1)
        count = devices * per // width
        share = devices // count
        keep = col // per == dev % share
        return [
            jnp.sum(jnp.where(keep & (dev // share == i), flat, 0.0), axis=0, keepdims=True) for i in range(count)
        ]

    lines = line(0, rows) + line(rows, 2 * rows) + line(7 * rows, rows)
    vec[...] = jnp.zeros_like(vec)
    for i, v in enumerate(lines):
        vec[i : i + 1, :] = v
    for i, v in enumerate(line(3 * rows, 4 * rows)):
        b_mlp[i : i + 1, :] = v
    yield


def rows_at(base, rows):
    return pl.ds(pl.multiple_of(base, 16), rows)


def stored(refs, sem):
    for i, r in enumerate(refs):
        whole_wait(r, sem.at[i])()


def store_block(scal, g, refs, sem, t):
    half, part = scal[0] ^ (t // 2), t % 2
    rows = refs[0].shape[2]

    def send(at, core, side, k, slot, p):
        src = g.at[t, rows_at(device_of(scal, k, side, core) * rows, rows), :]
        pltpu.make_async_copy(src, refs[at].at[p, slot], sem.at[at]).start()

    for i in range(2):

        @pl.when((part == 0) & (half == i))
        def _(i=i):
            for core in range(2):
                for side in range(2):
                    for k in range(4):
                        send(core * 2 + i, core, side, k, side * 4 + k, 0)

    @pl.when(part == 1)
    def _():
        for core in range(2):
            for side in range(2):
                for k in range(4):
                    send(core * 2 + side, core, side, k, half * 4 + k, 1)


def store_rows(scal, g, refs, sem, t):
    k = scal[1] ^ t
    rows = refs[0].shape[2]
    for core in range(2):
        for side in range(2):
            dev = (t * 2 + (scal[2] ^ side)) * 2 + (scal[3] ^ core)
            for half in range(2):
                for part in range(2):
                    i, s = (half, side) if part == 0 else (side, half)
                    at = core * 2 + i
                    src = g.at[rows_at((dev * 4 + (scal[0] ^ half) * 2 + part) * rows, rows), :]
                    pltpu.make_async_copy(src, refs[at].at[part, s * 4 + k], sem.at[at]).start()


def load_whole_blocks(scal, refs, w, sem, blocks=(0, 1, 2, 3)):
    for i, b in enumerate(blocks):
        pltpu.make_async_copy(refs[b], w.at[i], sem.at[b]).start()


def load_whole_rows(scal, refs, w, sem):
    width = w.shape[1]
    for t in range(w.shape[0] // width):
        r = tile_of(t, width)
        pltpu.make_async_copy(refs[0].at[r, :], w.at[r, :], sem.at[t]).start()


def store_whole_blocks(scal, g, refs, sem, t):
    for i, r in enumerate(refs):

        @pl.when(t == i)
        def _(i=i, r=r):
            pltpu.make_async_copy(g.at[i], r, sem.at[i]).start()


def store_whole_rows(scal, g, refs, sem, t):
    r = tile_of(t, g.shape[1])
    pltpu.make_async_copy(g.at[r, :], refs[0].at[r, :], sem.at[0]).start()


def body(sizes, tokens, image_ids, cotangent, w_joined, w_out, w_mlp, norm_gain, bias_attn, bias_mlp, bias_out):
    micro, length, width = tokens.shape
    narrow, wide = sizes
    paired = narrow == 2 and wide == 16
    rows = width // wide
    tiles = w_mlp.shape[0] // rows
    x = tokens.reshape(micro * length, width)
    cot = cotangent.reshape(micro * length, width)
    n = lax.axis_index("narrow")
    w = lax.axis_index("wide")
    last = image_ids.reshape(-1, 512)[:, -1]
    scal = [n, w >> 2, (w >> 1) & 1, w & 1] + [jnp.int32(0)] * 4 + [last[b] for b in range(last.shape[0])]
    scal = jnp.stack([jnp.asarray(s, jnp.int32) for s in scal])
    vec_own = jnp.concatenate([norm_gain, bias_attn, bias_mlp, bias_out])

    def vectors(vec):
        vec = vec.astype(F32)
        b_at = 3 * rows
        b_mlp = vec[:, b_at : b_at + tiles * rows].reshape(tiles, width)
        head = [
            vec[:, :rows].reshape(1, width),
            vec[:, rows:b_at].reshape(2, width),
            vec[:, b_at + tiles * rows :].reshape(1, width),
            jnp.zeros((4, width), F32),
        ]
        return jnp.concatenate(head), b_mlp

    def vector_grads(sums_a, sums_d, sums_x):
        return jnp.concatenate(
            [
                sums_x[0].reshape(wide, rows),
                sums_a[:2].reshape(wide, 2 * rows),
                sums_d[:tiles].reshape(wide, tiles * rows),
                sums_a[2].reshape(wide, rows),
            ],
            axis=1,
        )

    if not paired:
        full = lax.all_gather(w_joined, "wide", axis=0, tiled=True)
        parts = [full[:, i * width : (i + 1) * width] for i in range(3 + tiles)]
        attn_w = parts[:3] + [lax.all_gather(w_out, "wide", axis=0, tiled=True)]
        up_w = parts[3:]
        down_w = [lax.all_gather(w_mlp, "wide", axis=0, tiled=True)]
        vec, b_mlp = vectors(lax.all_gather(vec_own, "wide", axis=0))
        square = [sds((width, width))]
        xn, q, k, v, da, wa = project_call(scal, x, cot, vec, attn_w, load_whole_blocks)
        part = core_call(0, scal, q, k, v, da, wa)
        for b in range(1, last.shape[0]):
            part = core_call(b, scal, q, k, v, da, wa, *part)
        o, d, dn = part
        sums_a, *g_attn = attn_grad_call(scal, xn, o, d, cot, store_whole_blocks, square * 4)
        act, gp, wu = up_call(0, tiles // 2, scal, xn, b_mlp, (), up_w, load_whole_blocks)
        act, gp = up_call(tiles // 2, tiles - tiles // 2, scal, xn, b_mlp, (act, gp, wu), [], None)
        wd, *g_down = down_grad_call(
            scal, act, cot, down_w, load_whole_rows, store_whole_rows, [sds((tiles * width, width))]
        )
        dpre, sums_d = dpre_call(scal, cot, gp, wd)
        wo, *g_up = up_grad_call(scal, xn, dpre, attn_w, load_whole_blocks, store_whole_blocks, square * tiles)
        sums_x, d_x = input_grad_call(scal, x, cot, dn, dpre, vec, wu)
        out = out_call(scal, x, o, act, vec, wo, wd)

        def reduce(g):
            g = lax.psum_scatter(g.astype(F32), "wide", scatter_dimension=0, tiled=True)
            return lax.psum(g, "narrow")

        grad_joined = reduce(jnp.concatenate([*g_attn[:3], *g_up], axis=1))
        grad_out = reduce(g_attn[3])
        grad_mlp = reduce(g_down[0])
        vg = reduce(vector_grads(sums_a, sums_d, sums_x))[0]
        vg = jnp.split(vg, [rows, 3 * rows, (3 + tiles) * rows])
    else:
        col = lambda i: w_joined[:, i * width : (i + 1) * width]
        pair = lambda f: jnp.stack([jnp.where(n == 0, f(0), f(2)), jnp.where(n == 0, f(1), f(3))])
        half_a, half_b = [jnp.where(n == 0, f, g) for f, g in ((col(0), col(2)), (col(1), w_out))]
        v_rows = jnp.pad(vec_own, (0, width - vec_own.shape[0]))
        half = jnp.concatenate([half_a, jnp.broadcast_to(v_rows, (8, width)), half_b])
        got = gather_z(half)
        za = jnp.stack([t[: rows + 8] for t in (half, *got)])
        zb = jnp.stack([t[rows + 8 :] for t in (half, *got)])
        c_half = jnp.stack([jnp.where(n == 0, col(3 + t), w_mlp[t * rows : (t + 1) * rows]) for t in range(tiles)])
        c_half = behind(c_half.reshape(2, tiles // 2, rows, width), za, zb)
        first = gather_first(za, zb)
        c2 = swap(c_half, 8)
        first, c2, c_half = lax.optimization_barrier((first, c2, c_half))
        second = gather_second(*first[:2])
        own = pieces_of(za, zb, first, second)
        ((joined,),) = mix("join_a", [join_job([own[i] for i in (0, 1, 2, 4, 5, 6)])])
        joined, c1, c3 = swap(joined, 1), swap(c_half, 4), swap(c_half, 12)
        second, joined, c1, c3 = lax.optimization_barrier((second, joined, c1, c3))
        own = pieces_of(za, zb, first, second)
        attn_w = [*own, joined, swap(second[0], 1), swap(second[1], 1)]
        cza, czb = [jnp.stack([t[i] for t in (c_half, c1, c2, c3)]) for i in range(2)]
        x_p, attn_w, cza, czb = lax.optimization_barrier((x, attn_w, cza, czb))
        c_first = gather_first(cza, czb)
        xn, q, k, v, da, wa, vec, b_mlp = project_call(scal, x_p, cot, None, attn_w, load_columns, read_vectors)
        part = core_call(0, scal, q, k, v, da, wa)

        part, c_first = lax.optimization_barrier((part, c_first))
        c_second = gather_second(*c_first[:2])
        czs = [swap(cza, 1), swap(czb, 1)]
        o, d, dn = core_call(1, scal, q, k, v, da, wa, *part)

        d, c_second, czs = lax.optimization_barrier((d, c_second, czs))
        c_own = pieces_of(cza, czb, c_first, c_second)
        ((c_joined,),) = mix("join_c", [join_job([t for t in c_own if t is not cza and t is not czb])])
        d, c_joined = lax.optimization_barrier((d, c_joined))
        c_other = swap(c_joined, 1)
        attn_shapes = [sds((2, 8, rows, width))] * 4
        sums_a, *ga = attn_grad_call(scal, xn, o, d, cot, store_block, attn_shapes)

        c_other, ga = behind((c_other, ga), sums_a)
        xn_u, ga, c_own, c_other = lax.optimization_barrier((xn, ga, c_own, c_other))
        a_got1, a_got0 = swap(ga[3], 1), swap(ga[2], 1)
        half_tiles = tiles // 2
        c_all = [*c_own, c_other, *czs]
        act, gp, wu = up_call(0, half_tiles, scal, xn_u, b_mlp, (), c_all, load_half(0))

        a_got1, a_got0 = behind((a_got1, a_got0), gp)
        ((sa, sb),) = mix("sums_1", [sum1_job(ga[1], a_got1)])
        act, sa, sb = lax.optimization_barrier((act, sa, sb))
        a_xy = swap_y(sa), swap(sb, 2)
        act, gp = up_call(half_tiles, half_tiles, scal, xn_u, b_mlp, (act, gp, wu), [], None)
        wd, *gd = down_grad_call(
            scal, act, cot, c_all, load_half(1), store_rows, attn_shapes
        )

        a_xy = behind(a_xy, gd)
        ((sa, sb),) = mix("sums_2", [sum2_job(ga[0], a_got0, a_xy)])
        gp, sa, sb, gd = lax.optimization_barrier((gp, sa, sb, gd))
        a_yx = swap(sa, 2), swap_y(sb)
        d_got1, d_got0 = swap(gd[3], 1), swap(gd[2], 1)
        dpre, sums_d = dpre_call(scal, cot, gp, wd)

        a_yx, d_got1, d_got0 = behind((a_yx, d_got1, d_got0), dpre)
        a_t, (sa, sb) = mix("sums_3", [sum3_job(ga[0], a_got0, a_xy, a_yx), sum1_job(gd[1], d_got1)])
        dpre_g, a_t, sa, sb = lax.optimization_barrier((dpre, a_t, sa, sb))
        d_xy = swap_y(sa), swap(sb, 2)
        a_z = [swap(a_t[k], k << 2) for k in (1, 2, 3)]
        wo, *gu = up_grad_call(scal, xn, dpre_g, attn_w, load_columns, store_block, attn_shapes)

        a_z, d_xy = behind((a_z, d_xy), gu)
        (a_sum,), (sa, sb) = mix("sums_4", [sum4_job(a_t[0], a_z), sum2_job(gd[0], d_got0, d_xy)])
        x_i, sa, sb, gu, a_sum = lax.optimization_barrier((x, sa, sb, gu, a_sum))
        u_got1, u_got0 = swap(gu[3], 1), swap(gu[2], 1)
        d_yx = swap(sa, 2), swap_y(sb)
        a_other = swap_y(a_sum)
        sums_x, d_x = input_grad_call(scal, x_i, cot, dn, dpre, vec, wu)

        d_yx, u_got1, u_got0, a_other = behind((d_yx, u_got1, u_got0, a_other), d_x)
        (sa, sb), d_t, (v_own,) = mix(
            "sums_5",
            [
                sum1_job(gu[1], u_got1),
                sum3_job(gd[0], d_got0, d_xy, d_yx),
                vector_job(sums_a, sums_d, sums_x),
            ],
        )
        x_o, sa, sb, d_t = lax.optimization_barrier((x, sa, sb, d_t))
        u_xy = swap_y(sa), swap(sb, 2)
        d_z = [swap(d_t[k], k << 2) for k in (1, 2, 3)]
        out = out_call(scal, x_o, o, act, vec, wo, wd)

        u_xy, d_z, v_own = behind((u_xy, d_z, v_own), out)
        (sa, sb), (d_sum,) = mix("sums_6", [sum2_job(gu[0], u_got0, u_xy), sum4_job(d_t[0], d_z)])
        sa, sb, d_sum, v_own = lax.optimization_barrier((sa, sb, d_sum, v_own))
        u_yx = swap(sa, 2), swap_y(sb)
        v_got = [swap(v_own, k << 2) for k in (1, 2, 3)]
        u_t, (v_sum,) = mix("sums_7", [sum3_job(gu[0], u_got0, u_xy, u_yx), add_job([v_own, *v_got])])
        u_t, v_sum, d_sum = lax.optimization_barrier((u_t, v_sum, d_sum))
        u_z = [swap(u_t[k], k << 2) for k in (1, 2, 3)]
        v_other, d_other = swap_y(v_sum), swap_y(d_sum)
        placed, grad_out, grad_mlp = place_call(scal, [a_sum, a_other, d_sum, d_other])
        u_z, placed = lax.optimization_barrier((u_z, placed))
        (u_sum,), (v_sum,) = mix("sums_8", [sum4_job(u_t[0], u_z), add_job([v_sum, v_other])])
        u_other = swap_y(u_sum)
        vg = sum([v_sum, *[swap(v_sum, i) for i in (1, 2, 3)]])
        own = lambda v, per: lax.dynamic_slice(v.reshape(-1), (w * per,), (per,))
        vg = [own(vg[0], rows), own(vg[1:3], 2 * rows), own(vg[3:7], tiles * rows), own(vg[7], rows)]
        grad_joined = place_last_call(scal, placed, u_sum, u_other)
    return (out.reshape(tokens.shape), d_x.reshape(tokens.shape), grad_joined, grad_out, grad_mlp, *vg)


def solution(mesh):
    sizes = (mesh.shape["narrow"], mesh.shape["wide"])
    rows = P(None, ("narrow", "wide"), None)
    placed = (rows, P(None, ("narrow", "wide")), rows) + (P("wide", None),) * 3 + (P("wide"),) * 4
    return jax.shard_map(
        functools.partial(body, sizes),
        mesh=mesh,
        in_specs=placed,
        out_specs=(rows, rows) + (P("wide", None),) * 3 + (P("wide"),) * 4,
        check_vma=False,
    )
```

```python
import functools

import jax
import jax.numpy as jnp
from jax import lax
from jax.experimental import pallas as pl
from jax.experimental.pallas import tpu as pltpu
from jax.sharding import PartitionSpec as P

HEADS = 12
HEAD = 64
IMG = 196
EPS = 1e-06
GELU_C = 0.7978845608028654
GELU_A = 0.044715

F32 = jnp.float32
BF16 = jnp.bfloat16
HBM = pl.BlockSpec(memory_space=pltpu.HBM)
VMEM = pl.BlockSpec(memory_space=pltpu.VMEM)
SMEM = pl.BlockSpec(memory_space=pltpu.SMEM)


def dot_nn(a, b):
    return lax.dot_general(a, b, (((1,), (0,)), ((), ())), preferred_element_type=F32)


def dot_nt(a, b):
    return lax.dot_general(a, b, (((1,), (1,)), ((), ())), preferred_element_type=F32)


def dot_tn(a, b):
    return lax.dot_general(a, b, (((0,), (0,)), ((), ())), preferred_element_type=F32)


def norm_rows(rows):
    rows = rows.astype(F32)
    mean = jnp.mean(rows, axis=1, keepdims=True)
    centered = rows - mean
    inv = lax.rsqrt(jnp.mean(centered * centered, axis=1, keepdims=True) + EPS)
    return centered * inv, inv


def attend(refs, base, cols, windows):
    q_ref, k_ref, v_ref, da_ref, o_ref, dq_ref, dk_ref, dv_ref = refs
    zero = jnp.zeros((), BF16)
    jobs, ends = [], {}
    for start, rows, lo, hi, merge in windows:
        win = pl.ds(pl.multiple_of(base + start, 16), rows)
        tiles = [r[win, cols] for r in (q_ref, k_ref, v_ref, da_ref)]
        lane = lax.broadcasted_iota(jnp.int32, (rows, 128), 1)
        sums = {}
        step = 256 if rows == 512 else rows
        for at in range(0, rows, step):
            for h in range(2):
                keep = (lane < 64) if h == 0 else (lane >= 64)
                heads = [jnp.where(keep, t, zero) for t in tiles]
                jobs.append([tiles, heads, rows, lo, hi, at, step, sums])
        ends[len(jobs) - 1] = (start, rows, merge, sums)

    def products(job):
        tiles, heads, _, _, _, at, step, _ = job
        qs = slice(at, at + step)
        job += [dot_nt(tiles[1], heads[0][qs]), dot_nt(tiles[2], heads[3][qs])]

    def soften(job):
        _, _, rows, lo, hi, at, step, _, s, dp = job
        masked = lo > 0 or hi < rows
        if masked:
            key = lax.broadcasted_iota(jnp.int32, (rows, step), 0)
            s = jnp.where((key >= lo) & (key < hi), s, -1e30)
        e = jnp.exp(s - jnp.max(s, axis=0, keepdims=True))
        scale = 1.0 / jnp.sum(e, axis=0, keepdims=True)
        if masked:
            query = lax.broadcasted_iota(jnp.int32, (1, step), 1) + at
            scale = jnp.where((query >= lo) & (query < hi), scale, 0.0)
        p = e * scale
        inner = jnp.sum(p * dp, axis=0, keepdims=True)
        job[8:] = [p.astype(BF16), (p * (dp - inner)).astype(BF16)]

    def gather(job):
        _, heads, _, _, _, at, step, sums, p, ds = job
        qs = slice(at, at + step)
        parts = (
            (("o", at), dot_tn(p, heads[2])),
            (("q", at), dot_tn(ds, heads[1])),
            (("v", 0), dot_nn(p, heads[3][qs])),
            (("k", 0), dot_nn(ds, heads[0][qs])),
        )
        for key, val in parts:
            sums[key] = sums[key] + val if key in sums else val

    def write(start, rows, merge, sums):
        for name, ref in (("o", o_ref), ("q", dq_ref), ("k", dk_ref), ("v", dv_ref)):
            for (n, at), val in sums.items():
                if n != name:
                    continue
                val = (val * 0.125 if n == "q" else val).astype(BF16)
                size = val.shape[0]
                if merge and at == 0:
                    head = pl.ds(pl.multiple_of(base + start, 16), merge)
                    ref[head, cols] = ref[head, cols] + val[:merge]
                    val, at, size = val[merge:], merge, size - merge
                ref[pl.ds(pl.multiple_of(base + start + at, 16), size), cols] = val

    for i in range(len(jobs) + 2):
        if i < len(jobs):
            products(jobs[i])
        if 0 <= i - 1 < len(jobs):
            soften(jobs[i - 1])
        if 0 <= i - 2:
            gather(jobs[i - 2])
            if i - 2 in ends:
                write(*ends[i - 2])


WHOLE = ((0, 512, 0, 512, 0),)
SMALL = (
    (0, 208, 0, IMG, 0),
    (192, 208, IMG - 192, 2 * IMG - 192, 16),
    (384, 128, 2 * IMG - 384, 128, 16),
)


def sds(shape, dtype=BF16):
    return jax.ShapeDtypeStruct(shape, dtype)


def kept(shape, dtype=BF16):
    return pltpu.VMEM(shape, dtype)


def call(kernel, name, operands, pieces, outs, g_shapes, scratch, flops, limit=14, alias=None):
    n_p, n_g = len(pieces), len(g_shapes)
    scal, *rest = operands
    rest = [pltpu.with_memory_space_constraint(v, pltpu.VMEM) for v in rest]
    pieces = [pltpu.with_memory_space_constraint(v, pltpu.HBM) for v in pieces]
    g_shapes = [pltpu.HBM(g.shape, g.dtype) for g in g_shapes]
    return pl.pallas_call(
        kernel,
        name=name,
        out_shape=list(outs) + list(g_shapes),
        in_specs=[SMEM] + [VMEM] * len(rest) + [HBM] * n_p,
        out_specs=[VMEM] * len(outs) + [HBM] * n_g,
        scratch_shapes=scratch,
        compiler_params=pltpu.CompilerParams(vmem_limit_bytes=limit << 20),
        input_output_aliases=alias or {},
        cost_estimate=pl.CostEstimate(flops=flops, bytes_accessed=1 << 20, transcendentals=0),
    )(scal, *rest, *pieces)


def loop(count, fn, after=None):
    def step(i, c):
        fn(i)
        if after is not None:
            after(i)
        return c

    lax.fori_loop(0, count, step, 0)


def send_rows(src, dst, i, size, sem):
    per = dst.shape[1] // size
    pltpu.make_async_copy(src.at[rows_of(i, size), :], dst.at[i // per, rows_of(i % per, size), :], sem).start()


def rows_of(i, size):
    return pl.ds(pl.multiple_of(i * size, size), size)


def project_kernel(load, read, n_w, *refs):
    n_v = 0 if read else 1
    scal, x_ref, cot_ref = refs[:3]
    w_refs = refs[3 + n_v : 3 + n_v + n_w]
    xn, q, k, v, da, w, *rest = refs[3 + n_v + n_w :]
    sem = rest[-1]
    if read:
        vec_ref, b_mlp, buf, vsem = rest[:4]
        steps = read(scal, w_refs, vec_ref, b_mlp, buf, vsem)
        next(steps)
        load(scal, w_refs, w, sem)
        next(steps)
    else:
        vec_ref = refs[3]
        load(scal, w_refs, w, sem)
    tokens = x_ref.shape[0]

    def norm(i):
        r = rows_of(i, 256)
        standard, _ = norm_rows(x_ref[r, :])
        xn[r, :] = (standard * vec_ref[0:1, :]).astype(BF16)

    loop(tokens // 256, norm)

    def ready(i):
        whole_wait(w.at[i], sem.at[i])()

    def each(fn):
        loop(tokens // 512, lambda i: fn(rows_of(i, 512)))

    def queries(r):
        q[r, :] = (dot_nn(xn[r, :], w[0]) + vec_ref[1:2, :]).astype(BF16) * jnp.asarray(0.125, BF16)

    def keys(r):
        k[r, :] = dot_nn(xn[r, :], w[1]).astype(BF16)

    def values(r):
        v[r, :] = (dot_nn(xn[r, :], w[2]) + vec_ref[2:3, :]).astype(BF16)

    def attended(r):
        da[r, :] = dot_nt(cot_ref[r, :], w[3]).astype(BF16)

    for i, fn in enumerate((queries, keys, values, attended)):
        ready(i)
        each(fn)


def project_call(scal, x, cot, vec, weights, load, read=None):
    tokens, width = x.shape
    return call(
        functools.partial(project_kernel, load, read, len(weights)),
        "project",
        (scal, x, cot) if read else (scal, x, cot, vec),
        weights,
        [kept(x.shape)] * 5
        + [kept((4, width, width))]
        + ([kept((8, width), F32), kept((4, width), F32)] if read else []),
        [],
        ([pltpu.VMEM((16, 8, width), BF16), pltpu.SemaphoreType.DMA] if read else [])
        + [pltpu.SemaphoreType.DMA((4,))],
        8 * tokens * width * width,
        limit=10,
    )


def core_kernel(b, scal, q, k, v, da, w, *refs):
    o, d, dn = refs[-3:]
    refs = (q, k, v, da, o, d.at[0], d.at[1], d.at[2])
    whole = scal[8 + b] == 0

    def pair(i):
        cols = pl.ds(pl.multiple_of(i * 128, 128), 128)

        @pl.when(whole)
        def _():
            attend(refs, b * 512, cols, WHOLE)

        @pl.when(jnp.logical_not(whole))
        def _():
            attend(refs, b * 512, cols, SMALL)

    loop(q.shape[1] // 128, pair)

    def back(i):
        r = rows_of(b * 2 + i, 256)
        dn[r, :] = dot_nt(d[0, r, :], w[0]) + dot_nt(d[1, r, :], w[1]) + dot_nt(d[2, r, :], w[2])

    loop(2, back)


def core_call(b, scal, q, k, v, da, w, *before):
    return call(
        functools.partial(core_kernel, b),
        "core",
        (scal, q, k, v, da, w, *before),
        [],
        [kept(q.shape), kept((3, *q.shape)), kept(q.shape, F32)],
        [],
        [],
        10 << 30,
        alias={6 + i: i for i in range(len(before))},
        limit=8,
    )


def attn_grad_kernel(store, scal, xn, o, d, cot, sums, *refs):
    *g_refs, g, sem = refs
    tokens, width = xn.shape

    def grad(b):
        g[b] = dot_tn(xn[...], d[b]).astype(BF16)
        store(scal, g, g_refs, sem, b)

    loop(3, grad)
    g[3] = dot_tn(o[...], cot[...]).astype(BF16)
    store(scal, g, g_refs, sem, 3)
    for i, v in enumerate((d[0], d[2], cot[...])):
        sums[i : i + 1, :] = jnp.sum(v.astype(F32), axis=0, keepdims=True)
    stored(g_refs, sem)


def attn_grad_call(scal, xn, o, d, cot, store, g_shapes):
    tokens, width = xn.shape
    return call(
        functools.partial(attn_grad_kernel, store),
        "attn_grad",
        (scal, xn, o, d, cot),
        [],
        [kept((8, width), F32)],
        g_shapes,
        [pltpu.VMEM((4, width, width), BF16), pltpu.SemaphoreType.DMA((len(g_shapes),))],
        8 * tokens * width * width,
        limit=10,
    )


def gelu_parts(u):
    u2 = u * u
    half = 0.5 * jnp.tanh(u * (GELU_C + (GELU_C * GELU_A) * u2)) + 0.5
    act = u * half
    grad = half + act * (1.0 - half) * (2.0 * GELU_C + (6.0 * GELU_C * GELU_A) * u2)
    return act, grad

def tile_of(t, width):
    return pl.ds(t * width if isinstance(t, int) else pl.multiple_of(t * width, 128), width)


def wait_tile(w, sem, t, width):
    whole_wait(w.at[tile_of(t, width), :], sem.at[t])()


def up_kernel(load, first, count, n_p, *refs):
    scal, xn, bias = refs[:3]
    even, odd, sem = refs[-3:]
    tokens, width = xn.shape
    if n_p:
        act, gp, w = refs[-6:-3]
        load(scal, refs[3 : 3 + n_p], w, sem)
        for t in range(count):
            whole_wait(w.at[t], sem.at[t])()
    else:
        act, gp = refs[-5:-3]
        w = refs[5]
    rows = even.shape[0]
    per = tokens // rows

    def product(i):
        return dot_nn(xn[rows_of(i % per, rows), :], w[first + i // per])

    def finish(i, u):
        t, r = first + i // per, rows_of(i % per, rows)
        a, gr = gelu_parts(u + bias[pl.ds(t, 1), :])
        act[t, r, :] = a.astype(BF16)
        gp[t, r, :] = gr.astype(BF16)

    even[...] = product(0)

    def step(i):
        odd[...] = product(2 * i + 1)
        finish(2 * i, even[...])
        even[...] = product(jnp.minimum(2 * i + 2, count * per - 1))
        finish(2 * i + 1, odd[...])

    loop(count * per // 2, step)
    if n_p:
        for t in range(count, bias.shape[0]):
            whole_wait(w.at[t], sem.at[t])()


def up_call(first, count, scal, xn, bias, before, pieces, load):
    tokens, width = xn.shape
    tiles = bias.shape[0]
    return call(
        functools.partial(up_kernel, load, first, count, len(pieces)),
        "up",
        (scal, xn, bias, *before),
        pieces,
        [kept((tiles, tokens, width))] * 2 + [kept((tiles, width, width))] * (1 if pieces else 0),
        [],
        [pltpu.VMEM((256, width), F32)] * 2 + [pltpu.SemaphoreType.DMA((tiles,))],
        2 * count * tokens * width * width,
        alias={3: 0, 4: 1} if before else None,
        limit=7,
    )


def down_grad_kernel(load, store, n_p, scal, act, cot, *refs):
    w, *g_refs, g, wsem, sem = refs[n_p:]
    tiles, tokens, width = act.shape
    load(scal, refs[:n_p], w, wsem)

    def grad(t):
        g[tile_of(t, width), :] = dot_tn(act[t], cot[...]).astype(BF16)
        store(scal, g, g_refs, sem, t)

    loop(tiles, grad)
    for t in range(tiles):
        wait_tile(w, wsem, t, width)
    stored(g_refs, sem)


def down_grad_call(scal, act, cot, pieces, load, store, g_shapes):
    tiles, tokens, width = act.shape
    return call(
        functools.partial(down_grad_kernel, load, store, len(pieces)),
        "down_grad",
        (scal, act, cot),
        pieces,
        [kept((tiles * width, width))],
        g_shapes,
        [
            pltpu.VMEM((tiles * width, width), BF16),
            pltpu.SemaphoreType.DMA((tiles,)),
            pltpu.SemaphoreType.DMA((len(g_shapes),)),
        ],
        2 * tiles * tokens * width * width,
        limit=12,
    )


def dpre_kernel(scal, cot, gp, w, dpre, sums):
    tiles, tokens, width = gp.shape

    def down(t):
        d = (dot_nt(cot[...], w[tile_of(t, width), :]) * gp[t].astype(F32)).astype(BF16)
        dpre[t] = d
        sums[pl.ds(t, 1), :] = jnp.sum(d.astype(F32), axis=0, keepdims=True)

    loop(tiles, down)


def dpre_call(scal, cot, gp, w):
    tiles, tokens, width = gp.shape
    return call(
        dpre_kernel,
        "dpre",
        (scal, cot, gp, w),
        [],
        [kept(gp.shape), kept((8, width), F32)],
        [],
        [],
        2 * tiles * tokens * width * width,
        alias={2: 0},
        limit=8,
    )


def up_grad_kernel(load, store, n_p, scal, xn, dpre, *refs):
    w, *g_refs, g, wsem, sem = refs[n_p:]
    load(scal, refs[:n_p], w, wsem, (3,))

    def grad(t):
        g[t] = dot_tn(xn[...], dpre[t]).astype(BF16)
        store(scal, g, g_refs, sem, t)

    loop(dpre.shape[0], grad)
    whole_wait(w, wsem.at[3])()
    stored(g_refs, sem)


def up_grad_call(scal, xn, dpre, pieces, load, store, g_shapes):
    tiles, tokens, width = dpre.shape
    return call(
        functools.partial(up_grad_kernel, load, store, len(pieces)),
        "up_grad",
        (scal, xn, dpre),
        pieces,
        [kept((1, width, width))],
        g_shapes,
        [
            pltpu.VMEM((tiles, width, width), BF16),
            pltpu.SemaphoreType.DMA((4,)),
            pltpu.SemaphoreType.DMA((len(g_shapes),)),
        ],
        2 * tiles * tokens * width * width,
        limit=10,
    )


def input_grad_kernel(scal, x, cot, dn, dpre, vec, wu, sums, dx_ref, dx, sem):
    tiles, tokens, width = dpre.shape
    sums[...] = jnp.zeros_like(sums)

    def step(i):
        r = rows_of(i, 256)
        dnr = dn[r, :]
        for t in range(tiles):
            dnr += dot_nt(dpre[t, r, :], wu[t])
        standard, inv = norm_rows(x[r, :])
        sums[0:1, :] += jnp.sum(dnr * standard, axis=0, keepdims=True)
        gs = dnr * vec[0:1, :]
        mean_g = jnp.mean(gs, axis=1, keepdims=True)
        mean_p = jnp.mean(gs * standard, axis=1, keepdims=True)
        dx[r, :] = (cot[r, :].astype(F32) + inv * (gs - mean_g - standard * mean_p)).astype(BF16)

    loop(tokens // 256, step, lambda i: send_rows(dx, dx_ref, i, 256, sem))
    whole_wait(dx_ref, sem)()


def input_grad_call(scal, x, cot, dn, dpre, vec, wu):
    tiles, tokens, width = dpre.shape
    return call(
        input_grad_kernel,
        "input_grad",
        (scal, x, cot, dn, dpre, vec, wu),
        [],
        [kept((8, width), F32)],
        [sds((tokens // 512, 512, width))],
        [pltpu.VMEM((tokens, width), BF16), pltpu.SemaphoreType.DMA],
        2 * (tiles + 3) * tokens * width * width,
        limit=8,
    )


def out_kernel(scal, x, o, act, vec, wo, wd, out_ref, out, sem):
    tiles, tokens, width = act.shape

    def step(i):
        r = rows_of(i, 256)
        total = x[r, :].astype(F32) + vec[3:4, :] + dot_nn(o[r, :], wo[0])
        for t in range(tiles):
            total += dot_nn(act[t, r, :], wd[tile_of(t, width), :])
        out[r, :] = total.astype(BF16)

    loop(tokens // 256, step, lambda i: send_rows(out, out_ref, i, 256, sem))
    whole_wait(out_ref, sem)()


def out_call(scal, x, o, act, vec, wo, wd):
    tiles, tokens, width = act.shape
    (out,) = call(
        out_kernel,
        "out",
        (scal, x, o, act, vec, wo, wd),
        [],
        [],
        [sds((tokens // 512, 512, width))],
        [pltpu.VMEM((tokens, width), BF16), pltpu.SemaphoreType.DMA],
        2 * (tiles + 1) * tokens * width * width,
        limit=8,
    )
    return out


def swap(value, mask):
    return lax.ppermute(value, "wide", [(i, i ^ mask) for i in range(16)])


def swap_y(value):
    return lax.ppermute(value, "narrow", [(0, 1), (1, 0)])


def slots():
    for part in range(2):
        for i in range(2):
            for s in range(2):
                half, side = (i, s) if part == 0 else (s, i)
                for k in range(4):
                    yield part, i, s * 4 + k, half, side, k


def device_of(scal, k, side, core):
    return ((scal[1] ^ k) * 2 + (scal[2] ^ side)) * 2 + (scal[3] ^ core)


def behind(value, *marks):
    return lax.optimization_barrier((value, marks))[0]


def gather_z(value):
    return [swap(value, k << 2) for k in (1, 2, 3)]


def gather_first(za, zb):
    return swap(za, 2), swap_y(zb), swap_y(za), swap(zb, 2)


def gather_second(xa, yb):
    return swap_y(xa), swap(yb, 2)


def pieces_of(za, zb, first, second):
    xa, yb, ya, xb = first
    return [za, xa, ya, second[0], zb, xb, yb, second[1]]


def join_job(values):
    def fn(held, near, outs):
        size = near[0].shape[0]
        for i, v in enumerate(near):
            at = slice(i * size, (i + 1) * size)
            if v.ndim == 3:
                outs[0][at, : v.shape[1], :] = v[...]
            else:
                outs[0][at] = v[...]

    return fn, [], values, [kept((len(values) * values[0].shape[0], *values[0].shape[1:]))]


def mix(name, jobs):
    held = [v for job in jobs for v in job[1]]
    near = [v for job in jobs for v in job[2]]
    outs = [o for job in jobs for o in job[3]]

    def kernel(*refs):
        at = len(near) + len(held)
        scratch = refs[at + len(outs) :]
        copies = [
            pltpu.make_async_copy(refs[len(near) + i].at[:, pl.ds(v[1], v[2])], scratch[i], scratch[-1].at[i])
            for i, v in enumerate(held)
        ]
        for cp in copies:
            cp.start()
        h = n = o = 0
        for fn, job_h, job_n, job_o in jobs:
            for i in range(len(job_h)):
                copies[h + i].wait()
            fn(
                scratch[h : h + len(job_h)],
                refs[n : n + len(job_n)],
                refs[at + o : at + o + len(job_o)],
            )
            h, n, o = h + len(job_h), n + len(job_n), o + len(job_o)

    got = pl.pallas_call(
        kernel,
        name=name,
        out_shape=outs,
        in_specs=[VMEM] * len(near) + [HBM] * len(held),
        out_specs=[VMEM] * len(outs),
        scratch_shapes=[pltpu.VMEM((v.shape[0], size, *v.shape[2:]), v.dtype) for v, _, size in held]
        + [pltpu.SemaphoreType.DMA((max(len(held), 1),))],
        compiler_params=pltpu.CompilerParams(vmem_limit_bytes=8 << 20),
        cost_estimate=pl.CostEstimate(flops=1 << 20, bytes_accessed=1 << 20, transcendentals=0),
    )(
        *[pltpu.with_memory_space_constraint(v, pltpu.VMEM) for v in near],
        *[pltpu.with_memory_space_constraint(v[0], pltpu.HBM) for v in held],
    )
    split, at = [], 0
    for job in jobs:
        split.append(got[at : at + len(job[3])])
        at += len(job[3])
    return split


def total(*parts):
    return sum(v.astype(F32) for v in parts)


def stack_job(values):
    def fn(held, near, outs):
        for k, v in enumerate(near):
            for i in range(2):
                outs[i][k] = v[i]

    return fn, [], list(values), [kept((len(values), *values[0].shape[1:]))] * 2


def vector_job(sums_a, sums_d, sums_x, wide, rows):
    width = sums_a.shape[1]

    def spread(rows_in, per):
        flat = jnp.concatenate([rows_in[w * per // width][None] for w in range(wide)])
        col = lax.broadcasted_iota(jnp.int32, (wide, width), 1)
        own = lax.broadcasted_iota(jnp.int32, (wide, width), 0) * per % width
        flat = jnp.where((col >= own) & (col < own + per), flat, 0.0)
        pick = lax.broadcasted_iota(jnp.int32, (width, per), 0) % per
        pick = (pick == lax.broadcasted_iota(jnp.int32, (width, per), 1)).astype(BF16)
        got = jnp.zeros((wide, per), F32)
        for _ in range(3):
            high = flat.astype(BF16)
            flat = flat - high.astype(F32)
            got += dot_nn(high, pick)
        return got

    def fn(held, near, outs):
        a, d, x, scal = near
        tiles = 4
        at = 0
        for got in (
            spread([x[0]], rows),
            spread([a[0], a[1]], 2 * rows),
            spread([d[t] for t in range(tiles)], tiles * rows),
            spread([a[2]], rows),
        ):
            outs[4][:, at : at + got.shape[1]] = got
            at += got.shape[1]
        for k in range(4):
            outs[k][...] = jnp.zeros_like(outs[k])
            for r in range(4):
                outs[k][r : r + 1, :] = outs[4][pl.ds((scal[1] ^ k) * 4 + r, 1), :]

    return fn, [], [sums_a, sums_d, sums_x], [kept((8, 8 * rows), F32)] * 4 + [kept((wide, 8 * rows), F32)]


def add_job(values):
    def fn(held, near, outs):
        outs[0][...] = sum(near[i][...] for i in range(len(values)))

    return fn, [], list(values), [kept(values[0].shape, F32)]


def vector_job(sums_a, sums_d, sums_x):
    def fn(held, near, outs):
        a, d, x = near
        outs[0][0:1, :] = x[0:1, :]
        outs[0][1:3, :] = a[0:2, :]
        outs[0][3:7, :] = d[0:4, :]
        outs[0][7:8, :] = a[2:3, :]

    return fn, [], [sums_a, sums_d, sums_x], [kept(sums_a.shape, F32)]


def sum1_job(keep1, got1):
    def fn(held, near, outs):
        for i in range(2):
            outs[i][...] = total(held[0][i], near[0][i]).astype(BF16)

    return fn, [(keep1, 0, keep1.shape[1])], [got1], [kept(keep1.shape[1:])] * 2


def sum2_job(keep0, got0, got):
    half = keep0.shape[1] // 2

    def fn(held, near, outs):
        for i in range(2):
            outs[i][...] = total(held[0][i], near[0][i, half:], near[1 + i][half:]).astype(BF16)

    return fn, [(keep0, half, half)], [got0, *got], [kept((half, *keep0.shape[2:]))] * 2


def sum3_job(keep0, got0, got, got2):
    half = keep0.shape[1] // 2

    def fn(held, near, outs):
        for k in range(half):
            for i in range(2):
                outs[k][i] = total(held[0][i, k], near[0][i, k], near[1 + i][k], near[3 + i][k]).astype(BF16)

    return fn, [(keep0, 0, half)], [got0, *got, *got2], [kept((2, *keep0.shape[2:]))] * half


def sum4_job(own, got):
    def fn(held, near, outs):
        outs[0][...] = total(*[near[i][...] for i in range(1 + len(got))]).astype(BF16)

    return fn, [], [own, *got], [kept(own.shape)]


def place_kernel(scal, a_mine, a_other, d_mine, d_other, joined_ref, out, down, joined, sem):
    _, rows, width = a_mine.shape

    def place(half, a, d):
        for p in range(2):
            block = half * 2 + p
            down[pl.ds(block * rows, rows), :] = d[p].astype(F32)
            if block < 3:
                joined[block] = a[p].astype(F32)
                dst = joined_ref.at[:, block * width : (block + 1) * width]
                pltpu.make_async_copy(joined.at[block], dst, sem).start()
            else:
                out[...] = a[p].astype(F32)

    @pl.when(scal[0] == 0)
    def _():
        place(0, a_mine, d_mine)
        place(1, a_other, d_other)

    @pl.when(scal[0] != 0)
    def _():
        place(1, a_mine, d_mine)
        place(0, a_other, d_other)

    whole_wait(joined, sem)()


def place_call(scal, parts):
    _, rows, width = parts[0].shape
    return pl.pallas_call(
        place_kernel,
        name="place",
        out_shape=[sds((rows, 7 * width), F32), sds((rows, width), F32), sds((4 * rows, width), F32)],
        in_specs=[SMEM] + [VMEM] * 4,
        out_specs=[HBM, VMEM, VMEM],
        scratch_shapes=[pltpu.VMEM((3, rows, width), F32), pltpu.SemaphoreType.DMA],
        compiler_params=pltpu.CompilerParams(vmem_limit_bytes=8 << 20),
    )(scal, *[pltpu.with_memory_space_constraint(v, pltpu.VMEM) for v in parts])


def place_last_kernel(scal, placed, mine, other, v0, v1, v2, v3, joined_ref, gain, b_attn, b_mlp, b_out, wide, sem):
    _, rows, width = other.shape
    for i, ref in enumerate((mine, other)):
        for p in range(2):
            wide[i * 2 + p] = ref[p].astype(F32)
            at = pl.multiple_of((3 + (scal[0] ^ i) * 2 + p) * width, 128)
            pltpu.make_async_copy(wide.at[i * 2 + p], joined_ref.at[:, pl.ds(at, width)], sem).start()
    total = (v0[...] + v1[...]) + (v2[...] + v3[...])
    row = lax.broadcasted_iota(jnp.int32, total.shape, 0)
    dev = (scal[1] * 2 + scal[2]) * 2 + scal[3]
    for first, out in ((0, gain), (1, b_attn), (3, b_mlp), (7, b_out)):
        per = out.shape[0]
        share = width // per
        line = jnp.sum(jnp.where(row == first + dev // share, total, 0.0), axis=0, keepdims=True)
        line = jnp.broadcast_to(line, total.shape)
        line = pltpu.roll(line, (share - dev % share) % share * per, 1)
        out[...] = line[0, :per]
    whole_wait(wide, sem)()


def place_last_call(scal, placed, mine, other, vectors):
    _, rows, width = other.shape
    near = [pltpu.with_memory_space_constraint(v, pltpu.VMEM) for v in (mine, other, *vectors)]
    return pl.pallas_call(
        place_last_kernel,
        name="place_last",
        out_shape=[sds(placed.shape, F32)] + [sds((n * rows,), F32) for n in (1, 2, 4, 1)],
        in_specs=[SMEM, HBM] + [VMEM] * 6,
        out_specs=[HBM] + [VMEM] * 4,
        scratch_shapes=[pltpu.VMEM((4, *other.shape[1:]), F32), pltpu.SemaphoreType.DMA],
        compiler_params=pltpu.CompilerParams(vmem_limit_bytes=8 << 20),
        input_output_aliases={1: 0},
    )(scal, placed, *near)


def whole_wait(ref, sem):
    return pltpu.make_async_copy(ref, ref, sem).wait


def piece(refs, at, core, k, alone):
    if core == 0:
        return refs[at].at[k]
    if at in alone:
        return refs[9 + alone.index(at)].at[k]
    return refs[8].at[(at - sum(i < at for i in alone)) * 4 + k]


def load_columns(scal, refs, w, sem, blocks=(0, 1, 2, 3)):
    rows = w.shape[1] // 16

    def start(own):
        for block in blocks:
            for core in range(2):
                for part, _, _, half, side, k in slots():
                    if (own ^ half) * 2 + part != block:
                        continue
                    src = piece(refs, part * 4 + half * 2 + side, core, k, (3, 7)).at[pl.ds(0, rows), :]
                    dst = w.at[blocks.index(block), rows_at(device_of(scal, k, side, core) * rows, rows), :]
                    pltpu.make_async_copy(src, dst, sem.at[block]).start()

    @pl.when(scal[0] == 0)
    def _():
        start(0)

    @pl.when(scal[0] != 0)
    def _():
        start(1)


def load_half(which):
    def load(scal, refs, w, sem):
        def start(rel):
            for core in range(2):
                for part, _, _, half, side, k in slots():
                    if half != rel:
                        continue
                    src = piece(refs, part * 4 + half * 2 + side, core, k, (0, 4))
                    per, rows, width = src.shape
                    dev = device_of(scal, k, side, core)
                    for b in range(per):
                        block = part * per + b
                        if which == 0:
                            dst, tile = w.at[block, rows_at(dev * rows, rows), :], block
                        else:
                            dst, tile = w.at[rows_at((dev * 2 * per + block) * rows, rows), :], scal[1] ^ k
                        pltpu.make_async_copy(src.at[b], dst, sem.at[tile]).start()

        @pl.when(scal[0] == which)
        def _():
            start(0)

        @pl.when(scal[0] != which)
        def _():
            start(1)

    return load


def read_vectors(scal, refs, vec, b_mlp, buf, sem):
    width = vec.shape[1]
    rows = width // 16
    for core in range(2):
        for side in range(2):
            for k in range(4):
                src = piece(refs, side, core, k, (3, 7)).at[pl.ds(rows, 8), :]
                pltpu.make_async_copy(src, buf.at[device_of(scal, k, side, core)], sem).start()
    yield
    whole_wait(buf, sem)()
    values = buf[:, 0, :].astype(F32)
    devices = values.shape[0]

    def line(at, per):
        pick = lax.broadcasted_iota(jnp.int32, (per, width), 1) % per
        pick = (pick == lax.broadcasted_iota(jnp.int32, (per, width), 0)).astype(BF16)
        flat = dot_nn(values[:, at : at + per].astype(BF16), pick)
        dev = lax.broadcasted_iota(jnp.int32, flat.shape, 0)
        col = lax.broadcasted_iota(jnp.int32, flat.shape, 1)
        count = devices * per // width
        share = devices // count
        keep = col // per == dev % share
        return [
            jnp.sum(jnp.where(keep & (dev // share == i), flat, 0.0), axis=0, keepdims=True) for i in range(count)
        ]

    lines = line(0, rows) + line(rows, 2 * rows) + line(7 * rows, rows)
    vec[...] = jnp.zeros_like(vec)
    for i, v in enumerate(lines):
        vec[i : i + 1, :] = v
    for i, v in enumerate(line(3 * rows, 4 * rows)):
        b_mlp[i : i + 1, :] = v
    yield


def rows_at(base, rows):
    return pl.ds(pl.multiple_of(base, 16), rows)


def stored(refs, sem):
    for i, r in enumerate(refs):
        whole_wait(r, sem.at[i])()


def store_block(scal, g, refs, sem, t):
    half, part = scal[0] ^ (t // 2), t % 2
    rows = refs[0].shape[2]

    def send(at, core, side, k, slot, p):
        src = g.at[t, rows_at(device_of(scal, k, side, core) * rows, rows), :]
        pltpu.make_async_copy(src, refs[at].at[p, slot], sem.at[at]).start()

    for i in range(2):

        @pl.when((part == 0) & (half == i))
        def _(i=i):
            for core in range(2):
                for side in range(2):
                    for k in range(4):
                        send(core * 2 + i, core, side, k, side * 4 + k, 0)

    @pl.when(part == 1)
    def _():
        for core in range(2):
            for side in range(2):
                for k in range(4):
                    send(core * 2 + side, core, side, k, half * 4 + k, 1)


def store_rows(scal, g, refs, sem, t):
    k = scal[1] ^ t
    rows = refs[0].shape[2]
    for core in range(2):
        for side in range(2):
            dev = (t * 2 + (scal[2] ^ side)) * 2 + (scal[3] ^ core)
            for half in range(2):
                for part in range(2):
                    i, s = (half, side) if part == 0 else (side, half)
                    at = core * 2 + i
                    src = g.at[rows_at((dev * 4 + (scal[0] ^ half) * 2 + part) * rows, rows), :]
                    pltpu.make_async_copy(src, refs[at].at[part, s * 4 + k], sem.at[at]).start()


def load_whole_blocks(scal, refs, w, sem, blocks=(0, 1, 2, 3)):
    for i, b in enumerate(blocks):
        pltpu.make_async_copy(refs[b], w.at[i], sem.at[b]).start()


def load_whole_rows(scal, refs, w, sem):
    width = w.shape[1]
    for t in range(w.shape[0] // width):
        r = tile_of(t, width)
        pltpu.make_async_copy(refs[0].at[r, :], w.at[r, :], sem.at[t]).start()


def store_whole_blocks(scal, g, refs, sem, t):
    for i, r in enumerate(refs):

        @pl.when(t == i)
        def _(i=i, r=r):
            pltpu.make_async_copy(g.at[i], r, sem.at[i]).start()


def store_whole_rows(scal, g, refs, sem, t):
    r = tile_of(t, g.shape[1])
    pltpu.make_async_copy(g.at[r, :], refs[0].at[r, :], sem.at[0]).start()


def body(sizes, tokens, image_ids, cotangent, w_joined, w_out, w_mlp, norm_gain, bias_attn, bias_mlp, bias_out):
    micro, length, width = tokens.shape
    narrow, wide = sizes
    paired = narrow == 2 and wide == 16
    rows = width // wide
    tiles = w_mlp.shape[0] // rows
    x = tokens.reshape(micro * length, width)
    cot = cotangent.reshape(micro * length, width)
    n = lax.axis_index("narrow")
    w = lax.axis_index("wide")
    last = image_ids.reshape(-1, 512)[:, -1]
    scal = [n, w >> 2, (w >> 1) & 1, w & 1] + [jnp.int32(0)] * 4 + [last[b] for b in range(last.shape[0])]
    scal = jnp.stack([jnp.asarray(s, jnp.int32) for s in scal])
    vec_own = jnp.concatenate([norm_gain, bias_attn, bias_mlp, bias_out])

    def vectors(vec):
        vec = vec.astype(F32)
        b_at = 3 * rows
        b_mlp = vec[:, b_at : b_at + tiles * rows].reshape(tiles, width)
        head = [
            vec[:, :rows].reshape(1, width),
            vec[:, rows:b_at].reshape(2, width),
            vec[:, b_at + tiles * rows :].reshape(1, width),
            jnp.zeros((4, width), F32),
        ]
        return jnp.concatenate(head), b_mlp

    def vector_grads(sums_a, sums_d, sums_x):
        return jnp.concatenate(
            [
                sums_x[0].reshape(wide, rows),
                sums_a[:2].reshape(wide, 2 * rows),
                sums_d[:tiles].reshape(wide, tiles * rows),
                sums_a[2].reshape(wide, rows),
            ],
            axis=1,
        )

    if not paired:
        full = lax.all_gather(w_joined, "wide", axis=0, tiled=True)
        parts = [full[:, i * width : (i + 1) * width] for i in range(3 + tiles)]
        attn_w = parts[:3] + [lax.all_gather(w_out, "wide", axis=0, tiled=True)]
        up_w = parts[3:]
        down_w = [lax.all_gather(w_mlp, "wide", axis=0, tiled=True)]
        vec, b_mlp = vectors(lax.all_gather(vec_own, "wide", axis=0))
        square = [sds((width, width))]
        xn, q, k, v, da, wa = project_call(scal, x, cot, vec, attn_w, load_whole_blocks)
        part = core_call(0, scal, q, k, v, da, wa)
        for b in range(1, last.shape[0]):
            part = core_call(b, scal, q, k, v, da, wa, *part)
        o, d, dn = part
        sums_a, *g_attn = attn_grad_call(scal, xn, o, d, cot, store_whole_blocks, square * 4)
        act, gp, wu = up_call(0, tiles // 2, scal, xn, b_mlp, (), up_w, load_whole_blocks)
        act, gp = up_call(tiles // 2, tiles - tiles // 2, scal, xn, b_mlp, (act, gp, wu), [], None)
        wd, *g_down = down_grad_call(
            scal, act, cot, down_w, load_whole_rows, store_whole_rows, [sds((tiles * width, width))]
        )
        dpre, sums_d = dpre_call(scal, cot, gp, wd)
        wo, *g_up = up_grad_call(scal, xn, dpre, attn_w, load_whole_blocks, store_whole_blocks, square * tiles)
        sums_x, d_x = input_grad_call(scal, x, cot, dn, dpre, vec, wu)
        out = out_call(scal, x, o, act, vec, wo, wd)

        def reduce(g):
            g = lax.psum_scatter(g.astype(F32), "wide", scatter_dimension=0, tiled=True)
            return lax.psum(g, "narrow")

        grad_joined = reduce(jnp.concatenate([*g_attn[:3], *g_up], axis=1))
        grad_out = reduce(g_attn[3])
        grad_mlp = reduce(g_down[0])
        vg = reduce(vector_grads(sums_a, sums_d, sums_x))[0]
        vg = jnp.split(vg, [rows, 3 * rows, (3 + tiles) * rows])
    else:
        col = lambda i: w_joined[:, i * width : (i + 1) * width]
        pair = lambda f: jnp.stack([jnp.where(n == 0, f(0), f(2)), jnp.where(n == 0, f(1), f(3))])
        half_a, half_b = [jnp.where(n == 0, f, g) for f, g in ((col(0), col(2)), (col(1), w_out))]
        v_rows = jnp.pad(vec_own, (0, width - vec_own.shape[0]))
        half = jnp.concatenate([half_a, jnp.broadcast_to(v_rows, (8, width)), half_b])
        got = gather_z(half)
        za = jnp.stack([t[: rows + 8] for t in (half, *got)])
        zb = jnp.stack([t[rows + 8 :] for t in (half, *got)])
        c_half = jnp.stack([jnp.where(n == 0, col(3 + t), w_mlp[t * rows : (t + 1) * rows]) for t in range(tiles)])
        c_half = behind(c_half.reshape(2, tiles // 2, rows, width), za, zb)
        first = gather_first(za, zb)
        c2 = swap(c_half, 8)
        first, c2, c_half = lax.optimization_barrier((first, c2, c_half))
        second = gather_second(*first[:2])
        own = pieces_of(za, zb, first, second)
        ((joined,),) = mix("join_a", [join_job([own[i] for i in (0, 1, 2, 4, 5, 6)])])
        joined, c1, c3 = swap(joined, 1), swap(c_half, 4), swap(c_half, 12)
        second, joined, c1, c3 = lax.optimization_barrier((second, joined, c1, c3))
        own = pieces_of(za, zb, first, second)
        attn_w = [*own, joined, swap(second[0], 1), swap(second[1], 1)]
        cza, czb = [jnp.stack([t[i] for t in (c_half, c1, c2, c3)]) for i in range(2)]
        x_p, attn_w, cza, czb = lax.optimization_barrier((x, attn_w, cza, czb))
        c_first = gather_first(cza, czb)
        xn, q, k, v, da, wa, vec, b_mlp = project_call(scal, x_p, cot, None, attn_w, load_columns, read_vectors)
        part = core_call(0, scal, q, k, v, da, wa)

        part, c_first = lax.optimization_barrier((part, c_first))
        c_second = gather_second(*c_first[:2])
        czs = [swap(cza, 1), swap(czb, 1)]
        o, d, dn = core_call(1, scal, q, k, v, da, wa, *part)

        d, c_second, czs = lax.optimization_barrier((d, c_second, czs))
        c_own = pieces_of(cza, czb, c_first, c_second)
        ((c_joined,),) = mix("join_c", [join_job([t for t in c_own if t is not cza and t is not czb])])
        d, c_joined = lax.optimization_barrier((d, c_joined))
        c_other = swap(c_joined, 1)
        attn_shapes = [sds((2, 8, rows, width))] * 4
        sums_a, *ga = attn_grad_call(scal, xn, o, d, cot, store_block, attn_shapes)

        c_other, ga = behind((c_other, ga), sums_a)
        xn_u, ga, c_own, c_other = lax.optimization_barrier((xn, ga, c_own, c_other))
        a_got1, a_got0 = swap(ga[3], 1), swap(ga[2], 1)
        half_tiles = tiles // 2
        c_all = [*c_own, c_other, *czs]
        act, gp, wu = up_call(0, half_tiles, scal, xn_u, b_mlp, (), c_all, load_half(0))

        a_got1, a_got0 = behind((a_got1, a_got0), gp)
        ((sa, sb),) = mix("sums_1", [sum1_job(ga[1], a_got1)])
        act, sa, sb = lax.optimization_barrier((act, sa, sb))
        a_xy = swap_y(sa), swap(sb, 2)
        act, gp = up_call(half_tiles, half_tiles, scal, xn_u, b_mlp, (act, gp, wu), [], None)
        wd, *gd = down_grad_call(
            scal, act, cot, c_all, load_half(1), store_rows, attn_shapes
        )

        a_xy = behind(a_xy, gd)
        ((sa, sb),) = mix("sums_2", [sum2_job(ga[0], a_got0, a_xy)])
        gp, sa, sb, gd = lax.optimization_barrier((gp, sa, sb, gd))
        a_yx = swap(sa, 2), swap_y(sb)
        d_got1, d_got0 = swap(gd[3], 1), swap(gd[2], 1)
        dpre, sums_d = dpre_call(scal, cot, gp, wd)

        a_yx, d_got1, d_got0 = behind((a_yx, d_got1, d_got0), dpre)
        a_t, (sa, sb) = mix("sums_3", [sum3_job(ga[0], a_got0, a_xy, a_yx), sum1_job(gd[1], d_got1)])
        dpre_g, a_t, sa, sb = lax.optimization_barrier((dpre, a_t, sa, sb))
        d_xy = swap_y(sa), swap(sb, 2)
        a_z = [swap(a_t[k], k << 2) for k in (1, 2, 3)]
        wo, *gu = up_grad_call(scal, xn, dpre_g, attn_w, load_columns, store_block, attn_shapes)

        a_z, d_xy = behind((a_z, d_xy), gu)
        (a_sum,), (sa, sb) = mix("sums_4", [sum4_job(a_t[0], a_z), sum2_job(gd[0], d_got0, d_xy)])
        x_i, sa, sb, gu, a_sum = lax.optimization_barrier((x, sa, sb, gu, a_sum))
        u_got1, u_got0 = swap(gu[3], 1), swap(gu[2], 1)
        d_yx = swap(sa, 2), swap_y(sb)
        a_other = swap_y(a_sum)
        sums_x, d_x = input_grad_call(scal, x_i, cot, dn, dpre, vec, wu)

        d_yx, u_got1, u_got0, a_other = behind((d_yx, u_got1, u_got0, a_other), d_x)
        (sa, sb), d_t, (v_own,) = mix(
            "sums_5",
            [
                sum1_job(gu[1], u_got1),
                sum3_job(gd[0], d_got0, d_xy, d_yx),
                vector_job(sums_a, sums_d, sums_x),
            ],
        )
        x_o, sa, sb, d_t = lax.optimization_barrier((x, sa, sb, d_t))
        u_xy = swap_y(sa), swap(sb, 2)
        d_z = [swap(d_t[k], k << 2) for k in (1, 2, 3)]
        out = out_call(scal, x_o, o, act, vec, wo, wd)

        u_xy, d_z, v_own = behind((u_xy, d_z, v_own), out)
        (sa, sb), (d_sum,) = mix("sums_6", [sum2_job(gu[0], u_got0, u_xy), sum4_job(d_t[0], d_z)])
        sa, sb, d_sum, v_own = lax.optimization_barrier((sa, sb, d_sum, v_own))
        u_yx = swap(sa, 2), swap_y(sb)
        v_got = [swap(v_own, k << 2) for k in (1, 2, 3)]
        u_t, (v_sum,) = mix("sums_7", [sum3_job(gu[0], u_got0, u_xy, u_yx), add_job([v_own, *v_got])])
        u_t, v_sum, d_sum = lax.optimization_barrier((u_t, v_sum, d_sum))
        u_z = [swap(u_t[k], k << 2) for k in (1, 2, 3)]
        v_other, d_other = swap_y(v_sum), swap_y(d_sum)
        placed, grad_out, grad_mlp = place_call(scal, [a_sum, a_other, d_sum, d_other])
        u_z, placed = lax.optimization_barrier((u_z, placed))
        (u_sum,), (v_sum,) = mix("sums_8", [sum4_job(u_t[0], u_z), add_job([v_sum, v_other])])
        u_other = swap_y(u_sum)
        v_all = [v_sum, *[swap(v_sum, i) for i in (1, 2, 3)]]
        grad_joined, *vg = place_last_call(scal, placed, u_sum, u_other, v_all)
    return (out.reshape(tokens.shape), d_x.reshape(tokens.shape), grad_joined, grad_out, grad_mlp, *vg)


def solution(mesh):
    sizes = (mesh.shape["narrow"], mesh.shape["wide"])
    rows = P(None, ("narrow", "wide"), None)
    placed = (rows, P(None, ("narrow", "wide")), rows) + (P("wide", None),) * 3 + (P("wide"),) * 4
    return jax.shard_map(
        functools.partial(body, sizes),
        mesh=mesh,
        in_specs=placed,
        out_specs=(rows, rows) + (P("wide", None),) * 3 + (P("wide"),) * 4,
        check_vma=False,
    )
```

```python
import functools

import jax
import jax.numpy as jnp
from jax import lax
from jax.experimental import pallas as pl
from jax.experimental.pallas import tpu as pltpu
from jax.sharding import PartitionSpec as P

HEADS = 12
HEAD = 64
IMG = 196
EPS = 1e-06
GELU_C = 0.7978845608028654
GELU_A = 0.044715

F32 = jnp.float32
BF16 = jnp.bfloat16
HBM = pl.BlockSpec(memory_space=pltpu.HBM)
VMEM = pl.BlockSpec(memory_space=pltpu.VMEM)
SMEM = pl.BlockSpec(memory_space=pltpu.SMEM)


def dot_nn(a, b):
    return lax.dot_general(a, b, (((1,), (0,)), ((), ())), preferred_element_type=F32)


def dot_nt(a, b):
    return lax.dot_general(a, b, (((1,), (1,)), ((), ())), preferred_element_type=F32)


def dot_tn(a, b):
    return lax.dot_general(a, b, (((0,), (0,)), ((), ())), preferred_element_type=F32)


def norm_rows(rows):
    rows = rows.astype(F32)
    mean = jnp.mean(rows, axis=1, keepdims=True)
    centered = rows - mean
    inv = lax.rsqrt(jnp.mean(centered * centered, axis=1, keepdims=True) + EPS)
    return centered * inv, inv


def attend(refs, base, cols, windows):
    q_ref, k_ref, v_ref, da_ref, o_ref, dq_ref, dk_ref, dv_ref = refs
    zero = jnp.zeros((), BF16)
    jobs, ends = [], {}
    for start, rows, lo, hi, merge in windows:
        win = pl.ds(pl.multiple_of(base + start, 16), rows)
        tiles = [r[win, cols] for r in (q_ref, k_ref, v_ref, da_ref)]
        lane = lax.broadcasted_iota(jnp.int32, (rows, 128), 1)
        sums = {}
        step = 256 if rows == 512 else rows
        for at in range(0, rows, step):
            for h in range(2):
                keep = (lane < 64) if h == 0 else (lane >= 64)
                heads = [jnp.where(keep, t, zero) for t in tiles]
                jobs.append([tiles, heads, rows, lo, hi, at, step, sums])
        ends[len(jobs) - 1] = (start, rows, merge, sums)

    def products(job):
        tiles, heads, _, _, _, at, step, _ = job
        qs = slice(at, at + step)
        job += [dot_nt(tiles[1], heads[0][qs]), dot_nt(tiles[2], heads[3][qs])]

    def soften(job):
        _, _, rows, lo, hi, at, step, _, s, dp = job
        masked = lo > 0 or hi < rows
        if masked:
            key = lax.broadcasted_iota(jnp.int32, (rows, step), 0)
            s = jnp.where((key >= lo) & (key < hi), s, -1e30)
        e = jnp.exp(s - jnp.max(s, axis=0, keepdims=True))
        scale = 1.0 / jnp.sum(e, axis=0, keepdims=True)
        if masked:
            query = lax.broadcasted_iota(jnp.int32, (1, step), 1) + at
            scale = jnp.where((query >= lo) & (query < hi), scale, 0.0)
        p = e * scale
        inner = jnp.sum(p * dp, axis=0, keepdims=True)
        job[8:] = [p.astype(BF16), (p * (dp - inner)).astype(BF16)]

    def gather(job):
        _, heads, _, _, _, at, step, sums, p, ds = job
        qs = slice(at, at + step)
        parts = (
            (("o", at), dot_tn(p, heads[2])),
            (("q", at), dot_tn(ds, heads[1])),
            (("v", 0), dot_nn(p, heads[3][qs])),
            (("k", 0), dot_nn(ds, heads[0][qs])),
        )
        for key, val in parts:
            sums[key] = sums[key] + val if key in sums else val

    def write(start, rows, merge, sums):
        for name, ref in (("o", o_ref), ("q", dq_ref), ("k", dk_ref), ("v", dv_ref)):
            for (n, at), val in sums.items():
                if n != name:
                    continue
                val = (val * 0.125 if n == "q" else val).astype(BF16)
                size = val.shape[0]
                if merge and at == 0:
                    head = pl.ds(pl.multiple_of(base + start, 16), merge)
                    ref[head, cols] = ref[head, cols] + val[:merge]
                    val, at, size = val[merge:], merge, size - merge
                ref[pl.ds(pl.multiple_of(base + start + at, 16), size), cols] = val

    for i in range(len(jobs) + 2):
        if i < len(jobs):
            products(jobs[i])
        if 0 <= i - 1 < len(jobs):
            soften(jobs[i - 1])
        if 0 <= i - 2:
            gather(jobs[i - 2])
            if i - 2 in ends:
                write(*ends[i - 2])


WHOLE = ((0, 512, 0, 512, 0),)
SMALL = (
    (0, 208, 0, IMG, 0),
    (192, 208, IMG - 192, 2 * IMG - 192, 16),
    (384, 128, 2 * IMG - 384, 128, 16),
)


def sds(shape, dtype=BF16):
    return jax.ShapeDtypeStruct(shape, dtype)


def kept(shape, dtype=BF16):
    return pltpu.VMEM(shape, dtype)


def call(kernel, name, operands, pieces, outs, g_shapes, scratch, flops, limit=14, alias=None):
    n_p, n_g = len(pieces), len(g_shapes)
    scal, *rest = operands
    rest = [pltpu.with_memory_space_constraint(v, pltpu.VMEM) for v in rest]
    pieces = [pltpu.with_memory_space_constraint(v, pltpu.HBM) for v in pieces]
    g_shapes = [pltpu.HBM(g.shape, g.dtype) for g in g_shapes]
    return pl.pallas_call(
        kernel,
        name=name,
        out_shape=list(outs) + list(g_shapes),
        in_specs=[SMEM] + [VMEM] * len(rest) + [HBM] * n_p,
        out_specs=[VMEM] * len(outs) + [HBM] * n_g,
        scratch_shapes=scratch,
        compiler_params=pltpu.CompilerParams(vmem_limit_bytes=limit << 20),
        input_output_aliases=alias or {},
        cost_estimate=pl.CostEstimate(flops=flops, bytes_accessed=1 << 20, transcendentals=0),
    )(scal, *rest, *pieces)


def loop(count, fn, after=None):
    def step(i, c):
        fn(i)
        if after is not None:
            after(i)
        return c

    lax.fori_loop(0, count, step, 0)


def send_rows(src, dst, i, size, sem):
    per = dst.shape[1] // size
    pltpu.make_async_copy(src.at[rows_of(i, size), :], dst.at[i // per, rows_of(i % per, size), :], sem).start()


def rows_of(i, size):
    return pl.ds(pl.multiple_of(i * size, size), size)


def project_kernel(load, read, n_w, *refs):
    n_v = 0 if read else 1
    scal, x_ref, cot_ref = refs[:3]
    w_refs = refs[3 + n_v : 3 + n_v + n_w]
    xn, q, k, v, da, w, *rest = refs[3 + n_v + n_w :]
    sem = rest[-1]
    if read:
        vec_ref, b_mlp, buf, vsem = rest[:4]
        steps = read(scal, w_refs, vec_ref, b_mlp, buf, vsem)
        next(steps)
        load(scal, w_refs, w, sem)
        next(steps)
    else:
        vec_ref = refs[3]
        load(scal, w_refs, w, sem)
    tokens = x_ref.shape[0]

    def norm(i):
        r = rows_of(i, 256)
        standard, _ = norm_rows(x_ref[r, :])
        xn[r, :] = (standard * vec_ref[0:1, :]).astype(BF16)

    loop(tokens // 256, norm)

    def ready(i):
        whole_wait(w.at[i], sem.at[i])()

    def each(fn):
        loop(tokens // 512, lambda i: fn(rows_of(i, 512)))

    def queries(r):
        q[r, :] = (dot_nn(xn[r, :], w[0]) + vec_ref[1:2, :]).astype(BF16) * jnp.asarray(0.125, BF16)

    def keys(r):
        k[r, :] = dot_nn(xn[r, :], w[1]).astype(BF16)

    def values(r):
        v[r, :] = (dot_nn(xn[r, :], w[2]) + vec_ref[2:3, :]).astype(BF16)

    def attended(r):
        da[r, :] = dot_nt(cot_ref[r, :], w[3]).astype(BF16)

    for i, fn in enumerate((queries, keys, values, attended)):
        ready(i)
        each(fn)


def project_call(scal, x, cot, vec, weights, load, read=None):
    tokens, width = x.shape
    return call(
        functools.partial(project_kernel, load, read, len(weights)),
        "project",
        (scal, x, cot) if read else (scal, x, cot, vec),
        weights,
        [kept(x.shape)] * 5
        + [kept((4, width, width))]
        + ([kept((8, width), F32), kept((4, width), F32)] if read else []),
        [],
        ([pltpu.VMEM((16, 8, width), BF16), pltpu.SemaphoreType.DMA] if read else [])
        + [pltpu.SemaphoreType.DMA((4,))],
        8 * tokens * width * width,
        limit=10,
    )


def core_kernel(b, scal, q, k, v, da, w, *refs):
    o, d, dn = refs[-3:]
    refs = (q, k, v, da, o, d.at[0], d.at[1], d.at[2])
    whole = scal[8 + b] == 0

    def pair(i):
        cols = pl.ds(pl.multiple_of(i * 128, 128), 128)

        @pl.when(whole)
        def _():
            attend(refs, b * 512, cols, WHOLE)

        @pl.when(jnp.logical_not(whole))
        def _():
            attend(refs, b * 512, cols, SMALL)

    loop(q.shape[1] // 128, pair)

    def back(i):
        r = rows_of(b * 2 + i, 256)
        dn[r, :] = dot_nt(d[0, r, :], w[0]) + dot_nt(d[1, r, :], w[1]) + dot_nt(d[2, r, :], w[2])

    loop(2, back)


def core_call(b, scal, q, k, v, da, w, *before):
    return call(
        functools.partial(core_kernel, b),
        "core",
        (scal, q, k, v, da, w, *before),
        [],
        [kept(q.shape), kept((3, *q.shape)), kept(q.shape, F32)],
        [],
        [],
        10 << 30,
        alias={6 + i: i for i in range(len(before))},
        limit=8,
    )


def attn_grad_kernel(store, scal, xn, o, d, cot, sums, *refs):
    *g_refs, g, sem = refs
    tokens, width = xn.shape

    def grad(b):
        g[b] = dot_tn(xn[...], d[b]).astype(BF16)
        store(scal, g, g_refs, sem, b)

    loop(3, grad)
    g[3] = dot_tn(o[...], cot[...]).astype(BF16)
    store(scal, g, g_refs, sem, 3)
    for i, v in enumerate((d[0], d[2], cot[...])):
        sums[i : i + 1, :] = jnp.sum(v.astype(F32), axis=0, keepdims=True)
    stored(g_refs, sem)


def attn_grad_call(scal, xn, o, d, cot, store, g_shapes):
    tokens, width = xn.shape
    return call(
        functools.partial(attn_grad_kernel, store),
        "attn_grad",
        (scal, xn, o, d, cot),
        [],
        [kept((8, width), F32)],
        g_shapes,
        [pltpu.VMEM((4, width, width), BF16), pltpu.SemaphoreType.DMA((len(g_shapes),))],
        8 * tokens * width * width,
        limit=10,
    )


def gelu_parts(u):
    u2 = u * u
    half = 0.5 * jnp.tanh(u * (GELU_C + (GELU_C * GELU_A) * u2)) + 0.5
    act = u * half
    grad = half + act * (1.0 - half) * (2.0 * GELU_C + (6.0 * GELU_C * GELU_A) * u2)
    return act, grad

def tile_of(t, width):
    return pl.ds(t * width if isinstance(t, int) else pl.multiple_of(t * width, 128), width)


def wait_tile(w, sem, t, width):
    whole_wait(w.at[tile_of(t, width), :], sem.at[t])()


def up_kernel(load, first, count, n_p, *refs):
    scal, xn, bias = refs[:3]
    even, odd, sem = refs[-3:]
    tokens, width = xn.shape
    if n_p:
        act, gp, w = refs[-6:-3]
        load(scal, refs[3 : 3 + n_p], w, sem)
        for t in range(count):
            whole_wait(w.at[t], sem.at[t])()
    else:
        act, gp = refs[-5:-3]
        w = refs[5]
    rows = even.shape[0]
    per = tokens // rows

    def product(i):
        return dot_nn(xn[rows_of(i % per, rows), :], w[first + i // per])

    def finish(i, u):
        t, r = first + i // per, rows_of(i % per, rows)
        a, gr = gelu_parts(u + bias[pl.ds(t, 1), :])
        act[t, r, :] = a.astype(BF16)
        gp[t, r, :] = gr.astype(BF16)

    even[...] = product(0)

    def step(i):
        odd[...] = product(2 * i + 1)
        finish(2 * i, even[...])
        even[...] = product(jnp.minimum(2 * i + 2, count * per - 1))
        finish(2 * i + 1, odd[...])

    loop(count * per // 2, step)
    if n_p:
        for t in range(count, bias.shape[0]):
            whole_wait(w.at[t], sem.at[t])()


def up_call(first, count, scal, xn, bias, before, pieces, load):
    tokens, width = xn.shape
    tiles = bias.shape[0]
    return call(
        functools.partial(up_kernel, load, first, count, len(pieces)),
        "up",
        (scal, xn, bias, *before),
        pieces,
        [kept((tiles, tokens, width))] * 2 + [kept((tiles, width, width))] * (1 if pieces else 0),
        [],
        [pltpu.VMEM((256, width), F32)] * 2 + [pltpu.SemaphoreType.DMA((tiles,))],
        2 * count * tokens * width * width,
        alias={3: 0, 4: 1} if before else None,
        limit=7,
    )


def down_grad_kernel(load, store, n_p, scal, act, cot, *refs):
    w, *g_refs, g, wsem, sem = refs[n_p:]
    tiles, tokens, width = act.shape
    load(scal, refs[:n_p], w, wsem)

    def grad(t):
        g[tile_of(t, width), :] = dot_tn(act[t], cot[...]).astype(BF16)
        store(scal, g, g_refs, sem, t)

    loop(tiles, grad)
    for t in range(tiles):
        wait_tile(w, wsem, t, width)
    stored(g_refs, sem)


def down_grad_call(scal, act, cot, pieces, load, store, g_shapes):
    tiles, tokens, width = act.shape
    return call(
        functools.partial(down_grad_kernel, load, store, len(pieces)),
        "down_grad",
        (scal, act, cot),
        pieces,
        [kept((tiles * width, width))],
        g_shapes,
        [
            pltpu.VMEM((tiles * width, width), BF16),
            pltpu.SemaphoreType.DMA((tiles,)),
            pltpu.SemaphoreType.DMA((len(g_shapes),)),
        ],
        2 * tiles * tokens * width * width,
        limit=12,
    )


def dpre_kernel(scal, cot, gp, w, dpre, sums):
    tiles, tokens, width = gp.shape

    def down(t):
        d = (dot_nt(cot[...], w[tile_of(t, width), :]) * gp[t].astype(F32)).astype(BF16)
        dpre[t] = d
        sums[pl.ds(t, 1), :] = jnp.sum(d.astype(F32), axis=0, keepdims=True)

    loop(tiles, down)


def dpre_call(scal, cot, gp, w):
    tiles, tokens, width = gp.shape
    return call(
        dpre_kernel,
        "dpre",
        (scal, cot, gp, w),
        [],
        [kept(gp.shape), kept((8, width), F32)],
        [],
        [],
        2 * tiles * tokens * width * width,
        alias={2: 0},
        limit=8,
    )


def up_grad_kernel(load, store, n_p, scal, xn, dpre, *refs):
    w, *g_refs, g, wsem, sem = refs[n_p:]
    load(scal, refs[:n_p], w, wsem, (3,))

    def grad(t):
        g[t] = dot_tn(xn[...], dpre[t]).astype(BF16)
        store(scal, g, g_refs, sem, t)

    loop(dpre.shape[0], grad)
    whole_wait(w, wsem.at[3])()
    stored(g_refs, sem)


def up_grad_call(scal, xn, dpre, pieces, load, store, g_shapes):
    tiles, tokens, width = dpre.shape
    return call(
        functools.partial(up_grad_kernel, load, store, len(pieces)),
        "up_grad",
        (scal, xn, dpre),
        pieces,
        [kept((1, width, width))],
        g_shapes,
        [
            pltpu.VMEM((tiles, width, width), BF16),
            pltpu.SemaphoreType.DMA((4,)),
            pltpu.SemaphoreType.DMA((len(g_shapes),)),
        ],
        2 * tiles * tokens * width * width,
        limit=10,
    )


def input_grad_kernel(scal, x, cot, dn, dpre, vec, wu, sums, dx_ref, dx, sem):
    tiles, tokens, width = dpre.shape
    sums[...] = jnp.zeros_like(sums)

    def step(i):
        r = rows_of(i, 256)
        dnr = dn[r, :]
        for t in range(tiles):
            dnr += dot_nt(dpre[t, r, :], wu[t])
        standard, inv = norm_rows(x[r, :])
        sums[0:1, :] += jnp.sum(dnr * standard, axis=0, keepdims=True)
        gs = dnr * vec[0:1, :]
        mean_g = jnp.mean(gs, axis=1, keepdims=True)
        mean_p = jnp.mean(gs * standard, axis=1, keepdims=True)
        dx[r, :] = (cot[r, :].astype(F32) + inv * (gs - mean_g - standard * mean_p)).astype(BF16)

    loop(tokens // 256, step, lambda i: send_rows(dx, dx_ref, i, 256, sem))
    whole_wait(dx_ref, sem)()


def input_grad_call(scal, x, cot, dn, dpre, vec, wu):
    tiles, tokens, width = dpre.shape
    return call(
        input_grad_kernel,
        "input_grad",
        (scal, x, cot, dn, dpre, vec, wu),
        [],
        [kept((8, width), F32)],
        [sds((tokens // 512, 512, width))],
        [pltpu.VMEM((tokens, width), BF16), pltpu.SemaphoreType.DMA],
        2 * (tiles + 3) * tokens * width * width,
        limit=8,
    )


def out_kernel(scal, x, o, act, vec, wo, wd, out_ref, out, sem):
    tiles, tokens, width = act.shape

    def step(i):
        r = rows_of(i, 256)
        total = x[r, :].astype(F32) + vec[3:4, :] + dot_nn(o[r, :], wo[0])
        for t in range(tiles):
            total += dot_nn(act[t, r, :], wd[tile_of(t, width), :])
        out[r, :] = total.astype(BF16)

    loop(tokens // 256, step, lambda i: send_rows(out, out_ref, i, 256, sem))
    whole_wait(out_ref, sem)()


def out_call(scal, x, o, act, vec, wo, wd):
    tiles, tokens, width = act.shape
    (out,) = call(
        out_kernel,
        "out",
        (scal, x, o, act, vec, wo, wd),
        [],
        [],
        [sds((tokens // 512, 512, width))],
        [pltpu.VMEM((tokens, width), BF16), pltpu.SemaphoreType.DMA],
        2 * (tiles + 1) * tokens * width * width,
        limit=8,
    )
    return out


def swap(value, mask):
    return lax.ppermute(value, "wide", [(i, i ^ mask) for i in range(16)])


def swap_y(value):
    return lax.ppermute(value, "narrow", [(0, 1), (1, 0)])


def slots():
    for part in range(2):
        for i in range(2):
            for s in range(2):
                half, side = (i, s) if part == 0 else (s, i)
                for k in range(4):
                    yield part, i, s * 4 + k, half, side, k


def device_of(scal, k, side, core):
    return ((scal[1] ^ k) * 2 + (scal[2] ^ side)) * 2 + (scal[3] ^ core)


def behind(value, *marks):
    return lax.optimization_barrier((value, marks))[0]


def gather_z(value):
    return [swap(value, k << 2) for k in (1, 2, 3)]


def gather_first(za, zb):
    return swap(za, 2), swap_y(zb), swap_y(za), swap(zb, 2)


def gather_second(xa, yb):
    return swap_y(xa), swap(yb, 2)


def pieces_of(za, zb, first, second):
    xa, yb, ya, xb = first
    return [za, xa, ya, second[0], zb, xb, yb, second[1]]


def join_job(values):
    def fn(held, near, outs):
        size = near[0].shape[0]
        for i, v in enumerate(near):
            at = slice(i * size, (i + 1) * size)
            if v.ndim == 3:
                outs[0][at, : v.shape[1], :] = v[...]
            else:
                outs[0][at] = v[...]

    return fn, [], values, [kept((len(values) * values[0].shape[0], *values[0].shape[1:]))]


def mix(name, jobs):
    held = [v for job in jobs for v in job[1]]
    near = [v for job in jobs for v in job[2]]
    outs = [o for job in jobs for o in job[3]]

    def kernel(*refs):
        at = len(near) + len(held)
        scratch = refs[at + len(outs) :]
        copies = [
            pltpu.make_async_copy(refs[len(near) + i].at[:, pl.ds(v[1], v[2])], scratch[i], scratch[-1].at[i])
            for i, v in enumerate(held)
        ]
        for cp in copies:
            cp.start()
        h = n = o = 0
        for fn, job_h, job_n, job_o in jobs:
            for i in range(len(job_h)):
                copies[h + i].wait()
            fn(
                scratch[h : h + len(job_h)],
                refs[n : n + len(job_n)],
                refs[at + o : at + o + len(job_o)],
            )
            h, n, o = h + len(job_h), n + len(job_n), o + len(job_o)

    got = pl.pallas_call(
        kernel,
        name=name,
        out_shape=outs,
        in_specs=[VMEM] * len(near) + [HBM] * len(held),
        out_specs=[VMEM] * len(outs),
        scratch_shapes=[pltpu.VMEM((v.shape[0], size, *v.shape[2:]), v.dtype) for v, _, size in held]
        + [pltpu.SemaphoreType.DMA((max(len(held), 1),))],
        compiler_params=pltpu.CompilerParams(vmem_limit_bytes=8 << 20),
        cost_estimate=pl.CostEstimate(flops=1 << 20, bytes_accessed=1 << 20, transcendentals=0),
    )(
        *[pltpu.with_memory_space_constraint(v, pltpu.VMEM) for v in near],
        *[pltpu.with_memory_space_constraint(v[0], pltpu.HBM) for v in held],
    )
    split, at = [], 0
    for job in jobs:
        split.append(got[at : at + len(job[3])])
        at += len(job[3])
    return split


def total(*parts):
    return sum(v.astype(F32) for v in parts)


def stack_job(values):
    def fn(held, near, outs):
        for k, v in enumerate(near):
            for i in range(2):
                outs[i][k] = v[i]

    return fn, [], list(values), [kept((len(values), *values[0].shape[1:]))] * 2


def vector_job(sums_a, sums_d, sums_x, wide, rows):
    width = sums_a.shape[1]

    def spread(rows_in, per):
        flat = jnp.concatenate([rows_in[w * per // width][None] for w in range(wide)])
        col = lax.broadcasted_iota(jnp.int32, (wide, width), 1)
        own = lax.broadcasted_iota(jnp.int32, (wide, width), 0) * per % width
        flat = jnp.where((col >= own) & (col < own + per), flat, 0.0)
        pick = lax.broadcasted_iota(jnp.int32, (width, per), 0) % per
        pick = (pick == lax.broadcasted_iota(jnp.int32, (width, per), 1)).astype(BF16)
        got = jnp.zeros((wide, per), F32)
        for _ in range(3):
            high = flat.astype(BF16)
            flat = flat - high.astype(F32)
            got += dot_nn(high, pick)
        return got

    def fn(held, near, outs):
        a, d, x, scal = near
        tiles = 4
        at = 0
        for got in (
            spread([x[0]], rows),
            spread([a[0], a[1]], 2 * rows),
            spread([d[t] for t in range(tiles)], tiles * rows),
            spread([a[2]], rows),
        ):
            outs[4][:, at : at + got.shape[1]] = got
            at += got.shape[1]
        for k in range(4):
            outs[k][...] = jnp.zeros_like(outs[k])
            for r in range(4):
                outs[k][r : r + 1, :] = outs[4][pl.ds((scal[1] ^ k) * 4 + r, 1), :]

    return fn, [], [sums_a, sums_d, sums_x], [kept((8, 8 * rows), F32)] * 4 + [kept((wide, 8 * rows), F32)]


def add_job(values):
    def fn(held, near, outs):
        outs[0][...] = sum(near[i][...] for i in range(len(values)))

    return fn, [], list(values), [kept(values[0].shape, F32)]


def vector_job(sums_a, sums_d, sums_x):
    def fn(held, near, outs):
        a, d, x = near
        outs[0][0:1, :] = x[0:1, :]
        outs[0][1:3, :] = a[0:2, :]
        outs[0][3:7, :] = d[0:4, :]
        outs[0][7:8, :] = a[2:3, :]

    return fn, [], [sums_a, sums_d, sums_x], [kept(sums_a.shape, F32)]


def sum1_job(keep1, got1):
    def fn(held, near, outs):
        for i in range(2):
            outs[i][...] = total(held[0][i], near[0][i]).astype(BF16)

    return fn, [(keep1, 0, keep1.shape[1])], [got1], [kept(keep1.shape[1:])] * 2


def sum2_job(keep0, got0, got):
    half = keep0.shape[1] // 2

    def fn(held, near, outs):
        for i in range(2):
            outs[i][...] = total(held[0][i], near[0][i, half:], near[1 + i][half:]).astype(BF16)

    return fn, [(keep0, half, half)], [got0, *got], [kept((half, *keep0.shape[2:]))] * 2


def sum3_job(keep0, got0, got, got2):
    half = keep0.shape[1] // 2

    def fn(held, near, outs):
        for k in range(half):
            for i in range(2):
                outs[k][i] = total(held[0][i, k], near[0][i, k], near[1 + i][k], near[3 + i][k]).astype(BF16)

    return fn, [(keep0, 0, half)], [got0, *got, *got2], [kept((2, *keep0.shape[2:]))] * half


def sum4_job(own, got):
    def fn(held, near, outs):
        outs[0][...] = total(*[near[i][...] for i in range(1 + len(got))]).astype(BF16)

    return fn, [], [own, *got], [kept(own.shape)]


def place_kernel(scal, a_mine, a_other, d_mine, d_other, joined_ref, out, down, joined, sem):
    _, rows, width = a_mine.shape

    def place(half, a, d):
        for p in range(2):
            block = half * 2 + p
            down[pl.ds(block * rows, rows), :] = d[p].astype(F32)
            if block < 3:
                joined[block] = a[p].astype(F32)
                dst = joined_ref.at[:, block * width : (block + 1) * width]
                pltpu.make_async_copy(joined.at[block], dst, sem).start()
            else:
                out[...] = a[p].astype(F32)

    @pl.when(scal[0] == 0)
    def _():
        place(0, a_mine, d_mine)
        place(1, a_other, d_other)

    @pl.when(scal[0] != 0)
    def _():
        place(1, a_mine, d_mine)
        place(0, a_other, d_other)

    whole_wait(joined, sem)()


def place_call(scal, parts):
    _, rows, width = parts[0].shape
    return pl.pallas_call(
        place_kernel,
        name="place",
        out_shape=[sds((rows, 7 * width), F32), sds((rows, width), F32), sds((4 * rows, width), F32)],
        in_specs=[SMEM] + [VMEM] * 4,
        out_specs=[HBM, VMEM, VMEM],
        scratch_shapes=[pltpu.VMEM((3, rows, width), F32), pltpu.SemaphoreType.DMA],
        compiler_params=pltpu.CompilerParams(vmem_limit_bytes=8 << 20),
    )(scal, *[pltpu.with_memory_space_constraint(v, pltpu.VMEM) for v in parts])


def place_last_kernel(scal, placed, mine, other, v0, v1, v2, v3, joined_ref, gain, b_attn, b_mlp, b_out, wide, sem):
    _, rows, width = other.shape
    for i, ref in enumerate((mine, other)):
        for p in range(2):
            wide[i * 2 + p] = ref[p].astype(F32)
            at = pl.multiple_of((3 + (scal[0] ^ i) * 2 + p) * width, 128)
            pltpu.make_async_copy(wide.at[i * 2 + p], joined_ref.at[:, pl.ds(at, width)], sem).start()
    total = (v0[...] + v1[...]) + (v2[...] + v3[...])
    row = lax.broadcasted_iota(jnp.int32, total.shape, 0)
    dev = (scal[1] * 2 + scal[2]) * 2 + scal[3]
    for first, out in ((0, gain), (1, b_attn), (3, b_mlp), (7, b_out)):
        per = out.shape[0]
        share = width // per
        line = jnp.sum(jnp.where(row == first + dev // share, total, 0.0), axis=0, keepdims=True)
        line = jnp.broadcast_to(line, total.shape)
        line = pltpu.roll(line, (share - dev % share) % share * per, 1)
        out[...] = line[0, :per]
    whole_wait(wide, sem)()


def place_last_call(scal, placed, mine, other, vectors):
    _, rows, width = other.shape
    near = [pltpu.with_memory_space_constraint(v, pltpu.VMEM) for v in (mine, other, *vectors)]
    return pl.pallas_call(
        place_last_kernel,
        name="place_last",
        out_shape=[sds(placed.shape, F32)] + [sds((n * rows,), F32) for n in (1, 2, 4, 1)],
        in_specs=[SMEM, HBM] + [VMEM] * 6,
        out_specs=[HBM] + [VMEM] * 4,
        scratch_shapes=[pltpu.VMEM((4, *other.shape[1:]), F32), pltpu.SemaphoreType.DMA],
        compiler_params=pltpu.CompilerParams(vmem_limit_bytes=8 << 20),
        input_output_aliases={1: 0},
    )(scal, placed, *near)


def whole_wait(ref, sem):
    return pltpu.make_async_copy(ref, ref, sem).wait


def piece(refs, at, core, k, alone):
    if core == 0:
        return refs[at].at[k]
    if at in alone:
        return refs[9 + alone.index(at)].at[k]
    return refs[8].at[(at - sum(i < at for i in alone)) * 4 + k]


def load_columns(scal, refs, w, sem, blocks=(0, 1, 2, 3)):
    rows = w.shape[1] // 16

    def start(own):
        for block in blocks:
            for core in range(2):
                for part, _, _, half, side, k in slots():
                    if (own ^ half) * 2 + part != block:
                        continue
                    src = piece(refs, part * 4 + half * 2 + side, core, k, (3, 7)).at[pl.ds(0, rows), :]
                    dst = w.at[blocks.index(block), rows_at(device_of(scal, k, side, core) * rows, rows), :]
                    pltpu.make_async_copy(src, dst, sem.at[block]).start()

    @pl.when(scal[0] == 0)
    def _():
        start(0)

    @pl.when(scal[0] != 0)
    def _():
        start(1)


def load_half(which):
    def load(scal, refs, w, sem):
        def start(rel):
            for block in range(4):
                for core in range(2):
                    for part, _, _, half, side, k in slots():
                        src = piece(refs, part * 4 + half * 2 + side, core, k, (0, 4))
                        per, rows, width = src.shape
                        if half != rel or block // per != part:
                            continue
                        dev = device_of(scal, k, side, core)
                        if which == 0:
                            dst, tile = w.at[block, rows_at(dev * rows, rows), :], block
                        else:
                            dst, tile = w.at[rows_at((dev * 2 * per + block) * rows, rows), :], scal[1] ^ k
                        pltpu.make_async_copy(src.at[block % per], dst, sem.at[tile]).start()

        @pl.when(scal[0] == which)
        def _():
            start(0)

        @pl.when(scal[0] != which)
        def _():
            start(1)

    return load


def read_vectors(scal, refs, vec, b_mlp, buf, sem):
    width = vec.shape[1]
    rows = width // 16
    for core in range(2):
        for side in range(2):
            for k in range(4):
                src = piece(refs, side, core, k, (3, 7)).at[pl.ds(rows, 8), :]
                pltpu.make_async_copy(src, buf.at[device_of(scal, k, side, core)], sem).start()
    yield
    whole_wait(buf, sem)()
    values = buf[:, 0, :].astype(F32)
    devices = values.shape[0]

    def line(at, per):
        pick = lax.broadcasted_iota(jnp.int32, (per, width), 1) % per
        pick = (pick == lax.broadcasted_iota(jnp.int32, (per, width), 0)).astype(BF16)
        flat = dot_nn(values[:, at : at + per].astype(BF16), pick)
        dev = lax.broadcasted_iota(jnp.int32, flat.shape, 0)
        col = lax.broadcasted_iota(jnp.int32, flat.shape, 1)
        count = devices * per // width
        share = devices // count
        keep = col // per == dev % share
        return [
            jnp.sum(jnp.where(keep & (dev // share == i), flat, 0.0), axis=0, keepdims=True) for i in range(count)
        ]

    lines = line(0, rows) + line(rows, 2 * rows) + line(7 * rows, rows)
    vec[...] = jnp.zeros_like(vec)
    for i, v in enumerate(lines):
        vec[i : i + 1, :] = v
    for i, v in enumerate(line(3 * rows, 4 * rows)):
        b_mlp[i : i + 1, :] = v
    yield


def rows_at(base, rows):
    return pl.ds(pl.multiple_of(base, 16), rows)


def stored(refs, sem):
    for i, r in enumerate(refs):
        whole_wait(r, sem.at[i])()


def store_block(scal, g, refs, sem, t):
    half, part = scal[0] ^ (t // 2), t % 2
    rows = refs[0].shape[2]

    def send(at, core, side, k, slot, p):
        src = g.at[t, rows_at(device_of(scal, k, side, core) * rows, rows), :]
        pltpu.make_async_copy(src, refs[at].at[p, slot], sem.at[at]).start()

    for i in range(2):

        @pl.when((part == 0) & (half == i))
        def _(i=i):
            for core in range(2):
                for side in range(2):
                    for k in range(4):
                        send(core * 2 + i, core, side, k, side * 4 + k, 0)

    @pl.when(part == 1)
    def _():
        for core in range(2):
            for side in range(2):
                for k in range(4):
                    send(core * 2 + side, core, side, k, half * 4 + k, 1)


def store_rows(scal, g, refs, sem, t):
    k = scal[1] ^ t
    rows = refs[0].shape[2]
    for core in range(2):
        for side in range(2):
            dev = (t * 2 + (scal[2] ^ side)) * 2 + (scal[3] ^ core)
            for half in range(2):
                for part in range(2):
                    i, s = (half, side) if part == 0 else (side, half)
                    at = core * 2 + i
                    src = g.at[rows_at((dev * 4 + (scal[0] ^ half) * 2 + part) * rows, rows), :]
                    pltpu.make_async_copy(src, refs[at].at[part, s * 4 + k], sem.at[at]).start()


def load_whole_blocks(scal, refs, w, sem, blocks=(0, 1, 2, 3)):
    for i, b in enumerate(blocks):
        pltpu.make_async_copy(refs[b], w.at[i], sem.at[b]).start()


def load_whole_rows(scal, refs, w, sem):
    width = w.shape[1]
    for t in range(w.shape[0] // width):
        r = tile_of(t, width)
        pltpu.make_async_copy(refs[0].at[r, :], w.at[r, :], sem.at[t]).start()


def store_whole_blocks(scal, g, refs, sem, t):
    for i, r in enumerate(refs):

        @pl.when(t == i)
        def _(i=i, r=r):
            pltpu.make_async_copy(g.at[i], r, sem.at[i]).start()


def store_whole_rows(scal, g, refs, sem, t):
    r = tile_of(t, g.shape[1])
    pltpu.make_async_copy(g.at[r, :], refs[0].at[r, :], sem.at[0]).start()


def body(sizes, tokens, image_ids, cotangent, w_joined, w_out, w_mlp, norm_gain, bias_attn, bias_mlp, bias_out):
    micro, length, width = tokens.shape
    narrow, wide = sizes
    paired = narrow == 2 and wide == 16
    rows = width // wide
    tiles = w_mlp.shape[0] // rows
    x = tokens.reshape(micro * length, width)
    cot = cotangent.reshape(micro * length, width)
    n = lax.axis_index("narrow")
    w = lax.axis_index("wide")
    last = image_ids.reshape(-1, 512)[:, -1]
    scal = [n, w >> 2, (w >> 1) & 1, w & 1] + [jnp.int32(0)] * 4 + [last[b] for b in range(last.shape[0])]
    scal = jnp.stack([jnp.asarray(s, jnp.int32) for s in scal])
    vec_own = jnp.concatenate([norm_gain, bias_attn, bias_mlp, bias_out])

    def vectors(vec):
        vec = vec.astype(F32)
        b_at = 3 * rows
        b_mlp = vec[:, b_at : b_at + tiles * rows].reshape(tiles, width)
        head = [
            vec[:, :rows].reshape(1, width),
            vec[:, rows:b_at].reshape(2, width),
            vec[:, b_at + tiles * rows :].reshape(1, width),
            jnp.zeros((4, width), F32),
        ]
        return jnp.concatenate(head), b_mlp

    def vector_grads(sums_a, sums_d, sums_x):
        return jnp.concatenate(
            [
                sums_x[0].reshape(wide, rows),
                sums_a[:2].reshape(wide, 2 * rows),
                sums_d[:tiles].reshape(wide, tiles * rows),
                sums_a[2].reshape(wide, rows),
            ],
            axis=1,
        )

    if not paired:
        full = lax.all_gather(w_joined, "wide", axis=0, tiled=True)
        parts = [full[:, i * width : (i + 1) * width] for i in range(3 + tiles)]
        attn_w = parts[:3] + [lax.all_gather(w_out, "wide", axis=0, tiled=True)]
        up_w = parts[3:]
        down_w = [lax.all_gather(w_mlp, "wide", axis=0, tiled=True)]
        vec, b_mlp = vectors(lax.all_gather(vec_own, "wide", axis=0))
        square = [sds((width, width))]
        xn, q, k, v, da, wa = project_call(scal, x, cot, vec, attn_w, load_whole_blocks)
        part = core_call(0, scal, q, k, v, da, wa)
        for b in range(1, last.shape[0]):
            part = core_call(b, scal, q, k, v, da, wa, *part)
        o, d, dn = part
        sums_a, *g_attn = attn_grad_call(scal, xn, o, d, cot, store_whole_blocks, square * 4)
        act, gp, wu = up_call(0, tiles // 2, scal, xn, b_mlp, (), up_w, load_whole_blocks)
        act, gp = up_call(tiles // 2, tiles - tiles // 2, scal, xn, b_mlp, (act, gp, wu), [], None)
        wd, *g_down = down_grad_call(
            scal, act, cot, down_w, load_whole_rows, store_whole_rows, [sds((tiles * width, width))]
        )
        dpre, sums_d = dpre_call(scal, cot, gp, wd)
        wo, *g_up = up_grad_call(scal, xn, dpre, attn_w, load_whole_blocks, store_whole_blocks, square * tiles)
        sums_x, d_x = input_grad_call(scal, x, cot, dn, dpre, vec, wu)
        out = out_call(scal, x, o, act, vec, wo, wd)

        def reduce(g):
            g = lax.psum_scatter(g.astype(F32), "wide", scatter_dimension=0, tiled=True)
            return lax.psum(g, "narrow")

        grad_joined = reduce(jnp.concatenate([*g_attn[:3], *g_up], axis=1))
        grad_out = reduce(g_attn[3])
        grad_mlp = reduce(g_down[0])
        vg = reduce(vector_grads(sums_a, sums_d, sums_x))[0]
        vg = jnp.split(vg, [rows, 3 * rows, (3 + tiles) * rows])
    else:
        col = lambda i: w_joined[:, i * width : (i + 1) * width]
        pair = lambda f: jnp.stack([jnp.where(n == 0, f(0), f(2)), jnp.where(n == 0, f(1), f(3))])
        half_a, half_b = [jnp.where(n == 0, f, g) for f, g in ((col(0), col(2)), (col(1), w_out))]
        v_rows = jnp.pad(vec_own, (0, width - vec_own.shape[0]))
        half = jnp.concatenate([half_a, jnp.broadcast_to(v_rows, (8, width)), half_b])
        got = gather_z(half)
        za = jnp.stack([t[: rows + 8] for t in (half, *got)])
        zb = jnp.stack([t[rows + 8 :] for t in (half, *got)])
        c_half = jnp.stack([jnp.where(n == 0, col(3 + t), w_mlp[t * rows : (t + 1) * rows]) for t in range(tiles)])
        c_half = behind(c_half.reshape(2, tiles // 2, rows, width), za, zb)
        first = gather_first(za, zb)
        c2 = swap(c_half, 8)
        first, c2, c_half = lax.optimization_barrier((first, c2, c_half))
        second = gather_second(*first[:2])
        own = pieces_of(za, zb, first, second)
        ((joined,),) = mix("join_a", [join_job([own[i] for i in (0, 1, 2, 4, 5, 6)])])
        joined, c1, c3 = swap(joined, 1), swap(c_half, 4), swap(c_half, 12)
        second, joined, c1, c3 = lax.optimization_barrier((second, joined, c1, c3))
        own = pieces_of(za, zb, first, second)
        attn_w = [*own, joined, swap(second[0], 1), swap(second[1], 1)]
        cza, czb = [jnp.stack([t[i] for t in (c_half, c1, c2, c3)]) for i in range(2)]
        c_xa, c_yb = swap(cza, 2), swap_y(czb)
        x_p, attn_w, cza, czb = lax.optimization_barrier((x, attn_w, cza, czb))
        c_first = (c_xa, c_yb, swap_y(cza), swap(czb, 2))
        xn, q, k, v, da, wa, vec, b_mlp = project_call(scal, x_p, cot, None, attn_w, load_columns, read_vectors)
        part = core_call(0, scal, q, k, v, da, wa)

        part, c_xa, c_yb, z_a, czb_b = lax.optimization_barrier((part, *c_first[:2], swap(cza, 1), czb))
        c_second = gather_second(c_xa, c_yb)
        czs = [z_a, swap(czb_b, 1)]
        o, d, dn = core_call(1, scal, q, k, v, da, wa, *part)

        d, c_second, czs, c_first = lax.optimization_barrier((d, c_second, czs, (c_xa, c_yb, *c_first[2:])))
        c_own = pieces_of(cza, czb, c_first, c_second)
        ((c_joined,),) = mix("join_c", [join_job([t for t in c_own if t is not cza and t is not czb])])
        d, c_joined = lax.optimization_barrier((d, c_joined))
        c_other = swap(c_joined, 1)
        attn_shapes = [sds((2, 8, rows, width))] * 4
        sums_a, *ga = attn_grad_call(scal, xn, o, d, cot, store_block, attn_shapes)

        c_other, ga = behind((c_other, ga), sums_a)
        xn_u, ga, c_own, c_other = lax.optimization_barrier((xn, ga, c_own, c_other))
        a_got1, a_got0 = swap(ga[3], 1), swap(ga[2], 1)
        half_tiles = tiles // 2
        c_all = [*c_own, c_other, *czs]
        act, gp, wu = up_call(0, half_tiles, scal, xn_u, b_mlp, (), c_all, load_half(0))

        a_got1, a_got0 = behind((a_got1, a_got0), gp)
        ((sa, sb),) = mix("sums_1", [sum1_job(ga[1], a_got1)])
        act, sa, sb = lax.optimization_barrier((act, sa, sb))
        a_xy = swap_y(sa), swap(sb, 2)
        act, gp = up_call(half_tiles, half_tiles, scal, xn_u, b_mlp, (act, gp, wu), [], None)
        wd, *gd = down_grad_call(
            scal, act, cot, c_all, load_half(1), store_rows, attn_shapes
        )

        a_xy = behind(a_xy, gd)
        ((sa, sb),) = mix("sums_2", [sum2_job(ga[0], a_got0, a_xy)])
        gp, sa, sb, gd = lax.optimization_barrier((gp, sa, sb, gd))
        a_yx = swap(sa, 2), swap_y(sb)
        d_got1, d_got0 = swap(gd[3], 1), swap(gd[2], 1)
        dpre, sums_d = dpre_call(scal, cot, gp, wd)

        a_yx, d_got1, d_got0 = behind((a_yx, d_got1, d_got0), dpre)
        a_t, (sa, sb) = mix("sums_3", [sum3_job(ga[0], a_got0, a_xy, a_yx), sum1_job(gd[1], d_got1)])
        dpre_g, a_t, sa, sb = lax.optimization_barrier((dpre, a_t, sa, sb))
        d_xy = swap_y(sa), swap(sb, 2)
        a_z = [swap(a_t[k], k << 2) for k in (1, 2, 3)]
        wo, *gu = up_grad_call(scal, xn, dpre_g, attn_w, load_columns, store_block, attn_shapes)

        a_z, d_xy = behind((a_z, d_xy), gu)
        (a_sum,), (sa, sb) = mix("sums_4", [sum4_job(a_t[0], a_z), sum2_job(gd[0], d_got0, d_xy)])
        x_i, sa, sb, gu, a_sum = lax.optimization_barrier((x, sa, sb, gu, a_sum))
        u_got1, u_got0 = swap(gu[3], 1), swap(gu[2], 1)
        d_yx = swap(sa, 2), swap_y(sb)
        a_other = swap_y(a_sum)
        sums_x, d_x = input_grad_call(scal, x_i, cot, dn, dpre, vec, wu)

        d_yx, u_got1, u_got0, a_other = behind((d_yx, u_got1, u_got0, a_other), d_x)
        (sa, sb), d_t, (v_own,) = mix(
            "sums_5",
            [
                sum1_job(gu[1], u_got1),
                sum3_job(gd[0], d_got0, d_xy, d_yx),
                vector_job(sums_a, sums_d, sums_x),
            ],
        )
        x_o, sa, sb, d_t = lax.optimization_barrier((x, sa, sb, d_t))
        u_xy = swap_y(sa), swap(sb, 2)
        d_z = [swap(d_t[k], k << 2) for k in (1, 2, 3)]
        out = out_call(scal, x_o, o, act, vec, wo, wd)

        u_xy, d_z, v_own = behind((u_xy, d_z, v_own), out)
        (sa, sb), (d_sum,) = mix("sums_6", [sum2_job(gu[0], u_got0, u_xy), sum4_job(d_t[0], d_z)])
        sa, sb, d_sum, v_own = lax.optimization_barrier((sa, sb, d_sum, v_own))
        u_yx = swap(sa, 2), swap_y(sb)
        v_got = [swap(v_own, k << 2) for k in (1, 2, 3)]
        u_t, (v_sum,) = mix("sums_7", [sum3_job(gu[0], u_got0, u_xy, u_yx), add_job([v_own, *v_got])])
        u_t, v_sum, d_sum = lax.optimization_barrier((u_t, v_sum, d_sum))
        u_z = [swap(u_t[k], k << 2) for k in (1, 2, 3)]
        v_other, d_other = swap_y(v_sum), swap_y(d_sum)
        placed, grad_out, grad_mlp = place_call(scal, [a_sum, a_other, d_sum, d_other])
        u_z, placed = lax.optimization_barrier((u_z, placed))
        (u_sum,), (v_sum,) = mix("sums_8", [sum4_job(u_t[0], u_z), add_job([v_sum, v_other])])
        u_other = swap_y(u_sum)
        v_all = [v_sum, *[swap(v_sum, i) for i in (1, 2, 3)]]
        grad_joined, *vg = place_last_call(scal, placed, u_sum, u_other, v_all)
    return (out.reshape(tokens.shape), d_x.reshape(tokens.shape), grad_joined, grad_out, grad_mlp, *vg)


def solution(mesh):
    sizes = (mesh.shape["narrow"], mesh.shape["wide"])
    rows = P(None, ("narrow", "wide"), None)
    placed = (rows, P(None, ("narrow", "wide")), rows) + (P("wide", None),) * 3 + (P("wide"),) * 4
    return jax.shard_map(
        functools.partial(body, sizes),
        mesh=mesh,
        in_specs=placed,
        out_specs=(rows, rows) + (P("wide", None),) * 3 + (P("wide"),) * 4,
        check_vma=False,
    )
```

```python
import functools

import jax
import jax.numpy as jnp
from jax import lax
from jax.experimental import pallas as pl
from jax.experimental.pallas import tpu as pltpu
from jax.sharding import PartitionSpec as P

HEADS = 12
HEAD = 64
IMG = 196
EPS = 1e-06
GELU_C = 0.7978845608028654
GELU_A = 0.044715

F32 = jnp.float32
BF16 = jnp.bfloat16
HBM = pl.BlockSpec(memory_space=pltpu.HBM)
VMEM = pl.BlockSpec(memory_space=pltpu.VMEM)
SMEM = pl.BlockSpec(memory_space=pltpu.SMEM)


def dot_nn(a, b):
    return lax.dot_general(a, b, (((1,), (0,)), ((), ())), preferred_element_type=F32)


def dot_nt(a, b):
    return lax.dot_general(a, b, (((1,), (1,)), ((), ())), preferred_element_type=F32)


def dot_tn(a, b):
    return lax.dot_general(a, b, (((0,), (0,)), ((), ())), preferred_element_type=F32)


def norm_rows(rows):
    rows = rows.astype(F32)
    mean = jnp.mean(rows, axis=1, keepdims=True)
    centered = rows - mean
    inv = lax.rsqrt(jnp.mean(centered * centered, axis=1, keepdims=True) + EPS)
    return centered * inv, inv


def attend(refs, base, cols, windows):
    q_ref, k_ref, v_ref, da_ref, o_ref, dq_ref, dk_ref, dv_ref = refs
    zero = jnp.zeros((), BF16)
    jobs, ends = [], {}
    for start, rows, lo, hi, merge in windows:
        win = pl.ds(pl.multiple_of(base + start, 16), rows)
        tiles = [r[win, cols] for r in (q_ref, k_ref, v_ref, da_ref)]
        lane = lax.broadcasted_iota(jnp.int32, (rows, 128), 1)
        sums = {}
        step = 256 if rows == 512 else rows
        for at in range(0, rows, step):
            for h in range(2):
                keep = (lane < 64) if h == 0 else (lane >= 64)
                heads = [jnp.where(keep, t, zero) for t in tiles]
                jobs.append([tiles, heads, rows, lo, hi, at, step, sums])
        ends[len(jobs) - 1] = (start, rows, merge, sums)

    def products(job):
        tiles, heads, _, _, _, at, step, _ = job
        qs = slice(at, at + step)
        job += [dot_nt(tiles[1], heads[0][qs]), dot_nt(tiles[2], heads[3][qs])]

    def soften(job):
        _, _, rows, lo, hi, at, step, _, s, dp = job
        masked = lo > 0 or hi < rows
        if masked:
            key = lax.broadcasted_iota(jnp.int32, (rows, step), 0)
            s = jnp.where((key >= lo) & (key < hi), s, -1e30)
        e = jnp.exp(s - jnp.max(s, axis=0, keepdims=True))
        scale = 1.0 / jnp.sum(e, axis=0, keepdims=True)
        if masked:
            query = lax.broadcasted_iota(jnp.int32, (1, step), 1) + at
            scale = jnp.where((query >= lo) & (query < hi), scale, 0.0)
        p = e * scale
        inner = jnp.sum(p * dp, axis=0, keepdims=True)
        job[8:] = [p.astype(BF16), (p * (dp - inner)).astype(BF16)]

    def gather(job):
        _, heads, _, _, _, at, step, sums, p, ds = job
        qs = slice(at, at + step)
        parts = (
            (("o", at), dot_tn(p, heads[2])),
            (("q", at), dot_tn(ds, heads[1])),
            (("v", 0), dot_nn(p, heads[3][qs])),
            (("k", 0), dot_nn(ds, heads[0][qs])),
        )
        for key, val in parts:
            sums[key] = sums[key] + val if key in sums else val

    def write(start, rows, merge, sums):
        for name, ref in (("o", o_ref), ("q", dq_ref), ("k", dk_ref), ("v", dv_ref)):
            for (n, at), val in sums.items():
                if n != name:
                    continue
                val = (val * 0.125 if n == "q" else val).astype(BF16)
                size = val.shape[0]
                if merge and at == 0:
                    head = pl.ds(pl.multiple_of(base + start, 16), merge)
                    ref[head, cols] = ref[head, cols] + val[:merge]
                    val, at, size = val[merge:], merge, size - merge
                ref[pl.ds(pl.multiple_of(base + start + at, 16), size), cols] = val

    for i in range(len(jobs) + 2):
        if i < len(jobs):
            products(jobs[i])
        if 0 <= i - 1 < len(jobs):
            soften(jobs[i - 1])
        if 0 <= i - 2:
            gather(jobs[i - 2])
            if i - 2 in ends:
                write(*ends[i - 2])


WHOLE = ((0, 512, 0, 512, 0),)
SMALL = (
    (0, 208, 0, IMG, 0),
    (192, 208, IMG - 192, 2 * IMG - 192, 16),
    (384, 128, 2 * IMG - 384, 128, 16),
)


def sds(shape, dtype=BF16):
    return jax.ShapeDtypeStruct(shape, dtype)


def kept(shape, dtype=BF16):
    return pltpu.VMEM(shape, dtype)


def call(kernel, name, operands, pieces, outs, g_shapes, scratch, flops, limit=14, alias=None):
    n_p, n_g = len(pieces), len(g_shapes)
    scal, *rest = operands
    rest = [pltpu.with_memory_space_constraint(v, pltpu.VMEM) for v in rest]
    pieces = [pltpu.with_memory_space_constraint(v, pltpu.HBM) for v in pieces]
    g_shapes = [pltpu.HBM(g.shape, g.dtype) for g in g_shapes]
    return pl.pallas_call(
        kernel,
        name=name,
        out_shape=list(outs) + list(g_shapes),
        in_specs=[SMEM] + [VMEM] * len(rest) + [HBM] * n_p,
        out_specs=[VMEM] * len(outs) + [HBM] * n_g,
        scratch_shapes=scratch,
        compiler_params=pltpu.CompilerParams(vmem_limit_bytes=limit << 20),
        input_output_aliases=alias or {},
        cost_estimate=pl.CostEstimate(flops=flops, bytes_accessed=1 << 20, transcendentals=0),
    )(scal, *rest, *pieces)


def loop(count, fn, after=None):
    def step(i, c):
        fn(i)
        if after is not None:
            after(i)
        return c

    lax.fori_loop(0, count, step, 0)


def send_rows(src, dst, i, size, sem):
    per = dst.shape[1] // size
    pltpu.make_async_copy(src.at[rows_of(i, size), :], dst.at[i // per, rows_of(i % per, size), :], sem).start()


def rows_of(i, size):
    return pl.ds(pl.multiple_of(i * size, size), size)


def project_kernel(load, read, n_w, *refs):
    n_v = 0 if read else 1
    scal, x_ref, cot_ref = refs[:3]
    w_refs = refs[3 + n_v : 3 + n_v + n_w]
    xn, q, k, v, da, w, *rest = refs[3 + n_v + n_w :]
    sem = rest[-1]
    if read:
        vec_ref, b_mlp, buf, vsem = rest[:4]
        steps = read(scal, w_refs, vec_ref, b_mlp, buf, vsem)
        next(steps)
        load(scal, w_refs, w, sem)
        next(steps)
    else:
        vec_ref = refs[3]
        load(scal, w_refs, w, sem)
    tokens = x_ref.shape[0]

    def norm(i):
        r = rows_of(i, 256)
        standard, _ = norm_rows(x_ref[r, :])
        xn[r, :] = (standard * vec_ref[0:1, :]).astype(BF16)

    loop(tokens // 256, norm)

    def ready(i):
        whole_wait(w.at[i], sem.at[i])()

    def each(fn):
        loop(tokens // 512, lambda i: fn(rows_of(i, 512)))

    def queries(r):
        q[r, :] = (dot_nn(xn[r, :], w[0]) + vec_ref[1:2, :]).astype(BF16) * jnp.asarray(0.125, BF16)

    def keys(r):
        k[r, :] = dot_nn(xn[r, :], w[1]).astype(BF16)

    def values(r):
        v[r, :] = (dot_nn(xn[r, :], w[2]) + vec_ref[2:3, :]).astype(BF16)

    def attended(r):
        da[r, :] = dot_nt(cot_ref[r, :], w[3]).astype(BF16)

    for i, fn in enumerate((queries, keys, values, attended)):
        ready(i)
        each(fn)


def project_call(scal, x, cot, vec, weights, load, read=None):
    tokens, width = x.shape
    return call(
        functools.partial(project_kernel, load, read, len(weights)),
        "project",
        (scal, x, cot) if read else (scal, x, cot, vec),
        weights,
        [kept(x.shape)] * 5
        + [kept((4, width, width))]
        + ([kept((8, width), F32), kept((4, width), F32)] if read else []),
        [],
        ([pltpu.VMEM((16, 8, width), BF16), pltpu.SemaphoreType.DMA] if read else [])
        + [pltpu.SemaphoreType.DMA((4,))],
        8 * tokens * width * width,
        limit=10,
    )


def core_kernel(b, scal, q, k, v, da, w, *refs):
    o, d, dn = refs[-3:]
    refs = (q, k, v, da, o, d.at[0], d.at[1], d.at[2])
    whole = scal[8 + b] == 0

    def pair(i):
        cols = pl.ds(pl.multiple_of(i * 128, 128), 128)

        @pl.when(whole)
        def _():
            attend(refs, b * 512, cols, WHOLE)

        @pl.when(jnp.logical_not(whole))
        def _():
            attend(refs, b * 512, cols, SMALL)

    loop(q.shape[1] // 128, pair)

    def back(i):
        r = rows_of(b * 2 + i, 256)
        dn[r, :] = dot_nt(d[0, r, :], w[0]) + dot_nt(d[1, r, :], w[1]) + dot_nt(d[2, r, :], w[2])

    loop(2, back)


def core_call(b, scal, q, k, v, da, w, *before):
    return call(
        functools.partial(core_kernel, b),
        "core",
        (scal, q, k, v, da, w, *before),
        [],
        [kept(q.shape), kept((3, *q.shape)), kept(q.shape, F32)],
        [],
        [],
        10 << 30,
        alias={6 + i: i for i in range(len(before))},
        limit=8,
    )


def attn_grad_kernel(store, scal, xn, o, d, cot, sums, *refs):
    *g_refs, g, sem = refs
    tokens, width = xn.shape

    def grad(b):
        g[b] = dot_tn(xn[...], d[b]).astype(BF16)
        store(scal, g, g_refs, sem, b)

    loop(3, grad)
    g[3] = dot_tn(o[...], cot[...]).astype(BF16)
    store(scal, g, g_refs, sem, 3)
    for i, v in enumerate((d[0], d[2], cot[...])):
        sums[i : i + 1, :] = jnp.sum(v.astype(F32), axis=0, keepdims=True)
    stored(g_refs, sem)


def attn_grad_call(scal, xn, o, d, cot, store, g_shapes):
    tokens, width = xn.shape
    return call(
        functools.partial(attn_grad_kernel, store),
        "attn_grad",
        (scal, xn, o, d, cot),
        [],
        [kept((8, width), F32)],
        g_shapes,
        [pltpu.VMEM((4, width, width), BF16), pltpu.SemaphoreType.DMA((len(g_shapes),))],
        8 * tokens * width * width,
        limit=10,
    )


def gelu_parts(u):
    u2 = u * u
    half = 0.5 * jnp.tanh(u * (GELU_C + (GELU_C * GELU_A) * u2)) + 0.5
    act = u * half
    grad = half + act * (1.0 - half) * (2.0 * GELU_C + (6.0 * GELU_C * GELU_A) * u2)
    return act, grad

def tile_of(t, width):
    return pl.ds(t * width if isinstance(t, int) else pl.multiple_of(t * width, 128), width)


def wait_tile(w, sem, t, width):
    whole_wait(w.at[tile_of(t, width), :], sem.at[t])()


def up_kernel(load, first, count, n_p, *refs):
    scal, xn, bias = refs[:3]
    even, odd, sem = refs[-3:]
    tokens, width = xn.shape
    if n_p:
        act, gp, w = refs[-6:-3]
        load(scal, refs[3 : 3 + n_p], w, sem)
        for t in range(count):
            whole_wait(w.at[t], sem.at[t])()
    else:
        act, gp = refs[-5:-3]
        w = refs[5]
    rows = even.shape[0]
    per = tokens // rows

    def product(i):
        return dot_nn(xn[rows_of(i % per, rows), :], w[first + i // per])

    def finish(i, u):
        t, r = first + i // per, rows_of(i % per, rows)
        a, gr = gelu_parts(u + bias[pl.ds(t, 1), :])
        act[t, r, :] = a.astype(BF16)
        gp[t, r, :] = gr.astype(BF16)

    even[...] = product(0)

    def step(i):
        odd[...] = product(2 * i + 1)
        finish(2 * i, even[...])
        even[...] = product(jnp.minimum(2 * i + 2, count * per - 1))
        finish(2 * i + 1, odd[...])

    loop(count * per // 2, step)
    if n_p:
        for t in range(count, bias.shape[0]):
            whole_wait(w.at[t], sem.at[t])()


def up_call(first, count, scal, xn, bias, before, pieces, load):
    tokens, width = xn.shape
    tiles = bias.shape[0]
    return call(
        functools.partial(up_kernel, load, first, count, len(pieces)),
        "up",
        (scal, xn, bias, *before),
        pieces,
        [kept((tiles, tokens, width))] * 2 + [kept((tiles, width, width))] * (1 if pieces else 0),
        [],
        [pltpu.VMEM((256, width), F32)] * 2 + [pltpu.SemaphoreType.DMA((tiles,))],
        2 * count * tokens * width * width,
        alias={3: 0, 4: 1} if before else None,
        limit=7,
    )


def down_grad_kernel(load, store, n_p, scal, act, cot, *refs):
    w, *g_refs, g, wsem, sem = refs[n_p:]
    tiles, tokens, width = act.shape
    load(scal, refs[:n_p], w, wsem)

    def grad(t):
        g[tile_of(t, width), :] = dot_tn(act[t], cot[...]).astype(BF16)
        store(scal, g, g_refs, sem, t)

    loop(tiles, grad)
    for t in range(tiles):
        wait_tile(w, wsem, t, width)
    stored(g_refs, sem)


def down_grad_call(scal, act, cot, pieces, load, store, g_shapes):
    tiles, tokens, width = act.shape
    return call(
        functools.partial(down_grad_kernel, load, store, len(pieces)),
        "down_grad",
        (scal, act, cot),
        pieces,
        [kept((tiles * width, width))],
        g_shapes,
        [
            pltpu.VMEM((tiles * width, width), BF16),
            pltpu.SemaphoreType.DMA((tiles,)),
            pltpu.SemaphoreType.DMA((len(g_shapes),)),
        ],
        2 * tiles * tokens * width * width,
        limit=12,
    )


def dpre_kernel(scal, cot, gp, w, dpre, sums):
    tiles, tokens, width = gp.shape

    def down(t):
        d = (dot_nt(cot[...], w[tile_of(t, width), :]) * gp[t].astype(F32)).astype(BF16)
        dpre[t] = d
        sums[pl.ds(t, 1), :] = jnp.sum(d.astype(F32), axis=0, keepdims=True)

    loop(tiles, down)


def dpre_call(scal, cot, gp, w):
    tiles, tokens, width = gp.shape
    return call(
        dpre_kernel,
        "dpre",
        (scal, cot, gp, w),
        [],
        [kept(gp.shape), kept((8, width), F32)],
        [],
        [],
        2 * tiles * tokens * width * width,
        alias={2: 0},
        limit=8,
    )


def up_grad_kernel(load, store, n_p, scal, xn, dpre, *refs):
    w, *g_refs, g, wsem, sem = refs[n_p:]
    load(scal, refs[:n_p], w, wsem, (3,))

    def grad(t):
        g[t] = dot_tn(xn[...], dpre[t]).astype(BF16)
        store(scal, g, g_refs, sem, t)

    loop(dpre.shape[0], grad)
    whole_wait(w, wsem.at[3])()
    stored(g_refs, sem)


def up_grad_call(scal, xn, dpre, pieces, load, store, g_shapes):
    tiles, tokens, width = dpre.shape
    return call(
        functools.partial(up_grad_kernel, load, store, len(pieces)),
        "up_grad",
        (scal, xn, dpre),
        pieces,
        [kept((1, width, width))],
        g_shapes,
        [
            pltpu.VMEM((tiles, width, width), BF16),
            pltpu.SemaphoreType.DMA((4,)),
            pltpu.SemaphoreType.DMA((len(g_shapes),)),
        ],
        2 * tiles * tokens * width * width,
        limit=10,
    )


def input_grad_kernel(scal, x, cot, dn, dpre, vec, wu, sums, dx_ref, dx, sem):
    tiles, tokens, width = dpre.shape
    sums[...] = jnp.zeros_like(sums)

    def step(i):
        r = rows_of(i, 256)
        dnr = dn[r, :]
        for t in range(tiles):
            dnr += dot_nt(dpre[t, r, :], wu[t])
        standard, inv = norm_rows(x[r, :])
        sums[0:1, :] += jnp.sum(dnr * standard, axis=0, keepdims=True)
        gs = dnr * vec[0:1, :]
        mean_g = jnp.mean(gs, axis=1, keepdims=True)
        mean_p = jnp.mean(gs * standard, axis=1, keepdims=True)
        dx[r, :] = (cot[r, :].astype(F32) + inv * (gs - mean_g - standard * mean_p)).astype(BF16)

    loop(tokens // 256, step, lambda i: send_rows(dx, dx_ref, i, 256, sem))
    whole_wait(dx_ref, sem)()


def input_grad_call(scal, x, cot, dn, dpre, vec, wu):
    tiles, tokens, width = dpre.shape
    return call(
        input_grad_kernel,
        "input_grad",
        (scal, x, cot, dn, dpre, vec, wu),
        [],
        [kept((8, width), F32)],
        [sds((tokens // 512, 512, width))],
        [pltpu.VMEM((tokens, width), BF16), pltpu.SemaphoreType.DMA],
        2 * (tiles + 3) * tokens * width * width,
        limit=8,
    )


def out_kernel(scal, x, o, act, vec, wo, wd, out_ref, out, sem):
    tiles, tokens, width = act.shape

    def step(i):
        r = rows_of(i, 512)
        total = x[r, :].astype(F32) + vec[3:4, :] + dot_nn(o[r, :], wo[0])
        for t in range(tiles):
            total += dot_nn(act[t, r, :], wd[tile_of(t, width), :])
        out[r, :] = total.astype(BF16)

    loop(tokens // 512, step, lambda i: send_rows(out, out_ref, i, 512, sem))
    whole_wait(out_ref, sem)()


def out_call(scal, x, o, act, vec, wo, wd):
    tiles, tokens, width = act.shape
    (out,) = call(
        out_kernel,
        "out",
        (scal, x, o, act, vec, wo, wd),
        [],
        [],
        [sds((tokens // 512, 512, width))],
        [pltpu.VMEM((tokens, width), BF16), pltpu.SemaphoreType.DMA],
        2 * (tiles + 1) * tokens * width * width,
        limit=8,
    )
    return out


def swap(value, mask):
    return lax.ppermute(value, "wide", [(i, i ^ mask) for i in range(16)])


def swap_y(value):
    return lax.ppermute(value, "narrow", [(0, 1), (1, 0)])


def slots():
    for part in range(2):
        for i in range(2):
            for s in range(2):
                half, side = (i, s) if part == 0 else (s, i)
                for k in range(4):
                    yield part, i, s * 4 + k, half, side, k


def device_of(scal, k, side, core):
    return ((scal[1] ^ k) * 2 + (scal[2] ^ side)) * 2 + (scal[3] ^ core)


def behind(value, *marks):
    return lax.optimization_barrier((value, marks))[0]


def gather_z(value):
    return [swap(value, k << 2) for k in (1, 2, 3)]


def gather_first(za, zb):
    return swap(za, 2), swap_y(zb), swap_y(za), swap(zb, 2)


def gather_second(xa, yb):
    return swap_y(xa), swap(yb, 2)


def pieces_of(za, zb, first, second):
    xa, yb, ya, xb = first
    return [za, xa, ya, second[0], zb, xb, yb, second[1]]


def join_job(values):
    def fn(held, near, outs):
        size = near[0].shape[0]
        for i, v in enumerate(near):
            at = slice(i * size, (i + 1) * size)
            if v.ndim == 3:
                outs[0][at, : v.shape[1], :] = v[...]
            else:
                outs[0][at] = v[...]

    return fn, [], values, [kept((len(values) * values[0].shape[0], *values[0].shape[1:]))]


def mix(name, jobs):
    held = [v for job in jobs for v in job[1]]
    near = [v for job in jobs for v in job[2]]
    outs = [o for job in jobs for o in job[3]]

    def kernel(*refs):
        at = len(near) + len(held)
        scratch = refs[at + len(outs) :]
        copies = [
            pltpu.make_async_copy(refs[len(near) + i].at[:, pl.ds(v[1], v[2])], scratch[i], scratch[-1].at[i])
            for i, v in enumerate(held)
        ]
        for cp in copies:
            cp.start()
        h = n = o = 0
        for fn, job_h, job_n, job_o in jobs:
            for i in range(len(job_h)):
                copies[h + i].wait()
            fn(
                scratch[h : h + len(job_h)],
                refs[n : n + len(job_n)],
                refs[at + o : at + o + len(job_o)],
            )
            h, n, o = h + len(job_h), n + len(job_n), o + len(job_o)

    got = pl.pallas_call(
        kernel,
        name=name,
        out_shape=outs,
        in_specs=[VMEM] * len(near) + [HBM] * len(held),
        out_specs=[VMEM] * len(outs),
        scratch_shapes=[pltpu.VMEM((v.shape[0], size, *v.shape[2:]), v.dtype) for v, _, size in held]
        + [pltpu.SemaphoreType.DMA((max(len(held), 1),))],
        compiler_params=pltpu.CompilerParams(vmem_limit_bytes=8 << 20),
        cost_estimate=pl.CostEstimate(flops=1 << 20, bytes_accessed=1 << 20, transcendentals=0),
    )(
        *[pltpu.with_memory_space_constraint(v, pltpu.VMEM) for v in near],
        *[pltpu.with_memory_space_constraint(v[0], pltpu.HBM) for v in held],
    )
    split, at = [], 0
    for job in jobs:
        split.append(got[at : at + len(job[3])])
        at += len(job[3])
    return split


def total(*parts):
    return sum(v.astype(F32) for v in parts)


def stack_job(values):
    def fn(held, near, outs):
        for k, v in enumerate(near):
            for i in range(2):
                outs[i][k] = v[i]

    return fn, [], list(values), [kept((len(values), *values[0].shape[1:]))] * 2


def vector_job(sums_a, sums_d, sums_x, wide, rows):
    width = sums_a.shape[1]

    def spread(rows_in, per):
        flat = jnp.concatenate([rows_in[w * per // width][None] for w in range(wide)])
        col = lax.broadcasted_iota(jnp.int32, (wide, width), 1)
        own = lax.broadcasted_iota(jnp.int32, (wide, width), 0) * per % width
        flat = jnp.where((col >= own) & (col < own + per), flat, 0.0)
        pick = lax.broadcasted_iota(jnp.int32, (width, per), 0) % per
        pick = (pick == lax.broadcasted_iota(jnp.int32, (width, per), 1)).astype(BF16)
        got = jnp.zeros((wide, per), F32)
        for _ in range(3):
            high = flat.astype(BF16)
            flat = flat - high.astype(F32)
            got += dot_nn(high, pick)
        return got

    def fn(held, near, outs):
        a, d, x, scal = near
        tiles = 4
        at = 0
        for got in (
            spread([x[0]], rows),
            spread([a[0], a[1]], 2 * rows),
            spread([d[t] for t in range(tiles)], tiles * rows),
            spread([a[2]], rows),
        ):
            outs[4][:, at : at + got.shape[1]] = got
            at += got.shape[1]
        for k in range(4):
            outs[k][...] = jnp.zeros_like(outs[k])
            for r in range(4):
                outs[k][r : r + 1, :] = outs[4][pl.ds((scal[1] ^ k) * 4 + r, 1), :]

    return fn, [], [sums_a, sums_d, sums_x], [kept((8, 8 * rows), F32)] * 4 + [kept((wide, 8 * rows), F32)]


def add_job(values):
    def fn(held, near, outs):
        outs[0][...] = sum(near[i][...] for i in range(len(values)))

    return fn, [], list(values), [kept(values[0].shape, F32)]


def vector_job(sums_a, sums_d, sums_x):
    def fn(held, near, outs):
        a, d, x = near
        outs[0][0:1, :] = x[0:1, :]
        outs[0][1:3, :] = a[0:2, :]
        outs[0][3:7, :] = d[0:4, :]
        outs[0][7:8, :] = a[2:3, :]

    return fn, [], [sums_a, sums_d, sums_x], [kept(sums_a.shape, F32)]


def sum1_job(keep1, got1):
    def fn(held, near, outs):
        for i in range(2):
            outs[i][...] = total(held[0][i], near[0][i]).astype(BF16)

    return fn, [(keep1, 0, keep1.shape[1])], [got1], [kept(keep1.shape[1:])] * 2


def sum2_job(keep0, got0, got):
    half = keep0.shape[1] // 2

    def fn(held, near, outs):
        for i in range(2):
            outs[i][...] = total(held[0][i], near[0][i, half:], near[1 + i][half:]).astype(BF16)

    return fn, [(keep0, half, half)], [got0, *got], [kept((half, *keep0.shape[2:]))] * 2


def sum3_job(keep0, got0, got, got2):
    half = keep0.shape[1] // 2

    def fn(held, near, outs):
        for k in range(half):
            for i in range(2):
                outs[k][i] = total(held[0][i, k], near[0][i, k], near[1 + i][k], near[3 + i][k]).astype(BF16)

    return fn, [(keep0, 0, half)], [got0, *got, *got2], [kept((2, *keep0.shape[2:]))] * half


def sum4_job(own, got):
    def fn(held, near, outs):
        outs[0][...] = total(*[near[i][...] for i in range(1 + len(got))]).astype(BF16)

    return fn, [], [own, *got], [kept(own.shape)]


def place_kernel(scal, a_mine, a_other, d_mine, d_other, joined_ref, out, down, joined, sem):
    _, rows, width = a_mine.shape

    def place(half, a, d):
        for p in range(2):
            block = half * 2 + p
            down[pl.ds(block * rows, rows), :] = d[p].astype(F32)
            if block < 3:
                joined[block] = a[p].astype(F32)
                dst = joined_ref.at[:, block * width : (block + 1) * width]
                pltpu.make_async_copy(joined.at[block], dst, sem).start()
            else:
                out[...] = a[p].astype(F32)

    @pl.when(scal[0] == 0)
    def _():
        place(0, a_mine, d_mine)
        place(1, a_other, d_other)

    @pl.when(scal[0] != 0)
    def _():
        place(1, a_mine, d_mine)
        place(0, a_other, d_other)

    whole_wait(joined, sem)()


def place_call(scal, parts):
    _, rows, width = parts[0].shape
    return pl.pallas_call(
        place_kernel,
        name="place",
        out_shape=[sds((rows, 7 * width), F32), sds((rows, width), F32), sds((4 * rows, width), F32)],
        in_specs=[SMEM] + [VMEM] * 4,
        out_specs=[HBM, VMEM, VMEM],
        scratch_shapes=[pltpu.VMEM((3, rows, width), F32), pltpu.SemaphoreType.DMA],
        compiler_params=pltpu.CompilerParams(vmem_limit_bytes=8 << 20),
    )(scal, *[pltpu.with_memory_space_constraint(v, pltpu.VMEM) for v in parts])


def place_last_kernel(scal, placed, mine, other, v0, v1, v2, v3, joined_ref, gain, b_attn, b_mlp, b_out, wide, sem):
    _, rows, width = other.shape
    for i, ref in enumerate((mine, other)):
        for p in range(2):
            wide[i * 2 + p] = ref[p].astype(F32)
            at = pl.multiple_of((3 + (scal[0] ^ i) * 2 + p) * width, 128)
            pltpu.make_async_copy(wide.at[i * 2 + p], joined_ref.at[:, pl.ds(at, width)], sem).start()
    total = (v0[...] + v1[...]) + (v2[...] + v3[...])
    row = lax.broadcasted_iota(jnp.int32, total.shape, 0)
    dev = (scal[1] * 2 + scal[2]) * 2 + scal[3]
    for first, out in ((0, gain), (1, b_attn), (3, b_mlp), (7, b_out)):
        per = out.shape[0]
        share = width // per
        line = jnp.sum(jnp.where(row == first + dev // share, total, 0.0), axis=0, keepdims=True)
        line = jnp.broadcast_to(line, total.shape)
        line = pltpu.roll(line, (share - dev % share) % share * per, 1)
        out[...] = line[0, :per]
    whole_wait(wide, sem)()


def place_last_call(scal, placed, mine, other, vectors):
    _, rows, width = other.shape
    near = [pltpu.with_memory_space_constraint(v, pltpu.VMEM) for v in (mine, other, *vectors)]
    return pl.pallas_call(
        place_last_kernel,
        name="place_last",
        out_shape=[sds(placed.shape, F32)] + [sds((n * rows,), F32) for n in (1, 2, 4, 1)],
        in_specs=[SMEM, HBM] + [VMEM] * 6,
        out_specs=[HBM] + [VMEM] * 4,
        scratch_shapes=[pltpu.VMEM((4, *other.shape[1:]), F32), pltpu.SemaphoreType.DMA],
        compiler_params=pltpu.CompilerParams(vmem_limit_bytes=8 << 20),
        input_output_aliases={1: 0},
    )(scal, placed, *near)


def whole_wait(ref, sem):
    return pltpu.make_async_copy(ref, ref, sem).wait


def piece(refs, at, core, k, alone):
    if core == 0:
        return refs[at].at[k]
    if at in alone:
        return refs[9 + alone.index(at)].at[k]
    return refs[8].at[(at - sum(i < at for i in alone)) * 4 + k]


def load_columns(scal, refs, w, sem, blocks=(0, 1, 2, 3)):
    rows = w.shape[1] // 16

    def start(own):
        for block in blocks:
            for core in range(2):
                for part, _, _, half, side, k in slots():
                    if (own ^ half) * 2 + part != block:
                        continue
                    src = piece(refs, part * 4 + half * 2 + side, core, k, (3, 7)).at[pl.ds(0, rows), :]
                    dst = w.at[blocks.index(block), rows_at(device_of(scal, k, side, core) * rows, rows), :]
                    pltpu.make_async_copy(src, dst, sem.at[block]).start()

    @pl.when(scal[0] == 0)
    def _():
        start(0)

    @pl.when(scal[0] != 0)
    def _():
        start(1)


def load_half(which):
    def load(scal, refs, w, sem):
        def start(rel):
            for block in range(4):
                for core in range(2):
                    for part, _, _, half, side, k in slots():
                        src = piece(refs, part * 4 + half * 2 + side, core, k, (0, 4))
                        per, rows, width = src.shape
                        if half != rel or block // per != part:
                            continue
                        dev = device_of(scal, k, side, core)
                        if which == 0:
                            dst, tile = w.at[block, rows_at(dev * rows, rows), :], block
                        else:
                            dst, tile = w.at[rows_at((dev * 2 * per + block) * rows, rows), :], scal[1] ^ k
                        pltpu.make_async_copy(src.at[block % per], dst, sem.at[tile]).start()

        @pl.when(scal[0] == which)
        def _():
            start(0)

        @pl.when(scal[0] != which)
        def _():
            start(1)

    return load


def read_vectors(scal, refs, vec, b_mlp, buf, sem):
    width = vec.shape[1]
    rows = width // 16
    for core in range(2):
        for side in range(2):
            for k in range(4):
                src = piece(refs, side, core, k, (3, 7)).at[pl.ds(rows, 8), :]
                pltpu.make_async_copy(src, buf.at[device_of(scal, k, side, core)], sem).start()
    yield
    whole_wait(buf, sem)()
    values = buf[:, 0, :].astype(F32)
    devices = values.shape[0]

    def line(at, per):
        pick = lax.broadcasted_iota(jnp.int32, (per, width), 1) % per
        pick = (pick == lax.broadcasted_iota(jnp.int32, (per, width), 0)).astype(BF16)
        flat = dot_nn(values[:, at : at + per].astype(BF16), pick)
        dev = lax.broadcasted_iota(jnp.int32, flat.shape, 0)
        col = lax.broadcasted_iota(jnp.int32, flat.shape, 1)
        count = devices * per // width
        share = devices // count
        keep = col // per == dev % share
        return [
            jnp.sum(jnp.where(keep & (dev // share == i), flat, 0.0), axis=0, keepdims=True) for i in range(count)
        ]

    lines = line(0, rows) + line(rows, 2 * rows) + line(7 * rows, rows)
    vec[...] = jnp.zeros_like(vec)
    for i, v in enumerate(lines):
        vec[i : i + 1, :] = v
    for i, v in enumerate(line(3 * rows, 4 * rows)):
        b_mlp[i : i + 1, :] = v
    yield


def rows_at(base, rows):
    return pl.ds(pl.multiple_of(base, 16), rows)


def stored(refs, sem):
    for i, r in enumerate(refs):
        whole_wait(r, sem.at[i])()


def store_block(scal, g, refs, sem, t):
    half, part = scal[0] ^ (t // 2), t % 2
    rows = refs[0].shape[2]

    def send(at, core, side, k, slot, p):
        src = g.at[t, rows_at(device_of(scal, k, side, core) * rows, rows), :]
        pltpu.make_async_copy(src, refs[at].at[p, slot], sem.at[at]).start()

    for i in range(2):

        @pl.when((part == 0) & (half == i))
        def _(i=i):
            for core in range(2):
                for side in range(2):
                    for k in range(4):
                        send(core * 2 + i, core, side, k, side * 4 + k, 0)

    @pl.when(part == 1)
    def _():
        for core in range(2):
            for side in range(2):
                for k in range(4):
                    send(core * 2 + side, core, side, k, half * 4 + k, 1)


def store_rows(scal, g, refs, sem, t):
    k = scal[1] ^ t
    rows = refs[0].shape[2]
    for core in range(2):
        for side in range(2):
            dev = (t * 2 + (scal[2] ^ side)) * 2 + (scal[3] ^ core)
            for half in range(2):
                for part in range(2):
                    i, s = (half, side) if part == 0 else (side, half)
                    at = core * 2 + i
                    src = g.at[rows_at((dev * 4 + (scal[0] ^ half) * 2 + part) * rows, rows), :]
                    pltpu.make_async_copy(src, refs[at].at[part, s * 4 + k], sem.at[at]).start()


def load_whole_blocks(scal, refs, w, sem, blocks=(0, 1, 2, 3)):
    for i, b in enumerate(blocks):
        pltpu.make_async_copy(refs[b], w.at[i], sem.at[b]).start()


def load_whole_rows(scal, refs, w, sem):
    width = w.shape[1]
    for t in range(w.shape[0] // width):
        r = tile_of(t, width)
        pltpu.make_async_copy(refs[0].at[r, :], w.at[r, :], sem.at[t]).start()


def store_whole_blocks(scal, g, refs, sem, t):
    for i, r in enumerate(refs):

        @pl.when(t == i)
        def _(i=i, r=r):
            pltpu.make_async_copy(g.at[i], r, sem.at[i]).start()


def store_whole_rows(scal, g, refs, sem, t):
    r = tile_of(t, g.shape[1])
    pltpu.make_async_copy(g.at[r, :], refs[0].at[r, :], sem.at[0]).start()


def body(sizes, tokens, image_ids, cotangent, w_joined, w_out, w_mlp, norm_gain, bias_attn, bias_mlp, bias_out):
    micro, length, width = tokens.shape
    narrow, wide = sizes
    paired = narrow == 2 and wide == 16
    rows = width // wide
    tiles = w_mlp.shape[0] // rows
    x = tokens.reshape(micro * length, width)
    cot = cotangent.reshape(micro * length, width)
    n = lax.axis_index("narrow")
    w = lax.axis_index("wide")
    last = image_ids.reshape(-1, 512)[:, -1]
    scal = [n, w >> 2, (w >> 1) & 1, w & 1] + [jnp.int32(0)] * 4 + [last[b] for b in range(last.shape[0])]
    scal = jnp.stack([jnp.asarray(s, jnp.int32) for s in scal])
    vec_own = jnp.concatenate([norm_gain, bias_attn, bias_mlp, bias_out])

    def vectors(vec):
        vec = vec.astype(F32)
        b_at = 3 * rows
        b_mlp = vec[:, b_at : b_at + tiles * rows].reshape(tiles, width)
        head = [
            vec[:, :rows].reshape(1, width),
            vec[:, rows:b_at].reshape(2, width),
            vec[:, b_at + tiles * rows :].reshape(1, width),
            jnp.zeros((4, width), F32),
        ]
        return jnp.concatenate(head), b_mlp

    def vector_grads(sums_a, sums_d, sums_x):
        return jnp.concatenate(
            [
                sums_x[0].reshape(wide, rows),
                sums_a[:2].reshape(wide, 2 * rows),
                sums_d[:tiles].reshape(wide, tiles * rows),
                sums_a[2].reshape(wide, rows),
            ],
            axis=1,
        )

    if not paired:
        full = lax.all_gather(w_joined, "wide", axis=0, tiled=True)
        parts = [full[:, i * width : (i + 1) * width] for i in range(3 + tiles)]
        attn_w = parts[:3] + [lax.all_gather(w_out, "wide", axis=0, tiled=True)]
        up_w = parts[3:]
        down_w = [lax.all_gather(w_mlp, "wide", axis=0, tiled=True)]
        vec, b_mlp = vectors(lax.all_gather(vec_own, "wide", axis=0))
        square = [sds((width, width))]
        xn, q, k, v, da, wa = project_call(scal, x, cot, vec, attn_w, load_whole_blocks)
        part = core_call(0, scal, q, k, v, da, wa)
        for b in range(1, last.shape[0]):
            part = core_call(b, scal, q, k, v, da, wa, *part)
        o, d, dn = part
        sums_a, *g_attn = attn_grad_call(scal, xn, o, d, cot, store_whole_blocks, square * 4)
        act, gp, wu = up_call(0, tiles // 2, scal, xn, b_mlp, (), up_w, load_whole_blocks)
        act, gp = up_call(tiles // 2, tiles - tiles // 2, scal, xn, b_mlp, (act, gp, wu), [], None)
        wd, *g_down = down_grad_call(
            scal, act, cot, down_w, load_whole_rows, store_whole_rows, [sds((tiles * width, width))]
        )
        dpre, sums_d = dpre_call(scal, cot, gp, wd)
        wo, *g_up = up_grad_call(scal, xn, dpre, attn_w, load_whole_blocks, store_whole_blocks, square * tiles)
        sums_x, d_x = input_grad_call(scal, x, cot, dn, dpre, vec, wu)
        out = out_call(scal, x, o, act, vec, wo, wd)

        def reduce(g):
            g = lax.psum_scatter(g.astype(F32), "wide", scatter_dimension=0, tiled=True)
            return lax.psum(g, "narrow")

        grad_joined = reduce(jnp.concatenate([*g_attn[:3], *g_up], axis=1))
        grad_out = reduce(g_attn[3])
        grad_mlp = reduce(g_down[0])
        vg = reduce(vector_grads(sums_a, sums_d, sums_x))[0]
        vg = jnp.split(vg, [rows, 3 * rows, (3 + tiles) * rows])
    else:
        col = lambda i: w_joined[:, i * width : (i + 1) * width]
        pair = lambda f: jnp.stack([jnp.where(n == 0, f(0), f(2)), jnp.where(n == 0, f(1), f(3))])
        half_a, half_b = [jnp.where(n == 0, f, g) for f, g in ((col(0), col(2)), (col(1), w_out))]
        v_rows = jnp.pad(vec_own, (0, width - vec_own.shape[0]))
        half = jnp.concatenate([half_a, jnp.broadcast_to(v_rows, (8, width)), half_b])
        got = gather_z(half)
        za = jnp.stack([t[: rows + 8] for t in (half, *got)])
        zb = jnp.stack([t[rows + 8 :] for t in (half, *got)])
        c_half = jnp.stack([jnp.where(n == 0, col(3 + t), w_mlp[t * rows : (t + 1) * rows]) for t in range(tiles)])
        c_half = behind(c_half.reshape(2, tiles // 2, rows, width), za, zb)
        first = gather_first(za, zb)
        c2 = swap(c_half, 8)
        first, c2, c_half = lax.optimization_barrier((first, c2, c_half))
        second = gather_second(*first[:2])
        own = pieces_of(za, zb, first, second)
        ((joined,),) = mix("join_a", [join_job([own[i] for i in (0, 1, 2, 4, 5, 6)])])
        joined, c1, c3 = swap(joined, 1), swap(c_half, 4), swap(c_half, 12)
        second, joined, c1, c3 = lax.optimization_barrier((second, joined, c1, c3))
        own = pieces_of(za, zb, first, second)
        attn_w = [*own, joined, swap(second[0], 1), swap(second[1], 1)]
        cza, czb = [jnp.stack([t[i] for t in (c_half, c1, c2, c3)]) for i in range(2)]
        c_xa, c_yb = swap(cza, 2), swap_y(czb)
        x_p, attn_w, cza, czb = lax.optimization_barrier((x, attn_w, cza, czb))
        c_first = (c_xa, c_yb, swap_y(cza), swap(czb, 2))
        xn, q, k, v, da, wa, vec, b_mlp = project_call(scal, x_p, cot, None, attn_w, load_columns, read_vectors)
        part = core_call(0, scal, q, k, v, da, wa)

        part, c_xa, c_yb, z_a, czb_b = lax.optimization_barrier((part, *c_first[:2], swap(cza, 1), czb))
        c_second = gather_second(c_xa, c_yb)
        czs = [z_a, swap(czb_b, 1)]
        o, d, dn = core_call(1, scal, q, k, v, da, wa, *part)

        d, c_second, czs, c_first = lax.optimization_barrier((d, c_second, czs, (c_xa, c_yb, *c_first[2:])))
        c_own = pieces_of(cza, czb, c_first, c_second)
        ((c_joined,),) = mix("join_c", [join_job([t for t in c_own if t is not cza and t is not czb])])
        d, c_joined = lax.optimization_barrier((d, c_joined))
        c_other = swap(c_joined, 1)
        attn_shapes = [sds((2, 8, rows, width))] * 4
        sums_a, *ga = attn_grad_call(scal, xn, o, d, cot, store_block, attn_shapes)

        c_other, ga = behind((c_other, ga), sums_a)
        xn_u, ga, c_own, c_other = lax.optimization_barrier((xn, ga, c_own, c_other))
        a_got1, a_got0 = swap(ga[3], 1), swap(ga[2], 1)
        half_tiles = tiles // 2
        c_all = [*c_own, c_other, *czs]
        act, gp, wu = up_call(0, half_tiles, scal, xn_u, b_mlp, (), c_all, load_half(0))

        a_got1, a_got0 = behind((a_got1, a_got0), gp)
        ((sa, sb),) = mix("sums_1", [sum1_job(ga[1], a_got1)])
        act, sa, sb = lax.optimization_barrier((act, sa, sb))
        a_xy = swap_y(sa), swap(sb, 2)
        act, gp = up_call(half_tiles, half_tiles, scal, xn_u, b_mlp, (act, gp, wu), [], None)
        wd, *gd = down_grad_call(
            scal, act, cot, c_all, load_half(1), store_rows, attn_shapes
        )

        a_xy = behind(a_xy, gd)
        ((sa, sb),) = mix("sums_2", [sum2_job(ga[0], a_got0, a_xy)])
        gp, sa, sb, gd = lax.optimization_barrier((gp, sa, sb, gd))
        a_yx = swap(sa, 2), swap_y(sb)
        d_got1, d_got0 = swap(gd[3], 1), swap(gd[2], 1)
        dpre, sums_d = dpre_call(scal, cot, gp, wd)

        a_yx, d_got1, d_got0 = behind((a_yx, d_got1, d_got0), dpre)
        a_t, (sa, sb) = mix("sums_3", [sum3_job(ga[0], a_got0, a_xy, a_yx), sum1_job(gd[1], d_got1)])
        dpre_g, a_t, sa, sb = lax.optimization_barrier((dpre, a_t, sa, sb))
        d_xy = swap_y(sa), swap(sb, 2)
        a_z = [swap(a_t[k], k << 2) for k in (1, 2, 3)]
        wo, *gu = up_grad_call(scal, xn, dpre_g, attn_w, load_columns, store_block, attn_shapes)

        a_z, d_xy = behind((a_z, d_xy), gu)
        (a_sum,), (sa, sb) = mix("sums_4", [sum4_job(a_t[0], a_z), sum2_job(gd[0], d_got0, d_xy)])
        x_i, sa, sb, gu, a_sum = lax.optimization_barrier((x, sa, sb, gu, a_sum))
        u_got1, u_got0 = swap(gu[3], 1), swap(gu[2], 1)
        d_yx = swap(sa, 2), swap_y(sb)
        a_other = swap_y(a_sum)
        sums_x, d_x = input_grad_call(scal, x_i, cot, dn, dpre, vec, wu)

        d_yx, u_got1, u_got0, a_other = behind((d_yx, u_got1, u_got0, a_other), d_x)
        (sa, sb), d_t, (v_own,) = mix(
            "sums_5",
            [
                sum1_job(gu[1], u_got1),
                sum3_job(gd[0], d_got0, d_xy, d_yx),
                vector_job(sums_a, sums_d, sums_x),
            ],
        )
        x_o, sa, sb, d_t = lax.optimization_barrier((x, sa, sb, d_t))
        u_xy = swap_y(sa), swap(sb, 2)
        d_z = [swap(d_t[k], k << 2) for k in (1, 2, 3)]
        out = out_call(scal, x_o, o, act, vec, wo, wd)

        u_xy, d_z, v_own = behind((u_xy, d_z, v_own), out)
        (sa, sb), (d_sum,) = mix("sums_6", [sum2_job(gu[0], u_got0, u_xy), sum4_job(d_t[0], d_z)])
        sa, sb, d_sum, v_own = lax.optimization_barrier((sa, sb, d_sum, v_own))
        u_yx = swap(sa, 2), swap_y(sb)
        v_got = [swap(v_own, k << 2) for k in (1, 2, 3)]
        u_t, (v_sum,) = mix("sums_7", [sum3_job(gu[0], u_got0, u_xy, u_yx), add_job([v_own, *v_got])])
        u_t, v_sum, d_sum = lax.optimization_barrier((u_t, v_sum, d_sum))
        u_z = [swap(u_t[k], k << 2) for k in (1, 2, 3)]
        v_other, d_other = swap_y(v_sum), swap_y(d_sum)
        placed, grad_out, grad_mlp = place_call(scal, [a_sum, a_other, d_sum, d_other])
        u_z, placed = lax.optimization_barrier((u_z, placed))
        (u_sum,), (v_sum,) = mix("sums_8", [sum4_job(u_t[0], u_z), add_job([v_sum, v_other])])
        u_other = swap_y(u_sum)
        v_all = [v_sum, *[swap(v_sum, i) for i in (1, 2, 3)]]
        grad_joined, *vg = place_last_call(scal, placed, u_sum, u_other, v_all)
    return (out.reshape(tokens.shape), d_x.reshape(tokens.shape), grad_joined, grad_out, grad_mlp, *vg)


def solution(mesh):
    sizes = (mesh.shape["narrow"], mesh.shape["wide"])
    rows = P(None, ("narrow", "wide"), None)
    placed = (rows, P(None, ("narrow", "wide")), rows) + (P("wide", None),) * 3 + (P("wide"),) * 4
    return jax.shard_map(
        functools.partial(body, sizes),
        mesh=mesh,
        in_specs=placed,
        out_specs=(rows, rows) + (P("wide", None),) * 3 + (P("wide"),) * 4,
        check_vma=False,
    )
```
